128 devices in a mesh: req: 8 (over x, z_lo), blk: 16 (over y, z_hi, core).
Axes of the slice: x: 4, y: 4, z: 4 (z_hi: 2, z_lo: 2; z = z_hi * 2 + z_lo), core: 2. Of those that a mesh axis runs over, the one named last changes fastest.
Arguments:
- new_states: bfloat16 [4096, 1024], P('req'), may hold values from -50 to 50
- encoder_out: bfloat16 [4096, 1024], P('req'), may hold values from -90 to 90
- cache_in: bfloat16 [8, 4096, 2048], P(None, 'blk', 'req'), may hold values from -90 to 90
- slot_order: int32 [8], replicated, may hold values from 0 to 7, each once
- new_lengths: int32 [8], replicated, may hold values from 1 to 512, 2560 in all
- cache_lengths: int32 [8], replicated, may hold values from 1 to 4096, 16384 in all
- enc_lengths: int32 [8], replicated, may hold values from 1 to 512, 3072 in all
- bucket_of: int32 [4608], replicated, may hold values from 0 to 31, as said below
- rel_bias: float32 [32, 16], replicated, may hold values from -4 to 4
- norm_gain: float32 [3, 1024], replicated, may hold values from 0.25 to 1.75
- self_q: bfloat16 [1024, 1024], P('req', 'blk'), may hold values from -0.09375 to 0.09375
- self_kv: bfloat16 [1024, 2, 1024], P('req', None, 'blk'), may hold values from -0.1875 to 0.1875
- self_out: bfloat16 [1024, 1024], P('blk', 'req'), may hold values from -0.1875 to 0.1875
- cross_q: bfloat16 [1024, 1024], P('req', 'blk'), may hold values from -0.09375 to 0.09375
- cross_kv: bfloat16 [1024, 2, 1024], P('req', None, 'blk'), may hold values from -0.1875 to 0.1875
- cross_out: bfloat16 [1024, 1024], P('blk', 'req'), may hold values from -0.1875 to 0.1875
- ff_in: bfloat16 [1024, 2, 2816], P('req', None, 'blk'), may hold values from -0.1875 to 0.1875
- ff_out: bfloat16 [2816, 1024], P('blk', 'req'), may hold values from -0.109375 to 0.109375
Outputs:
- layer_out: bfloat16 [4096, 1024], P('req')
- cache_out: bfloat16 [8, 4096, 2048], P('req', None, 'blk')
The draws below stay inside these ranges and needn't reach their ends.
Inputs may be any that keep to these rules, and one draw needn't show every extreme that they name: Slot s holds request slot_order[s]; every request is held once. `new_lengths`: they sum to 2560 and the most is 512. `cache_lengths`: they sum to 16384 and the most is 4096. `enc_lengths`: they sum to 3072 and the most is 512. `bucket_of`: non-decreasing in the distance, 0 at distance 0 and 31 at distance 4608 - 1.
All inputs are finite; a program needn't handle non-finite values.
Results may differ from the reference program's by a relative error of at most 0.035.
Values may be sent and summed in bfloat16 or wider, within the bound.
A program may use at most 128 MiB of HBM per device.

```python
import math
import jax
import jax.numpy as jnp
import numpy as np
from jax import lax

D = 1024
H = 16
HD = 64
FF = 2816
NBUCKET = 32
Q = 512
CTX = 4096
ENC = 512
REQUESTS = 8
ROWS = 4096
ENC_ROWS = 4096
SPAN = 4608
N_BLK = 16


def draw_new_states(key, part):
    first, second, third = jax.random.split(key, 3)
    col_scale = jnp.exp(jax.random.uniform(third, (1, D), jnp.float32, -1.15, 1.15))
    base = jnp.clip(jax.random.normal(first, (ROWS, D), jnp.float32), -5.0, 5.0)
    row_scale = jnp.exp(jax.random.uniform(second, (ROWS, 1), jnp.float32, -1.15, 1.15))
    return (base * row_scale * col_scale).astype(jnp.bfloat16)


def draw_encoder_out(key, part):
    first = jax.random.fold_in(key, 0)
    third = jax.random.fold_in(key, 2)
    col_scale = jnp.exp(jax.random.uniform(third, (1, D), jnp.float32, -0.7, 0.7))
    base = jnp.clip(jax.random.normal(first, (ENC_ROWS, D), jnp.float32), -5.0, 5.0) * col_scale
    return base.astype(jnp.bfloat16)


def draw_cache_in(key, part):
    first = jax.random.fold_in(key, 0)
    base = jnp.clip(jax.random.normal(first, (REQUESTS, CTX, H, 2, HD), jnp.float32), -5.0, 5.0)
    return base.reshape(REQUESTS, CTX, H * 2 * HD).astype(jnp.bfloat16)


def draw_bucket_of(key, part):
    distance = jnp.arange(SPAN, dtype=jnp.int32)
    rolled = jax.random.randint(key, (SPAN,), 0, jnp.maximum(distance, 1))
    stepped = jnp.where(distance < 8, jnp.where(distance > 0, 1, 0), jnp.where(rolled < 4, 1, 0)).astype(jnp.int32)
    counted = jnp.cumsum(stepped).astype(jnp.int32)
    counted = jnp.where(distance == SPAN - 1, NBUCKET - 1, counted)
    return jnp.minimum(counted, NBUCKET - 1).astype(jnp.int32)


def shard_levels(stream_key, dims, shards, least, top_value):
    level, own = 1.0, jax.random.fold_in(stream_key, 6)
    for dim, blocks in shards:
        steps = jnp.exp(jax.random.uniform(jax.random.fold_in(own, dim), (blocks,), jnp.float32, least / len(shards), top_value / len(shards)))
        level = level * jnp.repeat(steps, dims[dim] // blocks).reshape([-1 if axis == dim else 1 for axis in range(len(dims))])
    return level


def length_profile(count, total, most, lean):
    loads = [(1 << 20) // math.isqrt(rank ** lean) + 1 for rank in range(2, count + 1)]
    rest, given = total - most - (count - 1), [1] * (count - 1)
    while rest > 0:
        movable = [i for i in range(count - 1) if given[i] < most]
        pool, left = sum([loads[i] for i in movable]), rest
        for i in movable:
            extra = min(most - given[i], max(1, left * loads[i] // pool), rest)
            given[i] = given[i] + extra
            rest = rest - extra
    return np.array([most] + given)


def ragged_sizes(key, amount, total, bound, slope):
    if amount == 2:
        one = jax.random.randint(key, (), max(1, total - bound), min(bound, total - 1) + 1)
        return jnp.stack([one, total - one])
    sizes = jnp.asarray(length_profile(amount, total, bound, slope), jnp.int32)
    twos = (amount - 1) // 2
    giver, sink = sizes[1:1 + 2 * twos:2], sizes[2:2 + 2 * twos:2]
    slack = jnp.minimum(giver - 1, bound - sink)
    shifted = jax.random.randint(jax.random.fold_in(key, 1), (twos,), 0, 1 << 20) % (slack + 1)
    sizes = sizes.at[1:1 + 2 * twos:2].set(giver - shifted).at[2:2 + 2 * twos:2].set(sink + shifted)
    return sizes[jax.random.permutation(jax.random.fold_in(key, 2), amount)]


def normal_values(stream_key, extent, scale, limit, pieces=(), held_as=jnp.bfloat16):
    result = scale * jax.random.normal(stream_key, extent, jnp.float32)
    if pieces:
        result = result * shard_levels(stream_key, extent, pieces, -0.22, 0.18)
    return jnp.clip(result, -limit, limit).astype(held_as)


def setup_inputs(seed: int = 0) -> dict:
    seeds = jax.random.split(jax.random.key(seed), 19)
    return {
        "new_states": draw_new_states(jax.random.fold_in(seeds[18], 71), 0),
        "encoder_out": draw_encoder_out(jax.random.fold_in(seeds[18], 71), 0),
        "cache_in": draw_cache_in(jax.random.fold_in(seeds[18], 71), 0),
        "slot_order": jax.random.permutation(seeds[3], REQUESTS).astype(jnp.int32),
        "new_lengths": ragged_sizes(seeds[4], REQUESTS, 5 * REQUESTS * Q // 8, Q, 2).astype(jnp.int32),
        "cache_lengths": ragged_sizes(seeds[5], REQUESTS, REQUESTS * CTX // 2, CTX, 2).astype(jnp.int32),
        "enc_lengths": ragged_sizes(seeds[6], REQUESTS, 3 * REQUESTS * ENC // 4, ENC, 1).astype(jnp.int32),
        "bucket_of": draw_bucket_of(jax.random.fold_in(seeds[18], 71), 0),
        "rel_bias": normal_values(seeds[8], (NBUCKET, H), 1.0, 4.0, (), jnp.float32),
        "norm_gain": jnp.clip(1.0 + 0.15 * jax.random.normal(seeds[9], (3, D), jnp.float32), 0.25, 1.75),
        "self_q": normal_values(seeds[10], (D, H * HD), (4 * D) ** -0.5, 0.09375, ((0, 8), (1, 16))),
        "self_kv": normal_values(seeds[11], (D, 2, H * HD), D ** -0.5, 0.1875, ((0, 8), (2, 16))),
        "self_out": normal_values(seeds[12], (H * HD, D), (H * HD) ** -0.5, 0.1875, ((0, 16), (1, 8))),
        "cross_q": normal_values(seeds[13], (D, H * HD), (4 * D) ** -0.5, 0.09375, ((0, 8), (1, 16))),
        "cross_kv": normal_values(seeds[14], (D, 2, H * HD), D ** -0.5, 0.1875, ((0, 8), (2, 16))),
        "cross_out": normal_values(seeds[15], (H * HD, D), (H * HD) ** -0.5, 0.1875, ((0, 16), (1, 8))),
        "ff_in": normal_values(seeds[16], (D, 2, FF), D ** -0.5, 0.1875, ((0, 8), (2, 16))),
        "ff_out": normal_values(seeds[17], (FF, D), FF ** -0.5, 0.109375, ((0, 16), (1, 8))),
    }


EPSILON = 1e-06
NEG_FILL = -1e+30

def rms_rows(row_block, gain):
    mean_square = lax.optimization_barrier(jnp.mean(row_block * row_block, axis=-1, keepdims=True))
    return (row_block * lax.rsqrt(mean_square + EPSILON) * gain).astype(jnp.bfloat16)

def softmax_rows(scores):
    row_top = lax.optimization_barrier(jnp.max(scores, axis=-1, keepdims=True))
    weights = jnp.exp(scores - row_top)
    return (weights / lax.optimization_barrier(jnp.sum(weights, axis=-1, keepdims=True))).astype(jnp.bfloat16)

def group_product(left_side, right_side, groups):
    row_count = left_side.shape[0]
    left_groups = left_side.reshape(row_count, groups, -1).astype(jnp.float32)
    right_groups = right_side.reshape(groups, -1, right_side.shape[1]).astype(jnp.float32)
    partials = jnp.einsum('tgk,gkd->tgd', left_groups, right_groups)
    rounded = lax.optimization_barrier(partials.astype(jnp.bfloat16))
    return lax.optimization_barrier(jnp.sum(rounded.astype(jnp.float32), axis=1))

def reference(new_states, encoder_out, cache_in, slot_order, new_lengths, cache_lengths, enc_lengths, bucket_of, rel_bias, norm_gain, self_q, self_kv, self_out, cross_q, cross_kv, cross_out, ff_in, ff_out):
    cache_out = jnp.take(cache_in, slot_order, axis=0)
    onehot = (bucket_of[:, None] == jnp.arange(NBUCKET, dtype=jnp.int32)[None, :]).astype(jnp.float32)
    bias_dist = jnp.dot(onehot, rel_bias, precision=lax.Precision.HIGHEST).T
    slot_new = jnp.take(new_lengths, slot_order)
    slot_old = jnp.take(cache_lengths, slot_order)
    slot_enc = jnp.take(enc_lengths, slot_order)
    positions = jnp.arange(Q, dtype=jnp.int32)
    cached_ids = jnp.arange(CTX, dtype=jnp.int32)
    encoder_ids = jnp.arange(ENC, dtype=jnp.int32)

    def one_slot(request):
        slot_id, fresh_len, old_len, enc_len = request
        states = lax.dynamic_slice_in_dim(new_states, (slot_id * Q).astype(jnp.int32), Q, 0).astype(jnp.float32)
        encoder_rows = lax.dynamic_slice_in_dim(encoder_out, (slot_id * ENC).astype(jnp.int32), ENC, 0)
        cache_rows = lax.dynamic_index_in_dim(cache_out, slot_id, 0, keepdims=False).reshape(CTX, H, 2, HD)
        normed = rms_rows(states, norm_gain[0])
        queries = jnp.dot(normed, self_q, preferred_element_type=jnp.float32).astype(jnp.bfloat16).reshape(Q, H, HD)
        key_value = jnp.einsum('td,dcn->tcn', normed.astype(jnp.float32), self_kv.astype(jnp.float32)).astype(jnp.bfloat16).reshape(Q, 2, H, HD)
        old_dist = jnp.clip(old_len + positions[:, None] - cached_ids[None, :], 0, SPAN - 1)
        old_scores = jnp.einsum('qhe,khe->hqk', queries.astype(jnp.float32), cache_rows[:, :, 0].astype(jnp.float32))
        old_scores = old_scores + bias_dist[:, old_dist]
        old_scores = jnp.where((cached_ids < old_len)[None, None, :], old_scores, NEG_FILL)
        fresh_dist = jnp.clip(positions[:, None] - positions[None, :], 0, SPAN - 1)
        fresh_scores = jnp.einsum('qhe,khe->hqk', queries.astype(jnp.float32), key_value[:, 0].astype(jnp.float32))
        fresh_scores = fresh_scores + bias_dist[:, fresh_dist]
        admitted = (positions[None, :] <= positions[:, None]) & (positions[None, :] < fresh_len)
        fresh_scores = jnp.where(admitted[None], fresh_scores, NEG_FILL)
        weights = softmax_rows(jnp.concatenate([old_scores, fresh_scores], axis=2))
        value_all = jnp.concatenate([cache_rows[:, :, 1], key_value[:, 1]], axis=0)
        context = jnp.einsum('hqk,khe->qhe', weights.astype(jnp.float32), value_all.astype(jnp.float32)).astype(jnp.bfloat16)
        states = states + group_product(context.reshape(Q, H * HD), self_out, N_BLK)
        normed = rms_rows(states, norm_gain[1])
        queries = jnp.dot(normed, cross_q, preferred_element_type=jnp.float32).astype(jnp.bfloat16).reshape(Q, H, HD)
        enc_pair = jnp.einsum('td,dcn->tcn', encoder_rows.astype(jnp.float32), cross_kv.astype(jnp.float32)).astype(jnp.bfloat16).reshape(ENC, 2, H, HD)
        scores = jnp.einsum('qhe,khe->hqk', queries.astype(jnp.float32), enc_pair[:, 0].astype(jnp.float32))
        scores = jnp.where((encoder_ids < enc_len)[None, None, :], scores, NEG_FILL)
        weights = softmax_rows(scores)
        context = jnp.einsum('hqk,khe->qhe', weights.astype(jnp.float32), enc_pair[:, 1].astype(jnp.float32)).astype(jnp.bfloat16)
        states = states + group_product(context.reshape(Q, H * HD), cross_out, N_BLK)
        normed = rms_rows(states, norm_gain[2])
        gate_up = jnp.einsum('td,dcf->tcf', normed.astype(jnp.float32), ff_in.astype(jnp.float32))
        hidden = (jax.nn.gelu(gate_up[:, 0], approximate=True) * gate_up[:, 1]).astype(jnp.bfloat16)
        states = states + group_product(hidden, ff_out, N_BLK)
        return states.astype(jnp.bfloat16)
    outputs = lax.map(one_slot, (jnp.arange(REQUESTS, dtype=jnp.int32), slot_new, slot_old, slot_enc))
    return (outputs.reshape(REQUESTS * Q, D), cache_out)
```

```python
import jax
import jax.numpy as jnp
from jax import lax
from jax.sharding import PartitionSpec as P
from jax.experimental import pallas as pl
from jax.experimental.pallas import tpu as pltpu

H = 16
HD = 64


EPSILON = 1e-06
NEG_FILL = -1e30


def rms_rows(row_block, gain):
    mean_square = jnp.mean(row_block * row_block, axis=-1, keepdims=True)
    return (row_block * lax.rsqrt(mean_square + EPSILON) * gain).astype(jnp.bfloat16)


def softmax_rows(scores):
    row_top = jnp.max(scores, axis=-1, keepdims=True)
    weights = jnp.exp(scores - row_top)
    return (weights / jnp.sum(weights, axis=-1, keepdims=True)).astype(jnp.bfloat16)


def pick_lengths(table, own_slots):
    matches = own_slots[:, None] == jnp.arange(table.shape[0], dtype=jnp.int32)[None, :]
    return jnp.sum(jnp.where(matches, table[None, :], 0), axis=1)


def shifted_bias(bias_dist, base, row_count, col_count):
    heads_here, span_len = bias_dist.shape
    line_len = row_count + col_count - 1
    steps = jnp.arange(line_len + 1, dtype=jnp.int32)
    line = bias_dist[:, jnp.clip(base + row_count - 1 - steps, 0, span_len - 1)]
    tiled = jnp.broadcast_to(line[:, None, :], (heads_here, row_count, line_len + 1))
    flat = tiled.reshape(heads_here, row_count * (line_len + 1))[:, : row_count * line_len]
    skewed = flat.reshape(heads_here, row_count, line_len)
    return skewed[:, :, row_count - 1 : row_count - 1 + col_count]


def row_total(left, weight):
    term = jnp.dot(left, weight, preferred_element_type=jnp.float32)
    return lax.psum(term.astype(jnp.bfloat16), "blk").astype(jnp.float32)


def cached_scores(queries, key_rows, first_col, old_len, bias_dist):
    col_ids = first_col + jnp.arange(key_rows.shape[0], dtype=jnp.int32)[None, :]
    scores = jnp.einsum("qhe,khe->hqk", queries, key_rows, preferred_element_type=jnp.float32)
    scores = scores + shifted_bias(
        bias_dist, old_len - first_col, queries.shape[0], key_rows.shape[0]
    )
    return jnp.where((col_ids < old_len)[None], scores, NEG_FILL)


def fresh_scores(queries, fresh_keys, fresh_len, bias_dist):
    row_ids = jnp.arange(queries.shape[0], dtype=jnp.int32)[:, None]
    col_ids = jnp.arange(fresh_keys.shape[0], dtype=jnp.int32)[None, :]
    scores = jnp.einsum("qhe,khe->hqk", queries, fresh_keys, preferred_element_type=jnp.float32)
    scores = scores + shifted_bias(bias_dist, 0, queries.shape[0], fresh_keys.shape[0])
    admitted = (col_ids <= row_ids) & (col_ids < fresh_len)
    return jnp.where(admitted[None], scores, NEG_FILL)


def self_padded(
    queries, key_rows, value_rows, fresh_keys, fresh_values, old_len, fresh_len, bias_dist
):
    scores = jnp.concatenate(
        [
            cached_scores(queries, key_rows, 0, old_len, bias_dist),
            fresh_scores(queries, fresh_keys, fresh_len, bias_dist),
        ],
        axis=2,
    )
    weights = softmax_rows(scores)
    value_all = jnp.concatenate([value_rows, fresh_values], axis=0)
    return jnp.einsum(
        "hqk,khe->qhe", weights, value_all, preferred_element_type=jnp.float32
    ).astype(jnp.bfloat16)


def self_attend(queries, key_value, cache_dec, slot_old, slot_new, bias_dist, heads_dev):
    req_dev, cache_len = (cache_dec.shape[0], cache_dec.shape[1])
    cache_split = cache_dec.reshape(req_dev, cache_len, heads_dev, 2, -1)

    def one_request(request):
        queries_one, pair_one, cache_one, old_len, fresh_len = request
        return self_padded(
            queries_one,
            cache_one[:, :, 0],
            cache_one[:, :, 1],
            pair_one[:, 0],
            pair_one[:, 1],
            old_len,
            fresh_len,
            bias_dist,
        )

    return lax.map(one_request, (queries, key_value, cache_split, slot_old, slot_new))


def cross_attend(queries, key_value, slot_enc):
    scores = jnp.einsum(
        "rqhe,rkhe->rhqk", queries, key_value[:, :, 0], preferred_element_type=jnp.float32
    )
    col_ids = jnp.arange(key_value.shape[1], dtype=jnp.int32)
    scores = jnp.where(
        col_ids[None, None, None, :] < slot_enc[:, None, None, None], scores, NEG_FILL
    )
    weights = softmax_rows(scores)
    return jnp.einsum(
        "rhqk,rkhe->rqhe", weights, key_value[:, :, 1], preferred_element_type=jnp.float32
    ).astype(jnp.bfloat16)


def add_branch(residual, left, weight, gain):
    residual = residual + row_total(left, weight)
    normed = rms_rows(residual, gain)
    return (residual, normed)


TQ = 128


def self_kernel(lens_ref, q_ref, c_ref, kn_ref, vn_ref, g_ref, f_ref, o_ref):
    old_len = lens_ref[0]
    fresh_len = lens_ref[1]
    n_q = q_ref.shape[0]
    n_ctx = c_ref.shape[0]
    wide_old = n_ctx + TQ
    wide_new = n_q + TQ
    k_old = c_ref[:, :HD]
    v_old = c_ref[:, HD:]
    k_new = kn_ref[...]
    v_new = vn_ref[...]
    dims = (((1,), (1,)), ((), ()))
    for t in range(n_q // TQ):
        q = q_ref[t * TQ : (t + 1) * TQ, :]
        start = n_q - TQ - t * TQ
        s_old = lax.dot_general(q, k_old, dims, preferred_element_type=jnp.float32)
        line = jnp.broadcast_to(g_ref[:, start : start + wide_old], (TQ, wide_old))
        bias = pltpu.roll(line, wide_old - (TQ - 1), 1, stride=1, stride_axis=0)[:, :n_ctx]
        col = lax.broadcasted_iota(jnp.int32, (TQ, n_ctx), 1)
        s_old = jnp.where(col < old_len, s_old + bias, NEG_FILL)
        s_new = lax.dot_general(q, k_new, dims, preferred_element_type=jnp.float32)
        line = jnp.broadcast_to(f_ref[:, start : start + wide_new], (TQ, wide_new))
        bias = pltpu.roll(line, wide_new - (TQ - 1), 1, stride=1, stride_axis=0)[:, :n_q]
        row = lax.broadcasted_iota(jnp.int32, (TQ, n_q), 0) + t * TQ
        col = lax.broadcasted_iota(jnp.int32, (TQ, n_q), 1)
        s_new = jnp.where((col <= row) & (col < fresh_len), s_new + bias, NEG_FILL)
        top = jnp.maximum(
            jnp.max(s_old, axis=1, keepdims=True), jnp.max(s_new, axis=1, keepdims=True)
        )
        p_old = jnp.exp(s_old - top)
        p_new = jnp.exp(s_new - top)
        total = jnp.sum(p_old, axis=1, keepdims=True) + jnp.sum(p_new, axis=1, keepdims=True)
        w_old = (p_old / total).astype(jnp.bfloat16)
        w_new = (p_new / total).astype(jnp.bfloat16)
        out = jnp.dot(w_old, v_old, preferred_element_type=jnp.float32) + jnp.dot(
            w_new, v_new, preferred_element_type=jnp.float32
        )
        o_ref[t * TQ : (t + 1) * TQ, :] = out.astype(jnp.bfloat16)


def bias_lines(line, old_len, n_q, n_ctx):
    span = line.shape[0]
    ext = jnp.concatenate([jnp.broadcast_to(line[:1], (n_ctx,)), line])
    rev = ext[::-1]
    g = lax.dynamic_slice_in_dim(rev, n_ctx - old_len, span)
    f = rev[n_ctx : n_ctx + 2 * n_q]
    return g[None, :], f[None, :]


def self_attention(q, cache_blk, k_new, v_new, line, old_len, fresh_len):
    n_q = q.shape[0]
    n_ctx = cache_blk.shape[0]
    g, f = bias_lines(line, old_len, n_q, n_ctx)
    lens = jnp.stack([old_len, fresh_len]).astype(jnp.int32)
    vmem = pl.BlockSpec(memory_space=pltpu.VMEM)
    return pl.pallas_call(
        self_kernel,
        out_shape=jax.ShapeDtypeStruct((n_q, HD), jnp.bfloat16),
        in_specs=[pl.BlockSpec(memory_space=pltpu.SMEM)] + [vmem] * 6,
        out_specs=vmem,
        compiler_params=pltpu.CompilerParams(vmem_limit_bytes=48 * 1024 * 1024),
    )(lens, q, cache_blk, k_new, v_new, g, f)


def pack_gather(pieces):
    flat = jnp.concatenate([w.reshape(-1) for w, _ in pieces])
    whole = lax.all_gather(flat, "req", axis=0, tiled=False)
    n_req = whole.shape[0]
    out, at = [], 0
    for w, axis in pieces:
        size = w.size
        part = whole[:, at : at + size].reshape((n_req,) + w.shape)
        at += size
        part = jnp.moveaxis(part, 0, axis)
        shape = list(w.shape)
        shape[axis] *= n_req
        out.append(part.reshape(shape))
    return out


def per_device(
    new_states,
    encoder_out,
    cache_in,
    slot_order,
    new_lengths,
    cache_lengths,
    enc_lengths,
    bucket_of,
    rel_bias,
    norm_gain,
    self_q,
    self_kv,
    self_out,
    cross_q,
    cross_kv,
    cross_out,
    ff_in,
    ff_out,
):
    blk_count = lax.axis_size("blk")
    heads_dev = H // blk_count
    width_dev = heads_dev * HD
    req_dev = cache_in.shape[0] // lax.axis_size("req")
    own_slots = lax.dynamic_slice_in_dim(slot_order, lax.axis_index("req") * req_dev, req_dev, 0)
    slot_new = pick_lengths(new_lengths, own_slots)
    slot_old = pick_lengths(cache_lengths, own_slots)
    slot_enc = pick_lengths(enc_lengths, own_slots)
    ordered = jnp.take(cache_in, slot_order, axis=0)
    cache_dec = lax.all_to_all(
        lax.all_to_all(ordered, "req", split_axis=0, concat_axis=2, tiled=True),
        "blk",
        split_axis=2,
        concat_axis=1,
        tiled=True,
    )
    onehot = (bucket_of[:, None] == jnp.arange(rel_bias.shape[0], dtype=jnp.int32)[None, :]).astype(
        jnp.float32
    )
    own_bias = lax.dynamic_slice_in_dim(rel_bias, lax.axis_index("blk") * heads_dev, heads_dev, 1)
    bias_dist = jnp.dot(onehot, own_bias, precision=lax.Precision.HIGHEST).T
    gathered = pack_gather(
        [
            (self_q, 0),
            (self_kv, 0),
            (self_out, 1),
            (cross_q, 0),
            (cross_kv, 0),
            (cross_out, 1),
            (ff_in, 0),
            (ff_out, 1),
        ]
    )
    wq_self, wkv_self, wo_self, wq_cross, wkv_cross, wo_cross, w_in, w_out = gathered
    states_full = new_states.astype(jnp.float32)
    normed = rms_rows(states_full, norm_gain[0])
    residual = states_full
    self_cat = jnp.concatenate([wq_self, wkv_self.reshape(wkv_self.shape[0], -1)], axis=1)
    projected = jnp.dot(normed, self_cat, preferred_element_type=jnp.float32).astype(
        jnp.bfloat16
    )
    context = self_attention(
        projected[:, :HD],
        cache_dec[0],
        projected[:, HD : 2 * HD],
        projected[:, 2 * HD :],
        bias_dist[0],
        slot_old[0],
        slot_new[0],
    )
    residual, normed = add_branch(residual, context.reshape(-1, width_dev), wo_self, norm_gain[1])
    queries = (
        jnp.dot(normed, wq_cross, preferred_element_type=jnp.float32)
        .astype(jnp.bfloat16)
        .reshape(req_dev, -1, heads_dev, HD)
    )
    cross_pair = wkv_cross.reshape(wkv_cross.shape[0], -1)
    key_value = (
        jnp.dot(encoder_out, cross_pair, preferred_element_type=jnp.float32)
        .astype(jnp.bfloat16)
        .reshape(req_dev, -1, 2, heads_dev, HD)
    )
    context = cross_attend(queries, key_value, slot_enc)
    residual, normed = add_branch(residual, context.reshape(-1, width_dev), wo_cross, norm_gain[2])
    ff_dev = w_in.shape[2]
    gate_up = jnp.dot(normed, w_in.reshape(w_in.shape[0], -1), preferred_element_type=jnp.float32)
    hidden = (jax.nn.gelu(gate_up[:, :ff_dev], approximate=True) * gate_up[:, ff_dev:]).astype(
        jnp.bfloat16
    )
    layer_out = (residual + row_total(hidden, w_out)).astype(jnp.bfloat16)
    return (layer_out, cache_dec)


def solution(mesh):
    in_specs = (
        P("req", None),
        P("req", None),
        P(None, "blk", "req"),
        P(),
        P(),
        P(),
        P(),
        P(),
        P(),
        P(),
        P("req", "blk"),
        P("req", None, "blk"),
        P("blk", "req"),
        P("req", "blk"),
        P("req", None, "blk"),
        P("blk", "req"),
        P("req", None, "blk"),
        P("blk", "req"),
    )
    out_specs = (P("req", None), P("req", None, "blk"))
    return jax.shard_map(
        per_device, mesh=mesh, in_specs=in_specs, out_specs=out_specs, check_vma=False
    )
```

```python
import functools

import jax
import jax.numpy as jnp
from jax import lax
from jax.sharding import PartitionSpec as P
from jax.experimental import pallas as pl
from jax.experimental.pallas import tpu as pltpu

H = 16
HD = 64


EPSILON = 1e-06
NEG_FILL = -1e30


def rms_rows(row_block, gain):
    mean_square = jnp.mean(row_block * row_block, axis=-1, keepdims=True)
    return (row_block * lax.rsqrt(mean_square + EPSILON) * gain).astype(jnp.bfloat16)


def softmax_rows(scores):
    row_top = jnp.max(scores, axis=-1, keepdims=True)
    weights = jnp.exp(scores - row_top)
    return (weights / jnp.sum(weights, axis=-1, keepdims=True)).astype(jnp.bfloat16)


def pick_lengths(table, own_slots):
    matches = own_slots[:, None] == jnp.arange(table.shape[0], dtype=jnp.int32)[None, :]
    return jnp.sum(jnp.where(matches, table[None, :], 0), axis=1)


def shifted_bias(bias_dist, base, row_count, col_count):
    heads_here, span_len = bias_dist.shape
    line_len = row_count + col_count - 1
    steps = jnp.arange(line_len + 1, dtype=jnp.int32)
    line = bias_dist[:, jnp.clip(base + row_count - 1 - steps, 0, span_len - 1)]
    tiled = jnp.broadcast_to(line[:, None, :], (heads_here, row_count, line_len + 1))
    flat = tiled.reshape(heads_here, row_count * (line_len + 1))[:, : row_count * line_len]
    skewed = flat.reshape(heads_here, row_count, line_len)
    return skewed[:, :, row_count - 1 : row_count - 1 + col_count]


def row_total(left, weight):
    term = jnp.dot(left, weight, preferred_element_type=jnp.float32)
    return lax.psum(term.astype(jnp.bfloat16), "blk").astype(jnp.float32)


def cached_scores(queries, key_rows, first_col, old_len, bias_dist):
    col_ids = first_col + jnp.arange(key_rows.shape[0], dtype=jnp.int32)[None, :]
    scores = jnp.einsum("qhe,khe->hqk", queries, key_rows, preferred_element_type=jnp.float32)
    scores = scores + shifted_bias(
        bias_dist, old_len - first_col, queries.shape[0], key_rows.shape[0]
    )
    return jnp.where((col_ids < old_len)[None], scores, NEG_FILL)


def fresh_scores(queries, fresh_keys, fresh_len, bias_dist):
    row_ids = jnp.arange(queries.shape[0], dtype=jnp.int32)[:, None]
    col_ids = jnp.arange(fresh_keys.shape[0], dtype=jnp.int32)[None, :]
    scores = jnp.einsum("qhe,khe->hqk", queries, fresh_keys, preferred_element_type=jnp.float32)
    scores = scores + shifted_bias(bias_dist, 0, queries.shape[0], fresh_keys.shape[0])
    admitted = (col_ids <= row_ids) & (col_ids < fresh_len)
    return jnp.where(admitted[None], scores, NEG_FILL)


def self_padded(
    queries, key_rows, value_rows, fresh_keys, fresh_values, old_len, fresh_len, bias_dist
):
    scores = jnp.concatenate(
        [
            cached_scores(queries, key_rows, 0, old_len, bias_dist),
            fresh_scores(queries, fresh_keys, fresh_len, bias_dist),
        ],
        axis=2,
    )
    weights = softmax_rows(scores)
    value_all = jnp.concatenate([value_rows, fresh_values], axis=0)
    return jnp.einsum(
        "hqk,khe->qhe", weights, value_all, preferred_element_type=jnp.float32
    ).astype(jnp.bfloat16)


def self_attend(queries, key_value, cache_dec, slot_old, slot_new, bias_dist, heads_dev):
    req_dev, cache_len = (cache_dec.shape[0], cache_dec.shape[1])
    cache_split = cache_dec.reshape(req_dev, cache_len, heads_dev, 2, -1)

    def one_request(request):
        queries_one, pair_one, cache_one, old_len, fresh_len = request
        return self_padded(
            queries_one,
            cache_one[:, :, 0],
            cache_one[:, :, 1],
            pair_one[:, 0],
            pair_one[:, 1],
            old_len,
            fresh_len,
            bias_dist,
        )

    return lax.map(one_request, (queries, key_value, cache_split, slot_old, slot_new))


def cross_attend(queries, key_value, slot_enc):
    scores = jnp.einsum(
        "rqhe,rkhe->rhqk", queries, key_value[:, :, 0], preferred_element_type=jnp.float32
    )
    col_ids = jnp.arange(key_value.shape[1], dtype=jnp.int32)
    scores = jnp.where(
        col_ids[None, None, None, :] < slot_enc[:, None, None, None], scores, NEG_FILL
    )
    weights = softmax_rows(scores)
    return jnp.einsum(
        "rhqk,rkhe->rqhe", weights, key_value[:, :, 1], preferred_element_type=jnp.float32
    ).astype(jnp.bfloat16)


def add_branch(residual, left, weight, gain):
    residual = residual + row_total(left, weight)
    normed = rms_rows(residual, gain)
    return (residual, normed)


TQ = 128


def self_kernel(lens_ref, q_ref, c_ref, kn_ref, vn_ref, g_ref, f_ref, o_ref):
    old_len = lens_ref[0]
    fresh_len = lens_ref[1]
    n_q = q_ref.shape[0]
    n_ctx = c_ref.shape[0]
    wide_old = n_ctx + TQ
    wide_new = n_q + TQ
    k_old = c_ref[:, :HD]
    v_old = c_ref[:, HD:]
    k_new = kn_ref[...]
    v_new = vn_ref[...]
    dims = (((1,), (1,)), ((), ()))
    for t in range(n_q // TQ):
        q = q_ref[t * TQ : (t + 1) * TQ, :]
        start = n_q - TQ - t * TQ
        s_old = lax.dot_general(q, k_old, dims, preferred_element_type=jnp.float32)
        line = jnp.broadcast_to(g_ref[:, start : start + wide_old], (TQ, wide_old))
        bias = pltpu.roll(line, wide_old - (TQ - 1), 1, stride=1, stride_axis=0)[:, :n_ctx]
        col = lax.broadcasted_iota(jnp.int32, (TQ, n_ctx), 1)
        s_old = jnp.where(col < old_len, s_old + bias, NEG_FILL)
        s_new = lax.dot_general(q, k_new, dims, preferred_element_type=jnp.float32)
        line = jnp.broadcast_to(f_ref[:, start : start + wide_new], (TQ, wide_new))
        bias = pltpu.roll(line, wide_new - (TQ - 1), 1, stride=1, stride_axis=0)[:, :n_q]
        row = lax.broadcasted_iota(jnp.int32, (TQ, n_q), 0) + t * TQ
        col = lax.broadcasted_iota(jnp.int32, (TQ, n_q), 1)
        s_new = jnp.where((col <= row) & (col < fresh_len), s_new + bias, NEG_FILL)
        top = jnp.maximum(
            jnp.max(s_old, axis=1, keepdims=True), jnp.max(s_new, axis=1, keepdims=True)
        )
        p_old = jnp.exp(s_old - top)
        p_new = jnp.exp(s_new - top)
        total = jnp.sum(p_old, axis=1, keepdims=True) + jnp.sum(p_new, axis=1, keepdims=True)
        w_old = (p_old / total).astype(jnp.bfloat16)
        w_new = (p_new / total).astype(jnp.bfloat16)
        out = jnp.dot(w_old, v_old, preferred_element_type=jnp.float32) + jnp.dot(
            w_new, v_new, preferred_element_type=jnp.float32
        )
        o_ref[t * TQ : (t + 1) * TQ, :] = out.astype(jnp.bfloat16)


def bias_lines(line, old_len, n_q, n_ctx):
    span = line.shape[0]
    ext = jnp.concatenate([jnp.broadcast_to(line[:1], (n_ctx,)), line])
    rev = ext[::-1]
    g = lax.dynamic_slice_in_dim(rev, n_ctx - old_len, span)
    f = rev[n_ctx : n_ctx + 2 * n_q]
    return g[None, :], f[None, :]


def self_attention(q, cache_blk, k_new, v_new, line, old_len, fresh_len):
    n_q = q.shape[0]
    n_ctx = cache_blk.shape[0]
    g, f = bias_lines(line, old_len, n_q, n_ctx)
    lens = jnp.stack([old_len, fresh_len]).astype(jnp.int32)
    vmem = pl.BlockSpec(memory_space=pltpu.VMEM)
    return pl.pallas_call(
        self_kernel,
        out_shape=jax.ShapeDtypeStruct((n_q, HD), jnp.bfloat16),
        in_specs=[pl.BlockSpec(memory_space=pltpu.SMEM)] + [vmem] * 6,
        out_specs=vmem,
        compiler_params=pltpu.CompilerParams(vmem_limit_bytes=48 * 1024 * 1024),
    )(lens, q, cache_blk, k_new, v_new, g, f)


def pack_gather(pieces):
    flat = jnp.concatenate([w.reshape(-1) for w, _ in pieces])
    whole = lax.all_gather(flat, "req", axis=0, tiled=False)
    n_req = whole.shape[0]
    out, at = [], 0
    for w, axis in pieces:
        size = w.size
        part = whole[:, at : at + size].reshape((n_req,) + w.shape)
        at += size
        part = jnp.moveaxis(part, 0, axis)
        shape = list(w.shape)
        shape[axis] *= n_req
        out.append(part.reshape(shape))
    return out


MESH_IDS = pl.DeviceIdType.MESH


def greet_all(n_blk, me, req):
    barrier = pltpu.get_barrier_semaphore()
    for k in range(1, n_blk):
        peer = lax.rem(me + k, n_blk)
        pl.semaphore_signal(barrier, inc=1, device_id=(req, peer), device_id_type=MESH_IDS)
    pl.semaphore_wait(barrier, n_blk - 1)


def scatter_kernel(n_blk, part_ref, out_ref, recv, send_sem, recv_sem):
    me = lax.axis_index("blk")
    req = lax.axis_index("req")
    rows = out_ref.shape[0]
    greet_all(n_blk, me, req)
    copies = []
    for k in range(1, n_blk):
        peer = lax.rem(me + k, n_blk)
        copy = pltpu.make_async_remote_copy(
            src_ref=part_ref.at[pl.ds(pl.multiple_of(peer * rows, rows), rows)],
            dst_ref=recv.at[me],
            send_sem=send_sem.at[peer],
            recv_sem=recv_sem.at[me],
            device_id=(req, peer),
            device_id_type=MESH_IDS,
        )
        copy.start()
        copies.append(copy)
    total = part_ref[pl.ds(pl.multiple_of(me * rows, rows), rows), :].astype(jnp.float32)
    for k in range(1, n_blk):
        src = lax.rem(me + n_blk - k, n_blk)
        incoming = pltpu.make_async_remote_copy(
            src_ref=part_ref.at[pl.ds(0, rows)],
            dst_ref=recv.at[src],
            send_sem=send_sem.at[src],
            recv_sem=recv_sem.at[src],
            device_id=(req, src),
            device_id_type=MESH_IDS,
        )
        incoming.wait_recv()
        total = total + recv[src].astype(jnp.float32)
    for copy in copies:
        copy.wait_send()
    out_ref[...] = total


def gather_kernel(n_blk, piece_ref, out_ref, recv, send_sem, recv_sem):
    me = lax.axis_index("blk")
    req = lax.axis_index("req")
    rows = piece_ref.shape[0]
    greet_all(n_blk, me, req)
    copies = []
    for k in range(1, n_blk):
        peer = lax.rem(me + k, n_blk)
        copy = pltpu.make_async_remote_copy(
            src_ref=piece_ref,
            dst_ref=recv.at[me],
            send_sem=send_sem.at[peer],
            recv_sem=recv_sem.at[me],
            device_id=(req, peer),
            device_id_type=MESH_IDS,
        )
        copy.start()
        copies.append(copy)
    out_ref[pl.ds(pl.multiple_of(me * rows, rows), rows), :] = piece_ref[...]
    for k in range(1, n_blk):
        src = lax.rem(me + n_blk - k, n_blk)
        incoming = pltpu.make_async_remote_copy(
            src_ref=piece_ref,
            dst_ref=recv.at[src],
            send_sem=send_sem.at[src],
            recv_sem=recv_sem.at[src],
            device_id=(req, src),
            device_id_type=MESH_IDS,
        )
        incoming.wait_recv()
        out_ref[pl.ds(pl.multiple_of(src * rows, rows), rows), :] = recv[src]
    for copy in copies:
        copy.wait_send()


def blk_scatter(part):
    n_blk = lax.axis_size("blk")
    rows = part.shape[0] // n_blk
    vmem = pl.BlockSpec(memory_space=pltpu.VMEM)
    return pl.pallas_call(
        functools.partial(scatter_kernel, n_blk),
        out_shape=jax.ShapeDtypeStruct((rows, part.shape[1]), jnp.float32),
        in_specs=[vmem],
        out_specs=vmem,
        scratch_shapes=[
            pltpu.VMEM((n_blk, rows, part.shape[1]), part.dtype),
            pltpu.SemaphoreType.DMA((n_blk,)),
            pltpu.SemaphoreType.DMA((n_blk,)),
        ],
        compiler_params=pltpu.CompilerParams(collective_id=1, has_side_effects=True),
    )(part)


def blk_gather(piece):
    n_blk = lax.axis_size("blk")
    rows = piece.shape[0]
    vmem = pl.BlockSpec(memory_space=pltpu.VMEM)
    return pl.pallas_call(
        functools.partial(gather_kernel, n_blk),
        out_shape=jax.ShapeDtypeStruct((rows * n_blk, piece.shape[1]), piece.dtype),
        in_specs=[vmem],
        out_specs=vmem,
        scratch_shapes=[
            pltpu.VMEM((n_blk, rows, piece.shape[1]), piece.dtype),
            pltpu.SemaphoreType.DMA((n_blk,)),
            pltpu.SemaphoreType.DMA((n_blk,)),
        ],
        compiler_params=pltpu.CompilerParams(collective_id=2, has_side_effects=True),
    )(piece)


def per_device(
    new_states,
    encoder_out,
    cache_in,
    slot_order,
    new_lengths,
    cache_lengths,
    enc_lengths,
    bucket_of,
    rel_bias,
    norm_gain,
    self_q,
    self_kv,
    self_out,
    cross_q,
    cross_kv,
    cross_out,
    ff_in,
    ff_out,
):
    blk_count = lax.axis_size("blk")
    heads_dev = H // blk_count
    width_dev = heads_dev * HD
    req_dev = cache_in.shape[0] // lax.axis_size("req")
    own_slots = lax.dynamic_slice_in_dim(slot_order, lax.axis_index("req") * req_dev, req_dev, 0)
    slot_new = pick_lengths(new_lengths, own_slots)
    slot_old = pick_lengths(cache_lengths, own_slots)
    slot_enc = pick_lengths(enc_lengths, own_slots)
    ordered = jnp.take(cache_in, slot_order, axis=0)
    cache_dec = lax.all_to_all(
        lax.all_to_all(ordered, "req", split_axis=0, concat_axis=2, tiled=True),
        "blk",
        split_axis=2,
        concat_axis=1,
        tiled=True,
    )
    onehot = (bucket_of[:, None] == jnp.arange(rel_bias.shape[0], dtype=jnp.int32)[None, :]).astype(
        jnp.float32
    )
    own_bias = lax.dynamic_slice_in_dim(rel_bias, lax.axis_index("blk") * heads_dev, heads_dev, 1)
    bias_dist = jnp.dot(onehot, own_bias, precision=lax.Precision.HIGHEST).T
    gathered = pack_gather(
        [
            (self_q, 0),
            (self_kv, 0),
            (self_out, 1),
            (cross_q, 0),
            (cross_kv, 0),
            (cross_out, 1),
            (ff_in, 0),
            (ff_out, 1),
        ]
    )
    wq_self, wkv_self, wo_self, wq_cross, wkv_cross, wo_cross, w_in, w_out = gathered
    n_blk = lax.axis_size("blk")
    rows_dev = new_states.shape[0] // n_blk
    own_rows = lax.dynamic_slice_in_dim(
        new_states, lax.axis_index("blk") * rows_dev, rows_dev, 0
    ).astype(jnp.float32)
    normed = rms_rows(new_states.astype(jnp.float32), norm_gain[0])
    self_cat = jnp.concatenate([wq_self, wkv_self.reshape(wkv_self.shape[0], -1)], axis=1)
    projected = jnp.dot(normed, self_cat, preferred_element_type=jnp.float32).astype(
        jnp.bfloat16
    )
    context = self_attention(
        projected[:, :HD],
        cache_dec[0],
        projected[:, HD : 2 * HD],
        projected[:, 2 * HD :],
        bias_dist[0],
        slot_old[0],
        slot_new[0],
    )
    part = jnp.dot(context, wo_self, preferred_element_type=jnp.float32).astype(jnp.bfloat16)
    residual = own_rows + blk_scatter(part)
    normed = blk_gather(rms_rows(residual, norm_gain[1]))
    queries = (
        jnp.dot(normed, wq_cross, preferred_element_type=jnp.float32)
        .astype(jnp.bfloat16)
        .reshape(req_dev, -1, heads_dev, HD)
    )
    cross_pair = wkv_cross.reshape(wkv_cross.shape[0], -1)
    key_value = (
        jnp.dot(encoder_out, cross_pair, preferred_element_type=jnp.float32)
        .astype(jnp.bfloat16)
        .reshape(req_dev, -1, 2, heads_dev, HD)
    )
    context = cross_attend(queries, key_value, slot_enc)
    part = jnp.dot(context.reshape(-1, width_dev), wo_cross, preferred_element_type=jnp.float32)
    residual = residual + blk_scatter(part.astype(jnp.bfloat16))
    normed = blk_gather(rms_rows(residual, norm_gain[2]))
    ff_dev = w_in.shape[2]
    gate_up = jnp.dot(normed, w_in.reshape(w_in.shape[0], -1), preferred_element_type=jnp.float32)
    hidden = (jax.nn.gelu(gate_up[:, :ff_dev], approximate=True) * gate_up[:, ff_dev:]).astype(
        jnp.bfloat16
    )
    part = jnp.dot(hidden, w_out, preferred_element_type=jnp.float32).astype(jnp.bfloat16)
    layer_out = blk_gather((residual + blk_scatter(part)).astype(jnp.bfloat16))
    return (layer_out, cache_dec)


def solution(mesh):
    in_specs = (
        P("req", None),
        P("req", None),
        P(None, "blk", "req"),
        P(),
        P(),
        P(),
        P(),
        P(),
        P(),
        P(),
        P("req", "blk"),
        P("req", None, "blk"),
        P("blk", "req"),
        P("req", "blk"),
        P("req", None, "blk"),
        P("blk", "req"),
        P("req", None, "blk"),
        P("blk", "req"),
    )
    out_specs = (P("req", None), P("req", None, "blk"))
    return jax.shard_map(
        per_device, mesh=mesh, in_specs=in_specs, out_specs=out_specs, check_vma=False
    )
```

```python
import functools

import jax
import jax.numpy as jnp
from jax import lax
from jax.sharding import PartitionSpec as P
from jax.experimental import pallas as pl
from jax.experimental.pallas import tpu as pltpu

H = 16
HD = 64


EPSILON = 1e-06
NEG_FILL = -1e30


def rms_rows(row_block, gain):
    mean_square = jnp.mean(row_block * row_block, axis=-1, keepdims=True)
    return (row_block * lax.rsqrt(mean_square + EPSILON) * gain).astype(jnp.bfloat16)


def softmax_rows(scores):
    row_top = jnp.max(scores, axis=-1, keepdims=True)
    weights = jnp.exp(scores - row_top)
    return (weights / jnp.sum(weights, axis=-1, keepdims=True)).astype(jnp.bfloat16)


def pick_lengths(table, own_slots):
    matches = own_slots[:, None] == jnp.arange(table.shape[0], dtype=jnp.int32)[None, :]
    return jnp.sum(jnp.where(matches, table[None, :], 0), axis=1)


def shifted_bias(bias_dist, base, row_count, col_count):
    heads_here, span_len = bias_dist.shape
    line_len = row_count + col_count - 1
    steps = jnp.arange(line_len + 1, dtype=jnp.int32)
    line = bias_dist[:, jnp.clip(base + row_count - 1 - steps, 0, span_len - 1)]
    tiled = jnp.broadcast_to(line[:, None, :], (heads_here, row_count, line_len + 1))
    flat = tiled.reshape(heads_here, row_count * (line_len + 1))[:, : row_count * line_len]
    skewed = flat.reshape(heads_here, row_count, line_len)
    return skewed[:, :, row_count - 1 : row_count - 1 + col_count]


def row_total(left, weight):
    term = jnp.dot(left, weight, preferred_element_type=jnp.float32)
    return lax.psum(term.astype(jnp.bfloat16), "blk").astype(jnp.float32)


def cached_scores(queries, key_rows, first_col, old_len, bias_dist):
    col_ids = first_col + jnp.arange(key_rows.shape[0], dtype=jnp.int32)[None, :]
    scores = jnp.einsum("qhe,khe->hqk", queries, key_rows, preferred_element_type=jnp.float32)
    scores = scores + shifted_bias(
        bias_dist, old_len - first_col, queries.shape[0], key_rows.shape[0]
    )
    return jnp.where((col_ids < old_len)[None], scores, NEG_FILL)


def fresh_scores(queries, fresh_keys, fresh_len, bias_dist):
    row_ids = jnp.arange(queries.shape[0], dtype=jnp.int32)[:, None]
    col_ids = jnp.arange(fresh_keys.shape[0], dtype=jnp.int32)[None, :]
    scores = jnp.einsum("qhe,khe->hqk", queries, fresh_keys, preferred_element_type=jnp.float32)
    scores = scores + shifted_bias(bias_dist, 0, queries.shape[0], fresh_keys.shape[0])
    admitted = (col_ids <= row_ids) & (col_ids < fresh_len)
    return jnp.where(admitted[None], scores, NEG_FILL)


def self_padded(
    queries, key_rows, value_rows, fresh_keys, fresh_values, old_len, fresh_len, bias_dist
):
    scores = jnp.concatenate(
        [
            cached_scores(queries, key_rows, 0, old_len, bias_dist),
            fresh_scores(queries, fresh_keys, fresh_len, bias_dist),
        ],
        axis=2,
    )
    weights = softmax_rows(scores)
    value_all = jnp.concatenate([value_rows, fresh_values], axis=0)
    return jnp.einsum(
        "hqk,khe->qhe", weights, value_all, preferred_element_type=jnp.float32
    ).astype(jnp.bfloat16)


def self_attend(queries, key_value, cache_dec, slot_old, slot_new, bias_dist, heads_dev):
    req_dev, cache_len = (cache_dec.shape[0], cache_dec.shape[1])
    cache_split = cache_dec.reshape(req_dev, cache_len, heads_dev, 2, -1)

    def one_request(request):
        queries_one, pair_one, cache_one, old_len, fresh_len = request
        return self_padded(
            queries_one,
            cache_one[:, :, 0],
            cache_one[:, :, 1],
            pair_one[:, 0],
            pair_one[:, 1],
            old_len,
            fresh_len,
            bias_dist,
        )

    return lax.map(one_request, (queries, key_value, cache_split, slot_old, slot_new))


def cross_attend(queries, key_value, slot_enc):
    scores = jnp.einsum(
        "rqhe,rkhe->rhqk", queries, key_value[:, :, 0], preferred_element_type=jnp.float32
    )
    col_ids = jnp.arange(key_value.shape[1], dtype=jnp.int32)
    scores = jnp.where(
        col_ids[None, None, None, :] < slot_enc[:, None, None, None], scores, NEG_FILL
    )
    weights = softmax_rows(scores)
    return jnp.einsum(
        "rhqk,rkhe->rqhe", weights, key_value[:, :, 1], preferred_element_type=jnp.float32
    ).astype(jnp.bfloat16)


def add_branch(residual, left, weight, gain):
    residual = residual + row_total(left, weight)
    normed = rms_rows(residual, gain)
    return (residual, normed)


TQ = 128


def self_kernel(lens_ref, q_ref, c_ref, kn_ref, vn_ref, g_ref, f_ref, o_ref):
    old_len = lens_ref[0]
    fresh_len = lens_ref[1]
    n_q = q_ref.shape[0]
    n_ctx = c_ref.shape[0]
    wide_old = n_ctx + TQ
    wide_new = n_q + TQ
    k_old = c_ref[:, :HD]
    v_old = c_ref[:, HD:]
    k_new = kn_ref[...]
    v_new = vn_ref[...]
    dims = (((1,), (1,)), ((), ()))
    for t in range(n_q // TQ):
        q = q_ref[t * TQ : (t + 1) * TQ, :]
        start = n_q - TQ - t * TQ
        s_old = lax.dot_general(q, k_old, dims, preferred_element_type=jnp.float32)
        line = jnp.broadcast_to(g_ref[:, start : start + wide_old], (TQ, wide_old))
        bias = pltpu.roll(line, wide_old - (TQ - 1), 1, stride=1, stride_axis=0)[:, :n_ctx]
        col = lax.broadcasted_iota(jnp.int32, (TQ, n_ctx), 1)
        s_old = jnp.where(col < old_len, s_old + bias, NEG_FILL)
        s_new = lax.dot_general(q, k_new, dims, preferred_element_type=jnp.float32)
        line = jnp.broadcast_to(f_ref[:, start : start + wide_new], (TQ, wide_new))
        bias = pltpu.roll(line, wide_new - (TQ - 1), 1, stride=1, stride_axis=0)[:, :n_q]
        row = lax.broadcasted_iota(jnp.int32, (TQ, n_q), 0) + t * TQ
        col = lax.broadcasted_iota(jnp.int32, (TQ, n_q), 1)
        s_new = jnp.where((col <= row) & (col < fresh_len), s_new + bias, NEG_FILL)
        top = jnp.maximum(
            jnp.max(s_old, axis=1, keepdims=True), jnp.max(s_new, axis=1, keepdims=True)
        )
        p_old = jnp.exp(s_old - top)
        p_new = jnp.exp(s_new - top)
        total = jnp.sum(p_old, axis=1, keepdims=True) + jnp.sum(p_new, axis=1, keepdims=True)
        w_old = (p_old / total).astype(jnp.bfloat16)
        w_new = (p_new / total).astype(jnp.bfloat16)
        out = jnp.dot(w_old, v_old, preferred_element_type=jnp.float32) + jnp.dot(
            w_new, v_new, preferred_element_type=jnp.float32
        )
        o_ref[t * TQ : (t + 1) * TQ, :] = out.astype(jnp.bfloat16)


def bias_lines(line, old_len, n_q, n_ctx):
    span = line.shape[0]
    ext = jnp.concatenate([jnp.broadcast_to(line[:1], (n_ctx,)), line])
    rev = ext[::-1]
    g = lax.dynamic_slice_in_dim(rev, n_ctx - old_len, span)
    f = rev[n_ctx : n_ctx + 2 * n_q]
    return g[None, :], f[None, :]


def self_attention(q, cache_blk, k_new, v_new, line, old_len, fresh_len):
    n_q = q.shape[0]
    n_ctx = cache_blk.shape[0]
    g, f = bias_lines(line, old_len, n_q, n_ctx)
    lens = jnp.stack([old_len, fresh_len]).astype(jnp.int32)
    vmem = pl.BlockSpec(memory_space=pltpu.VMEM)
    return pl.pallas_call(
        self_kernel,
        out_shape=jax.ShapeDtypeStruct((n_q, HD), jnp.bfloat16),
        in_specs=[pl.BlockSpec(memory_space=pltpu.SMEM)] + [vmem] * 6,
        out_specs=vmem,
        compiler_params=pltpu.CompilerParams(vmem_limit_bytes=48 * 1024 * 1024),
    )(lens, q, cache_blk, k_new, v_new, g, f)


def pack_gather(pieces):
    flat = jnp.concatenate([w.reshape(-1) for w, _ in pieces])
    whole = lax.all_gather(flat, "req", axis=0, tiled=False)
    n_req = whole.shape[0]
    out, at = [], 0
    for w, axis in pieces:
        size = w.size
        part = whole[:, at : at + size].reshape((n_req,) + w.shape)
        at += size
        part = jnp.moveaxis(part, 0, axis)
        shape = list(w.shape)
        shape[axis] *= n_req
        out.append(part.reshape(shape))
    return out


MESH_IDS = pl.DeviceIdType.MESH


def greet_all(n_blk, me, req):
    barrier = pltpu.get_barrier_semaphore()
    for k in range(1, n_blk):
        peer = lax.rem(me + k, n_blk)
        pl.semaphore_signal(barrier, inc=1, device_id=(req, peer), device_id_type=MESH_IDS)
    pl.semaphore_wait(barrier, n_blk - 1)


def scatter_kernel(n_blk, part_ref, out_ref, recv, send_sem, recv_sem):
    me = lax.axis_index("blk")
    req = lax.axis_index("req")
    rows = out_ref.shape[0]
    greet_all(n_blk, me, req)
    copies = []
    for k in range(1, n_blk):
        peer = lax.rem(me + k, n_blk)
        copy = pltpu.make_async_remote_copy(
            src_ref=part_ref.at[pl.ds(pl.multiple_of(peer * rows, rows), rows)],
            dst_ref=recv.at[me],
            send_sem=send_sem.at[peer],
            recv_sem=recv_sem.at[me],
            device_id=(req, peer),
            device_id_type=MESH_IDS,
        )
        copy.start()
        copies.append(copy)
    total = part_ref[pl.ds(pl.multiple_of(me * rows, rows), rows), :].astype(jnp.float32)
    for k in range(1, n_blk):
        src = lax.rem(me + n_blk - k, n_blk)
        incoming = pltpu.make_async_remote_copy(
            src_ref=part_ref.at[pl.ds(0, rows)],
            dst_ref=recv.at[src],
            send_sem=send_sem.at[src],
            recv_sem=recv_sem.at[src],
            device_id=(req, src),
            device_id_type=MESH_IDS,
        )
        incoming.wait_recv()
        total = total + recv[src].astype(jnp.float32)
    for copy in copies:
        copy.wait_send()
    out_ref[...] = total


def gather_kernel(n_blk, piece_ref, out_ref, recv, send_sem, recv_sem):
    me = lax.axis_index("blk")
    req = lax.axis_index("req")
    rows = piece_ref.shape[0]
    greet_all(n_blk, me, req)
    copies = []
    for k in range(1, n_blk):
        peer = lax.rem(me + k, n_blk)
        copy = pltpu.make_async_remote_copy(
            src_ref=piece_ref,
            dst_ref=recv.at[me],
            send_sem=send_sem.at[peer],
            recv_sem=recv_sem.at[me],
            device_id=(req, peer),
            device_id_type=MESH_IDS,
        )
        copy.start()
        copies.append(copy)
    out_ref[pl.ds(pl.multiple_of(me * rows, rows), rows), :] = piece_ref[...]
    for k in range(1, n_blk):
        src = lax.rem(me + n_blk - k, n_blk)
        incoming = pltpu.make_async_remote_copy(
            src_ref=piece_ref,
            dst_ref=recv.at[src],
            send_sem=send_sem.at[src],
            recv_sem=recv_sem.at[src],
            device_id=(req, src),
            device_id_type=MESH_IDS,
        )
        incoming.wait_recv()
        out_ref[pl.ds(pl.multiple_of(src * rows, rows), rows), :] = recv[src]
    for copy in copies:
        copy.wait_send()


def blk_scatter(part):
    n_blk = lax.axis_size("blk")
    rows = part.shape[0] // n_blk
    vmem = pl.BlockSpec(memory_space=pltpu.VMEM)
    return pl.pallas_call(
        functools.partial(scatter_kernel, n_blk),
        out_shape=jax.ShapeDtypeStruct((rows, part.shape[1]), jnp.float32),
        in_specs=[vmem],
        out_specs=vmem,
        scratch_shapes=[
            pltpu.VMEM((n_blk, rows, part.shape[1]), part.dtype),
            pltpu.SemaphoreType.DMA((n_blk,)),
            pltpu.SemaphoreType.DMA((n_blk,)),
        ],
        compiler_params=pltpu.CompilerParams(collective_id=1, has_side_effects=True),
    )(part)


def blk_gather(piece):
    n_blk = lax.axis_size("blk")
    rows = piece.shape[0]
    vmem = pl.BlockSpec(memory_space=pltpu.VMEM)
    return pl.pallas_call(
        functools.partial(gather_kernel, n_blk),
        out_shape=jax.ShapeDtypeStruct((rows * n_blk, piece.shape[1]), piece.dtype),
        in_specs=[vmem],
        out_specs=vmem,
        scratch_shapes=[
            pltpu.VMEM((n_blk, rows, piece.shape[1]), piece.dtype),
            pltpu.SemaphoreType.DMA((n_blk,)),
            pltpu.SemaphoreType.DMA((n_blk,)),
        ],
        compiler_params=pltpu.CompilerParams(collective_id=2, has_side_effects=True),
    )(piece)


def prologue_kernel(n_req, n_blk, ordered_ref, packed_ref, cache_ref, wts_ref, w_send, w_recv, c_send, c_recv, local_sem):
    r = lax.axis_index("req")
    b = lax.axis_index("blk")
    n_slot, span, width = ordered_ref.shape
    piece = width // 2
    copies = []
    for k in range(1, n_req):
        peer = lax.rem(r + k, n_req)
        copy = pltpu.make_async_remote_copy(
            src_ref=packed_ref,
            dst_ref=wts_ref.at[r],
            send_sem=w_send.at[peer],
            recv_sem=w_recv.at[r],
            device_id=(peer, b),
            device_id_type=MESH_IDS,
        )
        copy.start()
        copies.append(copy)
    rows = pl.ds(pl.multiple_of(b * span, span), span)
    for s in range(n_slot):
        for hh in range(2):
            head = 2 * r + hh
            is_self = jnp.logical_and(r == s, head == b)
            src = ordered_ref.at[s, :, pl.ds(hh * piece, piece)]
            copy = pltpu.make_async_remote_copy(
                src_ref=src,
                dst_ref=cache_ref.at[rows],
                send_sem=c_send.at[s * 2 + hh],
                recv_sem=c_recv.at[b],
                device_id=(s, head),
                device_id_type=MESH_IDS,
            )

            @pl.when(jnp.logical_not(is_self))
            def _():
                copy.start()

            @pl.when(is_self)
            def _():
                local = pltpu.make_async_copy(src, cache_ref.at[rows], local_sem.at[0])
                local.start()
                local.wait()

            copies.append((copy, is_self))
    wts_ref[r] = packed_ref[...]
    for k in range(1, n_req):
        src_req = lax.rem(r + n_req - k, n_req)
        incoming = pltpu.make_async_remote_copy(
            src_ref=packed_ref,
            dst_ref=wts_ref.at[src_req],
            send_sem=w_send.at[src_req],
            recv_sem=w_recv.at[src_req],
            device_id=(src_req, b),
            device_id_type=MESH_IDS,
        )
        incoming.wait_recv()
    owner = b // 2
    for j in range(n_blk):
        incoming = pltpu.make_async_remote_copy(
            src_ref=ordered_ref.at[0, :, pl.ds(0, piece)],
            dst_ref=cache_ref.at[pl.ds(j * span, span)],
            send_sem=c_send.at[0],
            recv_sem=c_recv.at[j],
            device_id=(owner, j),
            device_id_type=MESH_IDS,
        )

        @pl.when(jnp.logical_not(jnp.logical_and(owner == r, j == b)))
        def _():
            incoming.wait_recv()

    for item in copies:
        if isinstance(item, tuple):
            copy, is_self = item

            @pl.when(jnp.logical_not(is_self))
            def _():
                copy.wait_send()

        else:
            item.wait_send()


def prologue(ordered, packed):
    n_req = lax.axis_size("req")
    n_blk = lax.axis_size("blk")
    n_slot, span, width = ordered.shape
    any_spec = pl.BlockSpec(memory_space=pl.ANY)
    vmem = pl.BlockSpec(memory_space=pltpu.VMEM)
    return pl.pallas_call(
        functools.partial(prologue_kernel, n_req, n_blk),
        out_shape=(
            jax.ShapeDtypeStruct((span * n_blk, width // 2), ordered.dtype),
            jax.ShapeDtypeStruct((n_req,) + packed.shape, packed.dtype),
        ),
        in_specs=[any_spec, vmem],
        out_specs=(any_spec, vmem),
        scratch_shapes=[
            pltpu.SemaphoreType.DMA((n_req,)),
            pltpu.SemaphoreType.DMA((n_req,)),
            pltpu.SemaphoreType.DMA((2 * n_slot,)),
            pltpu.SemaphoreType.DMA((n_blk,)),
            pltpu.SemaphoreType.DMA((1,)),
        ],
        compiler_params=pltpu.CompilerParams(has_side_effects=True),
    )(ordered, packed)


def unpack(whole, pieces):
    n_req = whole.shape[0]
    whole = whole.reshape(n_req, -1)
    out, at = [], 0
    for w, axis in pieces:
        size = w.size
        part = whole[:, at : at + size].reshape((n_req,) + w.shape)
        at += size
        part = jnp.moveaxis(part, 0, axis)
        shape = list(w.shape)
        shape[axis] *= n_req
        out.append(part.reshape(shape))
    return out


def per_device(
    new_states,
    encoder_out,
    cache_in,
    slot_order,
    new_lengths,
    cache_lengths,
    enc_lengths,
    bucket_of,
    rel_bias,
    norm_gain,
    self_q,
    self_kv,
    self_out,
    cross_q,
    cross_kv,
    cross_out,
    ff_in,
    ff_out,
):
    blk_count = lax.axis_size("blk")
    heads_dev = H // blk_count
    width_dev = heads_dev * HD
    req_dev = cache_in.shape[0] // lax.axis_size("req")
    own_slots = lax.dynamic_slice_in_dim(slot_order, lax.axis_index("req") * req_dev, req_dev, 0)
    slot_new = pick_lengths(new_lengths, own_slots)
    slot_old = pick_lengths(cache_lengths, own_slots)
    slot_enc = pick_lengths(enc_lengths, own_slots)
    ordered = jnp.take(cache_in, slot_order, axis=0)
    onehot = (bucket_of[:, None] == jnp.arange(rel_bias.shape[0], dtype=jnp.int32)[None, :]).astype(
        jnp.float32
    )
    own_bias = lax.dynamic_slice_in_dim(rel_bias, lax.axis_index("blk") * heads_dev, heads_dev, 1)
    bias_dist = jnp.dot(onehot, own_bias, precision=lax.Precision.HIGHEST).T
    pieces = [
        (self_q, 0),
        (self_kv, 0),
        (self_out, 1),
        (cross_q, 0),
        (cross_kv, 0),
        (cross_out, 1),
        (ff_in, 0),
        (ff_out, 1),
    ]
    flat = jnp.concatenate([w.reshape(-1) for w, _ in pieces])
    cache_blk, whole = prologue(ordered, flat.reshape(-1, 128))
    cache_dec = cache_blk[None]
    gathered = unpack(whole, pieces)
    wq_self, wkv_self, wo_self, wq_cross, wkv_cross, wo_cross, w_in, w_out = gathered
    n_blk = lax.axis_size("blk")
    rows_dev = new_states.shape[0] // n_blk
    own_rows = lax.dynamic_slice_in_dim(
        new_states, lax.axis_index("blk") * rows_dev, rows_dev, 0
    ).astype(jnp.float32)
    normed = rms_rows(new_states.astype(jnp.float32), norm_gain[0])
    self_cat = jnp.concatenate([wq_self, wkv_self.reshape(wkv_self.shape[0], -1)], axis=1)
    projected = jnp.dot(normed, self_cat, preferred_element_type=jnp.float32).astype(
        jnp.bfloat16
    )
    context = self_attention(
        projected[:, :HD],
        cache_dec[0],
        projected[:, HD : 2 * HD],
        projected[:, 2 * HD :],
        bias_dist[0],
        slot_old[0],
        slot_new[0],
    )
    part = jnp.dot(context, wo_self, preferred_element_type=jnp.float32).astype(jnp.bfloat16)
    residual = own_rows + blk_scatter(part)
    normed = blk_gather(rms_rows(residual, norm_gain[1]))
    queries = (
        jnp.dot(normed, wq_cross, preferred_element_type=jnp.float32)
        .astype(jnp.bfloat16)
        .reshape(req_dev, -1, heads_dev, HD)
    )
    cross_pair = wkv_cross.reshape(wkv_cross.shape[0], -1)
    key_value = (
        jnp.dot(encoder_out, cross_pair, preferred_element_type=jnp.float32)
        .astype(jnp.bfloat16)
        .reshape(req_dev, -1, 2, heads_dev, HD)
    )
    context = cross_attend(queries, key_value, slot_enc)
    part = jnp.dot(context.reshape(-1, width_dev), wo_cross, preferred_element_type=jnp.float32)
    residual = residual + blk_scatter(part.astype(jnp.bfloat16))
    normed = blk_gather(rms_rows(residual, norm_gain[2]))
    ff_dev = w_in.shape[2]
    gate_up = jnp.dot(normed, w_in.reshape(w_in.shape[0], -1), preferred_element_type=jnp.float32)
    hidden = (jax.nn.gelu(gate_up[:, :ff_dev], approximate=True) * gate_up[:, ff_dev:]).astype(
        jnp.bfloat16
    )
    part = jnp.dot(hidden, w_out, preferred_element_type=jnp.float32).astype(jnp.bfloat16)
    layer_out = blk_gather((residual + blk_scatter(part)).astype(jnp.bfloat16))
    return (layer_out, cache_dec)


def solution(mesh):
    in_specs = (
        P("req", None),
        P("req", None),
        P(None, "blk", "req"),
        P(),
        P(),
        P(),
        P(),
        P(),
        P(),
        P(),
        P("req", "blk"),
        P("req", None, "blk"),
        P("blk", "req"),
        P("req", "blk"),
        P("req", None, "blk"),
        P("blk", "req"),
        P("req", None, "blk"),
        P("blk", "req"),
    )
    out_specs = (P("req", None), P("req", None, "blk"))
    return jax.shard_map(
        per_device, mesh=mesh, in_specs=in_specs, out_specs=out_specs, check_vma=False
    )
```

```python
import functools

import jax
import jax.numpy as jnp
from jax import lax
from jax.sharding import PartitionSpec as P
from jax.experimental import pallas as pl
from jax.experimental.pallas import tpu as pltpu

H = 16
HD = 64


EPSILON = 1e-06
NEG_FILL = -1e30


def rms_rows(row_block, gain):
    mean_square = jnp.mean(row_block * row_block, axis=-1, keepdims=True)
    return (row_block * lax.rsqrt(mean_square + EPSILON) * gain).astype(jnp.bfloat16)


def softmax_rows(scores):
    row_top = jnp.max(scores, axis=-1, keepdims=True)
    weights = jnp.exp(scores - row_top)
    return (weights / jnp.sum(weights, axis=-1, keepdims=True)).astype(jnp.bfloat16)


def pick_lengths(table, own_slots):
    matches = own_slots[:, None] == jnp.arange(table.shape[0], dtype=jnp.int32)[None, :]
    return jnp.sum(jnp.where(matches, table[None, :], 0), axis=1)


def shifted_bias(bias_dist, base, row_count, col_count):
    heads_here, span_len = bias_dist.shape
    line_len = row_count + col_count - 1
    steps = jnp.arange(line_len + 1, dtype=jnp.int32)
    line = bias_dist[:, jnp.clip(base + row_count - 1 - steps, 0, span_len - 1)]
    tiled = jnp.broadcast_to(line[:, None, :], (heads_here, row_count, line_len + 1))
    flat = tiled.reshape(heads_here, row_count * (line_len + 1))[:, : row_count * line_len]
    skewed = flat.reshape(heads_here, row_count, line_len)
    return skewed[:, :, row_count - 1 : row_count - 1 + col_count]


def row_total(left, weight):
    term = jnp.dot(left, weight, preferred_element_type=jnp.float32)
    return lax.psum(term.astype(jnp.bfloat16), "blk").astype(jnp.float32)


def cached_scores(queries, key_rows, first_col, old_len, bias_dist):
    col_ids = first_col + jnp.arange(key_rows.shape[0], dtype=jnp.int32)[None, :]
    scores = jnp.einsum("qhe,khe->hqk", queries, key_rows, preferred_element_type=jnp.float32)
    scores = scores + shifted_bias(
        bias_dist, old_len - first_col, queries.shape[0], key_rows.shape[0]
    )
    return jnp.where((col_ids < old_len)[None], scores, NEG_FILL)


def fresh_scores(queries, fresh_keys, fresh_len, bias_dist):
    row_ids = jnp.arange(queries.shape[0], dtype=jnp.int32)[:, None]
    col_ids = jnp.arange(fresh_keys.shape[0], dtype=jnp.int32)[None, :]
    scores = jnp.einsum("qhe,khe->hqk", queries, fresh_keys, preferred_element_type=jnp.float32)
    scores = scores + shifted_bias(bias_dist, 0, queries.shape[0], fresh_keys.shape[0])
    admitted = (col_ids <= row_ids) & (col_ids < fresh_len)
    return jnp.where(admitted[None], scores, NEG_FILL)


def self_padded(
    queries, key_rows, value_rows, fresh_keys, fresh_values, old_len, fresh_len, bias_dist
):
    scores = jnp.concatenate(
        [
            cached_scores(queries, key_rows, 0, old_len, bias_dist),
            fresh_scores(queries, fresh_keys, fresh_len, bias_dist),
        ],
        axis=2,
    )
    weights = softmax_rows(scores)
    value_all = jnp.concatenate([value_rows, fresh_values], axis=0)
    return jnp.einsum(
        "hqk,khe->qhe", weights, value_all, preferred_element_type=jnp.float32
    ).astype(jnp.bfloat16)


def self_attend(queries, key_value, cache_dec, slot_old, slot_new, bias_dist, heads_dev):
    req_dev, cache_len = (cache_dec.shape[0], cache_dec.shape[1])
    cache_split = cache_dec.reshape(req_dev, cache_len, heads_dev, 2, -1)

    def one_request(request):
        queries_one, pair_one, cache_one, old_len, fresh_len = request
        return self_padded(
            queries_one,
            cache_one[:, :, 0],
            cache_one[:, :, 1],
            pair_one[:, 0],
            pair_one[:, 1],
            old_len,
            fresh_len,
            bias_dist,
        )

    return lax.map(one_request, (queries, key_value, cache_split, slot_old, slot_new))


def cross_attend(queries, key_value, slot_enc):
    scores = jnp.einsum(
        "rqhe,rkhe->rhqk", queries, key_value[:, :, 0], preferred_element_type=jnp.float32
    )
    col_ids = jnp.arange(key_value.shape[1], dtype=jnp.int32)
    scores = jnp.where(
        col_ids[None, None, None, :] < slot_enc[:, None, None, None], scores, NEG_FILL
    )
    weights = softmax_rows(scores)
    return jnp.einsum(
        "rhqk,rkhe->rqhe", weights, key_value[:, :, 1], preferred_element_type=jnp.float32
    ).astype(jnp.bfloat16)


def add_branch(residual, left, weight, gain):
    residual = residual + row_total(left, weight)
    normed = rms_rows(residual, gain)
    return (residual, normed)


TQ = 128


def self_kernel(lens_ref, q_ref, c_ref, kn_ref, vn_ref, g_ref, f_ref, o_ref):
    old_len = lens_ref[0]
    fresh_len = lens_ref[1]
    n_q = q_ref.shape[0]
    n_ctx = c_ref.shape[0]
    wide_old = n_ctx + TQ
    wide_new = n_q + TQ
    k_old = c_ref[:, :HD]
    v_old = c_ref[:, HD:]
    k_new = kn_ref[...]
    v_new = vn_ref[...]
    dims = (((1,), (1,)), ((), ()))
    for t in range(n_q // TQ):
        q = q_ref[t * TQ : (t + 1) * TQ, :]
        start = n_q - TQ - t * TQ
        s_old = lax.dot_general(q, k_old, dims, preferred_element_type=jnp.float32)
        line = jnp.broadcast_to(g_ref[:, start : start + wide_old], (TQ, wide_old))
        bias = pltpu.roll(line, wide_old - (TQ - 1), 1, stride=1, stride_axis=0)[:, :n_ctx]
        col = lax.broadcasted_iota(jnp.int32, (TQ, n_ctx), 1)
        s_old = jnp.where(col < old_len, s_old + bias, NEG_FILL)
        s_new = lax.dot_general(q, k_new, dims, preferred_element_type=jnp.float32)
        line = jnp.broadcast_to(f_ref[:, start : start + wide_new], (TQ, wide_new))
        bias = pltpu.roll(line, wide_new - (TQ - 1), 1, stride=1, stride_axis=0)[:, :n_q]
        row = lax.broadcasted_iota(jnp.int32, (TQ, n_q), 0) + t * TQ
        col = lax.broadcasted_iota(jnp.int32, (TQ, n_q), 1)
        s_new = jnp.where((col <= row) & (col < fresh_len), s_new + bias, NEG_FILL)
        top = jnp.maximum(
            jnp.max(s_old, axis=1, keepdims=True), jnp.max(s_new, axis=1, keepdims=True)
        )
        p_old = jnp.exp(s_old - top)
        p_new = jnp.exp(s_new - top)
        total = jnp.sum(p_old, axis=1, keepdims=True) + jnp.sum(p_new, axis=1, keepdims=True)
        w_old = (p_old / total).astype(jnp.bfloat16)
        w_new = (p_new / total).astype(jnp.bfloat16)
        out = jnp.dot(w_old, v_old, preferred_element_type=jnp.float32) + jnp.dot(
            w_new, v_new, preferred_element_type=jnp.float32
        )
        o_ref[t * TQ : (t + 1) * TQ, :] = out.astype(jnp.bfloat16)


def bias_lines(line, old_len, n_q, n_ctx):
    span = line.shape[0]
    ext = jnp.concatenate([jnp.broadcast_to(line[:1], (n_ctx,)), line])
    rev = ext[::-1]
    g = lax.dynamic_slice_in_dim(rev, n_ctx - old_len, span)
    f = rev[n_ctx : n_ctx + 2 * n_q]
    return g[None, :], f[None, :]


def self_attention(q, cache_blk, k_new, v_new, line, old_len, fresh_len):
    n_q = q.shape[0]
    n_ctx = cache_blk.shape[0]
    g, f = bias_lines(line, old_len, n_q, n_ctx)
    lens = jnp.stack([old_len, fresh_len]).astype(jnp.int32)
    vmem = pl.BlockSpec(memory_space=pltpu.VMEM)
    return pl.pallas_call(
        self_kernel,
        out_shape=jax.ShapeDtypeStruct((n_q, HD), jnp.bfloat16),
        in_specs=[pl.BlockSpec(memory_space=pltpu.SMEM)] + [vmem] * 6,
        out_specs=vmem,
        compiler_params=pltpu.CompilerParams(vmem_limit_bytes=48 * 1024 * 1024),
    )(lens, q, cache_blk, k_new, v_new, g, f)


def pack_gather(pieces):
    flat = jnp.concatenate([w.reshape(-1) for w, _ in pieces])
    whole = lax.all_gather(flat, "req", axis=0, tiled=False)
    n_req = whole.shape[0]
    out, at = [], 0
    for w, axis in pieces:
        size = w.size
        part = whole[:, at : at + size].reshape((n_req,) + w.shape)
        at += size
        part = jnp.moveaxis(part, 0, axis)
        shape = list(w.shape)
        shape[axis] *= n_req
        out.append(part.reshape(shape))
    return out


MESH_IDS = pl.DeviceIdType.MESH


def greet_all(n_blk, me, req):
    barrier = pltpu.get_barrier_semaphore()
    for k in range(1, n_blk):
        peer = lax.rem(me + k, n_blk)
        pl.semaphore_signal(barrier, inc=1, device_id=(req, peer), device_id_type=MESH_IDS)
    pl.semaphore_wait(barrier, n_blk - 1)


def scatter_kernel(n_blk, part_ref, out_ref, recv, send_sem, recv_sem):
    me = lax.axis_index("blk")
    req = lax.axis_index("req")
    rows = out_ref.shape[0]
    greet_all(n_blk, me, req)
    copies = []
    for k in range(1, n_blk):
        peer = lax.rem(me + k, n_blk)
        copy = pltpu.make_async_remote_copy(
            src_ref=part_ref.at[pl.ds(pl.multiple_of(peer * rows, rows), rows)],
            dst_ref=recv.at[me],
            send_sem=send_sem.at[peer],
            recv_sem=recv_sem.at[me],
            device_id=(req, peer),
            device_id_type=MESH_IDS,
        )
        copy.start()
        copies.append(copy)
    total = part_ref[pl.ds(pl.multiple_of(me * rows, rows), rows), :].astype(jnp.float32)
    for k in range(1, n_blk):
        src = lax.rem(me + n_blk - k, n_blk)
        incoming = pltpu.make_async_remote_copy(
            src_ref=part_ref.at[pl.ds(0, rows)],
            dst_ref=recv.at[src],
            send_sem=send_sem.at[src],
            recv_sem=recv_sem.at[src],
            device_id=(req, src),
            device_id_type=MESH_IDS,
        )
        incoming.wait_recv()
        total = total + recv[src].astype(jnp.float32)
    for copy in copies:
        copy.wait_send()
    out_ref[...] = total


def gather_kernel(n_blk, piece_ref, out_ref, recv, send_sem, recv_sem):
    me = lax.axis_index("blk")
    req = lax.axis_index("req")
    rows = piece_ref.shape[0]
    greet_all(n_blk, me, req)
    copies = []
    for k in range(1, n_blk):
        peer = lax.rem(me + k, n_blk)
        copy = pltpu.make_async_remote_copy(
            src_ref=piece_ref,
            dst_ref=recv.at[me],
            send_sem=send_sem.at[peer],
            recv_sem=recv_sem.at[me],
            device_id=(req, peer),
            device_id_type=MESH_IDS,
        )
        copy.start()
        copies.append(copy)
    out_ref[pl.ds(pl.multiple_of(me * rows, rows), rows), :] = piece_ref[...]
    for k in range(1, n_blk):
        src = lax.rem(me + n_blk - k, n_blk)
        incoming = pltpu.make_async_remote_copy(
            src_ref=piece_ref,
            dst_ref=recv.at[src],
            send_sem=send_sem.at[src],
            recv_sem=recv_sem.at[src],
            device_id=(req, src),
            device_id_type=MESH_IDS,
        )
        incoming.wait_recv()
        out_ref[pl.ds(pl.multiple_of(src * rows, rows), rows), :] = recv[src]
    for copy in copies:
        copy.wait_send()


def blk_scatter(part):
    n_blk = lax.axis_size("blk")
    rows = part.shape[0] // n_blk
    vmem = pl.BlockSpec(memory_space=pltpu.VMEM)
    return pl.pallas_call(
        functools.partial(scatter_kernel, n_blk),
        out_shape=jax.ShapeDtypeStruct((rows, part.shape[1]), jnp.float32),
        in_specs=[vmem],
        out_specs=vmem,
        scratch_shapes=[
            pltpu.VMEM((n_blk, rows, part.shape[1]), part.dtype),
            pltpu.SemaphoreType.DMA((n_blk,)),
            pltpu.SemaphoreType.DMA((n_blk,)),
        ],
        compiler_params=pltpu.CompilerParams(collective_id=1, has_side_effects=True),
    )(part)


def blk_gather(piece):
    n_blk = lax.axis_size("blk")
    rows = piece.shape[0]
    vmem = pl.BlockSpec(memory_space=pltpu.VMEM)
    return pl.pallas_call(
        functools.partial(gather_kernel, n_blk),
        out_shape=jax.ShapeDtypeStruct((rows * n_blk, piece.shape[1]), piece.dtype),
        in_specs=[vmem],
        out_specs=vmem,
        scratch_shapes=[
            pltpu.VMEM((n_blk, rows, piece.shape[1]), piece.dtype),
            pltpu.SemaphoreType.DMA((n_blk,)),
            pltpu.SemaphoreType.DMA((n_blk,)),
        ],
        compiler_params=pltpu.CompilerParams(collective_id=2, has_side_effects=True),
    )(piece)


def prologue_kernel(n_req, n_blk, ordered_ref, packed_ref, cache_ref, wts_ref, w_send, w_recv, c_send, c_recv, local_sem):
    r = lax.axis_index("req")
    b = lax.axis_index("blk")
    n_slot, span, width = ordered_ref.shape
    piece = width // 2
    copies = []
    for k in range(1, n_req):
        peer = lax.rem(r + k, n_req)
        copy = pltpu.make_async_remote_copy(
            src_ref=packed_ref,
            dst_ref=wts_ref.at[r],
            send_sem=w_send.at[peer],
            recv_sem=w_recv.at[r],
            device_id=(peer, b),
            device_id_type=MESH_IDS,
        )
        copy.start()
        copies.append(copy)
    rows = pl.ds(pl.multiple_of(b * span, span), span)
    for s in range(n_slot):
        for hh in range(2):
            head = 2 * r + hh
            is_self = jnp.logical_and(r == s, head == b)
            src = ordered_ref.at[s, :, pl.ds(hh * piece, piece)]
            copy = pltpu.make_async_remote_copy(
                src_ref=src,
                dst_ref=cache_ref.at[rows],
                send_sem=c_send.at[s * 2 + hh],
                recv_sem=c_recv.at[b],
                device_id=(s, head),
                device_id_type=MESH_IDS,
            )

            @pl.when(jnp.logical_not(is_self))
            def _():
                copy.start()

            @pl.when(is_self)
            def _():
                local = pltpu.make_async_copy(src, cache_ref.at[rows], local_sem.at[0])
                local.start()
                local.wait()

            copies.append((copy, is_self))
    wts_ref[r] = packed_ref[...]
    for k in range(1, n_req):
        src_req = lax.rem(r + n_req - k, n_req)
        incoming = pltpu.make_async_remote_copy(
            src_ref=packed_ref,
            dst_ref=wts_ref.at[src_req],
            send_sem=w_send.at[src_req],
            recv_sem=w_recv.at[src_req],
            device_id=(src_req, b),
            device_id_type=MESH_IDS,
        )
        incoming.wait_recv()
    owner = b // 2
    for j in range(n_blk):
        incoming = pltpu.make_async_remote_copy(
            src_ref=ordered_ref.at[0, :, pl.ds(0, piece)],
            dst_ref=cache_ref.at[pl.ds(j * span, span)],
            send_sem=c_send.at[0],
            recv_sem=c_recv.at[j],
            device_id=(owner, j),
            device_id_type=MESH_IDS,
        )

        @pl.when(jnp.logical_not(jnp.logical_and(owner == r, j == b)))
        def _():
            incoming.wait_recv()

    for item in copies:
        if isinstance(item, tuple):
            copy, is_self = item

            @pl.when(jnp.logical_not(is_self))
            def _():
                copy.wait_send()

        else:
            item.wait_send()


def prologue(ordered, packed):
    n_req = lax.axis_size("req")
    n_blk = lax.axis_size("blk")
    n_slot, span, width = ordered.shape
    any_spec = pl.BlockSpec(memory_space=pl.ANY)
    vmem = pl.BlockSpec(memory_space=pltpu.VMEM)
    return pl.pallas_call(
        functools.partial(prologue_kernel, n_req, n_blk),
        out_shape=(
            jax.ShapeDtypeStruct((span * n_blk, width // 2), ordered.dtype),
            jax.ShapeDtypeStruct((n_req,) + packed.shape, packed.dtype),
        ),
        in_specs=[any_spec, vmem],
        out_specs=(any_spec, vmem),
        scratch_shapes=[
            pltpu.SemaphoreType.DMA((n_req,)),
            pltpu.SemaphoreType.DMA((n_req,)),
            pltpu.SemaphoreType.DMA((2 * n_slot,)),
            pltpu.SemaphoreType.DMA((n_blk,)),
            pltpu.SemaphoreType.DMA((1,)),
        ],
        compiler_params=pltpu.CompilerParams(has_side_effects=True),
    )(ordered, packed)


def unpack(whole, pieces):
    n_req = whole.shape[0]
    whole = whole.reshape(n_req, -1)
    out, at = [], 0
    for w, axis in pieces:
        size = w.size
        part = whole[:, at : at + size].reshape((n_req,) + w.shape)
        at += size
        part = jnp.moveaxis(part, 0, axis)
        shape = list(w.shape)
        shape[axis] *= n_req
        out.append(part.reshape(shape))
    return out


def per_device(
    new_states,
    encoder_out,
    cache_in,
    slot_order,
    new_lengths,
    cache_lengths,
    enc_lengths,
    bucket_of,
    rel_bias,
    norm_gain,
    self_q,
    self_kv,
    self_out,
    cross_q,
    cross_kv,
    cross_out,
    ff_in,
    ff_out,
):
    blk_count = lax.axis_size("blk")
    heads_dev = H // blk_count
    width_dev = heads_dev * HD
    req_dev = cache_in.shape[0] // lax.axis_size("req")
    own_slots = lax.dynamic_slice_in_dim(slot_order, lax.axis_index("req") * req_dev, req_dev, 0)
    slot_new = pick_lengths(new_lengths, own_slots)
    slot_old = pick_lengths(cache_lengths, own_slots)
    slot_enc = pick_lengths(enc_lengths, own_slots)
    ordered = jnp.take(cache_in, slot_order, axis=0)
    onehot = (bucket_of[:, None] == jnp.arange(rel_bias.shape[0], dtype=jnp.int32)[None, :]).astype(
        jnp.float32
    )
    own_bias = lax.dynamic_slice_in_dim(rel_bias, lax.axis_index("blk") * heads_dev, heads_dev, 1)
    bias_dist = jnp.dot(onehot, own_bias, precision=lax.Precision.HIGHEST).T
    early = [(self_q, 0), (self_kv, 0), (self_out, 1)]
    late = [(cross_q, 0), (cross_kv, 0), (cross_out, 1), (ff_in, 0), (ff_out, 1)]
    flat = jnp.concatenate([w.reshape(-1) for w, _ in early])
    cache_blk, whole = prologue(ordered, flat.reshape(-1, 128))
    cache_dec = cache_blk[None]
    gathered = unpack(whole, early) + pack_gather(late)
    wq_self, wkv_self, wo_self, wq_cross, wkv_cross, wo_cross, w_in, w_out = gathered
    n_blk = lax.axis_size("blk")
    rows_dev = new_states.shape[0] // n_blk
    own_rows = lax.dynamic_slice_in_dim(
        new_states, lax.axis_index("blk") * rows_dev, rows_dev, 0
    ).astype(jnp.float32)
    normed = rms_rows(new_states.astype(jnp.float32), norm_gain[0])
    self_cat = jnp.concatenate([wq_self, wkv_self.reshape(wkv_self.shape[0], -1)], axis=1)
    projected = jnp.dot(normed, self_cat, preferred_element_type=jnp.float32).astype(
        jnp.bfloat16
    )
    context = self_attention(
        projected[:, :HD],
        cache_dec[0],
        projected[:, HD : 2 * HD],
        projected[:, 2 * HD :],
        bias_dist[0],
        slot_old[0],
        slot_new[0],
    )
    part = jnp.dot(context, wo_self, preferred_element_type=jnp.float32).astype(jnp.bfloat16)
    residual = own_rows + blk_scatter(part)
    normed = blk_gather(rms_rows(residual, norm_gain[1]))
    queries = (
        jnp.dot(normed, wq_cross, preferred_element_type=jnp.float32)
        .astype(jnp.bfloat16)
        .reshape(req_dev, -1, heads_dev, HD)
    )
    cross_pair = wkv_cross.reshape(wkv_cross.shape[0], -1)
    key_value = (
        jnp.dot(encoder_out, cross_pair, preferred_element_type=jnp.float32)
        .astype(jnp.bfloat16)
        .reshape(req_dev, -1, 2, heads_dev, HD)
    )
    context = cross_attend(queries, key_value, slot_enc)
    part = jnp.dot(context.reshape(-1, width_dev), wo_cross, preferred_element_type=jnp.float32)
    residual = residual + blk_scatter(part.astype(jnp.bfloat16))
    normed = blk_gather(rms_rows(residual, norm_gain[2]))
    ff_dev = w_in.shape[2]
    gate_up = jnp.dot(normed, w_in.reshape(w_in.shape[0], -1), preferred_element_type=jnp.float32)
    hidden = (jax.nn.gelu(gate_up[:, :ff_dev], approximate=True) * gate_up[:, ff_dev:]).astype(
        jnp.bfloat16
    )
    part = jnp.dot(hidden, w_out, preferred_element_type=jnp.float32).astype(jnp.bfloat16)
    layer_out = blk_gather((residual + blk_scatter(part)).astype(jnp.bfloat16))
    return (layer_out, cache_dec)


def solution(mesh):
    in_specs = (
        P("req", None),
        P("req", None),
        P(None, "blk", "req"),
        P(),
        P(),
        P(),
        P(),
        P(),
        P(),
        P(),
        P("req", "blk"),
        P("req", None, "blk"),
        P("blk", "req"),
        P("req", "blk"),
        P("req", None, "blk"),
        P("blk", "req"),
        P("req", None, "blk"),
        P("blk", "req"),
    )
    out_specs = (P("req", None), P("req", None, "blk"))
    return jax.shard_map(
        per_device, mesh=mesh, in_specs=in_specs, out_specs=out_specs, check_vma=False
    )
```

```python
import functools

import jax
import jax.numpy as jnp
from jax import lax
from jax.sharding import PartitionSpec as P
from jax.experimental import pallas as pl
from jax.experimental.pallas import tpu as pltpu

H = 16
HD = 64


EPSILON = 1e-06
NEG_FILL = -1e30


def rms_rows(row_block, gain):
    mean_square = jnp.mean(row_block * row_block, axis=-1, keepdims=True)
    return (row_block * lax.rsqrt(mean_square + EPSILON) * gain).astype(jnp.bfloat16)


def softmax_rows(scores):
    row_top = jnp.max(scores, axis=-1, keepdims=True)
    weights = jnp.exp(scores - row_top)
    return (weights / jnp.sum(weights, axis=-1, keepdims=True)).astype(jnp.bfloat16)


def pick_lengths(table, own_slots):
    matches = own_slots[:, None] == jnp.arange(table.shape[0], dtype=jnp.int32)[None, :]
    return jnp.sum(jnp.where(matches, table[None, :], 0), axis=1)


def shifted_bias(bias_dist, base, row_count, col_count):
    heads_here, span_len = bias_dist.shape
    line_len = row_count + col_count - 1
    steps = jnp.arange(line_len + 1, dtype=jnp.int32)
    line = bias_dist[:, jnp.clip(base + row_count - 1 - steps, 0, span_len - 1)]
    tiled = jnp.broadcast_to(line[:, None, :], (heads_here, row_count, line_len + 1))
    flat = tiled.reshape(heads_here, row_count * (line_len + 1))[:, : row_count * line_len]
    skewed = flat.reshape(heads_here, row_count, line_len)
    return skewed[:, :, row_count - 1 : row_count - 1 + col_count]


def row_total(left, weight):
    term = jnp.dot(left, weight, preferred_element_type=jnp.float32)
    return lax.psum(term.astype(jnp.bfloat16), "blk").astype(jnp.float32)


def cached_scores(queries, key_rows, first_col, old_len, bias_dist):
    col_ids = first_col + jnp.arange(key_rows.shape[0], dtype=jnp.int32)[None, :]
    scores = jnp.einsum("qhe,khe->hqk", queries, key_rows, preferred_element_type=jnp.float32)
    scores = scores + shifted_bias(
        bias_dist, old_len - first_col, queries.shape[0], key_rows.shape[0]
    )
    return jnp.where((col_ids < old_len)[None], scores, NEG_FILL)


def fresh_scores(queries, fresh_keys, fresh_len, bias_dist):
    row_ids = jnp.arange(queries.shape[0], dtype=jnp.int32)[:, None]
    col_ids = jnp.arange(fresh_keys.shape[0], dtype=jnp.int32)[None, :]
    scores = jnp.einsum("qhe,khe->hqk", queries, fresh_keys, preferred_element_type=jnp.float32)
    scores = scores + shifted_bias(bias_dist, 0, queries.shape[0], fresh_keys.shape[0])
    admitted = (col_ids <= row_ids) & (col_ids < fresh_len)
    return jnp.where(admitted[None], scores, NEG_FILL)


def self_padded(
    queries, key_rows, value_rows, fresh_keys, fresh_values, old_len, fresh_len, bias_dist
):
    scores = jnp.concatenate(
        [
            cached_scores(queries, key_rows, 0, old_len, bias_dist),
            fresh_scores(queries, fresh_keys, fresh_len, bias_dist),
        ],
        axis=2,
    )
    weights = softmax_rows(scores)
    value_all = jnp.concatenate([value_rows, fresh_values], axis=0)
    return jnp.einsum(
        "hqk,khe->qhe", weights, value_all, preferred_element_type=jnp.float32
    ).astype(jnp.bfloat16)


def self_attend(queries, key_value, cache_dec, slot_old, slot_new, bias_dist, heads_dev):
    req_dev, cache_len = (cache_dec.shape[0], cache_dec.shape[1])
    cache_split = cache_dec.reshape(req_dev, cache_len, heads_dev, 2, -1)

    def one_request(request):
        queries_one, pair_one, cache_one, old_len, fresh_len = request
        return self_padded(
            queries_one,
            cache_one[:, :, 0],
            cache_one[:, :, 1],
            pair_one[:, 0],
            pair_one[:, 1],
            old_len,
            fresh_len,
            bias_dist,
        )

    return lax.map(one_request, (queries, key_value, cache_split, slot_old, slot_new))


def cross_attend(queries, key_value, slot_enc):
    scores = jnp.einsum(
        "rqhe,rkhe->rhqk", queries, key_value[:, :, 0], preferred_element_type=jnp.float32
    )
    col_ids = jnp.arange(key_value.shape[1], dtype=jnp.int32)
    scores = jnp.where(
        col_ids[None, None, None, :] < slot_enc[:, None, None, None], scores, NEG_FILL
    )
    weights = softmax_rows(scores)
    return jnp.einsum(
        "rhqk,rkhe->rqhe", weights, key_value[:, :, 1], preferred_element_type=jnp.float32
    ).astype(jnp.bfloat16)


def add_branch(residual, left, weight, gain):
    residual = residual + row_total(left, weight)
    normed = rms_rows(residual, gain)
    return (residual, normed)


TQ = 128


def self_kernel(lens_ref, q_ref, c_ref, kn_ref, vn_ref, g_ref, f_ref, o_ref):
    old_len = lens_ref[0]
    fresh_len = lens_ref[1]
    n_q = q_ref.shape[0]
    n_ctx = c_ref.shape[0]
    wide_old = n_ctx + TQ
    wide_new = n_q + TQ
    k_old = c_ref[:, :HD]
    v_old = c_ref[:, HD:]
    k_new = kn_ref[...]
    v_new = vn_ref[...]
    dims = (((1,), (1,)), ((), ()))
    for t in range(n_q // TQ):
        q = q_ref[t * TQ : (t + 1) * TQ, :]
        start = n_q - TQ - t * TQ
        s_old = lax.dot_general(q, k_old, dims, preferred_element_type=jnp.float32)
        line = jnp.broadcast_to(g_ref[:, start : start + wide_old], (TQ, wide_old))
        bias = pltpu.roll(line, wide_old - (TQ - 1), 1, stride=1, stride_axis=0)[:, :n_ctx]
        col = lax.broadcasted_iota(jnp.int32, (TQ, n_ctx), 1)
        s_old = jnp.where(col < old_len, s_old + bias, NEG_FILL)
        s_new = lax.dot_general(q, k_new, dims, preferred_element_type=jnp.float32)
        line = jnp.broadcast_to(f_ref[:, start : start + wide_new], (TQ, wide_new))
        bias = pltpu.roll(line, wide_new - (TQ - 1), 1, stride=1, stride_axis=0)[:, :n_q]
        row = lax.broadcasted_iota(jnp.int32, (TQ, n_q), 0) + t * TQ
        col = lax.broadcasted_iota(jnp.int32, (TQ, n_q), 1)
        s_new = jnp.where((col <= row) & (col < fresh_len), s_new + bias, NEG_FILL)
        top = jnp.maximum(
            jnp.max(s_old, axis=1, keepdims=True), jnp.max(s_new, axis=1, keepdims=True)
        )
        p_old = jnp.exp(s_old - top)
        p_new = jnp.exp(s_new - top)
        total = jnp.sum(p_old, axis=1, keepdims=True) + jnp.sum(p_new, axis=1, keepdims=True)
        w_old = (p_old / total).astype(jnp.bfloat16)
        w_new = (p_new / total).astype(jnp.bfloat16)
        out = jnp.dot(w_old, v_old, preferred_element_type=jnp.float32) + jnp.dot(
            w_new, v_new, preferred_element_type=jnp.float32
        )
        o_ref[t * TQ : (t + 1) * TQ, :] = out.astype(jnp.bfloat16)


def bias_lines(line, old_len, n_q, n_ctx):
    span = line.shape[0]
    ext = jnp.concatenate([jnp.broadcast_to(line[:1], (n_ctx,)), line])
    rev = ext[::-1]
    g = lax.dynamic_slice_in_dim(rev, n_ctx - old_len, span)
    f = rev[n_ctx : n_ctx + 2 * n_q]
    return g[None, :], f[None, :]


def self_attention(q, cache_blk, k_new, v_new, line, old_len, fresh_len):
    n_q = q.shape[0]
    n_ctx = cache_blk.shape[0]
    g, f = bias_lines(line, old_len, n_q, n_ctx)
    lens = jnp.stack([old_len, fresh_len]).astype(jnp.int32)
    vmem = pl.BlockSpec(memory_space=pltpu.VMEM)
    return pl.pallas_call(
        self_kernel,
        out_shape=jax.ShapeDtypeStruct((n_q, HD), jnp.bfloat16),
        in_specs=[pl.BlockSpec(memory_space=pltpu.SMEM)] + [vmem] * 6,
        out_specs=vmem,
        compiler_params=pltpu.CompilerParams(vmem_limit_bytes=48 * 1024 * 1024),
    )(lens, q, cache_blk, k_new, v_new, g, f)


def pack_gather(pieces):
    flat = jnp.concatenate([w.reshape(-1) for w, _ in pieces])
    whole = lax.all_gather(flat, "req", axis=0, tiled=False)
    n_req = whole.shape[0]
    out, at = [], 0
    for w, axis in pieces:
        size = w.size
        part = whole[:, at : at + size].reshape((n_req,) + w.shape)
        at += size
        part = jnp.moveaxis(part, 0, axis)
        shape = list(w.shape)
        shape[axis] *= n_req
        out.append(part.reshape(shape))
    return out


MESH_IDS = pl.DeviceIdType.MESH


def greet_all(n_blk, me, req):
    barrier = pltpu.get_barrier_semaphore()
    for k in range(1, n_blk):
        peer = lax.rem(me + k, n_blk)
        pl.semaphore_signal(barrier, inc=1, device_id=(req, peer), device_id_type=MESH_IDS)
    pl.semaphore_wait(barrier, n_blk - 1)


def chunk_of(b, n_blk):
    return lax.rem(b, 2) * (n_blk // 2) + b // 2


def scatter_kernel(n_blk, part_ref, out_ref, recv, send_sem, recv_sem):
    me = lax.axis_index("blk")
    req = lax.axis_index("req")
    rows = out_ref.shape[0]
    greet_all(n_blk, me, req)
    copies = []
    for k in range(1, n_blk):
        peer = lax.rem(me + k, n_blk)
        copy = pltpu.make_async_remote_copy(
            src_ref=part_ref.at[pl.ds(pl.multiple_of(chunk_of(peer, n_blk) * rows, rows), rows)],
            dst_ref=recv.at[me],
            send_sem=send_sem.at[peer],
            recv_sem=recv_sem.at[me],
            device_id=(req, peer),
            device_id_type=MESH_IDS,
        )
        copy.start()
        copies.append(copy)
    own = pl.ds(pl.multiple_of(chunk_of(me, n_blk) * rows, rows), rows)
    total = part_ref[own, :].astype(jnp.float32)
    for k in range(1, n_blk):
        src = lax.rem(me + n_blk - k, n_blk)
        incoming = pltpu.make_async_remote_copy(
            src_ref=part_ref.at[pl.ds(0, rows)],
            dst_ref=recv.at[src],
            send_sem=send_sem.at[src],
            recv_sem=recv_sem.at[src],
            device_id=(req, src),
            device_id_type=MESH_IDS,
        )
        incoming.wait_recv()
        total = total + recv[src].astype(jnp.float32)
    for copy in copies:
        copy.wait_send()
    out_ref[...] = total


def gather_kernel(n_blk, piece_ref, out_ref, send_sem, recv_sem):
    b = lax.axis_index("blk")
    req = lax.axis_index("req")
    n_grp = n_blk // 2
    g = b // 2
    c = lax.rem(b, 2)
    partner = g * 2 + 1 - c
    rows = piece_ref.shape[0]
    half = n_grp * rows
    barrier = pltpu.get_barrier_semaphore()
    for k in range(1, n_grp):
        peer = lax.rem(g + k, n_grp) * 2 + c
        pl.semaphore_signal(barrier, inc=1, device_id=(req, peer), device_id_type=MESH_IDS)
    pl.semaphore_signal(barrier, inc=1, device_id=(req, partner), device_id_type=MESH_IDS)
    pl.semaphore_wait(barrier, n_grp)
    mine = pl.ds(pl.multiple_of(c * half + g * rows, rows), rows)
    sends = []
    for k in range(1, n_grp):
        peer = lax.rem(g + k, n_grp) * 2 + c
        copy = pltpu.make_async_remote_copy(
            src_ref=piece_ref,
            dst_ref=out_ref.at[mine],
            send_sem=send_sem.at[k],
            recv_sem=recv_sem.at[g],
            device_id=(req, peer),
            device_id_type=MESH_IDS,
        )
        copy.start()
        sends.append(copy)
    copy = pltpu.make_async_remote_copy(
        src_ref=piece_ref,
        dst_ref=out_ref.at[mine],
        send_sem=send_sem.at[0],
        recv_sem=recv_sem.at[n_grp + g],
        device_id=(req, partner),
        device_id_type=MESH_IDS,
    )
    copy.start()
    sends.append(copy)
    out_ref[mine, :] = piece_ref[...]
    for k in range(1, n_grp):
        grp = lax.rem(g + n_grp - k, n_grp)
        there = pl.ds(pl.multiple_of(c * half + grp * rows, rows), rows)
        incoming = pltpu.make_async_remote_copy(
            src_ref=piece_ref,
            dst_ref=out_ref.at[there],
            send_sem=send_sem.at[0],
            recv_sem=recv_sem.at[grp],
            device_id=(req, grp * 2 + c),
            device_id_type=MESH_IDS,
        )
        incoming.wait_recv()
        forward = pltpu.make_async_remote_copy(
            src_ref=out_ref.at[there],
            dst_ref=out_ref.at[there],
            send_sem=send_sem.at[n_grp + k],
            recv_sem=recv_sem.at[n_grp + grp],
            device_id=(req, partner),
            device_id_type=MESH_IDS,
        )
        forward.start()
        sends.append(forward)
    for grp in range(n_grp):
        there = pl.ds(pl.multiple_of((1 - c) * half + grp * rows, rows), rows)
        incoming = pltpu.make_async_remote_copy(
            src_ref=piece_ref,
            dst_ref=out_ref.at[there],
            send_sem=send_sem.at[0],
            recv_sem=recv_sem.at[n_grp + grp],
            device_id=(req, partner),
            device_id_type=MESH_IDS,
        )
        incoming.wait_recv()
    for copy in sends:
        copy.wait_send()


def blk_scatter(part):
    n_blk = lax.axis_size("blk")
    rows = part.shape[0] // n_blk
    vmem = pl.BlockSpec(memory_space=pltpu.VMEM)
    return pl.pallas_call(
        functools.partial(scatter_kernel, n_blk),
        out_shape=jax.ShapeDtypeStruct((rows, part.shape[1]), jnp.float32),
        in_specs=[vmem],
        out_specs=vmem,
        scratch_shapes=[
            pltpu.VMEM((n_blk, rows, part.shape[1]), part.dtype),
            pltpu.SemaphoreType.DMA((n_blk,)),
            pltpu.SemaphoreType.DMA((n_blk,)),
        ],
        compiler_params=pltpu.CompilerParams(collective_id=1, has_side_effects=True),
    )(part)


def blk_gather(piece):
    n_blk = lax.axis_size("blk")
    rows = piece.shape[0]
    vmem = pl.BlockSpec(memory_space=pltpu.VMEM)
    return pl.pallas_call(
        functools.partial(gather_kernel, n_blk),
        out_shape=jax.ShapeDtypeStruct((rows * n_blk, piece.shape[1]), piece.dtype),
        in_specs=[vmem],
        out_specs=vmem,
        scratch_shapes=[
            pltpu.SemaphoreType.DMA((n_blk,)),
            pltpu.SemaphoreType.DMA((n_blk,)),
        ],
        compiler_params=pltpu.CompilerParams(collective_id=2, has_side_effects=True),
    )(piece)


def prologue_kernel(n_req, n_blk, ordered_ref, packed_ref, cache_ref, wts_ref, w_send, w_recv, c_send, c_recv, local_sem):
    r = lax.axis_index("req")
    b = lax.axis_index("blk")
    n_slot, span, width = ordered_ref.shape
    piece = width // 2
    copies = []
    for k in range(1, n_req):
        peer = lax.rem(r + k, n_req)
        copy = pltpu.make_async_remote_copy(
            src_ref=packed_ref,
            dst_ref=wts_ref.at[r],
            send_sem=w_send.at[peer],
            recv_sem=w_recv.at[r],
            device_id=(peer, b),
            device_id_type=MESH_IDS,
        )
        copy.start()
        copies.append(copy)
    rows = pl.ds(pl.multiple_of(b * span, span), span)
    for s in range(n_slot):
        for hh in range(2):
            head = 2 * r + hh
            is_self = jnp.logical_and(r == s, head == b)
            src = ordered_ref.at[s, :, pl.ds(hh * piece, piece)]
            copy = pltpu.make_async_remote_copy(
                src_ref=src,
                dst_ref=cache_ref.at[rows],
                send_sem=c_send.at[s * 2 + hh],
                recv_sem=c_recv.at[b],
                device_id=(s, head),
                device_id_type=MESH_IDS,
            )

            @pl.when(jnp.logical_not(is_self))
            def _():
                copy.start()

            @pl.when(is_self)
            def _():
                local = pltpu.make_async_copy(src, cache_ref.at[rows], local_sem.at[0])
                local.start()
                local.wait()

            copies.append((copy, is_self))
    wts_ref[r] = packed_ref[...]
    for k in range(1, n_req):
        src_req = lax.rem(r + n_req - k, n_req)
        incoming = pltpu.make_async_remote_copy(
            src_ref=packed_ref,
            dst_ref=wts_ref.at[src_req],
            send_sem=w_send.at[src_req],
            recv_sem=w_recv.at[src_req],
            device_id=(src_req, b),
            device_id_type=MESH_IDS,
        )
        incoming.wait_recv()
    owner = b // 2
    for j in range(n_blk):
        incoming = pltpu.make_async_remote_copy(
            src_ref=ordered_ref.at[0, :, pl.ds(0, piece)],
            dst_ref=cache_ref.at[pl.ds(j * span, span)],
            send_sem=c_send.at[0],
            recv_sem=c_recv.at[j],
            device_id=(owner, j),
            device_id_type=MESH_IDS,
        )

        @pl.when(jnp.logical_not(jnp.logical_and(owner == r, j == b)))
        def _():
            incoming.wait_recv()

    for item in copies:
        if isinstance(item, tuple):
            copy, is_self = item

            @pl.when(jnp.logical_not(is_self))
            def _():
                copy.wait_send()

        else:
            item.wait_send()


def prologue(ordered, packed):
    n_req = lax.axis_size("req")
    n_blk = lax.axis_size("blk")
    n_slot, span, width = ordered.shape
    any_spec = pl.BlockSpec(memory_space=pl.ANY)
    vmem = pl.BlockSpec(memory_space=pltpu.VMEM)
    return pl.pallas_call(
        functools.partial(prologue_kernel, n_req, n_blk),
        out_shape=(
            jax.ShapeDtypeStruct((span * n_blk, width // 2), ordered.dtype),
            jax.ShapeDtypeStruct((n_req,) + packed.shape, packed.dtype),
        ),
        in_specs=[any_spec, vmem],
        out_specs=(any_spec, vmem),
        scratch_shapes=[
            pltpu.SemaphoreType.DMA((n_req,)),
            pltpu.SemaphoreType.DMA((n_req,)),
            pltpu.SemaphoreType.DMA((2 * n_slot,)),
            pltpu.SemaphoreType.DMA((n_blk,)),
            pltpu.SemaphoreType.DMA((1,)),
        ],
        compiler_params=pltpu.CompilerParams(has_side_effects=True),
    )(ordered, packed)


def unpack(whole, pieces):
    n_req = whole.shape[0]
    whole = whole.reshape(n_req, -1)
    out, at = [], 0
    for w, axis in pieces:
        size = w.size
        part = whole[:, at : at + size].reshape((n_req,) + w.shape)
        at += size
        part = jnp.moveaxis(part, 0, axis)
        shape = list(w.shape)
        shape[axis] *= n_req
        out.append(part.reshape(shape))
    return out


def per_device(
    new_states,
    encoder_out,
    cache_in,
    slot_order,
    new_lengths,
    cache_lengths,
    enc_lengths,
    bucket_of,
    rel_bias,
    norm_gain,
    self_q,
    self_kv,
    self_out,
    cross_q,
    cross_kv,
    cross_out,
    ff_in,
    ff_out,
):
    blk_count = lax.axis_size("blk")
    heads_dev = H // blk_count
    width_dev = heads_dev * HD
    req_dev = cache_in.shape[0] // lax.axis_size("req")
    own_slots = lax.dynamic_slice_in_dim(slot_order, lax.axis_index("req") * req_dev, req_dev, 0)
    slot_new = pick_lengths(new_lengths, own_slots)
    slot_old = pick_lengths(cache_lengths, own_slots)
    slot_enc = pick_lengths(enc_lengths, own_slots)
    ordered = jnp.take(cache_in, slot_order, axis=0)
    onehot = (bucket_of[:, None] == jnp.arange(rel_bias.shape[0], dtype=jnp.int32)[None, :]).astype(
        jnp.float32
    )
    own_bias = lax.dynamic_slice_in_dim(rel_bias, lax.axis_index("blk") * heads_dev, heads_dev, 1)
    bias_dist = jnp.dot(onehot, own_bias, precision=lax.Precision.HIGHEST).T
    early = [(self_q, 0), (self_kv, 0), (self_out, 1)]
    late = [(cross_q, 0), (cross_kv, 0), (cross_out, 1), (ff_in, 0), (ff_out, 1)]
    flat = jnp.concatenate([w.reshape(-1) for w, _ in early])
    cache_blk, whole = prologue(ordered, flat.reshape(-1, 128))
    cache_dec = cache_blk[None]
    gathered = unpack(whole, early) + pack_gather(late)
    wq_self, wkv_self, wo_self, wq_cross, wkv_cross, wo_cross, w_in, w_out = gathered
    n_blk = lax.axis_size("blk")
    rows_dev = new_states.shape[0] // n_blk
    own_rows = lax.dynamic_slice_in_dim(
        new_states, chunk_of(lax.axis_index("blk"), n_blk) * rows_dev, rows_dev, 0
    ).astype(jnp.float32)
    normed = rms_rows(new_states.astype(jnp.float32), norm_gain[0])
    self_cat = jnp.concatenate([wq_self, wkv_self.reshape(wkv_self.shape[0], -1)], axis=1)
    projected = jnp.dot(normed, self_cat, preferred_element_type=jnp.float32).astype(
        jnp.bfloat16
    )
    context = self_attention(
        projected[:, :HD],
        cache_dec[0],
        projected[:, HD : 2 * HD],
        projected[:, 2 * HD :],
        bias_dist[0],
        slot_old[0],
        slot_new[0],
    )
    part = jnp.dot(context, wo_self, preferred_element_type=jnp.float32).astype(jnp.bfloat16)
    residual = own_rows + blk_scatter(part)
    normed = blk_gather(rms_rows(residual, norm_gain[1]))
    queries = (
        jnp.dot(normed, wq_cross, preferred_element_type=jnp.float32)
        .astype(jnp.bfloat16)
        .reshape(req_dev, -1, heads_dev, HD)
    )
    cross_pair = wkv_cross.reshape(wkv_cross.shape[0], -1)
    key_value = (
        jnp.dot(encoder_out, cross_pair, preferred_element_type=jnp.float32)
        .astype(jnp.bfloat16)
        .reshape(req_dev, -1, 2, heads_dev, HD)
    )
    context = cross_attend(queries, key_value, slot_enc)
    part = jnp.dot(context.reshape(-1, width_dev), wo_cross, preferred_element_type=jnp.float32)
    residual = residual + blk_scatter(part.astype(jnp.bfloat16))
    normed = blk_gather(rms_rows(residual, norm_gain[2]))
    ff_dev = w_in.shape[2]
    gate_up = jnp.dot(normed, w_in.reshape(w_in.shape[0], -1), preferred_element_type=jnp.float32)
    hidden = (jax.nn.gelu(gate_up[:, :ff_dev], approximate=True) * gate_up[:, ff_dev:]).astype(
        jnp.bfloat16
    )
    part = jnp.dot(hidden, w_out, preferred_element_type=jnp.float32).astype(jnp.bfloat16)
    layer_out = blk_gather((residual + blk_scatter(part)).astype(jnp.bfloat16))
    return (layer_out, cache_dec)


def solution(mesh):
    in_specs = (
        P("req", None),
        P("req", None),
        P(None, "blk", "req"),
        P(),
        P(),
        P(),
        P(),
        P(),
        P(),
        P(),
        P("req", "blk"),
        P("req", None, "blk"),
        P("blk", "req"),
        P("req", "blk"),
        P("req", None, "blk"),
        P("blk", "req"),
        P("req", None, "blk"),
        P("blk", "req"),
    )
    out_specs = (P("req", None), P("req", None, "blk"))
    return jax.shard_map(
        per_device, mesh=mesh, in_specs=in_specs, out_specs=out_specs, check_vma=False
    )
```

```python
import functools

import jax
import jax.numpy as jnp
from jax import lax
from jax.sharding import PartitionSpec as P
from jax.experimental import pallas as pl
from jax.experimental.pallas import tpu as pltpu

H = 16
HD = 64


EPSILON = 1e-06
NEG_FILL = -1e30


def rms_rows(row_block, gain):
    mean_square = jnp.mean(row_block * row_block, axis=-1, keepdims=True)
    return (row_block * lax.rsqrt(mean_square + EPSILON) * gain).astype(jnp.bfloat16)


def softmax_rows(scores):
    row_top = jnp.max(scores, axis=-1, keepdims=True)
    weights = jnp.exp(scores - row_top)
    return (weights / jnp.sum(weights, axis=-1, keepdims=True)).astype(jnp.bfloat16)


def pick_lengths(table, own_slots):
    matches = own_slots[:, None] == jnp.arange(table.shape[0], dtype=jnp.int32)[None, :]
    return jnp.sum(jnp.where(matches, table[None, :], 0), axis=1)


def shifted_bias(bias_dist, base, row_count, col_count):
    heads_here, span_len = bias_dist.shape
    line_len = row_count + col_count - 1
    steps = jnp.arange(line_len + 1, dtype=jnp.int32)
    line = bias_dist[:, jnp.clip(base + row_count - 1 - steps, 0, span_len - 1)]
    tiled = jnp.broadcast_to(line[:, None, :], (heads_here, row_count, line_len + 1))
    flat = tiled.reshape(heads_here, row_count * (line_len + 1))[:, : row_count * line_len]
    skewed = flat.reshape(heads_here, row_count, line_len)
    return skewed[:, :, row_count - 1 : row_count - 1 + col_count]


def row_total(left, weight):
    term = jnp.dot(left, weight, preferred_element_type=jnp.float32)
    return lax.psum(term.astype(jnp.bfloat16), "blk").astype(jnp.float32)


def cached_scores(queries, key_rows, first_col, old_len, bias_dist):
    col_ids = first_col + jnp.arange(key_rows.shape[0], dtype=jnp.int32)[None, :]
    scores = jnp.einsum("qhe,khe->hqk", queries, key_rows, preferred_element_type=jnp.float32)
    scores = scores + shifted_bias(
        bias_dist, old_len - first_col, queries.shape[0], key_rows.shape[0]
    )
    return jnp.where((col_ids < old_len)[None], scores, NEG_FILL)


def fresh_scores(queries, fresh_keys, fresh_len, bias_dist):
    row_ids = jnp.arange(queries.shape[0], dtype=jnp.int32)[:, None]
    col_ids = jnp.arange(fresh_keys.shape[0], dtype=jnp.int32)[None, :]
    scores = jnp.einsum("qhe,khe->hqk", queries, fresh_keys, preferred_element_type=jnp.float32)
    scores = scores + shifted_bias(bias_dist, 0, queries.shape[0], fresh_keys.shape[0])
    admitted = (col_ids <= row_ids) & (col_ids < fresh_len)
    return jnp.where(admitted[None], scores, NEG_FILL)


def self_padded(
    queries, key_rows, value_rows, fresh_keys, fresh_values, old_len, fresh_len, bias_dist
):
    scores = jnp.concatenate(
        [
            cached_scores(queries, key_rows, 0, old_len, bias_dist),
            fresh_scores(queries, fresh_keys, fresh_len, bias_dist),
        ],
        axis=2,
    )
    weights = softmax_rows(scores)
    value_all = jnp.concatenate([value_rows, fresh_values], axis=0)
    return jnp.einsum(
        "hqk,khe->qhe", weights, value_all, preferred_element_type=jnp.float32
    ).astype(jnp.bfloat16)


def self_attend(queries, key_value, cache_dec, slot_old, slot_new, bias_dist, heads_dev):
    req_dev, cache_len = (cache_dec.shape[0], cache_dec.shape[1])
    cache_split = cache_dec.reshape(req_dev, cache_len, heads_dev, 2, -1)

    def one_request(request):
        queries_one, pair_one, cache_one, old_len, fresh_len = request
        return self_padded(
            queries_one,
            cache_one[:, :, 0],
            cache_one[:, :, 1],
            pair_one[:, 0],
            pair_one[:, 1],
            old_len,
            fresh_len,
            bias_dist,
        )

    return lax.map(one_request, (queries, key_value, cache_split, slot_old, slot_new))


def cross_attend(queries, key_value, slot_enc):
    scores = jnp.einsum(
        "rqhe,rkhe->rhqk", queries, key_value[:, :, 0], preferred_element_type=jnp.float32
    )
    col_ids = jnp.arange(key_value.shape[1], dtype=jnp.int32)
    scores = jnp.where(
        col_ids[None, None, None, :] < slot_enc[:, None, None, None], scores, NEG_FILL
    )
    weights = softmax_rows(scores)
    return jnp.einsum(
        "rhqk,rkhe->rqhe", weights, key_value[:, :, 1], preferred_element_type=jnp.float32
    ).astype(jnp.bfloat16)


def add_branch(residual, left, weight, gain):
    residual = residual + row_total(left, weight)
    normed = rms_rows(residual, gain)
    return (residual, normed)


TQ = 128


def stage_kernel(n_blk, final, part_ref, resid_ref, gain_ref, res_out, full_ref, recv, rs_send, rs_recv, ag_send, ag_recv):
    me = lax.axis_index("blk")
    req = lax.axis_index("req")
    rows = resid_ref.shape[0]
    n_grp = n_blk // 2
    g = me // 2
    c = lax.rem(me, 2)
    partner = g * 2 + 1 - c
    half = n_grp * rows
    greet_all(n_blk, me, req)
    sends = []
    for k in range(1, n_blk):
        peer = lax.rem(me + k, n_blk)
        copy = pltpu.make_async_remote_copy(
            src_ref=part_ref.at[pl.ds(pl.multiple_of(chunk_of(peer, n_blk) * rows, rows), rows)],
            dst_ref=recv.at[me],
            send_sem=rs_send.at[peer],
            recv_sem=rs_recv.at[me],
            device_id=(req, peer),
            device_id_type=MESH_IDS,
        )
        copy.start()
        sends.append(copy)
    mine = pl.ds(pl.multiple_of(c * half + g * rows, rows), rows)
    total = part_ref[mine, :].astype(jnp.float32)
    for k in range(1, n_blk):
        src = lax.rem(me + n_blk - k, n_blk)
        incoming = pltpu.make_async_remote_copy(
            src_ref=part_ref.at[pl.ds(0, rows)],
            dst_ref=recv.at[src],
            send_sem=rs_send.at[src],
            recv_sem=rs_recv.at[src],
            device_id=(req, src),
            device_id_type=MESH_IDS,
        )
        incoming.wait_recv()
        total = total + recv[src].astype(jnp.float32)
    resid = resid_ref[...] + total
    res_out[...] = resid
    if final:
        full_ref[mine, :] = resid.astype(full_ref.dtype)
    else:
        mean_square = jnp.mean(resid * resid, axis=-1, keepdims=True)
        full_ref[mine, :] = (resid * lax.rsqrt(mean_square + EPSILON) * gain_ref[...]).astype(
            full_ref.dtype
        )
    for k in range(1, n_grp):
        peer = lax.rem(g + k, n_grp) * 2 + c
        copy = pltpu.make_async_remote_copy(
            src_ref=full_ref.at[mine],
            dst_ref=full_ref.at[mine],
            send_sem=ag_send.at[k],
            recv_sem=ag_recv.at[g],
            device_id=(req, peer),
            device_id_type=MESH_IDS,
        )
        copy.start()
        sends.append(copy)
    copy = pltpu.make_async_remote_copy(
        src_ref=full_ref.at[mine],
        dst_ref=full_ref.at[mine],
        send_sem=ag_send.at[0],
        recv_sem=ag_recv.at[n_grp + g],
        device_id=(req, partner),
        device_id_type=MESH_IDS,
    )
    copy.start()
    sends.append(copy)
    for k in range(1, n_grp):
        grp = lax.rem(g + n_grp - k, n_grp)
        there = pl.ds(pl.multiple_of(c * half + grp * rows, rows), rows)
        incoming = pltpu.make_async_remote_copy(
            src_ref=full_ref.at[there],
            dst_ref=full_ref.at[there],
            send_sem=ag_send.at[0],
            recv_sem=ag_recv.at[grp],
            device_id=(req, grp * 2 + c),
            device_id_type=MESH_IDS,
        )
        incoming.wait_recv()
        forward = pltpu.make_async_remote_copy(
            src_ref=full_ref.at[there],
            dst_ref=full_ref.at[there],
            send_sem=ag_send.at[n_grp + k],
            recv_sem=ag_recv.at[n_grp + grp],
            device_id=(req, partner),
            device_id_type=MESH_IDS,
        )
        forward.start()
        sends.append(forward)
    for grp in range(n_grp):
        there = pl.ds(pl.multiple_of((1 - c) * half + grp * rows, rows), rows)
        incoming = pltpu.make_async_remote_copy(
            src_ref=full_ref.at[there],
            dst_ref=full_ref.at[there],
            send_sem=ag_send.at[0],
            recv_sem=ag_recv.at[n_grp + grp],
            device_id=(req, partner),
            device_id_type=MESH_IDS,
        )
        incoming.wait_recv()
    for copy in sends:
        copy.wait_send()


def blk_stage(part, resid, gain, final):
    n_blk = lax.axis_size("blk")
    rows, width = resid.shape
    vmem = pl.BlockSpec(memory_space=pltpu.VMEM)
    return pl.pallas_call(
        functools.partial(stage_kernel, n_blk, final),
        out_shape=(
            jax.ShapeDtypeStruct((rows, width), jnp.float32),
            jax.ShapeDtypeStruct((rows * n_blk, width), jnp.bfloat16),
        ),
        in_specs=[vmem] * 3,
        out_specs=(vmem, vmem),
        scratch_shapes=[
            pltpu.VMEM((n_blk, rows, width), part.dtype),
            pltpu.SemaphoreType.DMA((n_blk,)),
            pltpu.SemaphoreType.DMA((n_blk,)),
            pltpu.SemaphoreType.DMA((n_blk,)),
            pltpu.SemaphoreType.DMA((n_blk,)),
        ],
        compiler_params=pltpu.CompilerParams(
            collective_id=4 if final else 3, has_side_effects=True
        ),
    )(part, resid, gain[None, :])


def self_kernel(lens_ref, q_ref, c_ref, kn_ref, vn_ref, g_ref, f_ref, o_ref):
    old_len = lens_ref[0]
    fresh_len = lens_ref[1]
    n_q = q_ref.shape[0]
    n_ctx = c_ref.shape[0]
    wide_old = n_ctx + TQ
    wide_new = n_q + TQ
    k_old = c_ref[:, :HD]
    v_old = c_ref[:, HD:]
    k_new = kn_ref[...]
    v_new = vn_ref[...]
    dims = (((1,), (1,)), ((), ()))
    for t in range(n_q // TQ):
        q = q_ref[t * TQ : (t + 1) * TQ, :]
        start = n_q - TQ - t * TQ
        s_old = lax.dot_general(q, k_old, dims, preferred_element_type=jnp.float32)
        line = jnp.broadcast_to(g_ref[:, start : start + wide_old], (TQ, wide_old))
        bias = pltpu.roll(line, wide_old - (TQ - 1), 1, stride=1, stride_axis=0)[:, :n_ctx]
        col = lax.broadcasted_iota(jnp.int32, (TQ, n_ctx), 1)
        s_old = jnp.where(col < old_len, s_old + bias, NEG_FILL)
        s_new = lax.dot_general(q, k_new, dims, preferred_element_type=jnp.float32)
        line = jnp.broadcast_to(f_ref[:, start : start + wide_new], (TQ, wide_new))
        bias = pltpu.roll(line, wide_new - (TQ - 1), 1, stride=1, stride_axis=0)[:, :n_q]
        row = lax.broadcasted_iota(jnp.int32, (TQ, n_q), 0) + t * TQ
        col = lax.broadcasted_iota(jnp.int32, (TQ, n_q), 1)
        s_new = jnp.where((col <= row) & (col < fresh_len), s_new + bias, NEG_FILL)
        top = jnp.maximum(
            jnp.max(s_old, axis=1, keepdims=True), jnp.max(s_new, axis=1, keepdims=True)
        )
        p_old = jnp.exp(s_old - top)
        p_new = jnp.exp(s_new - top)
        total = jnp.sum(p_old, axis=1, keepdims=True) + jnp.sum(p_new, axis=1, keepdims=True)
        w_old = (p_old / total).astype(jnp.bfloat16)
        w_new = (p_new / total).astype(jnp.bfloat16)
        out = jnp.dot(w_old, v_old, preferred_element_type=jnp.float32) + jnp.dot(
            w_new, v_new, preferred_element_type=jnp.float32
        )
        o_ref[t * TQ : (t + 1) * TQ, :] = out.astype(jnp.bfloat16)


def bias_lines(line, old_len, n_q, n_ctx):
    span = line.shape[0]
    ext = jnp.concatenate([jnp.broadcast_to(line[:1], (n_ctx,)), line])
    rev = ext[::-1]
    g = lax.dynamic_slice_in_dim(rev, n_ctx - old_len, span)
    f = rev[n_ctx : n_ctx + 2 * n_q]
    return g[None, :], f[None, :]


def self_attention(q, cache_blk, k_new, v_new, line, old_len, fresh_len):
    n_q = q.shape[0]
    n_ctx = cache_blk.shape[0]
    g, f = bias_lines(line, old_len, n_q, n_ctx)
    lens = jnp.stack([old_len, fresh_len]).astype(jnp.int32)
    vmem = pl.BlockSpec(memory_space=pltpu.VMEM)
    return pl.pallas_call(
        self_kernel,
        out_shape=jax.ShapeDtypeStruct((n_q, HD), jnp.bfloat16),
        in_specs=[pl.BlockSpec(memory_space=pltpu.SMEM)] + [vmem] * 6,
        out_specs=vmem,
        compiler_params=pltpu.CompilerParams(vmem_limit_bytes=48 * 1024 * 1024),
    )(lens, q, cache_blk, k_new, v_new, g, f)


def pack_gather(pieces):
    flat = jnp.concatenate([w.reshape(-1) for w, _ in pieces])
    whole = lax.all_gather(flat, "req", axis=0, tiled=False)
    n_req = whole.shape[0]
    out, at = [], 0
    for w, axis in pieces:
        size = w.size
        part = whole[:, at : at + size].reshape((n_req,) + w.shape)
        at += size
        part = jnp.moveaxis(part, 0, axis)
        shape = list(w.shape)
        shape[axis] *= n_req
        out.append(part.reshape(shape))
    return out


MESH_IDS = pl.DeviceIdType.MESH


def greet_all(n_blk, me, req):
    barrier = pltpu.get_barrier_semaphore()
    for k in range(1, n_blk):
        peer = lax.rem(me + k, n_blk)
        pl.semaphore_signal(barrier, inc=1, device_id=(req, peer), device_id_type=MESH_IDS)
    pl.semaphore_wait(barrier, n_blk - 1)


def chunk_of(b, n_blk):
    return lax.rem(b, 2) * (n_blk // 2) + b // 2


def scatter_kernel(n_blk, part_ref, out_ref, recv, send_sem, recv_sem):
    me = lax.axis_index("blk")
    req = lax.axis_index("req")
    rows = out_ref.shape[0]
    greet_all(n_blk, me, req)
    copies = []
    for k in range(1, n_blk):
        peer = lax.rem(me + k, n_blk)
        copy = pltpu.make_async_remote_copy(
            src_ref=part_ref.at[pl.ds(pl.multiple_of(chunk_of(peer, n_blk) * rows, rows), rows)],
            dst_ref=recv.at[me],
            send_sem=send_sem.at[peer],
            recv_sem=recv_sem.at[me],
            device_id=(req, peer),
            device_id_type=MESH_IDS,
        )
        copy.start()
        copies.append(copy)
    own = pl.ds(pl.multiple_of(chunk_of(me, n_blk) * rows, rows), rows)
    total = part_ref[own, :].astype(jnp.float32)
    for k in range(1, n_blk):
        src = lax.rem(me + n_blk - k, n_blk)
        incoming = pltpu.make_async_remote_copy(
            src_ref=part_ref.at[pl.ds(0, rows)],
            dst_ref=recv.at[src],
            send_sem=send_sem.at[src],
            recv_sem=recv_sem.at[src],
            device_id=(req, src),
            device_id_type=MESH_IDS,
        )
        incoming.wait_recv()
        total = total + recv[src].astype(jnp.float32)
    for copy in copies:
        copy.wait_send()
    out_ref[...] = total


def gather_kernel(n_blk, piece_ref, out_ref, send_sem, recv_sem):
    b = lax.axis_index("blk")
    req = lax.axis_index("req")
    n_grp = n_blk // 2
    g = b // 2
    c = lax.rem(b, 2)
    partner = g * 2 + 1 - c
    rows = piece_ref.shape[0]
    half = n_grp * rows
    barrier = pltpu.get_barrier_semaphore()
    for k in range(1, n_grp):
        peer = lax.rem(g + k, n_grp) * 2 + c
        pl.semaphore_signal(barrier, inc=1, device_id=(req, peer), device_id_type=MESH_IDS)
    pl.semaphore_signal(barrier, inc=1, device_id=(req, partner), device_id_type=MESH_IDS)
    pl.semaphore_wait(barrier, n_grp)
    mine = pl.ds(pl.multiple_of(c * half + g * rows, rows), rows)
    sends = []
    for k in range(1, n_grp):
        peer = lax.rem(g + k, n_grp) * 2 + c
        copy = pltpu.make_async_remote_copy(
            src_ref=piece_ref,
            dst_ref=out_ref.at[mine],
            send_sem=send_sem.at[k],
            recv_sem=recv_sem.at[g],
            device_id=(req, peer),
            device_id_type=MESH_IDS,
        )
        copy.start()
        sends.append(copy)
    copy = pltpu.make_async_remote_copy(
        src_ref=piece_ref,
        dst_ref=out_ref.at[mine],
        send_sem=send_sem.at[0],
        recv_sem=recv_sem.at[n_grp + g],
        device_id=(req, partner),
        device_id_type=MESH_IDS,
    )
    copy.start()
    sends.append(copy)
    out_ref[mine, :] = piece_ref[...]
    for k in range(1, n_grp):
        grp = lax.rem(g + n_grp - k, n_grp)
        there = pl.ds(pl.multiple_of(c * half + grp * rows, rows), rows)
        incoming = pltpu.make_async_remote_copy(
            src_ref=piece_ref,
            dst_ref=out_ref.at[there],
            send_sem=send_sem.at[0],
            recv_sem=recv_sem.at[grp],
            device_id=(req, grp * 2 + c),
            device_id_type=MESH_IDS,
        )
        incoming.wait_recv()
        forward = pltpu.make_async_remote_copy(
            src_ref=out_ref.at[there],
            dst_ref=out_ref.at[there],
            send_sem=send_sem.at[n_grp + k],
            recv_sem=recv_sem.at[n_grp + grp],
            device_id=(req, partner),
            device_id_type=MESH_IDS,
        )
        forward.start()
        sends.append(forward)
    for grp in range(n_grp):
        there = pl.ds(pl.multiple_of((1 - c) * half + grp * rows, rows), rows)
        incoming = pltpu.make_async_remote_copy(
            src_ref=piece_ref,
            dst_ref=out_ref.at[there],
            send_sem=send_sem.at[0],
            recv_sem=recv_sem.at[n_grp + grp],
            device_id=(req, partner),
            device_id_type=MESH_IDS,
        )
        incoming.wait_recv()
    for copy in sends:
        copy.wait_send()


def blk_scatter(part):
    n_blk = lax.axis_size("blk")
    rows = part.shape[0] // n_blk
    vmem = pl.BlockSpec(memory_space=pltpu.VMEM)
    return pl.pallas_call(
        functools.partial(scatter_kernel, n_blk),
        out_shape=jax.ShapeDtypeStruct((rows, part.shape[1]), jnp.float32),
        in_specs=[vmem],
        out_specs=vmem,
        scratch_shapes=[
            pltpu.VMEM((n_blk, rows, part.shape[1]), part.dtype),
            pltpu.SemaphoreType.DMA((n_blk,)),
            pltpu.SemaphoreType.DMA((n_blk,)),
        ],
        compiler_params=pltpu.CompilerParams(collective_id=1, has_side_effects=True),
    )(part)


def blk_gather(piece):
    n_blk = lax.axis_size("blk")
    rows = piece.shape[0]
    vmem = pl.BlockSpec(memory_space=pltpu.VMEM)
    return pl.pallas_call(
        functools.partial(gather_kernel, n_blk),
        out_shape=jax.ShapeDtypeStruct((rows * n_blk, piece.shape[1]), piece.dtype),
        in_specs=[vmem],
        out_specs=vmem,
        scratch_shapes=[
            pltpu.SemaphoreType.DMA((n_blk,)),
            pltpu.SemaphoreType.DMA((n_blk,)),
        ],
        compiler_params=pltpu.CompilerParams(collective_id=2, has_side_effects=True),
    )(piece)


def prologue_kernel(n_req, n_blk, ordered_ref, packed_ref, cache_ref, wts_ref, w_send, w_recv, c_send, c_recv, local_sem):
    r = lax.axis_index("req")
    b = lax.axis_index("blk")
    n_slot, span, width = ordered_ref.shape
    piece = width // 2
    copies = []
    for k in range(1, n_req):
        peer = lax.rem(r + k, n_req)
        copy = pltpu.make_async_remote_copy(
            src_ref=packed_ref,
            dst_ref=wts_ref.at[r],
            send_sem=w_send.at[peer],
            recv_sem=w_recv.at[r],
            device_id=(peer, b),
            device_id_type=MESH_IDS,
        )
        copy.start()
        copies.append(copy)
    rows = pl.ds(pl.multiple_of(b * span, span), span)
    for s in range(n_slot):
        for hh in range(2):
            head = 2 * r + hh
            is_self = jnp.logical_and(r == s, head == b)
            src = ordered_ref.at[s, :, pl.ds(hh * piece, piece)]
            copy = pltpu.make_async_remote_copy(
                src_ref=src,
                dst_ref=cache_ref.at[rows],
                send_sem=c_send.at[s * 2 + hh],
                recv_sem=c_recv.at[b],
                device_id=(s, head),
                device_id_type=MESH_IDS,
            )

            @pl.when(jnp.logical_not(is_self))
            def _():
                copy.start()

            @pl.when(is_self)
            def _():
                local = pltpu.make_async_copy(src, cache_ref.at[rows], local_sem.at[0])
                local.start()
                local.wait()

            copies.append((copy, is_self))
    wts_ref[r] = packed_ref[...]
    for k in range(1, n_req):
        src_req = lax.rem(r + n_req - k, n_req)
        incoming = pltpu.make_async_remote_copy(
            src_ref=packed_ref,
            dst_ref=wts_ref.at[src_req],
            send_sem=w_send.at[src_req],
            recv_sem=w_recv.at[src_req],
            device_id=(src_req, b),
            device_id_type=MESH_IDS,
        )
        incoming.wait_recv()
    owner = b // 2
    for j in range(n_blk):
        incoming = pltpu.make_async_remote_copy(
            src_ref=ordered_ref.at[0, :, pl.ds(0, piece)],
            dst_ref=cache_ref.at[pl.ds(j * span, span)],
            send_sem=c_send.at[0],
            recv_sem=c_recv.at[j],
            device_id=(owner, j),
            device_id_type=MESH_IDS,
        )

        @pl.when(jnp.logical_not(jnp.logical_and(owner == r, j == b)))
        def _():
            incoming.wait_recv()

    for item in copies:
        if isinstance(item, tuple):
            copy, is_self = item

            @pl.when(jnp.logical_not(is_self))
            def _():
                copy.wait_send()

        else:
            item.wait_send()


def prologue(ordered, packed):
    n_req = lax.axis_size("req")
    n_blk = lax.axis_size("blk")
    n_slot, span, width = ordered.shape
    any_spec = pl.BlockSpec(memory_space=pl.ANY)
    vmem = pl.BlockSpec(memory_space=pltpu.VMEM)
    return pl.pallas_call(
        functools.partial(prologue_kernel, n_req, n_blk),
        out_shape=(
            jax.ShapeDtypeStruct((span * n_blk, width // 2), ordered.dtype),
            jax.ShapeDtypeStruct((n_req,) + packed.shape, packed.dtype),
        ),
        in_specs=[any_spec, vmem],
        out_specs=(any_spec, vmem),
        scratch_shapes=[
            pltpu.SemaphoreType.DMA((n_req,)),
            pltpu.SemaphoreType.DMA((n_req,)),
            pltpu.SemaphoreType.DMA((2 * n_slot,)),
            pltpu.SemaphoreType.DMA((n_blk,)),
            pltpu.SemaphoreType.DMA((1,)),
        ],
        compiler_params=pltpu.CompilerParams(has_side_effects=True),
    )(ordered, packed)


def unpack(whole, pieces):
    n_req = whole.shape[0]
    whole = whole.reshape(n_req, -1)
    out, at = [], 0
    for w, axis in pieces:
        size = w.size
        part = whole[:, at : at + size].reshape((n_req,) + w.shape)
        at += size
        part = jnp.moveaxis(part, 0, axis)
        shape = list(w.shape)
        shape[axis] *= n_req
        out.append(part.reshape(shape))
    return out


def per_device(
    new_states,
    encoder_out,
    cache_in,
    slot_order,
    new_lengths,
    cache_lengths,
    enc_lengths,
    bucket_of,
    rel_bias,
    norm_gain,
    self_q,
    self_kv,
    self_out,
    cross_q,
    cross_kv,
    cross_out,
    ff_in,
    ff_out,
):
    blk_count = lax.axis_size("blk")
    heads_dev = H // blk_count
    width_dev = heads_dev * HD
    req_dev = cache_in.shape[0] // lax.axis_size("req")
    own_slots = lax.dynamic_slice_in_dim(slot_order, lax.axis_index("req") * req_dev, req_dev, 0)
    slot_new = pick_lengths(new_lengths, own_slots)
    slot_old = pick_lengths(cache_lengths, own_slots)
    slot_enc = pick_lengths(enc_lengths, own_slots)
    ordered = jnp.take(cache_in, slot_order, axis=0)
    onehot = (bucket_of[:, None] == jnp.arange(rel_bias.shape[0], dtype=jnp.int32)[None, :]).astype(
        jnp.float32
    )
    own_bias = lax.dynamic_slice_in_dim(rel_bias, lax.axis_index("blk") * heads_dev, heads_dev, 1)
    bias_dist = jnp.dot(onehot, own_bias, precision=lax.Precision.HIGHEST).T
    early = [(self_q, 0), (self_kv, 0), (self_out, 1)]
    late = [(cross_q, 0), (cross_kv, 0), (cross_out, 1), (ff_in, 0), (ff_out, 1)]
    flat = jnp.concatenate([w.reshape(-1) for w, _ in early])
    cache_blk, whole = prologue(ordered, flat.reshape(-1, 128))
    cache_dec = cache_blk[None]
    gathered = unpack(whole, early) + pack_gather(late)
    wq_self, wkv_self, wo_self, wq_cross, wkv_cross, wo_cross, w_in, w_out = gathered
    n_blk = lax.axis_size("blk")
    rows_dev = new_states.shape[0] // n_blk
    own_rows = lax.dynamic_slice_in_dim(
        new_states, chunk_of(lax.axis_index("blk"), n_blk) * rows_dev, rows_dev, 0
    ).astype(jnp.float32)
    normed = rms_rows(new_states.astype(jnp.float32), norm_gain[0])
    self_cat = jnp.concatenate([wq_self, wkv_self.reshape(wkv_self.shape[0], -1)], axis=1)
    projected = jnp.dot(normed, self_cat, preferred_element_type=jnp.float32).astype(
        jnp.bfloat16
    )
    context = self_attention(
        projected[:, :HD],
        cache_dec[0],
        projected[:, HD : 2 * HD],
        projected[:, 2 * HD :],
        bias_dist[0],
        slot_old[0],
        slot_new[0],
    )
    part = jnp.dot(context, wo_self, preferred_element_type=jnp.float32).astype(jnp.bfloat16)
    residual, normed = blk_stage(part, own_rows, norm_gain[1], False)
    queries = (
        jnp.dot(normed, wq_cross, preferred_element_type=jnp.float32)
        .astype(jnp.bfloat16)
        .reshape(req_dev, -1, heads_dev, HD)
    )
    cross_pair = wkv_cross.reshape(wkv_cross.shape[0], -1)
    key_value = (
        jnp.dot(encoder_out, cross_pair, preferred_element_type=jnp.float32)
        .astype(jnp.bfloat16)
        .reshape(req_dev, -1, 2, heads_dev, HD)
    )
    context = cross_attend(queries, key_value, slot_enc)
    part = jnp.dot(context.reshape(-1, width_dev), wo_cross, preferred_element_type=jnp.float32)
    residual, normed = blk_stage(part.astype(jnp.bfloat16), residual, norm_gain[2], False)
    ff_dev = w_in.shape[2]
    gate_up = jnp.dot(normed, w_in.reshape(w_in.shape[0], -1), preferred_element_type=jnp.float32)
    hidden = (jax.nn.gelu(gate_up[:, :ff_dev], approximate=True) * gate_up[:, ff_dev:]).astype(
        jnp.bfloat16
    )
    part = jnp.dot(hidden, w_out, preferred_element_type=jnp.float32).astype(jnp.bfloat16)
    _, layer_out = blk_stage(part, residual, norm_gain[2], True)
    return (layer_out, cache_dec)


def solution(mesh):
    in_specs = (
        P("req", None),
        P("req", None),
        P(None, "blk", "req"),
        P(),
        P(),
        P(),
        P(),
        P(),
        P(),
        P(),
        P("req", "blk"),
        P("req", None, "blk"),
        P("blk", "req"),
        P("req", "blk"),
        P("req", None, "blk"),
        P("blk", "req"),
        P("req", None, "blk"),
        P("blk", "req"),
    )
    out_specs = (P("req", None), P("req", None, "blk"))
    return jax.shard_map(
        per_device, mesh=mesh, in_specs=in_specs, out_specs=out_specs, check_vma=False
    )
```

```python
import functools

import jax
import jax.numpy as jnp
from jax import lax
from jax.sharding import PartitionSpec as P
from jax.experimental import pallas as pl
from jax.experimental.pallas import tpu as pltpu

H = 16
HD = 64


EPSILON = 1e-06
NEG_FILL = -1e30


def rms_rows(row_block, gain):
    mean_square = jnp.mean(row_block * row_block, axis=-1, keepdims=True)
    return (row_block * lax.rsqrt(mean_square + EPSILON) * gain).astype(jnp.bfloat16)


def softmax_rows(scores):
    row_top = jnp.max(scores, axis=-1, keepdims=True)
    weights = jnp.exp(scores - row_top)
    return (weights / jnp.sum(weights, axis=-1, keepdims=True)).astype(jnp.bfloat16)


def pick_lengths(table, own_slots):
    matches = own_slots[:, None] == jnp.arange(table.shape[0], dtype=jnp.int32)[None, :]
    return jnp.sum(jnp.where(matches, table[None, :], 0), axis=1)


def shifted_bias(bias_dist, base, row_count, col_count):
    heads_here, span_len = bias_dist.shape
    line_len = row_count + col_count - 1
    steps = jnp.arange(line_len + 1, dtype=jnp.int32)
    line = bias_dist[:, jnp.clip(base + row_count - 1 - steps, 0, span_len - 1)]
    tiled = jnp.broadcast_to(line[:, None, :], (heads_here, row_count, line_len + 1))
    flat = tiled.reshape(heads_here, row_count * (line_len + 1))[:, : row_count * line_len]
    skewed = flat.reshape(heads_here, row_count, line_len)
    return skewed[:, :, row_count - 1 : row_count - 1 + col_count]


def row_total(left, weight):
    term = jnp.dot(left, weight, preferred_element_type=jnp.float32)
    return lax.psum(term.astype(jnp.bfloat16), "blk").astype(jnp.float32)


def cached_scores(queries, key_rows, first_col, old_len, bias_dist):
    col_ids = first_col + jnp.arange(key_rows.shape[0], dtype=jnp.int32)[None, :]
    scores = jnp.einsum("qhe,khe->hqk", queries, key_rows, preferred_element_type=jnp.float32)
    scores = scores + shifted_bias(
        bias_dist, old_len - first_col, queries.shape[0], key_rows.shape[0]
    )
    return jnp.where((col_ids < old_len)[None], scores, NEG_FILL)


def fresh_scores(queries, fresh_keys, fresh_len, bias_dist):
    row_ids = jnp.arange(queries.shape[0], dtype=jnp.int32)[:, None]
    col_ids = jnp.arange(fresh_keys.shape[0], dtype=jnp.int32)[None, :]
    scores = jnp.einsum("qhe,khe->hqk", queries, fresh_keys, preferred_element_type=jnp.float32)
    scores = scores + shifted_bias(bias_dist, 0, queries.shape[0], fresh_keys.shape[0])
    admitted = (col_ids <= row_ids) & (col_ids < fresh_len)
    return jnp.where(admitted[None], scores, NEG_FILL)


def self_padded(
    queries, key_rows, value_rows, fresh_keys, fresh_values, old_len, fresh_len, bias_dist
):
    scores = jnp.concatenate(
        [
            cached_scores(queries, key_rows, 0, old_len, bias_dist),
            fresh_scores(queries, fresh_keys, fresh_len, bias_dist),
        ],
        axis=2,
    )
    weights = softmax_rows(scores)
    value_all = jnp.concatenate([value_rows, fresh_values], axis=0)
    return jnp.einsum(
        "hqk,khe->qhe", weights, value_all, preferred_element_type=jnp.float32
    ).astype(jnp.bfloat16)


def self_attend(queries, key_value, cache_dec, slot_old, slot_new, bias_dist, heads_dev):
    req_dev, cache_len = (cache_dec.shape[0], cache_dec.shape[1])
    cache_split = cache_dec.reshape(req_dev, cache_len, heads_dev, 2, -1)

    def one_request(request):
        queries_one, pair_one, cache_one, old_len, fresh_len = request
        return self_padded(
            queries_one,
            cache_one[:, :, 0],
            cache_one[:, :, 1],
            pair_one[:, 0],
            pair_one[:, 1],
            old_len,
            fresh_len,
            bias_dist,
        )

    return lax.map(one_request, (queries, key_value, cache_split, slot_old, slot_new))


def cross_attend(queries, key_value, slot_enc):
    scores = jnp.einsum(
        "rqhe,rkhe->rhqk", queries, key_value[:, :, 0], preferred_element_type=jnp.float32
    )
    col_ids = jnp.arange(key_value.shape[1], dtype=jnp.int32)
    scores = jnp.where(
        col_ids[None, None, None, :] < slot_enc[:, None, None, None], scores, NEG_FILL
    )
    weights = softmax_rows(scores)
    return jnp.einsum(
        "rhqk,rkhe->rqhe", weights, key_value[:, :, 1], preferred_element_type=jnp.float32
    ).astype(jnp.bfloat16)


def add_branch(residual, left, weight, gain):
    residual = residual + row_total(left, weight)
    normed = rms_rows(residual, gain)
    return (residual, normed)


TQ = 128


def stage_kernel(n_blk, final, extra, *refs):
    if extra:
        (part_ref, resid_ref, gain_ref, packed_ref, res_out, full_ref, wts_ref,
         recv, rs_send, rs_recv, ag_send, ag_recv, w_send, w_recv) = refs
    else:
        (part_ref, resid_ref, gain_ref, res_out, full_ref,
         recv, rs_send, rs_recv, ag_send, ag_recv) = refs
    me = lax.axis_index("blk")
    req = lax.axis_index("req")
    rows = resid_ref.shape[0]
    n_grp = n_blk // 2
    g = me // 2
    c = lax.rem(me, 2)
    partner = g * 2 + 1 - c
    half = n_grp * rows
    barrier = pltpu.get_barrier_semaphore()
    for k in range(1, n_blk):
        peer = lax.rem(me + k, n_blk)
        pl.semaphore_signal(barrier, inc=1, device_id=(req, peer), device_id_type=MESH_IDS)
    n_req = wts_ref.shape[0] if extra else 1
    for k in range(1, n_req):
        peer = lax.rem(req + k, n_req)
        pl.semaphore_signal(barrier, inc=1, device_id=(peer, me), device_id_type=MESH_IDS)
    pl.semaphore_wait(barrier, n_blk - 1 + n_req - 1)
    sends = []
    w_sends = []
    for k in range(1, n_req):
        peer = lax.rem(req + k, n_req)
        copy = pltpu.make_async_remote_copy(
            src_ref=packed_ref,
            dst_ref=wts_ref.at[req],
            send_sem=w_send.at[peer],
            recv_sem=w_recv.at[req],
            device_id=(peer, me),
            device_id_type=MESH_IDS,
        )
        copy.start()
        w_sends.append(copy)
    for k in range(1, n_blk):
        peer = lax.rem(me + k, n_blk)
        copy = pltpu.make_async_remote_copy(
            src_ref=part_ref.at[pl.ds(pl.multiple_of(chunk_of(peer, n_blk) * rows, rows), rows)],
            dst_ref=recv.at[me],
            send_sem=rs_send.at[peer],
            recv_sem=rs_recv.at[me],
            device_id=(req, peer),
            device_id_type=MESH_IDS,
        )
        copy.start()
        sends.append(copy)
    mine = pl.ds(pl.multiple_of(c * half + g * rows, rows), rows)
    total = part_ref[mine, :].astype(jnp.float32)
    for k in range(1, n_blk):
        src = lax.rem(me + n_blk - k, n_blk)
        incoming = pltpu.make_async_remote_copy(
            src_ref=part_ref.at[pl.ds(0, rows)],
            dst_ref=recv.at[src],
            send_sem=rs_send.at[src],
            recv_sem=rs_recv.at[src],
            device_id=(req, src),
            device_id_type=MESH_IDS,
        )
        incoming.wait_recv()
        total = total + recv[src].astype(jnp.float32)
    resid = resid_ref[...] + total
    res_out[...] = resid
    if final:
        full_ref[mine, :] = resid.astype(full_ref.dtype)
    else:
        mean_square = jnp.mean(resid * resid, axis=-1, keepdims=True)
        full_ref[mine, :] = (resid * lax.rsqrt(mean_square + EPSILON) * gain_ref[...]).astype(
            full_ref.dtype
        )
    for k in range(1, n_grp):
        peer = lax.rem(g + k, n_grp) * 2 + c
        copy = pltpu.make_async_remote_copy(
            src_ref=full_ref.at[mine],
            dst_ref=full_ref.at[mine],
            send_sem=ag_send.at[k],
            recv_sem=ag_recv.at[g],
            device_id=(req, peer),
            device_id_type=MESH_IDS,
        )
        copy.start()
        sends.append(copy)
    copy = pltpu.make_async_remote_copy(
        src_ref=full_ref.at[mine],
        dst_ref=full_ref.at[mine],
        send_sem=ag_send.at[0],
        recv_sem=ag_recv.at[n_grp + g],
        device_id=(req, partner),
        device_id_type=MESH_IDS,
    )
    copy.start()
    sends.append(copy)
    for k in range(1, n_grp):
        grp = lax.rem(g + n_grp - k, n_grp)
        there = pl.ds(pl.multiple_of(c * half + grp * rows, rows), rows)
        incoming = pltpu.make_async_remote_copy(
            src_ref=full_ref.at[there],
            dst_ref=full_ref.at[there],
            send_sem=ag_send.at[0],
            recv_sem=ag_recv.at[grp],
            device_id=(req, grp * 2 + c),
            device_id_type=MESH_IDS,
        )
        incoming.wait_recv()
        forward = pltpu.make_async_remote_copy(
            src_ref=full_ref.at[there],
            dst_ref=full_ref.at[there],
            send_sem=ag_send.at[n_grp + k],
            recv_sem=ag_recv.at[n_grp + grp],
            device_id=(req, partner),
            device_id_type=MESH_IDS,
        )
        forward.start()
        sends.append(forward)
    for grp in range(n_grp):
        there = pl.ds(pl.multiple_of((1 - c) * half + grp * rows, rows), rows)
        incoming = pltpu.make_async_remote_copy(
            src_ref=full_ref.at[there],
            dst_ref=full_ref.at[there],
            send_sem=ag_send.at[0],
            recv_sem=ag_recv.at[n_grp + grp],
            device_id=(req, partner),
            device_id_type=MESH_IDS,
        )
        incoming.wait_recv()
    if extra:
        wts_ref[req] = packed_ref[...]
        for k in range(1, n_req):
            src = lax.rem(req + n_req - k, n_req)
            incoming = pltpu.make_async_remote_copy(
                src_ref=packed_ref,
                dst_ref=wts_ref.at[src],
                send_sem=w_send.at[src],
                recv_sem=w_recv.at[src],
                device_id=(src, me),
                device_id_type=MESH_IDS,
            )
            incoming.wait_recv()
    for copy in sends + w_sends:
        copy.wait_send()


def blk_stage(part, resid, gain, final, packed=None):
    n_blk = lax.axis_size("blk")
    rows, width = resid.shape
    vmem = pl.BlockSpec(memory_space=pltpu.VMEM)
    extra = packed is not None
    outs = [
        jax.ShapeDtypeStruct((rows, width), jnp.float32),
        jax.ShapeDtypeStruct((rows * n_blk, width), jnp.bfloat16),
    ]
    scratch = [
        pltpu.VMEM((n_blk, rows, width), part.dtype),
        pltpu.SemaphoreType.DMA((n_blk,)),
        pltpu.SemaphoreType.DMA((n_blk,)),
        pltpu.SemaphoreType.DMA((n_blk,)),
        pltpu.SemaphoreType.DMA((n_blk,)),
    ]
    args = [part, resid, gain[None, :]]
    if extra:
        n_req = lax.axis_size("req")
        outs.append(jax.ShapeDtypeStruct((n_req,) + packed.shape, packed.dtype))
        scratch += [pltpu.SemaphoreType.DMA((n_req,)), pltpu.SemaphoreType.DMA((n_req,))]
        args.append(packed)
    return pl.pallas_call(
        functools.partial(stage_kernel, n_blk, final, extra),
        out_shape=tuple(outs),
        in_specs=[vmem] * len(args),
        out_specs=tuple([vmem] * len(outs)),
        scratch_shapes=scratch,
        compiler_params=pltpu.CompilerParams(
            collective_id=5 if extra else (4 if final else 3), has_side_effects=True
        ),
    )(*args)


def self_kernel(lens_ref, q_ref, c_ref, kn_ref, vn_ref, g_ref, f_ref, o_ref):
    old_len = lens_ref[0]
    fresh_len = lens_ref[1]
    n_q = q_ref.shape[0]
    n_ctx = c_ref.shape[0]
    wide_old = n_ctx + TQ
    wide_new = n_q + TQ
    k_old = c_ref[:, :HD]
    v_old = c_ref[:, HD:]
    k_new = kn_ref[...]
    v_new = vn_ref[...]
    dims = (((1,), (1,)), ((), ()))
    for t in range(n_q // TQ):
        q = q_ref[t * TQ : (t + 1) * TQ, :]
        start = n_q - TQ - t * TQ
        s_old = lax.dot_general(q, k_old, dims, preferred_element_type=jnp.float32)
        line = jnp.broadcast_to(g_ref[:, start : start + wide_old], (TQ, wide_old))
        bias = pltpu.roll(line, wide_old - (TQ - 1), 1, stride=1, stride_axis=0)[:, :n_ctx]
        col = lax.broadcasted_iota(jnp.int32, (TQ, n_ctx), 1)
        s_old = jnp.where(col < old_len, s_old + bias, NEG_FILL)
        s_new = lax.dot_general(q, k_new, dims, preferred_element_type=jnp.float32)
        line = jnp.broadcast_to(f_ref[:, start : start + wide_new], (TQ, wide_new))
        bias = pltpu.roll(line, wide_new - (TQ - 1), 1, stride=1, stride_axis=0)[:, :n_q]
        row = lax.broadcasted_iota(jnp.int32, (TQ, n_q), 0) + t * TQ
        col = lax.broadcasted_iota(jnp.int32, (TQ, n_q), 1)
        s_new = jnp.where((col <= row) & (col < fresh_len), s_new + bias, NEG_FILL)
        top = jnp.maximum(
            jnp.max(s_old, axis=1, keepdims=True), jnp.max(s_new, axis=1, keepdims=True)
        )
        p_old = jnp.exp(s_old - top)
        p_new = jnp.exp(s_new - top)
        total = jnp.sum(p_old, axis=1, keepdims=True) + jnp.sum(p_new, axis=1, keepdims=True)
        w_old = (p_old / total).astype(jnp.bfloat16)
        w_new = (p_new / total).astype(jnp.bfloat16)
        out = jnp.dot(w_old, v_old, preferred_element_type=jnp.float32) + jnp.dot(
            w_new, v_new, preferred_element_type=jnp.float32
        )
        o_ref[t * TQ : (t + 1) * TQ, :] = out.astype(jnp.bfloat16)


def bias_lines(line, old_len, n_q, n_ctx):
    span = line.shape[0]
    ext = jnp.concatenate([jnp.broadcast_to(line[:1], (n_ctx,)), line])
    rev = ext[::-1]
    g = lax.dynamic_slice_in_dim(rev, n_ctx - old_len, span)
    f = rev[n_ctx : n_ctx + 2 * n_q]
    return g[None, :], f[None, :]


def self_attention(q, cache_blk, k_new, v_new, line, old_len, fresh_len):
    n_q = q.shape[0]
    n_ctx = cache_blk.shape[0]
    g, f = bias_lines(line, old_len, n_q, n_ctx)
    lens = jnp.stack([old_len, fresh_len]).astype(jnp.int32)
    vmem = pl.BlockSpec(memory_space=pltpu.VMEM)
    return pl.pallas_call(
        self_kernel,
        out_shape=jax.ShapeDtypeStruct((n_q, HD), jnp.bfloat16),
        in_specs=[pl.BlockSpec(memory_space=pltpu.SMEM)] + [vmem] * 6,
        out_specs=vmem,
        compiler_params=pltpu.CompilerParams(vmem_limit_bytes=48 * 1024 * 1024),
    )(lens, q, cache_blk, k_new, v_new, g, f)


def pack_gather(pieces):
    flat = jnp.concatenate([w.reshape(-1) for w, _ in pieces])
    whole = lax.all_gather(flat, "req", axis=0, tiled=False)
    n_req = whole.shape[0]
    out, at = [], 0
    for w, axis in pieces:
        size = w.size
        part = whole[:, at : at + size].reshape((n_req,) + w.shape)
        at += size
        part = jnp.moveaxis(part, 0, axis)
        shape = list(w.shape)
        shape[axis] *= n_req
        out.append(part.reshape(shape))
    return out


MESH_IDS = pl.DeviceIdType.MESH


def greet_all(n_blk, me, req):
    barrier = pltpu.get_barrier_semaphore()
    for k in range(1, n_blk):
        peer = lax.rem(me + k, n_blk)
        pl.semaphore_signal(barrier, inc=1, device_id=(req, peer), device_id_type=MESH_IDS)
    pl.semaphore_wait(barrier, n_blk - 1)


def chunk_of(b, n_blk):
    return lax.rem(b, 2) * (n_blk // 2) + b // 2


def scatter_kernel(n_blk, part_ref, out_ref, recv, send_sem, recv_sem):
    me = lax.axis_index("blk")
    req = lax.axis_index("req")
    rows = out_ref.shape[0]
    greet_all(n_blk, me, req)
    copies = []
    for k in range(1, n_blk):
        peer = lax.rem(me + k, n_blk)
        copy = pltpu.make_async_remote_copy(
            src_ref=part_ref.at[pl.ds(pl.multiple_of(chunk_of(peer, n_blk) * rows, rows), rows)],
            dst_ref=recv.at[me],
            send_sem=send_sem.at[peer],
            recv_sem=recv_sem.at[me],
            device_id=(req, peer),
            device_id_type=MESH_IDS,
        )
        copy.start()
        copies.append(copy)
    own = pl.ds(pl.multiple_of(chunk_of(me, n_blk) * rows, rows), rows)
    total = part_ref[own, :].astype(jnp.float32)
    for k in range(1, n_blk):
        src = lax.rem(me + n_blk - k, n_blk)
        incoming = pltpu.make_async_remote_copy(
            src_ref=part_ref.at[pl.ds(0, rows)],
            dst_ref=recv.at[src],
            send_sem=send_sem.at[src],
            recv_sem=recv_sem.at[src],
            device_id=(req, src),
            device_id_type=MESH_IDS,
        )
        incoming.wait_recv()
        total = total + recv[src].astype(jnp.float32)
    for copy in copies:
        copy.wait_send()
    out_ref[...] = total


def gather_kernel(n_blk, piece_ref, out_ref, send_sem, recv_sem):
    b = lax.axis_index("blk")
    req = lax.axis_index("req")
    n_grp = n_blk // 2
    g = b // 2
    c = lax.rem(b, 2)
    partner = g * 2 + 1 - c
    rows = piece_ref.shape[0]
    half = n_grp * rows
    barrier = pltpu.get_barrier_semaphore()
    for k in range(1, n_grp):
        peer = lax.rem(g + k, n_grp) * 2 + c
        pl.semaphore_signal(barrier, inc=1, device_id=(req, peer), device_id_type=MESH_IDS)
    pl.semaphore_signal(barrier, inc=1, device_id=(req, partner), device_id_type=MESH_IDS)
    pl.semaphore_wait(barrier, n_grp)
    mine = pl.ds(pl.multiple_of(c * half + g * rows, rows), rows)
    sends = []
    for k in range(1, n_grp):
        peer = lax.rem(g + k, n_grp) * 2 + c
        copy = pltpu.make_async_remote_copy(
            src_ref=piece_ref,
            dst_ref=out_ref.at[mine],
            send_sem=send_sem.at[k],
            recv_sem=recv_sem.at[g],
            device_id=(req, peer),
            device_id_type=MESH_IDS,
        )
        copy.start()
        sends.append(copy)
    copy = pltpu.make_async_remote_copy(
        src_ref=piece_ref,
        dst_ref=out_ref.at[mine],
        send_sem=send_sem.at[0],
        recv_sem=recv_sem.at[n_grp + g],
        device_id=(req, partner),
        device_id_type=MESH_IDS,
    )
    copy.start()
    sends.append(copy)
    out_ref[mine, :] = piece_ref[...]
    for k in range(1, n_grp):
        grp = lax.rem(g + n_grp - k, n_grp)
        there = pl.ds(pl.multiple_of(c * half + grp * rows, rows), rows)
        incoming = pltpu.make_async_remote_copy(
            src_ref=piece_ref,
            dst_ref=out_ref.at[there],
            send_sem=send_sem.at[0],
            recv_sem=recv_sem.at[grp],
            device_id=(req, grp * 2 + c),
            device_id_type=MESH_IDS,
        )
        incoming.wait_recv()
        forward = pltpu.make_async_remote_copy(
            src_ref=out_ref.at[there],
            dst_ref=out_ref.at[there],
            send_sem=send_sem.at[n_grp + k],
            recv_sem=recv_sem.at[n_grp + grp],
            device_id=(req, partner),
            device_id_type=MESH_IDS,
        )
        forward.start()
        sends.append(forward)
    for grp in range(n_grp):
        there = pl.ds(pl.multiple_of((1 - c) * half + grp * rows, rows), rows)
        incoming = pltpu.make_async_remote_copy(
            src_ref=piece_ref,
            dst_ref=out_ref.at[there],
            send_sem=send_sem.at[0],
            recv_sem=recv_sem.at[n_grp + grp],
            device_id=(req, partner),
            device_id_type=MESH_IDS,
        )
        incoming.wait_recv()
    for copy in sends:
        copy.wait_send()


def blk_scatter(part):
    n_blk = lax.axis_size("blk")
    rows = part.shape[0] // n_blk
    vmem = pl.BlockSpec(memory_space=pltpu.VMEM)
    return pl.pallas_call(
        functools.partial(scatter_kernel, n_blk),
        out_shape=jax.ShapeDtypeStruct((rows, part.shape[1]), jnp.float32),
        in_specs=[vmem],
        out_specs=vmem,
        scratch_shapes=[
            pltpu.VMEM((n_blk, rows, part.shape[1]), part.dtype),
            pltpu.SemaphoreType.DMA((n_blk,)),
            pltpu.SemaphoreType.DMA((n_blk,)),
        ],
        compiler_params=pltpu.CompilerParams(collective_id=1, has_side_effects=True),
    )(part)


def blk_gather(piece):
    n_blk = lax.axis_size("blk")
    rows = piece.shape[0]
    vmem = pl.BlockSpec(memory_space=pltpu.VMEM)
    return pl.pallas_call(
        functools.partial(gather_kernel, n_blk),
        out_shape=jax.ShapeDtypeStruct((rows * n_blk, piece.shape[1]), piece.dtype),
        in_specs=[vmem],
        out_specs=vmem,
        scratch_shapes=[
            pltpu.SemaphoreType.DMA((n_blk,)),
            pltpu.SemaphoreType.DMA((n_blk,)),
        ],
        compiler_params=pltpu.CompilerParams(collective_id=2, has_side_effects=True),
    )(piece)


def prologue_kernel(n_req, n_blk, ordered_ref, packed_ref, cache_ref, wts_ref, w_send, w_recv, c_send, c_recv, local_sem):
    r = lax.axis_index("req")
    b = lax.axis_index("blk")
    n_slot, span, width = ordered_ref.shape
    piece = width // 2
    copies = []
    for k in range(1, n_req):
        peer = lax.rem(r + k, n_req)
        copy = pltpu.make_async_remote_copy(
            src_ref=packed_ref,
            dst_ref=wts_ref.at[r],
            send_sem=w_send.at[peer],
            recv_sem=w_recv.at[r],
            device_id=(peer, b),
            device_id_type=MESH_IDS,
        )
        copy.start()
        copies.append(copy)
    rows = pl.ds(pl.multiple_of(b * span, span), span)
    for s in range(n_slot):
        for hh in range(2):
            head = 2 * r + hh
            is_self = jnp.logical_and(r == s, head == b)
            src = ordered_ref.at[s, :, pl.ds(hh * piece, piece)]
            copy = pltpu.make_async_remote_copy(
                src_ref=src,
                dst_ref=cache_ref.at[rows],
                send_sem=c_send.at[s * 2 + hh],
                recv_sem=c_recv.at[b],
                device_id=(s, head),
                device_id_type=MESH_IDS,
            )

            @pl.when(jnp.logical_not(is_self))
            def _():
                copy.start()

            @pl.when(is_self)
            def _():
                local = pltpu.make_async_copy(src, cache_ref.at[rows], local_sem.at[0])
                local.start()
                local.wait()

            copies.append((copy, is_self))
    wts_ref[r] = packed_ref[...]
    for k in range(1, n_req):
        src_req = lax.rem(r + n_req - k, n_req)
        incoming = pltpu.make_async_remote_copy(
            src_ref=packed_ref,
            dst_ref=wts_ref.at[src_req],
            send_sem=w_send.at[src_req],
            recv_sem=w_recv.at[src_req],
            device_id=(src_req, b),
            device_id_type=MESH_IDS,
        )
        incoming.wait_recv()
    owner = b // 2
    for j in range(n_blk):
        incoming = pltpu.make_async_remote_copy(
            src_ref=ordered_ref.at[0, :, pl.ds(0, piece)],
            dst_ref=cache_ref.at[pl.ds(j * span, span)],
            send_sem=c_send.at[0],
            recv_sem=c_recv.at[j],
            device_id=(owner, j),
            device_id_type=MESH_IDS,
        )

        @pl.when(jnp.logical_not(jnp.logical_and(owner == r, j == b)))
        def _():
            incoming.wait_recv()

    for item in copies:
        if isinstance(item, tuple):
            copy, is_self = item

            @pl.when(jnp.logical_not(is_self))
            def _():
                copy.wait_send()

        else:
            item.wait_send()


def prologue(ordered, packed):
    n_req = lax.axis_size("req")
    n_blk = lax.axis_size("blk")
    n_slot, span, width = ordered.shape
    any_spec = pl.BlockSpec(memory_space=pl.ANY)
    vmem = pl.BlockSpec(memory_space=pltpu.VMEM)
    return pl.pallas_call(
        functools.partial(prologue_kernel, n_req, n_blk),
        out_shape=(
            jax.ShapeDtypeStruct((span * n_blk, width // 2), ordered.dtype),
            jax.ShapeDtypeStruct((n_req,) + packed.shape, packed.dtype),
        ),
        in_specs=[any_spec, vmem],
        out_specs=(any_spec, vmem),
        scratch_shapes=[
            pltpu.SemaphoreType.DMA((n_req,)),
            pltpu.SemaphoreType.DMA((n_req,)),
            pltpu.SemaphoreType.DMA((2 * n_slot,)),
            pltpu.SemaphoreType.DMA((n_blk,)),
            pltpu.SemaphoreType.DMA((1,)),
        ],
        compiler_params=pltpu.CompilerParams(has_side_effects=True),
    )(ordered, packed)


def unpack(whole, pieces):
    n_req = whole.shape[0]
    whole = whole.reshape(n_req, -1)
    out, at = [], 0
    for w, axis in pieces:
        size = w.size
        part = whole[:, at : at + size].reshape((n_req,) + w.shape)
        at += size
        part = jnp.moveaxis(part, 0, axis)
        shape = list(w.shape)
        shape[axis] *= n_req
        out.append(part.reshape(shape))
    return out


def per_device(
    new_states,
    encoder_out,
    cache_in,
    slot_order,
    new_lengths,
    cache_lengths,
    enc_lengths,
    bucket_of,
    rel_bias,
    norm_gain,
    self_q,
    self_kv,
    self_out,
    cross_q,
    cross_kv,
    cross_out,
    ff_in,
    ff_out,
):
    blk_count = lax.axis_size("blk")
    heads_dev = H // blk_count
    width_dev = heads_dev * HD
    req_dev = cache_in.shape[0] // lax.axis_size("req")
    own_slots = lax.dynamic_slice_in_dim(slot_order, lax.axis_index("req") * req_dev, req_dev, 0)
    slot_new = pick_lengths(new_lengths, own_slots)
    slot_old = pick_lengths(cache_lengths, own_slots)
    slot_enc = pick_lengths(enc_lengths, own_slots)
    ordered = jnp.take(cache_in, slot_order, axis=0)
    onehot = (bucket_of[:, None] == jnp.arange(rel_bias.shape[0], dtype=jnp.int32)[None, :]).astype(
        jnp.float32
    )
    own_bias = lax.dynamic_slice_in_dim(rel_bias, lax.axis_index("blk") * heads_dev, heads_dev, 1)
    bias_dist = jnp.dot(onehot, own_bias, precision=lax.Precision.HIGHEST).T
    early = [(self_q, 0), (self_kv, 0), (self_out, 1)]
    late = [(cross_q, 0), (cross_kv, 0), (cross_out, 1), (ff_in, 0), (ff_out, 1)]
    flat = jnp.concatenate([w.reshape(-1) for w, _ in early])
    cache_blk, whole = prologue(ordered, flat.reshape(-1, 128))
    cache_dec = cache_blk[None]
    late_flat = jnp.concatenate([w.reshape(-1) for w, _ in late]).reshape(-1, 128)
    gathered = unpack(whole, early)
    wq_self, wkv_self, wo_self = gathered
    n_blk = lax.axis_size("blk")
    rows_dev = new_states.shape[0] // n_blk
    own_rows = lax.dynamic_slice_in_dim(
        new_states, chunk_of(lax.axis_index("blk"), n_blk) * rows_dev, rows_dev, 0
    ).astype(jnp.float32)
    normed = rms_rows(new_states.astype(jnp.float32), norm_gain[0])
    self_cat = jnp.concatenate([wq_self, wkv_self.reshape(wkv_self.shape[0], -1)], axis=1)
    projected = jnp.dot(normed, self_cat, preferred_element_type=jnp.float32).astype(
        jnp.bfloat16
    )
    context = self_attention(
        projected[:, :HD],
        cache_dec[0],
        projected[:, HD : 2 * HD],
        projected[:, 2 * HD :],
        bias_dist[0],
        slot_old[0],
        slot_new[0],
    )
    part = jnp.dot(context, wo_self, preferred_element_type=jnp.float32).astype(jnp.bfloat16)
    residual, normed, late_whole = blk_stage(part, own_rows, norm_gain[1], False, late_flat)
    wq_cross, wkv_cross, wo_cross, w_in, w_out = unpack(late_whole, late)
    queries = (
        jnp.dot(normed, wq_cross, preferred_element_type=jnp.float32)
        .astype(jnp.bfloat16)
        .reshape(req_dev, -1, heads_dev, HD)
    )
    cross_pair = wkv_cross.reshape(wkv_cross.shape[0], -1)
    key_value = (
        jnp.dot(encoder_out, cross_pair, preferred_element_type=jnp.float32)
        .astype(jnp.bfloat16)
        .reshape(req_dev, -1, 2, heads_dev, HD)
    )
    context = cross_attend(queries, key_value, slot_enc)
    part = jnp.dot(context.reshape(-1, width_dev), wo_cross, preferred_element_type=jnp.float32)
    residual, normed = blk_stage(part.astype(jnp.bfloat16), residual, norm_gain[2], False)
    ff_dev = w_in.shape[2]
    gate_up = jnp.dot(normed, w_in.reshape(w_in.shape[0], -1), preferred_element_type=jnp.float32)
    hidden = (jax.nn.gelu(gate_up[:, :ff_dev], approximate=True) * gate_up[:, ff_dev:]).astype(
        jnp.bfloat16
    )
    part = jnp.dot(hidden, w_out, preferred_element_type=jnp.float32).astype(jnp.bfloat16)
    _, layer_out = blk_stage(part, residual, norm_gain[2], True)
    return (layer_out, cache_dec)


def solution(mesh):
    in_specs = (
        P("req", None),
        P("req", None),
        P(None, "blk", "req"),
        P(),
        P(),
        P(),
        P(),
        P(),
        P(),
        P(),
        P("req", "blk"),
        P("req", None, "blk"),
        P("blk", "req"),
        P("req", "blk"),
        P("req", None, "blk"),
        P("blk", "req"),
        P("req", None, "blk"),
        P("blk", "req"),
    )
    out_specs = (P("req", None), P("req", None, "blk"))
    return jax.shard_map(
        per_device, mesh=mesh, in_specs=in_specs, out_specs=out_specs, check_vma=False
    )
```

```python
import functools

import jax
import jax.numpy as jnp
from jax import lax
from jax.sharding import PartitionSpec as P
from jax.experimental import pallas as pl
from jax.experimental.pallas import tpu as pltpu

H = 16
HD = 64


EPSILON = 1e-06
NEG_FILL = -1e30


def rms_rows(row_block, gain):
    mean_square = jnp.mean(row_block * row_block, axis=-1, keepdims=True)
    return (row_block * lax.rsqrt(mean_square + EPSILON) * gain).astype(jnp.bfloat16)


def softmax_rows(scores):
    row_top = jnp.max(scores, axis=-1, keepdims=True)
    weights = jnp.exp(scores - row_top)
    return (weights / jnp.sum(weights, axis=-1, keepdims=True)).astype(jnp.bfloat16)


def pick_lengths(table, own_slots):
    matches = own_slots[:, None] == jnp.arange(table.shape[0], dtype=jnp.int32)[None, :]
    return jnp.sum(jnp.where(matches, table[None, :], 0), axis=1)


def shifted_bias(bias_dist, base, row_count, col_count):
    heads_here, span_len = bias_dist.shape
    line_len = row_count + col_count - 1
    steps = jnp.arange(line_len + 1, dtype=jnp.int32)
    line = bias_dist[:, jnp.clip(base + row_count - 1 - steps, 0, span_len - 1)]
    tiled = jnp.broadcast_to(line[:, None, :], (heads_here, row_count, line_len + 1))
    flat = tiled.reshape(heads_here, row_count * (line_len + 1))[:, : row_count * line_len]
    skewed = flat.reshape(heads_here, row_count, line_len)
    return skewed[:, :, row_count - 1 : row_count - 1 + col_count]


def row_total(left, weight):
    term = jnp.dot(left, weight, preferred_element_type=jnp.float32)
    return lax.psum(term.astype(jnp.bfloat16), "blk").astype(jnp.float32)


def cached_scores(queries, key_rows, first_col, old_len, bias_dist):
    col_ids = first_col + jnp.arange(key_rows.shape[0], dtype=jnp.int32)[None, :]
    scores = jnp.einsum("qhe,khe->hqk", queries, key_rows, preferred_element_type=jnp.float32)
    scores = scores + shifted_bias(
        bias_dist, old_len - first_col, queries.shape[0], key_rows.shape[0]
    )
    return jnp.where((col_ids < old_len)[None], scores, NEG_FILL)


def fresh_scores(queries, fresh_keys, fresh_len, bias_dist):
    row_ids = jnp.arange(queries.shape[0], dtype=jnp.int32)[:, None]
    col_ids = jnp.arange(fresh_keys.shape[0], dtype=jnp.int32)[None, :]
    scores = jnp.einsum("qhe,khe->hqk", queries, fresh_keys, preferred_element_type=jnp.float32)
    scores = scores + shifted_bias(bias_dist, 0, queries.shape[0], fresh_keys.shape[0])
    admitted = (col_ids <= row_ids) & (col_ids < fresh_len)
    return jnp.where(admitted[None], scores, NEG_FILL)


def self_padded(
    queries, key_rows, value_rows, fresh_keys, fresh_values, old_len, fresh_len, bias_dist
):
    scores = jnp.concatenate(
        [
            cached_scores(queries, key_rows, 0, old_len, bias_dist),
            fresh_scores(queries, fresh_keys, fresh_len, bias_dist),
        ],
        axis=2,
    )
    weights = softmax_rows(scores)
    value_all = jnp.concatenate([value_rows, fresh_values], axis=0)
    return jnp.einsum(
        "hqk,khe->qhe", weights, value_all, preferred_element_type=jnp.float32
    ).astype(jnp.bfloat16)


def self_attend(queries, key_value, cache_dec, slot_old, slot_new, bias_dist, heads_dev):
    req_dev, cache_len = (cache_dec.shape[0], cache_dec.shape[1])
    cache_split = cache_dec.reshape(req_dev, cache_len, heads_dev, 2, -1)

    def one_request(request):
        queries_one, pair_one, cache_one, old_len, fresh_len = request
        return self_padded(
            queries_one,
            cache_one[:, :, 0],
            cache_one[:, :, 1],
            pair_one[:, 0],
            pair_one[:, 1],
            old_len,
            fresh_len,
            bias_dist,
        )

    return lax.map(one_request, (queries, key_value, cache_split, slot_old, slot_new))


def cross_attend(queries, key_value, slot_enc):
    scores = jnp.einsum(
        "rqhe,rkhe->rhqk", queries, key_value[:, :, 0], preferred_element_type=jnp.float32
    )
    col_ids = jnp.arange(key_value.shape[1], dtype=jnp.int32)
    scores = jnp.where(
        col_ids[None, None, None, :] < slot_enc[:, None, None, None], scores, NEG_FILL
    )
    weights = softmax_rows(scores)
    return jnp.einsum(
        "rhqk,rkhe->rqhe", weights, key_value[:, :, 1], preferred_element_type=jnp.float32
    ).astype(jnp.bfloat16)


def add_branch(residual, left, weight, gain):
    residual = residual + row_total(left, weight)
    normed = rms_rows(residual, gain)
    return (residual, normed)


TQ = 128


def stage_kernel(n_blk, final, extra, *refs):
    if extra:
        (part_ref, resid_ref, gain_ref, packed_ref, res_out, full_ref, wts_ref,
         recv_a, send_b, recv_b, sems, b_send, b_recv, ag_send, ag_recv, w_send, w_recv) = refs
    else:
        (part_ref, resid_ref, gain_ref, res_out, full_ref,
         recv_a, send_b, recv_b, sems, b_send, b_recv, ag_send, ag_recv) = refs
    me = lax.axis_index("blk")
    req = lax.axis_index("req")
    rows = resid_ref.shape[0]
    n_grp = n_blk // 2
    g = me // 2
    c = lax.rem(me, 2)
    partner = g * 2 + 1 - c
    half = n_grp * rows
    n_req = wts_ref.shape[0] if extra else 1
    barrier = pltpu.get_barrier_semaphore()
    for k in range(1, n_grp):
        peer = lax.rem(g + k, n_grp) * 2 + c
        pl.semaphore_signal(barrier, inc=1, device_id=(req, peer), device_id_type=MESH_IDS)
    pl.semaphore_signal(barrier, inc=1, device_id=(req, partner), device_id_type=MESH_IDS)
    for k in range(1, n_req):
        peer = lax.rem(req + k, n_req)
        pl.semaphore_signal(barrier, inc=1, device_id=(peer, me), device_id_type=MESH_IDS)
    pl.semaphore_wait(barrier, n_grp + n_req - 1)
    sends = []
    exchange = pltpu.make_async_remote_copy(
        src_ref=part_ref.at[pl.ds(pl.multiple_of((1 - c) * half, half), half)],
        dst_ref=recv_a,
        send_sem=sems.at[0],
        recv_sem=sems.at[1],
        device_id=(req, partner),
        device_id_type=MESH_IDS,
    )
    exchange.start()
    sends.append(exchange)
    for k in range(1, n_req):
        peer = lax.rem(req + k, n_req)
        copy = pltpu.make_async_remote_copy(
            src_ref=packed_ref,
            dst_ref=wts_ref.at[req],
            send_sem=w_send.at[peer],
            recv_sem=w_recv.at[req],
            device_id=(peer, me),
            device_id_type=MESH_IDS,
        )
        copy.start()
        sends.append(copy)
    exchange.wait_recv()
    pair = part_ref[pl.ds(pl.multiple_of(c * half, half), half), :].astype(jnp.float32) + recv_a[
        ...
    ].astype(jnp.float32)
    send_b[...] = pair.astype(send_b.dtype)
    for k in range(1, n_grp):
        grp = lax.rem(g + k, n_grp)
        copy = pltpu.make_async_remote_copy(
            src_ref=send_b.at[pl.ds(pl.multiple_of(grp * rows, rows), rows)],
            dst_ref=recv_b.at[g],
            send_sem=b_send.at[grp],
            recv_sem=b_recv.at[g],
            device_id=(req, grp * 2 + c),
            device_id_type=MESH_IDS,
        )
        copy.start()
        sends.append(copy)
    total = send_b[pl.ds(pl.multiple_of(g * rows, rows), rows), :].astype(jnp.float32)
    for k in range(1, n_grp):
        grp = lax.rem(g + n_grp - k, n_grp)
        incoming = pltpu.make_async_remote_copy(
            src_ref=send_b.at[pl.ds(0, rows)],
            dst_ref=recv_b.at[grp],
            send_sem=b_send.at[grp],
            recv_sem=b_recv.at[grp],
            device_id=(req, grp * 2 + c),
            device_id_type=MESH_IDS,
        )
        incoming.wait_recv()
        total = total + recv_b[grp].astype(jnp.float32)
    mine = pl.ds(pl.multiple_of(c * half + g * rows, rows), rows)
    resid = resid_ref[...] + total
    res_out[...] = resid
    if final:
        full_ref[mine, :] = resid.astype(full_ref.dtype)
    else:
        mean_square = jnp.mean(resid * resid, axis=-1, keepdims=True)
        full_ref[mine, :] = (resid * lax.rsqrt(mean_square + EPSILON) * gain_ref[...]).astype(
            full_ref.dtype
        )
    for k in range(1, n_grp):
        peer = lax.rem(g + k, n_grp) * 2 + c
        copy = pltpu.make_async_remote_copy(
            src_ref=full_ref.at[mine],
            dst_ref=full_ref.at[mine],
            send_sem=ag_send.at[k],
            recv_sem=ag_recv.at[g],
            device_id=(req, peer),
            device_id_type=MESH_IDS,
        )
        copy.start()
        sends.append(copy)
    copy = pltpu.make_async_remote_copy(
        src_ref=full_ref.at[mine],
        dst_ref=full_ref.at[mine],
        send_sem=ag_send.at[0],
        recv_sem=ag_recv.at[n_grp + g],
        device_id=(req, partner),
        device_id_type=MESH_IDS,
    )
    copy.start()
    sends.append(copy)
    for k in range(1, n_grp):
        grp = lax.rem(g + n_grp - k, n_grp)
        there = pl.ds(pl.multiple_of(c * half + grp * rows, rows), rows)
        incoming = pltpu.make_async_remote_copy(
            src_ref=full_ref.at[there],
            dst_ref=full_ref.at[there],
            send_sem=ag_send.at[0],
            recv_sem=ag_recv.at[grp],
            device_id=(req, grp * 2 + c),
            device_id_type=MESH_IDS,
        )
        incoming.wait_recv()
        forward = pltpu.make_async_remote_copy(
            src_ref=full_ref.at[there],
            dst_ref=full_ref.at[there],
            send_sem=ag_send.at[n_grp + k],
            recv_sem=ag_recv.at[n_grp + grp],
            device_id=(req, partner),
            device_id_type=MESH_IDS,
        )
        forward.start()
        sends.append(forward)
    for grp in range(n_grp):
        there = pl.ds(pl.multiple_of((1 - c) * half + grp * rows, rows), rows)
        incoming = pltpu.make_async_remote_copy(
            src_ref=full_ref.at[there],
            dst_ref=full_ref.at[there],
            send_sem=ag_send.at[0],
            recv_sem=ag_recv.at[n_grp + grp],
            device_id=(req, partner),
            device_id_type=MESH_IDS,
        )
        incoming.wait_recv()
    if extra:
        wts_ref[req] = packed_ref[...]
        for k in range(1, n_req):
            src = lax.rem(req + n_req - k, n_req)
            incoming = pltpu.make_async_remote_copy(
                src_ref=packed_ref,
                dst_ref=wts_ref.at[src],
                send_sem=w_send.at[src],
                recv_sem=w_recv.at[src],
                device_id=(src, me),
                device_id_type=MESH_IDS,
            )
            incoming.wait_recv()
    for copy in sends:
        copy.wait_send()


def blk_stage(part, resid, gain, final, packed=None):
    n_blk = lax.axis_size("blk")
    rows, width = resid.shape
    vmem = pl.BlockSpec(memory_space=pltpu.VMEM)
    extra = packed is not None
    outs = [
        jax.ShapeDtypeStruct((rows, width), jnp.float32),
        jax.ShapeDtypeStruct((rows * n_blk, width), jnp.bfloat16),
    ]
    n_grp = n_blk // 2
    scratch = [
        pltpu.VMEM((n_grp * rows, width), part.dtype),
        pltpu.VMEM((n_grp * rows, width), part.dtype),
        pltpu.VMEM((n_grp, rows, width), part.dtype),
        pltpu.SemaphoreType.DMA((2,)),
        pltpu.SemaphoreType.DMA((n_grp,)),
        pltpu.SemaphoreType.DMA((n_grp,)),
        pltpu.SemaphoreType.DMA((n_blk,)),
        pltpu.SemaphoreType.DMA((n_blk,)),
    ]
    args = [part, resid, gain[None, :]]
    if extra:
        n_req = lax.axis_size("req")
        outs.append(jax.ShapeDtypeStruct((n_req,) + packed.shape, packed.dtype))
        scratch += [pltpu.SemaphoreType.DMA((n_req,)), pltpu.SemaphoreType.DMA((n_req,))]
        args.append(packed)
    return pl.pallas_call(
        functools.partial(stage_kernel, n_blk, final, extra),
        out_shape=tuple(outs),
        in_specs=[vmem] * len(args),
        out_specs=tuple([vmem] * len(outs)),
        scratch_shapes=scratch,
        compiler_params=pltpu.CompilerParams(
            collective_id=5 if extra else (4 if final else 3), has_side_effects=True
        ),
    )(*args)


def self_kernel(lens_ref, q_ref, c_ref, kn_ref, vn_ref, g_ref, f_ref, o_ref):
    old_len = lens_ref[0]
    fresh_len = lens_ref[1]
    n_q = q_ref.shape[0]
    n_ctx = c_ref.shape[0]
    wide_old = n_ctx + TQ
    wide_new = n_q + TQ
    k_old = c_ref[:, :HD]
    v_old = c_ref[:, HD:]
    k_new = kn_ref[...]
    v_new = vn_ref[...]
    dims = (((1,), (1,)), ((), ()))
    for t in range(n_q // TQ):
        q = q_ref[t * TQ : (t + 1) * TQ, :]
        start = n_q - TQ - t * TQ
        s_old = lax.dot_general(q, k_old, dims, preferred_element_type=jnp.float32)
        line = jnp.broadcast_to(g_ref[:, start : start + wide_old], (TQ, wide_old))
        bias = pltpu.roll(line, wide_old - (TQ - 1), 1, stride=1, stride_axis=0)[:, :n_ctx]
        col = lax.broadcasted_iota(jnp.int32, (TQ, n_ctx), 1)
        s_old = jnp.where(col < old_len, s_old + bias, NEG_FILL)
        s_new = lax.dot_general(q, k_new, dims, preferred_element_type=jnp.float32)
        line = jnp.broadcast_to(f_ref[:, start : start + wide_new], (TQ, wide_new))
        bias = pltpu.roll(line, wide_new - (TQ - 1), 1, stride=1, stride_axis=0)[:, :n_q]
        row = lax.broadcasted_iota(jnp.int32, (TQ, n_q), 0) + t * TQ
        col = lax.broadcasted_iota(jnp.int32, (TQ, n_q), 1)
        s_new = jnp.where((col <= row) & (col < fresh_len), s_new + bias, NEG_FILL)
        top = jnp.maximum(
            jnp.max(s_old, axis=1, keepdims=True), jnp.max(s_new, axis=1, keepdims=True)
        )
        p_old = jnp.exp(s_old - top)
        p_new = jnp.exp(s_new - top)
        total = jnp.sum(p_old, axis=1, keepdims=True) + jnp.sum(p_new, axis=1, keepdims=True)
        w_old = (p_old / total).astype(jnp.bfloat16)
        w_new = (p_new / total).astype(jnp.bfloat16)
        out = jnp.dot(w_old, v_old, preferred_element_type=jnp.float32) + jnp.dot(
            w_new, v_new, preferred_element_type=jnp.float32
        )
        o_ref[t * TQ : (t + 1) * TQ, :] = out.astype(jnp.bfloat16)


def bias_lines(line, old_len, n_q, n_ctx):
    span = line.shape[0]
    ext = jnp.concatenate([jnp.broadcast_to(line[:1], (n_ctx,)), line])
    rev = ext[::-1]
    g = lax.dynamic_slice_in_dim(rev, n_ctx - old_len, span)
    f = rev[n_ctx : n_ctx + 2 * n_q]
    return g[None, :], f[None, :]


def self_attention(q, cache_blk, k_new, v_new, line, old_len, fresh_len):
    n_q = q.shape[0]
    n_ctx = cache_blk.shape[0]
    g, f = bias_lines(line, old_len, n_q, n_ctx)
    lens = jnp.stack([old_len, fresh_len]).astype(jnp.int32)
    vmem = pl.BlockSpec(memory_space=pltpu.VMEM)
    return pl.pallas_call(
        self_kernel,
        out_shape=jax.ShapeDtypeStruct((n_q, HD), jnp.bfloat16),
        in_specs=[pl.BlockSpec(memory_space=pltpu.SMEM)] + [vmem] * 6,
        out_specs=vmem,
        compiler_params=pltpu.CompilerParams(vmem_limit_bytes=48 * 1024 * 1024),
    )(lens, q, cache_blk, k_new, v_new, g, f)


def pack_gather(pieces):
    flat = jnp.concatenate([w.reshape(-1) for w, _ in pieces])
    whole = lax.all_gather(flat, "req", axis=0, tiled=False)
    n_req = whole.shape[0]
    out, at = [], 0
    for w, axis in pieces:
        size = w.size
        part = whole[:, at : at + size].reshape((n_req,) + w.shape)
        at += size
        part = jnp.moveaxis(part, 0, axis)
        shape = list(w.shape)
        shape[axis] *= n_req
        out.append(part.reshape(shape))
    return out


MESH_IDS = pl.DeviceIdType.MESH


def greet_all(n_blk, me, req):
    barrier = pltpu.get_barrier_semaphore()
    for k in range(1, n_blk):
        peer = lax.rem(me + k, n_blk)
        pl.semaphore_signal(barrier, inc=1, device_id=(req, peer), device_id_type=MESH_IDS)
    pl.semaphore_wait(barrier, n_blk - 1)


def chunk_of(b, n_blk):
    return lax.rem(b, 2) * (n_blk // 2) + b // 2


def scatter_kernel(n_blk, part_ref, out_ref, recv, send_sem, recv_sem):
    me = lax.axis_index("blk")
    req = lax.axis_index("req")
    rows = out_ref.shape[0]
    greet_all(n_blk, me, req)
    copies = []
    for k in range(1, n_blk):
        peer = lax.rem(me + k, n_blk)
        copy = pltpu.make_async_remote_copy(
            src_ref=part_ref.at[pl.ds(pl.multiple_of(chunk_of(peer, n_blk) * rows, rows), rows)],
            dst_ref=recv.at[me],
            send_sem=send_sem.at[peer],
            recv_sem=recv_sem.at[me],
            device_id=(req, peer),
            device_id_type=MESH_IDS,
        )
        copy.start()
        copies.append(copy)
    own = pl.ds(pl.multiple_of(chunk_of(me, n_blk) * rows, rows), rows)
    total = part_ref[own, :].astype(jnp.float32)
    for k in range(1, n_blk):
        src = lax.rem(me + n_blk - k, n_blk)
        incoming = pltpu.make_async_remote_copy(
            src_ref=part_ref.at[pl.ds(0, rows)],
            dst_ref=recv.at[src],
            send_sem=send_sem.at[src],
            recv_sem=recv_sem.at[src],
            device_id=(req, src),
            device_id_type=MESH_IDS,
        )
        incoming.wait_recv()
        total = total + recv[src].astype(jnp.float32)
    for copy in copies:
        copy.wait_send()
    out_ref[...] = total


def gather_kernel(n_blk, piece_ref, out_ref, send_sem, recv_sem):
    b = lax.axis_index("blk")
    req = lax.axis_index("req")
    n_grp = n_blk // 2
    g = b // 2
    c = lax.rem(b, 2)
    partner = g * 2 + 1 - c
    rows = piece_ref.shape[0]
    half = n_grp * rows
    barrier = pltpu.get_barrier_semaphore()
    for k in range(1, n_grp):
        peer = lax.rem(g + k, n_grp) * 2 + c
        pl.semaphore_signal(barrier, inc=1, device_id=(req, peer), device_id_type=MESH_IDS)
    pl.semaphore_signal(barrier, inc=1, device_id=(req, partner), device_id_type=MESH_IDS)
    pl.semaphore_wait(barrier, n_grp)
    mine = pl.ds(pl.multiple_of(c * half + g * rows, rows), rows)
    sends = []
    for k in range(1, n_grp):
        peer = lax.rem(g + k, n_grp) * 2 + c
        copy = pltpu.make_async_remote_copy(
            src_ref=piece_ref,
            dst_ref=out_ref.at[mine],
            send_sem=send_sem.at[k],
            recv_sem=recv_sem.at[g],
            device_id=(req, peer),
            device_id_type=MESH_IDS,
        )
        copy.start()
        sends.append(copy)
    copy = pltpu.make_async_remote_copy(
        src_ref=piece_ref,
        dst_ref=out_ref.at[mine],
        send_sem=send_sem.at[0],
        recv_sem=recv_sem.at[n_grp + g],
        device_id=(req, partner),
        device_id_type=MESH_IDS,
    )
    copy.start()
    sends.append(copy)
    out_ref[mine, :] = piece_ref[...]
    for k in range(1, n_grp):
        grp = lax.rem(g + n_grp - k, n_grp)
        there = pl.ds(pl.multiple_of(c * half + grp * rows, rows), rows)
        incoming = pltpu.make_async_remote_copy(
            src_ref=piece_ref,
            dst_ref=out_ref.at[there],
            send_sem=send_sem.at[0],
            recv_sem=recv_sem.at[grp],
            device_id=(req, grp * 2 + c),
            device_id_type=MESH_IDS,
        )
        incoming.wait_recv()
        forward = pltpu.make_async_remote_copy(
            src_ref=out_ref.at[there],
            dst_ref=out_ref.at[there],
            send_sem=send_sem.at[n_grp + k],
            recv_sem=recv_sem.at[n_grp + grp],
            device_id=(req, partner),
            device_id_type=MESH_IDS,
        )
        forward.start()
        sends.append(forward)
    for grp in range(n_grp):
        there = pl.ds(pl.multiple_of((1 - c) * half + grp * rows, rows), rows)
        incoming = pltpu.make_async_remote_copy(
            src_ref=piece_ref,
            dst_ref=out_ref.at[there],
            send_sem=send_sem.at[0],
            recv_sem=recv_sem.at[n_grp + grp],
            device_id=(req, partner),
            device_id_type=MESH_IDS,
        )
        incoming.wait_recv()
    for copy in sends:
        copy.wait_send()


def blk_scatter(part):
    n_blk = lax.axis_size("blk")
    rows = part.shape[0] // n_blk
    vmem = pl.BlockSpec(memory_space=pltpu.VMEM)
    return pl.pallas_call(
        functools.partial(scatter_kernel, n_blk),
        out_shape=jax.ShapeDtypeStruct((rows, part.shape[1]), jnp.float32),
        in_specs=[vmem],
        out_specs=vmem,
        scratch_shapes=[
            pltpu.VMEM((n_blk, rows, part.shape[1]), part.dtype),
            pltpu.SemaphoreType.DMA((n_blk,)),
            pltpu.SemaphoreType.DMA((n_blk,)),
        ],
        compiler_params=pltpu.CompilerParams(collective_id=1, has_side_effects=True),
    )(part)


def blk_gather(piece):
    n_blk = lax.axis_size("blk")
    rows = piece.shape[0]
    vmem = pl.BlockSpec(memory_space=pltpu.VMEM)
    return pl.pallas_call(
        functools.partial(gather_kernel, n_blk),
        out_shape=jax.ShapeDtypeStruct((rows * n_blk, piece.shape[1]), piece.dtype),
        in_specs=[vmem],
        out_specs=vmem,
        scratch_shapes=[
            pltpu.SemaphoreType.DMA((n_blk,)),
            pltpu.SemaphoreType.DMA((n_blk,)),
        ],
        compiler_params=pltpu.CompilerParams(collective_id=2, has_side_effects=True),
    )(piece)


def prologue_kernel(n_req, n_blk, ordered_ref, packed_ref, cache_ref, wts_ref, w_send, w_recv, c_send, c_recv, local_sem):
    r = lax.axis_index("req")
    b = lax.axis_index("blk")
    n_slot, span, width = ordered_ref.shape
    piece = width // 2
    copies = []
    for k in range(1, n_req):
        peer = lax.rem(r + k, n_req)
        copy = pltpu.make_async_remote_copy(
            src_ref=packed_ref,
            dst_ref=wts_ref.at[r],
            send_sem=w_send.at[peer],
            recv_sem=w_recv.at[r],
            device_id=(peer, b),
            device_id_type=MESH_IDS,
        )
        copy.start()
        copies.append(copy)
    rows = pl.ds(pl.multiple_of(b * span, span), span)
    for s in range(n_slot):
        for hh in range(2):
            head = 2 * r + hh
            is_self = jnp.logical_and(r == s, head == b)
            src = ordered_ref.at[s, :, pl.ds(hh * piece, piece)]
            copy = pltpu.make_async_remote_copy(
                src_ref=src,
                dst_ref=cache_ref.at[rows],
                send_sem=c_send.at[s * 2 + hh],
                recv_sem=c_recv.at[b],
                device_id=(s, head),
                device_id_type=MESH_IDS,
            )

            @pl.when(jnp.logical_not(is_self))
            def _():
                copy.start()

            @pl.when(is_self)
            def _():
                local = pltpu.make_async_copy(src, cache_ref.at[rows], local_sem.at[0])
                local.start()
                local.wait()

            copies.append((copy, is_self))
    wts_ref[r] = packed_ref[...]
    for k in range(1, n_req):
        src_req = lax.rem(r + n_req - k, n_req)
        incoming = pltpu.make_async_remote_copy(
            src_ref=packed_ref,
            dst_ref=wts_ref.at[src_req],
            send_sem=w_send.at[src_req],
            recv_sem=w_recv.at[src_req],
            device_id=(src_req, b),
            device_id_type=MESH_IDS,
        )
        incoming.wait_recv()
    owner = b // 2
    for j in range(n_blk):
        incoming = pltpu.make_async_remote_copy(
            src_ref=ordered_ref.at[0, :, pl.ds(0, piece)],
            dst_ref=cache_ref.at[pl.ds(j * span, span)],
            send_sem=c_send.at[0],
            recv_sem=c_recv.at[j],
            device_id=(owner, j),
            device_id_type=MESH_IDS,
        )

        @pl.when(jnp.logical_not(jnp.logical_and(owner == r, j == b)))
        def _():
            incoming.wait_recv()

    for item in copies:
        if isinstance(item, tuple):
            copy, is_self = item

            @pl.when(jnp.logical_not(is_self))
            def _():
                copy.wait_send()

        else:
            item.wait_send()


def prologue(ordered, packed):
    n_req = lax.axis_size("req")
    n_blk = lax.axis_size("blk")
    n_slot, span, width = ordered.shape
    any_spec = pl.BlockSpec(memory_space=pl.ANY)
    vmem = pl.BlockSpec(memory_space=pltpu.VMEM)
    return pl.pallas_call(
        functools.partial(prologue_kernel, n_req, n_blk),
        out_shape=(
            jax.ShapeDtypeStruct((span * n_blk, width // 2), ordered.dtype),
            jax.ShapeDtypeStruct((n_req,) + packed.shape, packed.dtype),
        ),
        in_specs=[any_spec, vmem],
        out_specs=(any_spec, vmem),
        scratch_shapes=[
            pltpu.SemaphoreType.DMA((n_req,)),
            pltpu.SemaphoreType.DMA((n_req,)),
            pltpu.SemaphoreType.DMA((2 * n_slot,)),
            pltpu.SemaphoreType.DMA((n_blk,)),
            pltpu.SemaphoreType.DMA((1,)),
        ],
        compiler_params=pltpu.CompilerParams(has_side_effects=True),
    )(ordered, packed)


def unpack(whole, pieces):
    n_req = whole.shape[0]
    whole = whole.reshape(n_req, -1)
    out, at = [], 0
    for w, axis in pieces:
        size = w.size
        part = whole[:, at : at + size].reshape((n_req,) + w.shape)
        at += size
        part = jnp.moveaxis(part, 0, axis)
        shape = list(w.shape)
        shape[axis] *= n_req
        out.append(part.reshape(shape))
    return out


def per_device(
    new_states,
    encoder_out,
    cache_in,
    slot_order,
    new_lengths,
    cache_lengths,
    enc_lengths,
    bucket_of,
    rel_bias,
    norm_gain,
    self_q,
    self_kv,
    self_out,
    cross_q,
    cross_kv,
    cross_out,
    ff_in,
    ff_out,
):
    blk_count = lax.axis_size("blk")
    heads_dev = H // blk_count
    width_dev = heads_dev * HD
    req_dev = cache_in.shape[0] // lax.axis_size("req")
    own_slots = lax.dynamic_slice_in_dim(slot_order, lax.axis_index("req") * req_dev, req_dev, 0)
    slot_new = pick_lengths(new_lengths, own_slots)
    slot_old = pick_lengths(cache_lengths, own_slots)
    slot_enc = pick_lengths(enc_lengths, own_slots)
    ordered = jnp.take(cache_in, slot_order, axis=0)
    onehot = (bucket_of[:, None] == jnp.arange(rel_bias.shape[0], dtype=jnp.int32)[None, :]).astype(
        jnp.float32
    )
    own_bias = lax.dynamic_slice_in_dim(rel_bias, lax.axis_index("blk") * heads_dev, heads_dev, 1)
    bias_dist = jnp.dot(onehot, own_bias, precision=lax.Precision.HIGHEST).T
    early = [(self_q, 0), (self_kv, 0), (self_out, 1)]
    late = [(cross_q, 0), (cross_kv, 0), (cross_out, 1), (ff_in, 0), (ff_out, 1)]
    flat = jnp.concatenate([w.reshape(-1) for w, _ in early])
    cache_blk, whole = prologue(ordered, flat.reshape(-1, 128))
    cache_dec = cache_blk[None]
    late_flat = jnp.concatenate([w.reshape(-1) for w, _ in late]).reshape(-1, 128)
    gathered = unpack(whole, early)
    wq_self, wkv_self, wo_self = gathered
    n_blk = lax.axis_size("blk")
    rows_dev = new_states.shape[0] // n_blk
    own_rows = lax.dynamic_slice_in_dim(
        new_states, chunk_of(lax.axis_index("blk"), n_blk) * rows_dev, rows_dev, 0
    ).astype(jnp.float32)
    normed = rms_rows(new_states.astype(jnp.float32), norm_gain[0])
    self_cat = jnp.concatenate([wq_self, wkv_self.reshape(wkv_self.shape[0], -1)], axis=1)
    projected = jnp.dot(normed, self_cat, preferred_element_type=jnp.float32).astype(
        jnp.bfloat16
    )
    context = self_attention(
        projected[:, :HD],
        cache_dec[0],
        projected[:, HD : 2 * HD],
        projected[:, 2 * HD :],
        bias_dist[0],
        slot_old[0],
        slot_new[0],
    )
    part = jnp.dot(context, wo_self, preferred_element_type=jnp.float32).astype(jnp.bfloat16)
    residual, normed, late_whole = blk_stage(part, own_rows, norm_gain[1], False, late_flat)
    wq_cross, wkv_cross, wo_cross, w_in, w_out = unpack(late_whole, late)
    queries = (
        jnp.dot(normed, wq_cross, preferred_element_type=jnp.float32)
        .astype(jnp.bfloat16)
        .reshape(req_dev, -1, heads_dev, HD)
    )
    cross_pair = wkv_cross.reshape(wkv_cross.shape[0], -1)
    key_value = (
        jnp.dot(encoder_out, cross_pair, preferred_element_type=jnp.float32)
        .astype(jnp.bfloat16)
        .reshape(req_dev, -1, 2, heads_dev, HD)
    )
    context = cross_attend(queries, key_value, slot_enc)
    part = jnp.dot(context.reshape(-1, width_dev), wo_cross, preferred_element_type=jnp.float32)
    residual, normed = blk_stage(part.astype(jnp.bfloat16), residual, norm_gain[2], False)
    ff_dev = w_in.shape[2]
    gate_up = jnp.dot(normed, w_in.reshape(w_in.shape[0], -1), preferred_element_type=jnp.float32)
    hidden = (jax.nn.gelu(gate_up[:, :ff_dev], approximate=True) * gate_up[:, ff_dev:]).astype(
        jnp.bfloat16
    )
    part = jnp.dot(hidden, w_out, preferred_element_type=jnp.float32).astype(jnp.bfloat16)
    _, layer_out = blk_stage(part, residual, norm_gain[2], True)
    return (layer_out, cache_dec)


def solution(mesh):
    in_specs = (
        P("req", None),
        P("req", None),
        P(None, "blk", "req"),
        P(),
        P(),
        P(),
        P(),
        P(),
        P(),
        P(),
        P("req", "blk"),
        P("req", None, "blk"),
        P("blk", "req"),
        P("req", "blk"),
        P("req", None, "blk"),
        P("blk", "req"),
        P("req", None, "blk"),
        P("blk", "req"),
    )
    out_specs = (P("req", None), P("req", None, "blk"))
    return jax.shard_map(
        per_device, mesh=mesh, in_specs=in_specs, out_specs=out_specs, check_vma=False
    )
```

```python
import functools

import jax
import jax.numpy as jnp
from jax import lax
from jax.sharding import PartitionSpec as P
from jax.experimental import pallas as pl
from jax.experimental.pallas import tpu as pltpu

H = 16
HD = 64


EPSILON = 1e-06
NEG_FILL = -1e30


def rms_rows(row_block, gain):
    mean_square = jnp.mean(row_block * row_block, axis=-1, keepdims=True)
    return (row_block * lax.rsqrt(mean_square + EPSILON) * gain).astype(jnp.bfloat16)


def softmax_rows(scores):
    row_top = jnp.max(scores, axis=-1, keepdims=True)
    weights = jnp.exp(scores - row_top)
    return (weights / jnp.sum(weights, axis=-1, keepdims=True)).astype(jnp.bfloat16)


def pick_lengths(table, own_slots):
    matches = own_slots[:, None] == jnp.arange(table.shape[0], dtype=jnp.int32)[None, :]
    return jnp.sum(jnp.where(matches, table[None, :], 0), axis=1)


def shifted_bias(bias_dist, base, row_count, col_count):
    heads_here, span_len = bias_dist.shape
    line_len = row_count + col_count - 1
    steps = jnp.arange(line_len + 1, dtype=jnp.int32)
    line = bias_dist[:, jnp.clip(base + row_count - 1 - steps, 0, span_len - 1)]
    tiled = jnp.broadcast_to(line[:, None, :], (heads_here, row_count, line_len + 1))
    flat = tiled.reshape(heads_here, row_count * (line_len + 1))[:, : row_count * line_len]
    skewed = flat.reshape(heads_here, row_count, line_len)
    return skewed[:, :, row_count - 1 : row_count - 1 + col_count]


def row_total(left, weight):
    term = jnp.dot(left, weight, preferred_element_type=jnp.float32)
    return lax.psum(term.astype(jnp.bfloat16), "blk").astype(jnp.float32)


def cached_scores(queries, key_rows, first_col, old_len, bias_dist):
    col_ids = first_col + jnp.arange(key_rows.shape[0], dtype=jnp.int32)[None, :]
    scores = jnp.einsum("qhe,khe->hqk", queries, key_rows, preferred_element_type=jnp.float32)
    scores = scores + shifted_bias(
        bias_dist, old_len - first_col, queries.shape[0], key_rows.shape[0]
    )
    return jnp.where((col_ids < old_len)[None], scores, NEG_FILL)


def fresh_scores(queries, fresh_keys, fresh_len, bias_dist):
    row_ids = jnp.arange(queries.shape[0], dtype=jnp.int32)[:, None]
    col_ids = jnp.arange(fresh_keys.shape[0], dtype=jnp.int32)[None, :]
    scores = jnp.einsum("qhe,khe->hqk", queries, fresh_keys, preferred_element_type=jnp.float32)
    scores = scores + shifted_bias(bias_dist, 0, queries.shape[0], fresh_keys.shape[0])
    admitted = (col_ids <= row_ids) & (col_ids < fresh_len)
    return jnp.where(admitted[None], scores, NEG_FILL)


def self_padded(
    queries, key_rows, value_rows, fresh_keys, fresh_values, old_len, fresh_len, bias_dist
):
    scores = jnp.concatenate(
        [
            cached_scores(queries, key_rows, 0, old_len, bias_dist),
            fresh_scores(queries, fresh_keys, fresh_len, bias_dist),
        ],
        axis=2,
    )
    weights = softmax_rows(scores)
    value_all = jnp.concatenate([value_rows, fresh_values], axis=0)
    return jnp.einsum(
        "hqk,khe->qhe", weights, value_all, preferred_element_type=jnp.float32
    ).astype(jnp.bfloat16)


def self_attend(queries, key_value, cache_dec, slot_old, slot_new, bias_dist, heads_dev):
    req_dev, cache_len = (cache_dec.shape[0], cache_dec.shape[1])
    cache_split = cache_dec.reshape(req_dev, cache_len, heads_dev, 2, -1)

    def one_request(request):
        queries_one, pair_one, cache_one, old_len, fresh_len = request
        return self_padded(
            queries_one,
            cache_one[:, :, 0],
            cache_one[:, :, 1],
            pair_one[:, 0],
            pair_one[:, 1],
            old_len,
            fresh_len,
            bias_dist,
        )

    return lax.map(one_request, (queries, key_value, cache_split, slot_old, slot_new))


def cross_attend(queries, key_value, slot_enc):
    scores = jnp.einsum(
        "rqhe,rkhe->rhqk", queries, key_value[:, :, 0], preferred_element_type=jnp.float32
    )
    col_ids = jnp.arange(key_value.shape[1], dtype=jnp.int32)
    scores = jnp.where(
        col_ids[None, None, None, :] < slot_enc[:, None, None, None], scores, NEG_FILL
    )
    weights = softmax_rows(scores)
    return jnp.einsum(
        "rhqk,rkhe->rqhe", weights, key_value[:, :, 1], preferred_element_type=jnp.float32
    ).astype(jnp.bfloat16)


def add_branch(residual, left, weight, gain):
    residual = residual + row_total(left, weight)
    normed = rms_rows(residual, gain)
    return (residual, normed)


TQ = 128


def stage_kernel(n_blk, final, extra, *refs):
    if extra:
        (part_ref, resid_ref, gain_ref, packed_ref, res_out, full_ref, wts_ref,
         recv_a, send_b, recv_b, sems, b_send, b_recv, ag_send, ag_recv, w_send, w_recv) = refs
    else:
        (part_ref, resid_ref, gain_ref, res_out, full_ref,
         recv_a, send_b, recv_b, sems, b_send, b_recv, ag_send, ag_recv) = refs
    me = lax.axis_index("blk")
    req = lax.axis_index("req")
    rows = resid_ref.shape[0]
    n_grp = n_blk // 2
    g = me // 2
    c = lax.rem(me, 2)
    partner = g * 2 + 1 - c
    half = n_grp * rows
    n_req = wts_ref.shape[0] if extra else 1
    barrier = pltpu.get_barrier_semaphore()
    for k in range(1, n_grp):
        peer = lax.rem(g + k, n_grp) * 2 + c
        pl.semaphore_signal(barrier, inc=1, device_id=(req, peer), device_id_type=MESH_IDS)
    pl.semaphore_signal(barrier, inc=1, device_id=(req, partner), device_id_type=MESH_IDS)
    for k in range(1, n_req):
        peer = lax.rem(req + k, n_req)
        pl.semaphore_signal(barrier, inc=1, device_id=(peer, me), device_id_type=MESH_IDS)
    pl.semaphore_wait(barrier, n_grp + n_req - 1)
    sends = []
    exchange = pltpu.make_async_remote_copy(
        src_ref=part_ref.at[pl.ds(pl.multiple_of((1 - c) * half, half), half)],
        dst_ref=recv_a,
        send_sem=sems.at[0],
        recv_sem=sems.at[1],
        device_id=(req, partner),
        device_id_type=MESH_IDS,
    )
    exchange.start()
    sends.append(exchange)
    for k in range(1, n_req):
        peer = lax.rem(req + k, n_req)
        copy = pltpu.make_async_remote_copy(
            src_ref=packed_ref,
            dst_ref=wts_ref.at[req],
            send_sem=w_send.at[peer],
            recv_sem=w_recv.at[req],
            device_id=(peer, me),
            device_id_type=MESH_IDS,
        )
        copy.start()
        sends.append(copy)
    exchange.wait_recv()
    pair = part_ref[pl.ds(pl.multiple_of(c * half, half), half), :].astype(jnp.float32) + recv_a[
        ...
    ].astype(jnp.float32)
    send_b[...] = pair.astype(send_b.dtype)
    for k in range(1, n_grp):
        grp = lax.rem(g + k, n_grp)
        copy = pltpu.make_async_remote_copy(
            src_ref=send_b.at[pl.ds(pl.multiple_of(grp * rows, rows), rows)],
            dst_ref=recv_b.at[g],
            send_sem=b_send.at[grp],
            recv_sem=b_recv.at[g],
            device_id=(req, grp * 2 + c),
            device_id_type=MESH_IDS,
        )
        copy.start()
        sends.append(copy)
    total = send_b[pl.ds(pl.multiple_of(g * rows, rows), rows), :].astype(jnp.float32)
    for k in range(1, n_grp):
        grp = lax.rem(g + n_grp - k, n_grp)
        incoming = pltpu.make_async_remote_copy(
            src_ref=send_b.at[pl.ds(0, rows)],
            dst_ref=recv_b.at[grp],
            send_sem=b_send.at[grp],
            recv_sem=b_recv.at[grp],
            device_id=(req, grp * 2 + c),
            device_id_type=MESH_IDS,
        )
        incoming.wait_recv()
        total = total + recv_b[grp].astype(jnp.float32)
    mine = pl.ds(pl.multiple_of(c * half + g * rows, rows), rows)
    resid = resid_ref[...] + total
    res_out[...] = resid
    if final:
        full_ref[mine, :] = resid.astype(full_ref.dtype)
    else:
        mean_square = jnp.mean(resid * resid, axis=-1, keepdims=True)
        full_ref[mine, :] = (resid * lax.rsqrt(mean_square + EPSILON) * gain_ref[...]).astype(
            full_ref.dtype
        )
    for k in range(1, n_grp):
        peer = lax.rem(g + k, n_grp) * 2 + c
        copy = pltpu.make_async_remote_copy(
            src_ref=full_ref.at[mine],
            dst_ref=full_ref.at[mine],
            send_sem=ag_send.at[k],
            recv_sem=ag_recv.at[g],
            device_id=(req, peer),
            device_id_type=MESH_IDS,
        )
        copy.start()
        sends.append(copy)
    copy = pltpu.make_async_remote_copy(
        src_ref=full_ref.at[mine],
        dst_ref=full_ref.at[mine],
        send_sem=ag_send.at[0],
        recv_sem=ag_recv.at[n_grp + g],
        device_id=(req, partner),
        device_id_type=MESH_IDS,
    )
    copy.start()
    sends.append(copy)
    for k in range(1, n_grp):
        grp = lax.rem(g + n_grp - k, n_grp)
        there = pl.ds(pl.multiple_of(c * half + grp * rows, rows), rows)
        incoming = pltpu.make_async_remote_copy(
            src_ref=full_ref.at[there],
            dst_ref=full_ref.at[there],
            send_sem=ag_send.at[0],
            recv_sem=ag_recv.at[grp],
            device_id=(req, grp * 2 + c),
            device_id_type=MESH_IDS,
        )
        incoming.wait_recv()
        forward = pltpu.make_async_remote_copy(
            src_ref=full_ref.at[there],
            dst_ref=full_ref.at[there],
            send_sem=ag_send.at[n_grp + k],
            recv_sem=ag_recv.at[n_grp + grp],
            device_id=(req, partner),
            device_id_type=MESH_IDS,
        )
        forward.start()
        sends.append(forward)
    for grp in range(n_grp):
        there = pl.ds(pl.multiple_of((1 - c) * half + grp * rows, rows), rows)
        incoming = pltpu.make_async_remote_copy(
            src_ref=full_ref.at[there],
            dst_ref=full_ref.at[there],
            send_sem=ag_send.at[0],
            recv_sem=ag_recv.at[n_grp + grp],
            device_id=(req, partner),
            device_id_type=MESH_IDS,
        )
        incoming.wait_recv()
    if extra:
        wts_ref[req] = packed_ref[...]
        for k in range(1, n_req):
            src = lax.rem(req + n_req - k, n_req)
            incoming = pltpu.make_async_remote_copy(
                src_ref=packed_ref,
                dst_ref=wts_ref.at[src],
                send_sem=w_send.at[src],
                recv_sem=w_recv.at[src],
                device_id=(src, me),
                device_id_type=MESH_IDS,
            )
            incoming.wait_recv()
    for copy in sends:
        copy.wait_send()


def blk_stage(part, resid, gain, final, packed=None):
    n_blk = lax.axis_size("blk")
    rows, width = resid.shape
    vmem = pl.BlockSpec(memory_space=pltpu.VMEM)
    extra = packed is not None
    outs = [
        jax.ShapeDtypeStruct((rows, width), jnp.float32),
        jax.ShapeDtypeStruct((rows * n_blk, width), jnp.bfloat16),
    ]
    n_grp = n_blk // 2
    scratch = [
        pltpu.VMEM((n_grp * rows, width), part.dtype),
        pltpu.VMEM((n_grp * rows, width), part.dtype),
        pltpu.VMEM((n_grp, rows, width), part.dtype),
        pltpu.SemaphoreType.DMA((2,)),
        pltpu.SemaphoreType.DMA((n_grp,)),
        pltpu.SemaphoreType.DMA((n_grp,)),
        pltpu.SemaphoreType.DMA((n_blk,)),
        pltpu.SemaphoreType.DMA((n_blk,)),
    ]
    args = [part, resid, gain[None, :]]
    if extra:
        n_req = lax.axis_size("req")
        outs.append(jax.ShapeDtypeStruct((n_req,) + packed.shape, packed.dtype))
        scratch += [pltpu.SemaphoreType.DMA((n_req,)), pltpu.SemaphoreType.DMA((n_req,))]
        args.append(packed)
    return pl.pallas_call(
        functools.partial(stage_kernel, n_blk, final, extra),
        out_shape=tuple(outs),
        in_specs=[vmem] * len(args),
        out_specs=tuple([vmem] * len(outs)),
        scratch_shapes=scratch,
        compiler_params=pltpu.CompilerParams(
            collective_id=5 if extra else (4 if final else 3), has_side_effects=True
        ),
    )(*args)


def self_kernel(lens_ref, q_ref, c_ref, kn_ref, vn_ref, g_ref, f_ref, o_ref):
    old_len = lens_ref[0]
    fresh_len = lens_ref[1]
    n_q = q_ref.shape[0]
    n_ctx = c_ref.shape[0]
    wide_old = n_ctx + TQ
    wide_new = n_q + TQ
    k_old = c_ref[:, :HD]
    v_old = c_ref[:, HD:]
    k_new = kn_ref[...]
    v_new = vn_ref[...]
    dims = (((1,), (1,)), ((), ()))
    for t in range(n_q // TQ):
        q = q_ref[t * TQ : (t + 1) * TQ, :]
        start = n_q - TQ - t * TQ
        s_old = lax.dot_general(q, k_old, dims, preferred_element_type=jnp.float32)
        line = jnp.broadcast_to(g_ref[:, start : start + wide_old], (TQ, wide_old))
        bias = pltpu.roll(line, wide_old - (TQ - 1), 1, stride=1, stride_axis=0)[:, :n_ctx]
        col = lax.broadcasted_iota(jnp.int32, (TQ, n_ctx), 1)
        s_old = jnp.where(col < old_len, s_old + bias, NEG_FILL)
        s_new = lax.dot_general(q, k_new, dims, preferred_element_type=jnp.float32)
        line = jnp.broadcast_to(f_ref[:, start : start + wide_new], (TQ, wide_new))
        bias = pltpu.roll(line, wide_new - (TQ - 1), 1, stride=1, stride_axis=0)[:, :n_q]
        row = lax.broadcasted_iota(jnp.int32, (TQ, n_q), 0) + t * TQ
        col = lax.broadcasted_iota(jnp.int32, (TQ, n_q), 1)
        s_new = jnp.where((col <= row) & (col < fresh_len), s_new + bias, NEG_FILL)
        top = jnp.maximum(
            jnp.max(s_old, axis=1, keepdims=True), jnp.max(s_new, axis=1, keepdims=True)
        )
        p_old = jnp.exp(s_old - top)
        p_new = jnp.exp(s_new - top)
        total = jnp.sum(p_old, axis=1, keepdims=True) + jnp.sum(p_new, axis=1, keepdims=True)
        w_old = (p_old / total).astype(jnp.bfloat16)
        w_new = (p_new / total).astype(jnp.bfloat16)
        out = jnp.dot(w_old, v_old, preferred_element_type=jnp.float32) + jnp.dot(
            w_new, v_new, preferred_element_type=jnp.float32
        )
        o_ref[t * TQ : (t + 1) * TQ, :] = out.astype(jnp.bfloat16)


def bias_lines(line, old_len, n_q, n_ctx):
    span = line.shape[0]
    ext = jnp.concatenate([jnp.broadcast_to(line[:1], (n_ctx,)), line])
    rev = ext[::-1]
    g = lax.dynamic_slice_in_dim(rev, n_ctx - old_len, span)
    f = rev[n_ctx : n_ctx + 2 * n_q]
    return g[None, :], f[None, :]


def self_attention(q, cache_blk, k_new, v_new, line, old_len, fresh_len):
    n_q = q.shape[0]
    n_ctx = cache_blk.shape[0]
    g, f = bias_lines(line, old_len, n_q, n_ctx)
    lens = jnp.stack([old_len, fresh_len]).astype(jnp.int32)
    vmem = pl.BlockSpec(memory_space=pltpu.VMEM)
    return pl.pallas_call(
        self_kernel,
        out_shape=jax.ShapeDtypeStruct((n_q, HD), jnp.bfloat16),
        in_specs=[pl.BlockSpec(memory_space=pltpu.SMEM)] + [vmem] * 6,
        out_specs=vmem,
        compiler_params=pltpu.CompilerParams(vmem_limit_bytes=48 * 1024 * 1024),
    )(lens, q, cache_blk, k_new, v_new, g, f)


def pack_gather(pieces):
    flat = jnp.concatenate([w.reshape(-1) for w, _ in pieces])
    whole = lax.all_gather(flat, "req", axis=0, tiled=False)
    n_req = whole.shape[0]
    out, at = [], 0
    for w, axis in pieces:
        size = w.size
        part = whole[:, at : at + size].reshape((n_req,) + w.shape)
        at += size
        part = jnp.moveaxis(part, 0, axis)
        shape = list(w.shape)
        shape[axis] *= n_req
        out.append(part.reshape(shape))
    return out


MESH_IDS = pl.DeviceIdType.MESH


def greet_all(n_blk, me, req):
    barrier = pltpu.get_barrier_semaphore()
    for k in range(1, n_blk):
        peer = lax.rem(me + k, n_blk)
        pl.semaphore_signal(barrier, inc=1, device_id=(req, peer), device_id_type=MESH_IDS)
    pl.semaphore_wait(barrier, n_blk - 1)


def chunk_of(b, n_blk):
    return lax.rem(b, 2) * (n_blk // 2) + b // 2


def scatter_kernel(n_blk, part_ref, out_ref, recv, send_sem, recv_sem):
    me = lax.axis_index("blk")
    req = lax.axis_index("req")
    rows = out_ref.shape[0]
    greet_all(n_blk, me, req)
    copies = []
    for k in range(1, n_blk):
        peer = lax.rem(me + k, n_blk)
        copy = pltpu.make_async_remote_copy(
            src_ref=part_ref.at[pl.ds(pl.multiple_of(chunk_of(peer, n_blk) * rows, rows), rows)],
            dst_ref=recv.at[me],
            send_sem=send_sem.at[peer],
            recv_sem=recv_sem.at[me],
            device_id=(req, peer),
            device_id_type=MESH_IDS,
        )
        copy.start()
        copies.append(copy)
    own = pl.ds(pl.multiple_of(chunk_of(me, n_blk) * rows, rows), rows)
    total = part_ref[own, :].astype(jnp.float32)
    for k in range(1, n_blk):
        src = lax.rem(me + n_blk - k, n_blk)
        incoming = pltpu.make_async_remote_copy(
            src_ref=part_ref.at[pl.ds(0, rows)],
            dst_ref=recv.at[src],
            send_sem=send_sem.at[src],
            recv_sem=recv_sem.at[src],
            device_id=(req, src),
            device_id_type=MESH_IDS,
        )
        incoming.wait_recv()
        total = total + recv[src].astype(jnp.float32)
    for copy in copies:
        copy.wait_send()
    out_ref[...] = total


def gather_kernel(n_blk, piece_ref, out_ref, send_sem, recv_sem):
    b = lax.axis_index("blk")
    req = lax.axis_index("req")
    n_grp = n_blk // 2
    g = b // 2
    c = lax.rem(b, 2)
    partner = g * 2 + 1 - c
    rows = piece_ref.shape[0]
    half = n_grp * rows
    barrier = pltpu.get_barrier_semaphore()
    for k in range(1, n_grp):
        peer = lax.rem(g + k, n_grp) * 2 + c
        pl.semaphore_signal(barrier, inc=1, device_id=(req, peer), device_id_type=MESH_IDS)
    pl.semaphore_signal(barrier, inc=1, device_id=(req, partner), device_id_type=MESH_IDS)
    pl.semaphore_wait(barrier, n_grp)
    mine = pl.ds(pl.multiple_of(c * half + g * rows, rows), rows)
    sends = []
    for k in range(1, n_grp):
        peer = lax.rem(g + k, n_grp) * 2 + c
        copy = pltpu.make_async_remote_copy(
            src_ref=piece_ref,
            dst_ref=out_ref.at[mine],
            send_sem=send_sem.at[k],
            recv_sem=recv_sem.at[g],
            device_id=(req, peer),
            device_id_type=MESH_IDS,
        )
        copy.start()
        sends.append(copy)
    copy = pltpu.make_async_remote_copy(
        src_ref=piece_ref,
        dst_ref=out_ref.at[mine],
        send_sem=send_sem.at[0],
        recv_sem=recv_sem.at[n_grp + g],
        device_id=(req, partner),
        device_id_type=MESH_IDS,
    )
    copy.start()
    sends.append(copy)
    out_ref[mine, :] = piece_ref[...]
    for k in range(1, n_grp):
        grp = lax.rem(g + n_grp - k, n_grp)
        there = pl.ds(pl.multiple_of(c * half + grp * rows, rows), rows)
        incoming = pltpu.make_async_remote_copy(
            src_ref=piece_ref,
            dst_ref=out_ref.at[there],
            send_sem=send_sem.at[0],
            recv_sem=recv_sem.at[grp],
            device_id=(req, grp * 2 + c),
            device_id_type=MESH_IDS,
        )
        incoming.wait_recv()
        forward = pltpu.make_async_remote_copy(
            src_ref=out_ref.at[there],
            dst_ref=out_ref.at[there],
            send_sem=send_sem.at[n_grp + k],
            recv_sem=recv_sem.at[n_grp + grp],
            device_id=(req, partner),
            device_id_type=MESH_IDS,
        )
        forward.start()
        sends.append(forward)
    for grp in range(n_grp):
        there = pl.ds(pl.multiple_of((1 - c) * half + grp * rows, rows), rows)
        incoming = pltpu.make_async_remote_copy(
            src_ref=piece_ref,
            dst_ref=out_ref.at[there],
            send_sem=send_sem.at[0],
            recv_sem=recv_sem.at[n_grp + grp],
            device_id=(req, partner),
            device_id_type=MESH_IDS,
        )
        incoming.wait_recv()
    for copy in sends:
        copy.wait_send()


def blk_scatter(part):
    n_blk = lax.axis_size("blk")
    rows = part.shape[0] // n_blk
    vmem = pl.BlockSpec(memory_space=pltpu.VMEM)
    return pl.pallas_call(
        functools.partial(scatter_kernel, n_blk),
        out_shape=jax.ShapeDtypeStruct((rows, part.shape[1]), jnp.float32),
        in_specs=[vmem],
        out_specs=vmem,
        scratch_shapes=[
            pltpu.VMEM((n_blk, rows, part.shape[1]), part.dtype),
            pltpu.SemaphoreType.DMA((n_blk,)),
            pltpu.SemaphoreType.DMA((n_blk,)),
        ],
        compiler_params=pltpu.CompilerParams(collective_id=1, has_side_effects=True),
    )(part)


def blk_gather(piece):
    n_blk = lax.axis_size("blk")
    rows = piece.shape[0]
    vmem = pl.BlockSpec(memory_space=pltpu.VMEM)
    return pl.pallas_call(
        functools.partial(gather_kernel, n_blk),
        out_shape=jax.ShapeDtypeStruct((rows * n_blk, piece.shape[1]), piece.dtype),
        in_specs=[vmem],
        out_specs=vmem,
        scratch_shapes=[
            pltpu.SemaphoreType.DMA((n_blk,)),
            pltpu.SemaphoreType.DMA((n_blk,)),
        ],
        compiler_params=pltpu.CompilerParams(collective_id=2, has_side_effects=True),
    )(piece)


def prologue_kernel(n_req, n_blk, ordered_ref, packed_ref, cache_ref, wts_ref, w_send, w_recv, c_send, c_recv, local_sem):
    r = lax.axis_index("req")
    b = lax.axis_index("blk")
    n_slot, span, width = ordered_ref.shape
    piece = width // 2
    copies = []
    for k in range(1, n_req):
        peer = lax.rem(r + k, n_req)
        copy = pltpu.make_async_remote_copy(
            src_ref=packed_ref,
            dst_ref=wts_ref.at[r],
            send_sem=w_send.at[peer],
            recv_sem=w_recv.at[r],
            device_id=(peer, b),
            device_id_type=MESH_IDS,
        )
        copy.start()
        copies.append(copy)
    rows = pl.ds(pl.multiple_of(b * span, span), span)
    for s in range(n_slot):
        for hh in range(2):
            head = 2 * r + hh
            is_self = jnp.logical_and(r == s, head == b)
            src = ordered_ref.at[s, :, pl.ds(hh * piece, piece)]
            copy = pltpu.make_async_remote_copy(
                src_ref=src,
                dst_ref=cache_ref.at[rows],
                send_sem=c_send.at[s * 2 + hh],
                recv_sem=c_recv.at[b],
                device_id=(s, head),
                device_id_type=MESH_IDS,
            )

            @pl.when(jnp.logical_not(is_self))
            def _():
                copy.start()

            @pl.when(is_self)
            def _():
                local = pltpu.make_async_copy(src, cache_ref.at[rows], local_sem.at[0])
                local.start()
                local.wait()

            copies.append((copy, is_self))
    wts_ref[r] = packed_ref[...]
    for k in range(1, n_req):
        src_req = lax.rem(r + n_req - k, n_req)
        incoming = pltpu.make_async_remote_copy(
            src_ref=packed_ref,
            dst_ref=wts_ref.at[src_req],
            send_sem=w_send.at[src_req],
            recv_sem=w_recv.at[src_req],
            device_id=(src_req, b),
            device_id_type=MESH_IDS,
        )
        incoming.wait_recv()
    owner = b // 2
    for j in range(n_blk):
        incoming = pltpu.make_async_remote_copy(
            src_ref=ordered_ref.at[0, :, pl.ds(0, piece)],
            dst_ref=cache_ref.at[pl.ds(j * span, span)],
            send_sem=c_send.at[0],
            recv_sem=c_recv.at[j],
            device_id=(owner, j),
            device_id_type=MESH_IDS,
        )

        @pl.when(jnp.logical_not(jnp.logical_and(owner == r, j == b)))
        def _():
            incoming.wait_recv()

    for item in copies:
        if isinstance(item, tuple):
            copy, is_self = item

            @pl.when(jnp.logical_not(is_self))
            def _():
                copy.wait_send()

        else:
            item.wait_send()


def prologue(ordered, packed):
    n_req = lax.axis_size("req")
    n_blk = lax.axis_size("blk")
    n_slot, span, width = ordered.shape
    any_spec = pl.BlockSpec(memory_space=pl.ANY)
    vmem = pl.BlockSpec(memory_space=pltpu.VMEM)
    return pl.pallas_call(
        functools.partial(prologue_kernel, n_req, n_blk),
        out_shape=(
            jax.ShapeDtypeStruct((span * n_blk, width // 2), ordered.dtype),
            jax.ShapeDtypeStruct((n_req,) + packed.shape, packed.dtype),
        ),
        in_specs=[any_spec, vmem],
        out_specs=(any_spec, vmem),
        scratch_shapes=[
            pltpu.SemaphoreType.DMA((n_req,)),
            pltpu.SemaphoreType.DMA((n_req,)),
            pltpu.SemaphoreType.DMA((2 * n_slot,)),
            pltpu.SemaphoreType.DMA((n_blk,)),
            pltpu.SemaphoreType.DMA((1,)),
        ],
        compiler_params=pltpu.CompilerParams(has_side_effects=True),
    )(ordered, packed)


def unpack(whole, pieces):
    n_req = whole.shape[0]
    whole = whole.reshape(n_req, -1)
    out, at = [], 0
    for w, axis in pieces:
        size = w.size
        part = whole[:, at : at + size].reshape((n_req,) + w.shape)
        at += size
        part = jnp.moveaxis(part, 0, axis)
        shape = list(w.shape)
        shape[axis] *= n_req
        out.append(part.reshape(shape))
    return out


def per_device(
    new_states,
    encoder_out,
    cache_in,
    slot_order,
    new_lengths,
    cache_lengths,
    enc_lengths,
    bucket_of,
    rel_bias,
    norm_gain,
    self_q,
    self_kv,
    self_out,
    cross_q,
    cross_kv,
    cross_out,
    ff_in,
    ff_out,
):
    blk_count = lax.axis_size("blk")
    heads_dev = H // blk_count
    width_dev = heads_dev * HD
    req_dev = cache_in.shape[0] // lax.axis_size("req")
    own_slots = lax.dynamic_slice_in_dim(slot_order, lax.axis_index("req") * req_dev, req_dev, 0)
    slot_new = pick_lengths(new_lengths, own_slots)
    slot_old = pick_lengths(cache_lengths, own_slots)
    slot_enc = pick_lengths(enc_lengths, own_slots)
    ordered = jnp.take(cache_in, slot_order, axis=0)
    onehot = (bucket_of[:, None] == jnp.arange(rel_bias.shape[0], dtype=jnp.int32)[None, :]).astype(
        jnp.float32
    )
    own_bias = lax.dynamic_slice_in_dim(rel_bias, lax.axis_index("blk") * heads_dev, heads_dev, 1)
    bias_dist = jnp.dot(onehot, own_bias, precision=lax.Precision.HIGHEST).T
    early = [(self_q, 0), (self_kv, 0), (self_out, 1)]
    late = [(cross_q, 0), (cross_kv, 0), (cross_out, 1), (ff_in, 0), (ff_out, 1)]
    flat = jnp.concatenate([w.reshape(-1) for w, _ in early])
    cache_blk, whole = prologue(ordered, flat.reshape(-1, 128))
    cache_dec = cache_blk[None]
    gathered = unpack(whole, early)
    late_gathered = pack_gather(late)
    wq_self, wkv_self, wo_self = gathered
    n_blk = lax.axis_size("blk")
    rows_dev = new_states.shape[0] // n_blk
    own_rows = lax.dynamic_slice_in_dim(
        new_states, chunk_of(lax.axis_index("blk"), n_blk) * rows_dev, rows_dev, 0
    ).astype(jnp.float32)
    normed = rms_rows(new_states.astype(jnp.float32), norm_gain[0])
    self_cat = jnp.concatenate([wq_self, wkv_self.reshape(wkv_self.shape[0], -1)], axis=1)
    projected = jnp.dot(normed, self_cat, preferred_element_type=jnp.float32).astype(
        jnp.bfloat16
    )
    context = self_attention(
        projected[:, :HD],
        cache_dec[0],
        projected[:, HD : 2 * HD],
        projected[:, 2 * HD :],
        bias_dist[0],
        slot_old[0],
        slot_new[0],
    )
    part = jnp.dot(context, wo_self, preferred_element_type=jnp.float32).astype(jnp.bfloat16)
    residual, normed = blk_stage(part, own_rows, norm_gain[1], False)
    wq_cross, wkv_cross, wo_cross, w_in, w_out = late_gathered
    queries = (
        jnp.dot(normed, wq_cross, preferred_element_type=jnp.float32)
        .astype(jnp.bfloat16)
        .reshape(req_dev, -1, heads_dev, HD)
    )
    cross_pair = wkv_cross.reshape(wkv_cross.shape[0], -1)
    key_value = (
        jnp.dot(encoder_out, cross_pair, preferred_element_type=jnp.float32)
        .astype(jnp.bfloat16)
        .reshape(req_dev, -1, 2, heads_dev, HD)
    )
    context = cross_attend(queries, key_value, slot_enc)
    part = jnp.dot(context.reshape(-1, width_dev), wo_cross, preferred_element_type=jnp.float32)
    residual, normed = blk_stage(part.astype(jnp.bfloat16), residual, norm_gain[2], False)
    ff_dev = w_in.shape[2]
    gate_up = jnp.dot(normed, w_in.reshape(w_in.shape[0], -1), preferred_element_type=jnp.float32)
    hidden = (jax.nn.gelu(gate_up[:, :ff_dev], approximate=True) * gate_up[:, ff_dev:]).astype(
        jnp.bfloat16
    )
    part = jnp.dot(hidden, w_out, preferred_element_type=jnp.float32).astype(jnp.bfloat16)
    _, layer_out = blk_stage(part, residual, norm_gain[2], True)
    return (layer_out, cache_dec)


def solution(mesh):
    in_specs = (
        P("req", None),
        P("req", None),
        P(None, "blk", "req"),
        P(),
        P(),
        P(),
        P(),
        P(),
        P(),
        P(),
        P("req", "blk"),
        P("req", None, "blk"),
        P("blk", "req"),
        P("req", "blk"),
        P("req", None, "blk"),
        P("blk", "req"),
        P("req", None, "blk"),
        P("blk", "req"),
    )
    out_specs = (P("req", None), P("req", None, "blk"))
    return jax.shard_map(
        per_device, mesh=mesh, in_specs=in_specs, out_specs=out_specs, check_vma=False
    )
```

```python
import functools

import jax
import jax.numpy as jnp
from jax import lax
from jax.sharding import PartitionSpec as P
from jax.experimental import pallas as pl
from jax.experimental.pallas import tpu as pltpu

H = 16
HD = 64


EPSILON = 1e-06
NEG_FILL = -1e30


def rms_rows(row_block, gain):
    mean_square = jnp.mean(row_block * row_block, axis=-1, keepdims=True)
    return (row_block * lax.rsqrt(mean_square + EPSILON) * gain).astype(jnp.bfloat16)


def softmax_rows(scores):
    row_top = jnp.max(scores, axis=-1, keepdims=True)
    weights = jnp.exp(scores - row_top)
    return (weights / jnp.sum(weights, axis=-1, keepdims=True)).astype(jnp.bfloat16)


def pick_lengths(table, own_slots):
    matches = own_slots[:, None] == jnp.arange(table.shape[0], dtype=jnp.int32)[None, :]
    return jnp.sum(jnp.where(matches, table[None, :], 0), axis=1)


def shifted_bias(bias_dist, base, row_count, col_count):
    heads_here, span_len = bias_dist.shape
    line_len = row_count + col_count - 1
    steps = jnp.arange(line_len + 1, dtype=jnp.int32)
    line = bias_dist[:, jnp.clip(base + row_count - 1 - steps, 0, span_len - 1)]
    tiled = jnp.broadcast_to(line[:, None, :], (heads_here, row_count, line_len + 1))
    flat = tiled.reshape(heads_here, row_count * (line_len + 1))[:, : row_count * line_len]
    skewed = flat.reshape(heads_here, row_count, line_len)
    return skewed[:, :, row_count - 1 : row_count - 1 + col_count]


def row_total(left, weight):
    term = jnp.dot(left, weight, preferred_element_type=jnp.float32)
    return lax.psum(term.astype(jnp.bfloat16), "blk").astype(jnp.float32)


def cached_scores(queries, key_rows, first_col, old_len, bias_dist):
    col_ids = first_col + jnp.arange(key_rows.shape[0], dtype=jnp.int32)[None, :]
    scores = jnp.einsum("qhe,khe->hqk", queries, key_rows, preferred_element_type=jnp.float32)
    scores = scores + shifted_bias(
        bias_dist, old_len - first_col, queries.shape[0], key_rows.shape[0]
    )
    return jnp.where((col_ids < old_len)[None], scores, NEG_FILL)


def fresh_scores(queries, fresh_keys, fresh_len, bias_dist):
    row_ids = jnp.arange(queries.shape[0], dtype=jnp.int32)[:, None]
    col_ids = jnp.arange(fresh_keys.shape[0], dtype=jnp.int32)[None, :]
    scores = jnp.einsum("qhe,khe->hqk", queries, fresh_keys, preferred_element_type=jnp.float32)
    scores = scores + shifted_bias(bias_dist, 0, queries.shape[0], fresh_keys.shape[0])
    admitted = (col_ids <= row_ids) & (col_ids < fresh_len)
    return jnp.where(admitted[None], scores, NEG_FILL)


def self_padded(
    queries, key_rows, value_rows, fresh_keys, fresh_values, old_len, fresh_len, bias_dist
):
    scores = jnp.concatenate(
        [
            cached_scores(queries, key_rows, 0, old_len, bias_dist),
            fresh_scores(queries, fresh_keys, fresh_len, bias_dist),
        ],
        axis=2,
    )
    weights = softmax_rows(scores)
    value_all = jnp.concatenate([value_rows, fresh_values], axis=0)
    return jnp.einsum(
        "hqk,khe->qhe", weights, value_all, preferred_element_type=jnp.float32
    ).astype(jnp.bfloat16)


def self_attend(queries, key_value, cache_dec, slot_old, slot_new, bias_dist, heads_dev):
    req_dev, cache_len = (cache_dec.shape[0], cache_dec.shape[1])
    cache_split = cache_dec.reshape(req_dev, cache_len, heads_dev, 2, -1)

    def one_request(request):
        queries_one, pair_one, cache_one, old_len, fresh_len = request
        return self_padded(
            queries_one,
            cache_one[:, :, 0],
            cache_one[:, :, 1],
            pair_one[:, 0],
            pair_one[:, 1],
            old_len,
            fresh_len,
            bias_dist,
        )

    return lax.map(one_request, (queries, key_value, cache_split, slot_old, slot_new))


def cross_attend(queries, key_value, slot_enc):
    scores = jnp.einsum(
        "rqhe,rkhe->rhqk", queries, key_value[:, :, 0], preferred_element_type=jnp.float32
    )
    col_ids = jnp.arange(key_value.shape[1], dtype=jnp.int32)
    scores = jnp.where(
        col_ids[None, None, None, :] < slot_enc[:, None, None, None], scores, NEG_FILL
    )
    weights = softmax_rows(scores)
    return jnp.einsum(
        "rhqk,rkhe->rqhe", weights, key_value[:, :, 1], preferred_element_type=jnp.float32
    ).astype(jnp.bfloat16)


def add_branch(residual, left, weight, gain):
    residual = residual + row_total(left, weight)
    normed = rms_rows(residual, gain)
    return (residual, normed)


TQ = 128


def stage_kernel(n_blk, final, extra, *refs):
    if extra:
        (part_ref, resid_ref, gain_ref, packed_ref, res_out, full_ref, wts_ref,
         recv_a, send_b, recv_b, sems, b_send, b_recv, ag_send, ag_recv, w_send, w_recv) = refs
    else:
        (part_ref, resid_ref, gain_ref, res_out, full_ref,
         recv_a, send_b, recv_b, sems, b_send, b_recv, ag_send, ag_recv) = refs
    me = lax.axis_index("blk")
    req = lax.axis_index("req")
    rows = resid_ref.shape[0]
    n_grp = n_blk // 2
    g = me // 2
    c = lax.rem(me, 2)
    partner = g * 2 + 1 - c
    half = n_grp * rows
    n_req = wts_ref.shape[0] if extra else 1
    barrier = pltpu.get_barrier_semaphore()
    for k in range(1, n_grp):
        peer = lax.rem(g + k, n_grp) * 2 + c
        pl.semaphore_signal(barrier, inc=1, device_id=(req, peer), device_id_type=MESH_IDS)
    pl.semaphore_signal(barrier, inc=1, device_id=(req, partner), device_id_type=MESH_IDS)
    for k in range(1, n_req):
        peer = lax.rem(req + k, n_req)
        pl.semaphore_signal(barrier, inc=1, device_id=(peer, me), device_id_type=MESH_IDS)
    pl.semaphore_wait(barrier, n_grp + n_req - 1)
    sends = []
    exchange = pltpu.make_async_remote_copy(
        src_ref=part_ref.at[pl.ds(pl.multiple_of((1 - c) * half, half), half)],
        dst_ref=recv_a,
        send_sem=sems.at[0],
        recv_sem=sems.at[1],
        device_id=(req, partner),
        device_id_type=MESH_IDS,
    )
    exchange.start()
    sends.append(exchange)
    for k in range(1, n_req):
        peer = lax.rem(req + k, n_req)
        copy = pltpu.make_async_remote_copy(
            src_ref=packed_ref,
            dst_ref=wts_ref.at[req],
            send_sem=w_send.at[peer],
            recv_sem=w_recv.at[req],
            device_id=(peer, me),
            device_id_type=MESH_IDS,
        )
        copy.start()
        sends.append(copy)
    exchange.wait_recv()
    pair = part_ref[pl.ds(pl.multiple_of(c * half, half), half), :].astype(jnp.float32) + recv_a[
        ...
    ].astype(jnp.float32)
    send_b[...] = pair.astype(send_b.dtype)
    for k in range(1, n_grp):
        grp = lax.rem(g + k, n_grp)
        copy = pltpu.make_async_remote_copy(
            src_ref=send_b.at[pl.ds(pl.multiple_of(grp * rows, rows), rows)],
            dst_ref=recv_b.at[g],
            send_sem=b_send.at[grp],
            recv_sem=b_recv.at[g],
            device_id=(req, grp * 2 + c),
            device_id_type=MESH_IDS,
        )
        copy.start()
        sends.append(copy)
    total = send_b[pl.ds(pl.multiple_of(g * rows, rows), rows), :].astype(jnp.float32)
    for k in range(1, n_grp):
        grp = lax.rem(g + n_grp - k, n_grp)
        incoming = pltpu.make_async_remote_copy(
            src_ref=send_b.at[pl.ds(0, rows)],
            dst_ref=recv_b.at[grp],
            send_sem=b_send.at[grp],
            recv_sem=b_recv.at[grp],
            device_id=(req, grp * 2 + c),
            device_id_type=MESH_IDS,
        )
        incoming.wait_recv()
        total = total + recv_b[grp].astype(jnp.float32)
    mine = pl.ds(pl.multiple_of(c * half + g * rows, rows), rows)
    resid = resid_ref[...] + total
    res_out[...] = resid
    if final:
        full_ref[mine, :] = resid.astype(full_ref.dtype)
    else:
        mean_square = jnp.mean(resid * resid, axis=-1, keepdims=True)
        full_ref[mine, :] = (resid * lax.rsqrt(mean_square + EPSILON) * gain_ref[...]).astype(
            full_ref.dtype
        )
    for k in range(1, n_grp):
        peer = lax.rem(g + k, n_grp) * 2 + c
        copy = pltpu.make_async_remote_copy(
            src_ref=full_ref.at[mine],
            dst_ref=full_ref.at[mine],
            send_sem=ag_send.at[k],
            recv_sem=ag_recv.at[g],
            device_id=(req, peer),
            device_id_type=MESH_IDS,
        )
        copy.start()
        sends.append(copy)
    copy = pltpu.make_async_remote_copy(
        src_ref=full_ref.at[mine],
        dst_ref=full_ref.at[mine],
        send_sem=ag_send.at[0],
        recv_sem=ag_recv.at[n_grp + g],
        device_id=(req, partner),
        device_id_type=MESH_IDS,
    )
    copy.start()
    sends.append(copy)
    for k in range(1, n_grp):
        grp = lax.rem(g + n_grp - k, n_grp)
        there = pl.ds(pl.multiple_of(c * half + grp * rows, rows), rows)
        incoming = pltpu.make_async_remote_copy(
            src_ref=full_ref.at[there],
            dst_ref=full_ref.at[there],
            send_sem=ag_send.at[0],
            recv_sem=ag_recv.at[grp],
            device_id=(req, grp * 2 + c),
            device_id_type=MESH_IDS,
        )
        incoming.wait_recv()
        forward = pltpu.make_async_remote_copy(
            src_ref=full_ref.at[there],
            dst_ref=full_ref.at[there],
            send_sem=ag_send.at[n_grp + k],
            recv_sem=ag_recv.at[n_grp + grp],
            device_id=(req, partner),
            device_id_type=MESH_IDS,
        )
        forward.start()
        sends.append(forward)
    for grp in range(n_grp):
        there = pl.ds(pl.multiple_of((1 - c) * half + grp * rows, rows), rows)
        incoming = pltpu.make_async_remote_copy(
            src_ref=full_ref.at[there],
            dst_ref=full_ref.at[there],
            send_sem=ag_send.at[0],
            recv_sem=ag_recv.at[n_grp + grp],
            device_id=(req, partner),
            device_id_type=MESH_IDS,
        )
        incoming.wait_recv()
    if extra:
        wts_ref[req] = packed_ref[...]
        for k in range(1, n_req):
            src = lax.rem(req + n_req - k, n_req)
            incoming = pltpu.make_async_remote_copy(
                src_ref=packed_ref,
                dst_ref=wts_ref.at[src],
                send_sem=w_send.at[src],
                recv_sem=w_recv.at[src],
                device_id=(src, me),
                device_id_type=MESH_IDS,
            )
            incoming.wait_recv()
    for copy in sends:
        copy.wait_send()


def blk_stage(part, resid, gain, final, packed=None):
    n_blk = lax.axis_size("blk")
    rows, width = resid.shape
    vmem = pl.BlockSpec(memory_space=pltpu.VMEM)
    extra = packed is not None
    outs = [
        jax.ShapeDtypeStruct((rows, width), jnp.float32),
        jax.ShapeDtypeStruct((rows * n_blk, width), jnp.bfloat16),
    ]
    n_grp = n_blk // 2
    scratch = [
        pltpu.VMEM((n_grp * rows, width), part.dtype),
        pltpu.VMEM((n_grp * rows, width), part.dtype),
        pltpu.VMEM((n_grp, rows, width), part.dtype),
        pltpu.SemaphoreType.DMA((2,)),
        pltpu.SemaphoreType.DMA((n_grp,)),
        pltpu.SemaphoreType.DMA((n_grp,)),
        pltpu.SemaphoreType.DMA((n_blk,)),
        pltpu.SemaphoreType.DMA((n_blk,)),
    ]
    args = [part, resid, gain[None, :]]
    if extra:
        n_req = lax.axis_size("req")
        outs.append(jax.ShapeDtypeStruct((n_req,) + packed.shape, packed.dtype))
        scratch += [pltpu.SemaphoreType.DMA((n_req,)), pltpu.SemaphoreType.DMA((n_req,))]
        args.append(packed)
    return pl.pallas_call(
        functools.partial(stage_kernel, n_blk, final, extra),
        out_shape=tuple(outs),
        in_specs=[vmem] * len(args),
        out_specs=tuple([vmem] * len(outs)),
        scratch_shapes=scratch,
        compiler_params=pltpu.CompilerParams(
            collective_id=5 if extra else (4 if final else 3), has_side_effects=True
        ),
    )(*args)


def self_kernel(lens_ref, q_ref, c_ref, kn_ref, vn_ref, g_ref, f_ref, o_ref):
    old_len = lens_ref[0]
    fresh_len = lens_ref[1]
    n_q = q_ref.shape[0]
    n_ctx = c_ref.shape[0]
    wide_old = n_ctx + TQ
    wide_new = n_q + TQ
    k_old = c_ref[:, :HD]
    v_old = c_ref[:, HD:]
    k_new = kn_ref[...]
    v_new = vn_ref[...]
    dims = (((1,), (1,)), ((), ()))
    for t in range(n_q // TQ):
        q = q_ref[t * TQ : (t + 1) * TQ, :]
        start = n_q - TQ - t * TQ
        s_old = lax.dot_general(q, k_old, dims, preferred_element_type=jnp.float32)
        line = jnp.broadcast_to(g_ref[:, start : start + wide_old], (TQ, wide_old))
        bias = pltpu.roll(line, wide_old - (TQ - 1), 1, stride=1, stride_axis=0)[:, :n_ctx]
        col = lax.broadcasted_iota(jnp.int32, (TQ, n_ctx), 1)
        s_old = jnp.where(col < old_len, s_old + bias, NEG_FILL)
        s_new = lax.dot_general(q, k_new, dims, preferred_element_type=jnp.float32)
        line = jnp.broadcast_to(f_ref[:, start : start + wide_new], (TQ, wide_new))
        bias = pltpu.roll(line, wide_new - (TQ - 1), 1, stride=1, stride_axis=0)[:, :n_q]
        row = lax.broadcasted_iota(jnp.int32, (TQ, n_q), 0) + t * TQ
        col = lax.broadcasted_iota(jnp.int32, (TQ, n_q), 1)
        s_new = jnp.where((col <= row) & (col < fresh_len), s_new + bias, NEG_FILL)
        top = jnp.maximum(
            jnp.max(s_old, axis=1, keepdims=True), jnp.max(s_new, axis=1, keepdims=True)
        )
        p_old = jnp.exp(s_old - top)
        p_new = jnp.exp(s_new - top)
        total = jnp.sum(p_old, axis=1, keepdims=True) + jnp.sum(p_new, axis=1, keepdims=True)
        w_old = (p_old / total).astype(jnp.bfloat16)
        w_new = (p_new / total).astype(jnp.bfloat16)
        out = jnp.dot(w_old, v_old, preferred_element_type=jnp.float32) + jnp.dot(
            w_new, v_new, preferred_element_type=jnp.float32
        )
        o_ref[t * TQ : (t + 1) * TQ, :] = out.astype(jnp.bfloat16)


def bias_lines(line, old_len, n_q, n_ctx):
    span = line.shape[0]
    ext = jnp.concatenate([jnp.broadcast_to(line[:1], (n_ctx,)), line])
    rev = ext[::-1]
    g = lax.dynamic_slice_in_dim(rev, n_ctx - old_len, span)
    f = rev[n_ctx : n_ctx + 2 * n_q]
    return g[None, :], f[None, :]


def self_attention(q, cache_blk, k_new, v_new, line, old_len, fresh_len):
    n_q = q.shape[0]
    n_ctx = cache_blk.shape[0]
    g, f = bias_lines(line, old_len, n_q, n_ctx)
    lens = jnp.stack([old_len, fresh_len]).astype(jnp.int32)
    vmem = pl.BlockSpec(memory_space=pltpu.VMEM)
    return pl.pallas_call(
        self_kernel,
        out_shape=jax.ShapeDtypeStruct((n_q, HD), jnp.bfloat16),
        in_specs=[pl.BlockSpec(memory_space=pltpu.SMEM)] + [vmem] * 6,
        out_specs=vmem,
        compiler_params=pltpu.CompilerParams(vmem_limit_bytes=48 * 1024 * 1024),
    )(lens, q, cache_blk, k_new, v_new, g, f)


def pack_gather(pieces):
    flat = jnp.concatenate([w.reshape(-1) for w, _ in pieces])
    whole = lax.all_gather(flat, "req", axis=0, tiled=False)
    n_req = whole.shape[0]
    out, at = [], 0
    for w, axis in pieces:
        size = w.size
        part = whole[:, at : at + size].reshape((n_req,) + w.shape)
        at += size
        part = jnp.moveaxis(part, 0, axis)
        shape = list(w.shape)
        shape[axis] *= n_req
        out.append(part.reshape(shape))
    return out


MESH_IDS = pl.DeviceIdType.MESH


def greet_all(n_blk, me, req):
    barrier = pltpu.get_barrier_semaphore()
    for k in range(1, n_blk):
        peer = lax.rem(me + k, n_blk)
        pl.semaphore_signal(barrier, inc=1, device_id=(req, peer), device_id_type=MESH_IDS)
    pl.semaphore_wait(barrier, n_blk - 1)


def chunk_of(b, n_blk):
    return lax.rem(b, 2) * (n_blk // 2) + b // 2


def scatter_kernel(n_blk, part_ref, out_ref, recv, send_sem, recv_sem):
    me = lax.axis_index("blk")
    req = lax.axis_index("req")
    rows = out_ref.shape[0]
    greet_all(n_blk, me, req)
    copies = []
    for k in range(1, n_blk):
        peer = lax.rem(me + k, n_blk)
        copy = pltpu.make_async_remote_copy(
            src_ref=part_ref.at[pl.ds(pl.multiple_of(chunk_of(peer, n_blk) * rows, rows), rows)],
            dst_ref=recv.at[me],
            send_sem=send_sem.at[peer],
            recv_sem=recv_sem.at[me],
            device_id=(req, peer),
            device_id_type=MESH_IDS,
        )
        copy.start()
        copies.append(copy)
    own = pl.ds(pl.multiple_of(chunk_of(me, n_blk) * rows, rows), rows)
    total = part_ref[own, :].astype(jnp.float32)
    for k in range(1, n_blk):
        src = lax.rem(me + n_blk - k, n_blk)
        incoming = pltpu.make_async_remote_copy(
            src_ref=part_ref.at[pl.ds(0, rows)],
            dst_ref=recv.at[src],
            send_sem=send_sem.at[src],
            recv_sem=recv_sem.at[src],
            device_id=(req, src),
            device_id_type=MESH_IDS,
        )
        incoming.wait_recv()
        total = total + recv[src].astype(jnp.float32)
    for copy in copies:
        copy.wait_send()
    out_ref[...] = total


def gather_kernel(n_blk, piece_ref, out_ref, send_sem, recv_sem):
    b = lax.axis_index("blk")
    req = lax.axis_index("req")
    n_grp = n_blk // 2
    g = b // 2
    c = lax.rem(b, 2)
    partner = g * 2 + 1 - c
    rows = piece_ref.shape[0]
    half = n_grp * rows
    barrier = pltpu.get_barrier_semaphore()
    for k in range(1, n_grp):
        peer = lax.rem(g + k, n_grp) * 2 + c
        pl.semaphore_signal(barrier, inc=1, device_id=(req, peer), device_id_type=MESH_IDS)
    pl.semaphore_signal(barrier, inc=1, device_id=(req, partner), device_id_type=MESH_IDS)
    pl.semaphore_wait(barrier, n_grp)
    mine = pl.ds(pl.multiple_of(c * half + g * rows, rows), rows)
    sends = []
    for k in range(1, n_grp):
        peer = lax.rem(g + k, n_grp) * 2 + c
        copy = pltpu.make_async_remote_copy(
            src_ref=piece_ref,
            dst_ref=out_ref.at[mine],
            send_sem=send_sem.at[k],
            recv_sem=recv_sem.at[g],
            device_id=(req, peer),
            device_id_type=MESH_IDS,
        )
        copy.start()
        sends.append(copy)
    copy = pltpu.make_async_remote_copy(
        src_ref=piece_ref,
        dst_ref=out_ref.at[mine],
        send_sem=send_sem.at[0],
        recv_sem=recv_sem.at[n_grp + g],
        device_id=(req, partner),
        device_id_type=MESH_IDS,
    )
    copy.start()
    sends.append(copy)
    out_ref[mine, :] = piece_ref[...]
    for k in range(1, n_grp):
        grp = lax.rem(g + n_grp - k, n_grp)
        there = pl.ds(pl.multiple_of(c * half + grp * rows, rows), rows)
        incoming = pltpu.make_async_remote_copy(
            src_ref=piece_ref,
            dst_ref=out_ref.at[there],
            send_sem=send_sem.at[0],
            recv_sem=recv_sem.at[grp],
            device_id=(req, grp * 2 + c),
            device_id_type=MESH_IDS,
        )
        incoming.wait_recv()
        forward = pltpu.make_async_remote_copy(
            src_ref=out_ref.at[there],
            dst_ref=out_ref.at[there],
            send_sem=send_sem.at[n_grp + k],
            recv_sem=recv_sem.at[n_grp + grp],
            device_id=(req, partner),
            device_id_type=MESH_IDS,
        )
        forward.start()
        sends.append(forward)
    for grp in range(n_grp):
        there = pl.ds(pl.multiple_of((1 - c) * half + grp * rows, rows), rows)
        incoming = pltpu.make_async_remote_copy(
            src_ref=piece_ref,
            dst_ref=out_ref.at[there],
            send_sem=send_sem.at[0],
            recv_sem=recv_sem.at[n_grp + grp],
            device_id=(req, partner),
            device_id_type=MESH_IDS,
        )
        incoming.wait_recv()
    for copy in sends:
        copy.wait_send()


def blk_scatter(part):
    n_blk = lax.axis_size("blk")
    rows = part.shape[0] // n_blk
    vmem = pl.BlockSpec(memory_space=pltpu.VMEM)
    return pl.pallas_call(
        functools.partial(scatter_kernel, n_blk),
        out_shape=jax.ShapeDtypeStruct((rows, part.shape[1]), jnp.float32),
        in_specs=[vmem],
        out_specs=vmem,
        scratch_shapes=[
            pltpu.VMEM((n_blk, rows, part.shape[1]), part.dtype),
            pltpu.SemaphoreType.DMA((n_blk,)),
            pltpu.SemaphoreType.DMA((n_blk,)),
        ],
        compiler_params=pltpu.CompilerParams(collective_id=1, has_side_effects=True),
    )(part)


def blk_gather(piece):
    n_blk = lax.axis_size("blk")
    rows = piece.shape[0]
    vmem = pl.BlockSpec(memory_space=pltpu.VMEM)
    return pl.pallas_call(
        functools.partial(gather_kernel, n_blk),
        out_shape=jax.ShapeDtypeStruct((rows * n_blk, piece.shape[1]), piece.dtype),
        in_specs=[vmem],
        out_specs=vmem,
        scratch_shapes=[
            pltpu.SemaphoreType.DMA((n_blk,)),
            pltpu.SemaphoreType.DMA((n_blk,)),
        ],
        compiler_params=pltpu.CompilerParams(collective_id=2, has_side_effects=True),
    )(piece)


def prologue_kernel(n_req, n_blk, ordered_ref, packed_ref, cache_ref, wts_ref, w_send, w_recv, c_send, c_recv, local_sem):
    r = lax.axis_index("req")
    b = lax.axis_index("blk")
    n_slot, span, width = ordered_ref.shape
    piece = width // 2
    copies = []
    for k in range(1, n_req):
        peer = lax.rem(r + k, n_req)
        copy = pltpu.make_async_remote_copy(
            src_ref=packed_ref,
            dst_ref=wts_ref.at[r],
            send_sem=w_send.at[peer],
            recv_sem=w_recv.at[r],
            device_id=(peer, b),
            device_id_type=MESH_IDS,
        )
        copy.start()
        copies.append(copy)
    rows = pl.ds(pl.multiple_of(b * span, span), span)
    for k in range(n_slot):
        s = lax.rem(b + k, n_slot)
        for hh in range(2):
            head = 2 * r + hh
            is_self = jnp.logical_and(r == s, head == b)
            src = ordered_ref.at[s, :, pl.ds(hh * piece, piece)]
            copy = pltpu.make_async_remote_copy(
                src_ref=src,
                dst_ref=cache_ref.at[rows],
                send_sem=c_send.at[k * 2 + hh],
                recv_sem=c_recv.at[b],
                device_id=(s, head),
                device_id_type=MESH_IDS,
            )

            @pl.when(jnp.logical_not(is_self))
            def _():
                copy.start()

            @pl.when(is_self)
            def _():
                local = pltpu.make_async_copy(src, cache_ref.at[rows], local_sem.at[0])
                local.start()
                local.wait()

            copies.append((copy, is_self))
    wts_ref[r] = packed_ref[...]
    for k in range(1, n_req):
        src_req = lax.rem(r + n_req - k, n_req)
        incoming = pltpu.make_async_remote_copy(
            src_ref=packed_ref,
            dst_ref=wts_ref.at[src_req],
            send_sem=w_send.at[src_req],
            recv_sem=w_recv.at[src_req],
            device_id=(src_req, b),
            device_id_type=MESH_IDS,
        )
        incoming.wait_recv()
    owner = b // 2
    for j in range(n_blk):
        incoming = pltpu.make_async_remote_copy(
            src_ref=ordered_ref.at[0, :, pl.ds(0, piece)],
            dst_ref=cache_ref.at[pl.ds(j * span, span)],
            send_sem=c_send.at[0],
            recv_sem=c_recv.at[j],
            device_id=(owner, j),
            device_id_type=MESH_IDS,
        )

        @pl.when(jnp.logical_not(jnp.logical_and(owner == r, j == b)))
        def _():
            incoming.wait_recv()

    for item in copies:
        if isinstance(item, tuple):
            copy, is_self = item

            @pl.when(jnp.logical_not(is_self))
            def _():
                copy.wait_send()

        else:
            item.wait_send()


def prologue(ordered, packed):
    n_req = lax.axis_size("req")
    n_blk = lax.axis_size("blk")
    n_slot, span, width = ordered.shape
    any_spec = pl.BlockSpec(memory_space=pl.ANY)
    vmem = pl.BlockSpec(memory_space=pltpu.VMEM)
    return pl.pallas_call(
        functools.partial(prologue_kernel, n_req, n_blk),
        out_shape=(
            jax.ShapeDtypeStruct((span * n_blk, width // 2), ordered.dtype),
            jax.ShapeDtypeStruct((n_req,) + packed.shape, packed.dtype),
        ),
        in_specs=[any_spec, vmem],
        out_specs=(any_spec, vmem),
        scratch_shapes=[
            pltpu.SemaphoreType.DMA((n_req,)),
            pltpu.SemaphoreType.DMA((n_req,)),
            pltpu.SemaphoreType.DMA((2 * n_slot,)),
            pltpu.SemaphoreType.DMA((n_blk,)),
            pltpu.SemaphoreType.DMA((1,)),
        ],
        compiler_params=pltpu.CompilerParams(has_side_effects=True),
    )(ordered, packed)


def unpack(whole, pieces):
    n_req = whole.shape[0]
    whole = whole.reshape(n_req, -1)
    out, at = [], 0
    for w, axis in pieces:
        size = w.size
        part = whole[:, at : at + size].reshape((n_req,) + w.shape)
        at += size
        part = jnp.moveaxis(part, 0, axis)
        shape = list(w.shape)
        shape[axis] *= n_req
        out.append(part.reshape(shape))
    return out


def per_device(
    new_states,
    encoder_out,
    cache_in,
    slot_order,
    new_lengths,
    cache_lengths,
    enc_lengths,
    bucket_of,
    rel_bias,
    norm_gain,
    self_q,
    self_kv,
    self_out,
    cross_q,
    cross_kv,
    cross_out,
    ff_in,
    ff_out,
):
    blk_count = lax.axis_size("blk")
    heads_dev = H // blk_count
    width_dev = heads_dev * HD
    req_dev = cache_in.shape[0] // lax.axis_size("req")
    own_slots = lax.dynamic_slice_in_dim(slot_order, lax.axis_index("req") * req_dev, req_dev, 0)
    slot_new = pick_lengths(new_lengths, own_slots)
    slot_old = pick_lengths(cache_lengths, own_slots)
    slot_enc = pick_lengths(enc_lengths, own_slots)
    ordered = jnp.take(cache_in, slot_order, axis=0)
    onehot = (bucket_of[:, None] == jnp.arange(rel_bias.shape[0], dtype=jnp.int32)[None, :]).astype(
        jnp.float32
    )
    own_bias = lax.dynamic_slice_in_dim(rel_bias, lax.axis_index("blk") * heads_dev, heads_dev, 1)
    bias_dist = jnp.dot(onehot, own_bias, precision=lax.Precision.HIGHEST).T
    early = [(self_q, 0), (self_kv, 0), (self_out, 1)]
    late = [(cross_q, 0), (cross_kv, 0), (cross_out, 1), (ff_in, 0), (ff_out, 1)]
    flat = jnp.concatenate([w.reshape(-1) for w, _ in early])
    cache_blk, whole = prologue(ordered, flat.reshape(-1, 128))
    cache_dec = cache_blk[None]
    gathered = unpack(whole, early)
    late_gathered = pack_gather(late)
    wq_self, wkv_self, wo_self = gathered
    n_blk = lax.axis_size("blk")
    rows_dev = new_states.shape[0] // n_blk
    own_rows = lax.dynamic_slice_in_dim(
        new_states, chunk_of(lax.axis_index("blk"), n_blk) * rows_dev, rows_dev, 0
    ).astype(jnp.float32)
    normed = rms_rows(new_states.astype(jnp.float32), norm_gain[0])
    self_cat = jnp.concatenate([wq_self, wkv_self.reshape(wkv_self.shape[0], -1)], axis=1)
    projected = jnp.dot(normed, self_cat, preferred_element_type=jnp.float32).astype(
        jnp.bfloat16
    )
    context = self_attention(
        projected[:, :HD],
        cache_dec[0],
        projected[:, HD : 2 * HD],
        projected[:, 2 * HD :],
        bias_dist[0],
        slot_old[0],
        slot_new[0],
    )
    part = jnp.dot(context, wo_self, preferred_element_type=jnp.float32).astype(jnp.bfloat16)
    residual, normed = blk_stage(part, own_rows, norm_gain[1], False)
    wq_cross, wkv_cross, wo_cross, w_in, w_out = late_gathered
    queries = (
        jnp.dot(normed, wq_cross, preferred_element_type=jnp.float32)
        .astype(jnp.bfloat16)
        .reshape(req_dev, -1, heads_dev, HD)
    )
    cross_pair = wkv_cross.reshape(wkv_cross.shape[0], -1)
    key_value = (
        jnp.dot(encoder_out, cross_pair, preferred_element_type=jnp.float32)
        .astype(jnp.bfloat16)
        .reshape(req_dev, -1, 2, heads_dev, HD)
    )
    context = cross_attend(queries, key_value, slot_enc)
    part = jnp.dot(context.reshape(-1, width_dev), wo_cross, preferred_element_type=jnp.float32)
    residual, normed = blk_stage(part.astype(jnp.bfloat16), residual, norm_gain[2], False)
    ff_dev = w_in.shape[2]
    gate_up = jnp.dot(normed, w_in.reshape(w_in.shape[0], -1), preferred_element_type=jnp.float32)
    hidden = (jax.nn.gelu(gate_up[:, :ff_dev], approximate=True) * gate_up[:, ff_dev:]).astype(
        jnp.bfloat16
    )
    part = jnp.dot(hidden, w_out, preferred_element_type=jnp.float32).astype(jnp.bfloat16)
    _, layer_out = blk_stage(part, residual, norm_gain[2], True)
    return (layer_out, cache_dec)


def solution(mesh):
    in_specs = (
        P("req", None),
        P("req", None),
        P(None, "blk", "req"),
        P(),
        P(),
        P(),
        P(),
        P(),
        P(),
        P(),
        P("req", "blk"),
        P("req", None, "blk"),
        P("blk", "req"),
        P("req", "blk"),
        P("req", None, "blk"),
        P("blk", "req"),
        P("req", None, "blk"),
        P("blk", "req"),
    )
    out_specs = (P("req", None), P("req", None, "blk"))
    return jax.shard_map(
        per_device, mesh=mesh, in_specs=in_specs, out_specs=out_specs, check_vma=False
    )
```

```python
import functools

import jax
import jax.numpy as jnp
from jax import lax
from jax.sharding import PartitionSpec as P
from jax.experimental import pallas as pl
from jax.experimental.pallas import tpu as pltpu

H = 16
HD = 64


EPSILON = 1e-06
NEG_FILL = -1e30


def rms_rows(row_block, gain):
    mean_square = jnp.mean(row_block * row_block, axis=-1, keepdims=True)
    return (row_block * lax.rsqrt(mean_square + EPSILON) * gain).astype(jnp.bfloat16)


def softmax_rows(scores):
    row_top = jnp.max(scores, axis=-1, keepdims=True)
    weights = jnp.exp(scores - row_top)
    return (weights / jnp.sum(weights, axis=-1, keepdims=True)).astype(jnp.bfloat16)


def pick_lengths(table, own_slots):
    matches = own_slots[:, None] == jnp.arange(table.shape[0], dtype=jnp.int32)[None, :]
    return jnp.sum(jnp.where(matches, table[None, :], 0), axis=1)


def shifted_bias(bias_dist, base, row_count, col_count):
    heads_here, span_len = bias_dist.shape
    line_len = row_count + col_count - 1
    steps = jnp.arange(line_len + 1, dtype=jnp.int32)
    line = bias_dist[:, jnp.clip(base + row_count - 1 - steps, 0, span_len - 1)]
    tiled = jnp.broadcast_to(line[:, None, :], (heads_here, row_count, line_len + 1))
    flat = tiled.reshape(heads_here, row_count * (line_len + 1))[:, : row_count * line_len]
    skewed = flat.reshape(heads_here, row_count, line_len)
    return skewed[:, :, row_count - 1 : row_count - 1 + col_count]


def row_total(left, weight):
    term = jnp.dot(left, weight, preferred_element_type=jnp.float32)
    return lax.psum(term.astype(jnp.bfloat16), "blk").astype(jnp.float32)


def cached_scores(queries, key_rows, first_col, old_len, bias_dist):
    col_ids = first_col + jnp.arange(key_rows.shape[0], dtype=jnp.int32)[None, :]
    scores = jnp.einsum("qhe,khe->hqk", queries, key_rows, preferred_element_type=jnp.float32)
    scores = scores + shifted_bias(
        bias_dist, old_len - first_col, queries.shape[0], key_rows.shape[0]
    )
    return jnp.where((col_ids < old_len)[None], scores, NEG_FILL)


def fresh_scores(queries, fresh_keys, fresh_len, bias_dist):
    row_ids = jnp.arange(queries.shape[0], dtype=jnp.int32)[:, None]
    col_ids = jnp.arange(fresh_keys.shape[0], dtype=jnp.int32)[None, :]
    scores = jnp.einsum("qhe,khe->hqk", queries, fresh_keys, preferred_element_type=jnp.float32)
    scores = scores + shifted_bias(bias_dist, 0, queries.shape[0], fresh_keys.shape[0])
    admitted = (col_ids <= row_ids) & (col_ids < fresh_len)
    return jnp.where(admitted[None], scores, NEG_FILL)


def self_padded(
    queries, key_rows, value_rows, fresh_keys, fresh_values, old_len, fresh_len, bias_dist
):
    scores = jnp.concatenate(
        [
            cached_scores(queries, key_rows, 0, old_len, bias_dist),
            fresh_scores(queries, fresh_keys, fresh_len, bias_dist),
        ],
        axis=2,
    )
    weights = softmax_rows(scores)
    value_all = jnp.concatenate([value_rows, fresh_values], axis=0)
    return jnp.einsum(
        "hqk,khe->qhe", weights, value_all, preferred_element_type=jnp.float32
    ).astype(jnp.bfloat16)


def self_attend(queries, key_value, cache_dec, slot_old, slot_new, bias_dist, heads_dev):
    req_dev, cache_len = (cache_dec.shape[0], cache_dec.shape[1])
    cache_split = cache_dec.reshape(req_dev, cache_len, heads_dev, 2, -1)

    def one_request(request):
        queries_one, pair_one, cache_one, old_len, fresh_len = request
        return self_padded(
            queries_one,
            cache_one[:, :, 0],
            cache_one[:, :, 1],
            pair_one[:, 0],
            pair_one[:, 1],
            old_len,
            fresh_len,
            bias_dist,
        )

    return lax.map(one_request, (queries, key_value, cache_split, slot_old, slot_new))


def cross_attend(queries, key_value, slot_enc):
    scores = jnp.einsum(
        "rqhe,rkhe->rhqk", queries, key_value[:, :, 0], preferred_element_type=jnp.float32
    )
    col_ids = jnp.arange(key_value.shape[1], dtype=jnp.int32)
    scores = jnp.where(
        col_ids[None, None, None, :] < slot_enc[:, None, None, None], scores, NEG_FILL
    )
    weights = softmax_rows(scores)
    return jnp.einsum(
        "rhqk,rkhe->rqhe", weights, key_value[:, :, 1], preferred_element_type=jnp.float32
    ).astype(jnp.bfloat16)


def add_branch(residual, left, weight, gain):
    residual = residual + row_total(left, weight)
    normed = rms_rows(residual, gain)
    return (residual, normed)


TQ = 128


def stage_kernel(n_blk, final, extra, *refs):
    if extra:
        (part_ref, resid_ref, gain_ref, packed_ref, res_out, full_ref, wts_ref,
         recv_a, send_b, recv_b, x_send, x_recv, b_send, b_recv, ag_send, ag_recv, w_send, w_recv) = refs
    else:
        (part_ref, resid_ref, gain_ref, res_out, full_ref,
         recv_a, send_b, recv_b, x_send, x_recv, b_send, b_recv, ag_send, ag_recv) = refs
    me = lax.axis_index("blk")
    req = lax.axis_index("req")
    rows = resid_ref.shape[0]
    n_grp = n_blk // 2
    g = me // 2
    c = lax.rem(me, 2)
    partner = g * 2 + 1 - c
    half = n_grp * rows
    n_req = wts_ref.shape[0] if extra else 1
    barrier = pltpu.get_barrier_semaphore()
    for k in range(1, n_grp):
        peer = lax.rem(g + k, n_grp) * 2 + c
        pl.semaphore_signal(barrier, inc=1, device_id=(req, peer), device_id_type=MESH_IDS)
    pl.semaphore_signal(barrier, inc=1, device_id=(req, partner), device_id_type=MESH_IDS)
    for k in range(1, n_req):
        peer = lax.rem(req + k, n_req)
        pl.semaphore_signal(barrier, inc=1, device_id=(peer, me), device_id_type=MESH_IDS)
    pl.semaphore_wait(barrier, n_grp + n_req - 1)
    sends = []
    for k in range(n_grp):
        grp = lax.rem(g + 1 + k, n_grp)
        exchange = pltpu.make_async_remote_copy(
            src_ref=part_ref.at[pl.ds(pl.multiple_of((1 - c) * half + grp * rows, rows), rows)],
            dst_ref=recv_a.at[grp],
            send_sem=x_send.at[k],
            recv_sem=x_recv.at[grp],
            device_id=(req, partner),
            device_id_type=MESH_IDS,
        )
        exchange.start()
        sends.append(exchange)
    for k in range(1, n_req):
        peer = lax.rem(req + k, n_req)
        copy = pltpu.make_async_remote_copy(
            src_ref=packed_ref,
            dst_ref=wts_ref.at[req],
            send_sem=w_send.at[peer],
            recv_sem=w_recv.at[req],
            device_id=(peer, me),
            device_id_type=MESH_IDS,
        )
        copy.start()
        sends.append(copy)
    total = None
    for k in range(n_grp):
        grp = lax.rem(g + 1 + k, n_grp)
        incoming = pltpu.make_async_remote_copy(
            src_ref=part_ref.at[pl.ds(0, rows)],
            dst_ref=recv_a.at[grp],
            send_sem=x_send.at[k],
            recv_sem=x_recv.at[grp],
            device_id=(req, partner),
            device_id_type=MESH_IDS,
        )
        incoming.wait_recv()
        pair = part_ref[pl.ds(pl.multiple_of(c * half + grp * rows, rows), rows), :].astype(
            jnp.float32
        ) + recv_a[grp].astype(jnp.float32)
        if k == n_grp - 1:
            total = pair
        else:
            send_b[grp] = pair.astype(send_b.dtype)
            copy = pltpu.make_async_remote_copy(
                src_ref=send_b.at[grp],
                dst_ref=recv_b.at[g],
                send_sem=b_send.at[grp],
                recv_sem=b_recv.at[g],
                device_id=(req, grp * 2 + c),
                device_id_type=MESH_IDS,
            )
            copy.start()
            sends.append(copy)
    for k in range(1, n_grp):
        grp = lax.rem(g + n_grp - k, n_grp)
        incoming = pltpu.make_async_remote_copy(
            src_ref=send_b.at[0],
            dst_ref=recv_b.at[grp],
            send_sem=b_send.at[grp],
            recv_sem=b_recv.at[grp],
            device_id=(req, grp * 2 + c),
            device_id_type=MESH_IDS,
        )
        incoming.wait_recv()
        total = total + recv_b[grp].astype(jnp.float32)
    mine = pl.ds(pl.multiple_of(c * half + g * rows, rows), rows)
    resid = resid_ref[...] + total
    res_out[...] = resid
    if final:
        full_ref[mine, :] = resid.astype(full_ref.dtype)
    else:
        mean_square = jnp.mean(resid * resid, axis=-1, keepdims=True)
        full_ref[mine, :] = (resid * lax.rsqrt(mean_square + EPSILON) * gain_ref[...]).astype(
            full_ref.dtype
        )
    for k in range(1, n_grp):
        peer = lax.rem(g + k, n_grp) * 2 + c
        copy = pltpu.make_async_remote_copy(
            src_ref=full_ref.at[mine],
            dst_ref=full_ref.at[mine],
            send_sem=ag_send.at[k],
            recv_sem=ag_recv.at[g],
            device_id=(req, peer),
            device_id_type=MESH_IDS,
        )
        copy.start()
        sends.append(copy)
    copy = pltpu.make_async_remote_copy(
        src_ref=full_ref.at[mine],
        dst_ref=full_ref.at[mine],
        send_sem=ag_send.at[0],
        recv_sem=ag_recv.at[n_grp + g],
        device_id=(req, partner),
        device_id_type=MESH_IDS,
    )
    copy.start()
    sends.append(copy)
    for k in range(1, n_grp):
        grp = lax.rem(g + n_grp - k, n_grp)
        there = pl.ds(pl.multiple_of(c * half + grp * rows, rows), rows)
        incoming = pltpu.make_async_remote_copy(
            src_ref=full_ref.at[there],
            dst_ref=full_ref.at[there],
            send_sem=ag_send.at[0],
            recv_sem=ag_recv.at[grp],
            device_id=(req, grp * 2 + c),
            device_id_type=MESH_IDS,
        )
        incoming.wait_recv()
        forward = pltpu.make_async_remote_copy(
            src_ref=full_ref.at[there],
            dst_ref=full_ref.at[there],
            send_sem=ag_send.at[n_grp + k],
            recv_sem=ag_recv.at[n_grp + grp],
            device_id=(req, partner),
            device_id_type=MESH_IDS,
        )
        forward.start()
        sends.append(forward)
    for grp in range(n_grp):
        there = pl.ds(pl.multiple_of((1 - c) * half + grp * rows, rows), rows)
        incoming = pltpu.make_async_remote_copy(
            src_ref=full_ref.at[there],
            dst_ref=full_ref.at[there],
            send_sem=ag_send.at[0],
            recv_sem=ag_recv.at[n_grp + grp],
            device_id=(req, partner),
            device_id_type=MESH_IDS,
        )
        incoming.wait_recv()
    if extra:
        wts_ref[req] = packed_ref[...]
        for k in range(1, n_req):
            src = lax.rem(req + n_req - k, n_req)
            incoming = pltpu.make_async_remote_copy(
                src_ref=packed_ref,
                dst_ref=wts_ref.at[src],
                send_sem=w_send.at[src],
                recv_sem=w_recv.at[src],
                device_id=(src, me),
                device_id_type=MESH_IDS,
            )
            incoming.wait_recv()
    for copy in sends:
        copy.wait_send()


def blk_stage(part, resid, gain, final, packed=None):
    n_blk = lax.axis_size("blk")
    rows, width = resid.shape
    vmem = pl.BlockSpec(memory_space=pltpu.VMEM)
    extra = packed is not None
    outs = [
        jax.ShapeDtypeStruct((rows, width), jnp.float32),
        jax.ShapeDtypeStruct((rows * n_blk, width), jnp.bfloat16),
    ]
    n_grp = n_blk // 2
    scratch = [
        pltpu.VMEM((n_grp, rows, width), part.dtype),
        pltpu.VMEM((n_grp, rows, width), part.dtype),
        pltpu.VMEM((n_grp, rows, width), part.dtype),
        pltpu.SemaphoreType.DMA((n_grp,)),
        pltpu.SemaphoreType.DMA((n_grp,)),
        pltpu.SemaphoreType.DMA((n_grp,)),
        pltpu.SemaphoreType.DMA((n_grp,)),
        pltpu.SemaphoreType.DMA((n_blk,)),
        pltpu.SemaphoreType.DMA((n_blk,)),
    ]
    args = [part, resid, gain[None, :]]
    if extra:
        n_req = lax.axis_size("req")
        outs.append(jax.ShapeDtypeStruct((n_req,) + packed.shape, packed.dtype))
        scratch += [pltpu.SemaphoreType.DMA((n_req,)), pltpu.SemaphoreType.DMA((n_req,))]
        args.append(packed)
    return pl.pallas_call(
        functools.partial(stage_kernel, n_blk, final, extra),
        out_shape=tuple(outs),
        in_specs=[vmem] * len(args),
        out_specs=tuple([vmem] * len(outs)),
        scratch_shapes=scratch,
        compiler_params=pltpu.CompilerParams(
            collective_id=5 if extra else (4 if final else 3), has_side_effects=True
        ),
    )(*args)


def self_kernel(lens_ref, q_ref, c_ref, kn_ref, vn_ref, g_ref, f_ref, o_ref):
    old_len = lens_ref[0]
    fresh_len = lens_ref[1]
    n_q = q_ref.shape[0]
    n_ctx = c_ref.shape[0]
    wide_old = n_ctx + TQ
    wide_new = n_q + TQ
    k_old = c_ref[:, :HD]
    v_old = c_ref[:, HD:]
    k_new = kn_ref[...]
    v_new = vn_ref[...]
    dims = (((1,), (1,)), ((), ()))
    for t in range(n_q // TQ):
        q = q_ref[t * TQ : (t + 1) * TQ, :]
        start = n_q - TQ - t * TQ
        s_old = lax.dot_general(q, k_old, dims, preferred_element_type=jnp.float32)
        line = jnp.broadcast_to(g_ref[:, start : start + wide_old], (TQ, wide_old))
        bias = pltpu.roll(line, wide_old - (TQ - 1), 1, stride=1, stride_axis=0)[:, :n_ctx]
        col = lax.broadcasted_iota(jnp.int32, (TQ, n_ctx), 1)
        s_old = jnp.where(col < old_len, s_old + bias, NEG_FILL)
        s_new = lax.dot_general(q, k_new, dims, preferred_element_type=jnp.float32)
        line = jnp.broadcast_to(f_ref[:, start : start + wide_new], (TQ, wide_new))
        bias = pltpu.roll(line, wide_new - (TQ - 1), 1, stride=1, stride_axis=0)[:, :n_q]
        row = lax.broadcasted_iota(jnp.int32, (TQ, n_q), 0) + t * TQ
        col = lax.broadcasted_iota(jnp.int32, (TQ, n_q), 1)
        s_new = jnp.where((col <= row) & (col < fresh_len), s_new + bias, NEG_FILL)
        top = jnp.maximum(
            jnp.max(s_old, axis=1, keepdims=True), jnp.max(s_new, axis=1, keepdims=True)
        )
        p_old = jnp.exp(s_old - top)
        p_new = jnp.exp(s_new - top)
        total = jnp.sum(p_old, axis=1, keepdims=True) + jnp.sum(p_new, axis=1, keepdims=True)
        w_old = (p_old / total).astype(jnp.bfloat16)
        w_new = (p_new / total).astype(jnp.bfloat16)
        out = jnp.dot(w_old, v_old, preferred_element_type=jnp.float32) + jnp.dot(
            w_new, v_new, preferred_element_type=jnp.float32
        )
        o_ref[t * TQ : (t + 1) * TQ, :] = out.astype(jnp.bfloat16)


def bias_lines(line, old_len, n_q, n_ctx):
    span = line.shape[0]
    ext = jnp.concatenate([jnp.broadcast_to(line[:1], (n_ctx,)), line])
    rev = ext[::-1]
    g = lax.dynamic_slice_in_dim(rev, n_ctx - old_len, span)
    f = rev[n_ctx : n_ctx + 2 * n_q]
    return g[None, :], f[None, :]


def self_attention(q, cache_blk, k_new, v_new, line, old_len, fresh_len):
    n_q = q.shape[0]
    n_ctx = cache_blk.shape[0]
    g, f = bias_lines(line, old_len, n_q, n_ctx)
    lens = jnp.stack([old_len, fresh_len]).astype(jnp.int32)
    vmem = pl.BlockSpec(memory_space=pltpu.VMEM)
    return pl.pallas_call(
        self_kernel,
        out_shape=jax.ShapeDtypeStruct((n_q, HD), jnp.bfloat16),
        in_specs=[pl.BlockSpec(memory_space=pltpu.SMEM)] + [vmem] * 6,
        out_specs=vmem,
        compiler_params=pltpu.CompilerParams(vmem_limit_bytes=48 * 1024 * 1024),
    )(lens, q, cache_blk, k_new, v_new, g, f)


def pack_gather(pieces):
    flat = jnp.concatenate([w.reshape(-1) for w, _ in pieces])
    whole = lax.all_gather(flat, "req", axis=0, tiled=False)
    n_req = whole.shape[0]
    out, at = [], 0
    for w, axis in pieces:
        size = w.size
        part = whole[:, at : at + size].reshape((n_req,) + w.shape)
        at += size
        part = jnp.moveaxis(part, 0, axis)
        shape = list(w.shape)
        shape[axis] *= n_req
        out.append(part.reshape(shape))
    return out


MESH_IDS = pl.DeviceIdType.MESH


def greet_all(n_blk, me, req):
    barrier = pltpu.get_barrier_semaphore()
    for k in range(1, n_blk):
        peer = lax.rem(me + k, n_blk)
        pl.semaphore_signal(barrier, inc=1, device_id=(req, peer), device_id_type=MESH_IDS)
    pl.semaphore_wait(barrier, n_blk - 1)


def chunk_of(b, n_blk):
    return lax.rem(b, 2) * (n_blk // 2) + b // 2


def scatter_kernel(n_blk, part_ref, out_ref, recv, send_sem, recv_sem):
    me = lax.axis_index("blk")
    req = lax.axis_index("req")
    rows = out_ref.shape[0]
    greet_all(n_blk, me, req)
    copies = []
    for k in range(1, n_blk):
        peer = lax.rem(me + k, n_blk)
        copy = pltpu.make_async_remote_copy(
            src_ref=part_ref.at[pl.ds(pl.multiple_of(chunk_of(peer, n_blk) * rows, rows), rows)],
            dst_ref=recv.at[me],
            send_sem=send_sem.at[peer],
            recv_sem=recv_sem.at[me],
            device_id=(req, peer),
            device_id_type=MESH_IDS,
        )
        copy.start()
        copies.append(copy)
    own = pl.ds(pl.multiple_of(chunk_of(me, n_blk) * rows, rows), rows)
    total = part_ref[own, :].astype(jnp.float32)
    for k in range(1, n_blk):
        src = lax.rem(me + n_blk - k, n_blk)
        incoming = pltpu.make_async_remote_copy(
            src_ref=part_ref.at[pl.ds(0, rows)],
            dst_ref=recv.at[src],
            send_sem=send_sem.at[src],
            recv_sem=recv_sem.at[src],
            device_id=(req, src),
            device_id_type=MESH_IDS,
        )
        incoming.wait_recv()
        total = total + recv[src].astype(jnp.float32)
    for copy in copies:
        copy.wait_send()
    out_ref[...] = total


def gather_kernel(n_blk, piece_ref, out_ref, send_sem, recv_sem):
    b = lax.axis_index("blk")
    req = lax.axis_index("req")
    n_grp = n_blk // 2
    g = b // 2
    c = lax.rem(b, 2)
    partner = g * 2 + 1 - c
    rows = piece_ref.shape[0]
    half = n_grp * rows
    barrier = pltpu.get_barrier_semaphore()
    for k in range(1, n_grp):
        peer = lax.rem(g + k, n_grp) * 2 + c
        pl.semaphore_signal(barrier, inc=1, device_id=(req, peer), device_id_type=MESH_IDS)
    pl.semaphore_signal(barrier, inc=1, device_id=(req, partner), device_id_type=MESH_IDS)
    pl.semaphore_wait(barrier, n_grp)
    mine = pl.ds(pl.multiple_of(c * half + g * rows, rows), rows)
    sends = []
    for k in range(1, n_grp):
        peer = lax.rem(g + k, n_grp) * 2 + c
        copy = pltpu.make_async_remote_copy(
            src_ref=piece_ref,
            dst_ref=out_ref.at[mine],
            send_sem=send_sem.at[k],
            recv_sem=recv_sem.at[g],
            device_id=(req, peer),
            device_id_type=MESH_IDS,
        )
        copy.start()
        sends.append(copy)
    copy = pltpu.make_async_remote_copy(
        src_ref=piece_ref,
        dst_ref=out_ref.at[mine],
        send_sem=send_sem.at[0],
        recv_sem=recv_sem.at[n_grp + g],
        device_id=(req, partner),
        device_id_type=MESH_IDS,
    )
    copy.start()
    sends.append(copy)
    out_ref[mine, :] = piece_ref[...]
    for k in range(1, n_grp):
        grp = lax.rem(g + n_grp - k, n_grp)
        there = pl.ds(pl.multiple_of(c * half + grp * rows, rows), rows)
        incoming = pltpu.make_async_remote_copy(
            src_ref=piece_ref,
            dst_ref=out_ref.at[there],
            send_sem=send_sem.at[0],
            recv_sem=recv_sem.at[grp],
            device_id=(req, grp * 2 + c),
            device_id_type=MESH_IDS,
        )
        incoming.wait_recv()
        forward = pltpu.make_async_remote_copy(
            src_ref=out_ref.at[there],
            dst_ref=out_ref.at[there],
            send_sem=send_sem.at[n_grp + k],
            recv_sem=recv_sem.at[n_grp + grp],
            device_id=(req, partner),
            device_id_type=MESH_IDS,
        )
        forward.start()
        sends.append(forward)
    for grp in range(n_grp):
        there = pl.ds(pl.multiple_of((1 - c) * half + grp * rows, rows), rows)
        incoming = pltpu.make_async_remote_copy(
            src_ref=piece_ref,
            dst_ref=out_ref.at[there],
            send_sem=send_sem.at[0],
            recv_sem=recv_sem.at[n_grp + grp],
            device_id=(req, partner),
            device_id_type=MESH_IDS,
        )
        incoming.wait_recv()
    for copy in sends:
        copy.wait_send()


def blk_scatter(part):
    n_blk = lax.axis_size("blk")
    rows = part.shape[0] // n_blk
    vmem = pl.BlockSpec(memory_space=pltpu.VMEM)
    return pl.pallas_call(
        functools.partial(scatter_kernel, n_blk),
        out_shape=jax.ShapeDtypeStruct((rows, part.shape[1]), jnp.float32),
        in_specs=[vmem],
        out_specs=vmem,
        scratch_shapes=[
            pltpu.VMEM((n_blk, rows, part.shape[1]), part.dtype),
            pltpu.SemaphoreType.DMA((n_blk,)),
            pltpu.SemaphoreType.DMA((n_blk,)),
        ],
        compiler_params=pltpu.CompilerParams(collective_id=1, has_side_effects=True),
    )(part)


def blk_gather(piece):
    n_blk = lax.axis_size("blk")
    rows = piece.shape[0]
    vmem = pl.BlockSpec(memory_space=pltpu.VMEM)
    return pl.pallas_call(
        functools.partial(gather_kernel, n_blk),
        out_shape=jax.ShapeDtypeStruct((rows * n_blk, piece.shape[1]), piece.dtype),
        in_specs=[vmem],
        out_specs=vmem,
        scratch_shapes=[
            pltpu.SemaphoreType.DMA((n_blk,)),
            pltpu.SemaphoreType.DMA((n_blk,)),
        ],
        compiler_params=pltpu.CompilerParams(collective_id=2, has_side_effects=True),
    )(piece)


def prologue_kernel(n_req, n_blk, ordered_ref, packed_ref, cache_ref, wts_ref, w_send, w_recv, c_send, c_recv, local_sem):
    r = lax.axis_index("req")
    b = lax.axis_index("blk")
    n_slot, span, width = ordered_ref.shape
    piece = width // 2
    copies = []
    for k in range(1, n_req):
        peer = lax.rem(r + k, n_req)
        copy = pltpu.make_async_remote_copy(
            src_ref=packed_ref,
            dst_ref=wts_ref.at[r],
            send_sem=w_send.at[peer],
            recv_sem=w_recv.at[r],
            device_id=(peer, b),
            device_id_type=MESH_IDS,
        )
        copy.start()
        copies.append(copy)
    rows = pl.ds(pl.multiple_of(b * span, span), span)
    for k in range(n_slot):
        s = lax.rem(b + k, n_slot)
        for hh in range(2):
            head = 2 * r + hh
            is_self = jnp.logical_and(r == s, head == b)
            src = ordered_ref.at[s, :, pl.ds(hh * piece, piece)]
            copy = pltpu.make_async_remote_copy(
                src_ref=src,
                dst_ref=cache_ref.at[rows],
                send_sem=c_send.at[k * 2 + hh],
                recv_sem=c_recv.at[b],
                device_id=(s, head),
                device_id_type=MESH_IDS,
            )

            @pl.when(jnp.logical_not(is_self))
            def _():
                copy.start()

            @pl.when(is_self)
            def _():
                local = pltpu.make_async_copy(src, cache_ref.at[rows], local_sem.at[0])
                local.start()
                local.wait()

            copies.append((copy, is_self))
    wts_ref[r] = packed_ref[...]
    for k in range(1, n_req):
        src_req = lax.rem(r + n_req - k, n_req)
        incoming = pltpu.make_async_remote_copy(
            src_ref=packed_ref,
            dst_ref=wts_ref.at[src_req],
            send_sem=w_send.at[src_req],
            recv_sem=w_recv.at[src_req],
            device_id=(src_req, b),
            device_id_type=MESH_IDS,
        )
        incoming.wait_recv()
    owner = b // 2
    for j in range(n_blk):
        incoming = pltpu.make_async_remote_copy(
            src_ref=ordered_ref.at[0, :, pl.ds(0, piece)],
            dst_ref=cache_ref.at[pl.ds(j * span, span)],
            send_sem=c_send.at[0],
            recv_sem=c_recv.at[j],
            device_id=(owner, j),
            device_id_type=MESH_IDS,
        )

        @pl.when(jnp.logical_not(jnp.logical_and(owner == r, j == b)))
        def _():
            incoming.wait_recv()

    for item in copies:
        if isinstance(item, tuple):
            copy, is_self = item

            @pl.when(jnp.logical_not(is_self))
            def _():
                copy.wait_send()

        else:
            item.wait_send()


def prologue(ordered, packed):
    n_req = lax.axis_size("req")
    n_blk = lax.axis_size("blk")
    n_slot, span, width = ordered.shape
    any_spec = pl.BlockSpec(memory_space=pl.ANY)
    vmem = pl.BlockSpec(memory_space=pltpu.VMEM)
    return pl.pallas_call(
        functools.partial(prologue_kernel, n_req, n_blk),
        out_shape=(
            jax.ShapeDtypeStruct((span * n_blk, width // 2), ordered.dtype),
            jax.ShapeDtypeStruct((n_req,) + packed.shape, packed.dtype),
        ),
        in_specs=[any_spec, vmem],
        out_specs=(any_spec, vmem),
        scratch_shapes=[
            pltpu.SemaphoreType.DMA((n_req,)),
            pltpu.SemaphoreType.DMA((n_req,)),
            pltpu.SemaphoreType.DMA((2 * n_slot,)),
            pltpu.SemaphoreType.DMA((n_blk,)),
            pltpu.SemaphoreType.DMA((1,)),
        ],
        compiler_params=pltpu.CompilerParams(has_side_effects=True),
    )(ordered, packed)


def unpack(whole, pieces):
    n_req = whole.shape[0]
    whole = whole.reshape(n_req, -1)
    out, at = [], 0
    for w, axis in pieces:
        size = w.size
        part = whole[:, at : at + size].reshape((n_req,) + w.shape)
        at += size
        part = jnp.moveaxis(part, 0, axis)
        shape = list(w.shape)
        shape[axis] *= n_req
        out.append(part.reshape(shape))
    return out


def per_device(
    new_states,
    encoder_out,
    cache_in,
    slot_order,
    new_lengths,
    cache_lengths,
    enc_lengths,
    bucket_of,
    rel_bias,
    norm_gain,
    self_q,
    self_kv,
    self_out,
    cross_q,
    cross_kv,
    cross_out,
    ff_in,
    ff_out,
):
    blk_count = lax.axis_size("blk")
    heads_dev = H // blk_count
    width_dev = heads_dev * HD
    req_dev = cache_in.shape[0] // lax.axis_size("req")
    own_slots = lax.dynamic_slice_in_dim(slot_order, lax.axis_index("req") * req_dev, req_dev, 0)
    slot_new = pick_lengths(new_lengths, own_slots)
    slot_old = pick_lengths(cache_lengths, own_slots)
    slot_enc = pick_lengths(enc_lengths, own_slots)
    ordered = jnp.take(cache_in, slot_order, axis=0)
    onehot = (bucket_of[:, None] == jnp.arange(rel_bias.shape[0], dtype=jnp.int32)[None, :]).astype(
        jnp.float32
    )
    own_bias = lax.dynamic_slice_in_dim(rel_bias, lax.axis_index("blk") * heads_dev, heads_dev, 1)
    bias_dist = jnp.dot(onehot, own_bias, precision=lax.Precision.HIGHEST).T
    early = [(self_q, 0), (self_kv, 0), (self_out, 1)]
    late = [(cross_q, 0), (cross_kv, 0), (cross_out, 1), (ff_in, 0), (ff_out, 1)]
    flat = jnp.concatenate([w.reshape(-1) for w, _ in early])
    cache_blk, whole = prologue(ordered, flat.reshape(-1, 128))
    cache_dec = cache_blk[None]
    gathered = unpack(whole, early)
    late_gathered = pack_gather(late)
    wq_self, wkv_self, wo_self = gathered
    n_blk = lax.axis_size("blk")
    rows_dev = new_states.shape[0] // n_blk
    own_rows = lax.dynamic_slice_in_dim(
        new_states, chunk_of(lax.axis_index("blk"), n_blk) * rows_dev, rows_dev, 0
    ).astype(jnp.float32)
    normed = rms_rows(new_states.astype(jnp.float32), norm_gain[0])
    self_cat = jnp.concatenate([wq_self, wkv_self.reshape(wkv_self.shape[0], -1)], axis=1)
    projected = jnp.dot(normed, self_cat, preferred_element_type=jnp.float32).astype(
        jnp.bfloat16
    )
    context = self_attention(
        projected[:, :HD],
        cache_dec[0],
        projected[:, HD : 2 * HD],
        projected[:, 2 * HD :],
        bias_dist[0],
        slot_old[0],
        slot_new[0],
    )
    part = jnp.dot(context, wo_self, preferred_element_type=jnp.float32).astype(jnp.bfloat16)
    residual, normed = blk_stage(part, own_rows, norm_gain[1], False)
    wq_cross, wkv_cross, wo_cross, w_in, w_out = late_gathered
    queries = (
        jnp.dot(normed, wq_cross, preferred_element_type=jnp.float32)
        .astype(jnp.bfloat16)
        .reshape(req_dev, -1, heads_dev, HD)
    )
    cross_pair = wkv_cross.reshape(wkv_cross.shape[0], -1)
    key_value = (
        jnp.dot(encoder_out, cross_pair, preferred_element_type=jnp.float32)
        .astype(jnp.bfloat16)
        .reshape(req_dev, -1, 2, heads_dev, HD)
    )
    context = cross_attend(queries, key_value, slot_enc)
    part = jnp.dot(context.reshape(-1, width_dev), wo_cross, preferred_element_type=jnp.float32)
    residual, normed = blk_stage(part.astype(jnp.bfloat16), residual, norm_gain[2], False)
    ff_dev = w_in.shape[2]
    gate_up = jnp.dot(normed, w_in.reshape(w_in.shape[0], -1), preferred_element_type=jnp.float32)
    hidden = (jax.nn.gelu(gate_up[:, :ff_dev], approximate=True) * gate_up[:, ff_dev:]).astype(
        jnp.bfloat16
    )
    part = jnp.dot(hidden, w_out, preferred_element_type=jnp.float32).astype(jnp.bfloat16)
    _, layer_out = blk_stage(part, residual, norm_gain[2], True)
    return (layer_out, cache_dec)


def solution(mesh):
    in_specs = (
        P("req", None),
        P("req", None),
        P(None, "blk", "req"),
        P(),
        P(),
        P(),
        P(),
        P(),
        P(),
        P(),
        P("req", "blk"),
        P("req", None, "blk"),
        P("blk", "req"),
        P("req", "blk"),
        P("req", None, "blk"),
        P("blk", "req"),
        P("req", None, "blk"),
        P("blk", "req"),
    )
    out_specs = (P("req", None), P("req", None, "blk"))
    return jax.shard_map(
        per_device, mesh=mesh, in_specs=in_specs, out_specs=out_specs, check_vma=False
    )
```

```python
import functools

import jax
import jax.numpy as jnp
from jax import lax
from jax.sharding import PartitionSpec as P
from jax.experimental import pallas as pl
from jax.experimental.pallas import tpu as pltpu

H = 16
HD = 64


EPSILON = 1e-06
NEG_FILL = -1e30


def rms_rows(row_block, gain):
    mean_square = jnp.mean(row_block * row_block, axis=-1, keepdims=True)
    return (row_block * lax.rsqrt(mean_square + EPSILON) * gain).astype(jnp.bfloat16)


def softmax_rows(scores):
    row_top = jnp.max(scores, axis=-1, keepdims=True)
    weights = jnp.exp(scores - row_top)
    return (weights / jnp.sum(weights, axis=-1, keepdims=True)).astype(jnp.bfloat16)


def pick_lengths(table, own_slots):
    matches = own_slots[:, None] == jnp.arange(table.shape[0], dtype=jnp.int32)[None, :]
    return jnp.sum(jnp.where(matches, table[None, :], 0), axis=1)


def shifted_bias(bias_dist, base, row_count, col_count):
    heads_here, span_len = bias_dist.shape
    line_len = row_count + col_count - 1
    steps = jnp.arange(line_len + 1, dtype=jnp.int32)
    line = bias_dist[:, jnp.clip(base + row_count - 1 - steps, 0, span_len - 1)]
    tiled = jnp.broadcast_to(line[:, None, :], (heads_here, row_count, line_len + 1))
    flat = tiled.reshape(heads_here, row_count * (line_len + 1))[:, : row_count * line_len]
    skewed = flat.reshape(heads_here, row_count, line_len)
    return skewed[:, :, row_count - 1 : row_count - 1 + col_count]


def row_total(left, weight):
    term = jnp.dot(left, weight, preferred_element_type=jnp.float32)
    return lax.psum(term.astype(jnp.bfloat16), "blk").astype(jnp.float32)


def cached_scores(queries, key_rows, first_col, old_len, bias_dist):
    col_ids = first_col + jnp.arange(key_rows.shape[0], dtype=jnp.int32)[None, :]
    scores = jnp.einsum("qhe,khe->hqk", queries, key_rows, preferred_element_type=jnp.float32)
    scores = scores + shifted_bias(
        bias_dist, old_len - first_col, queries.shape[0], key_rows.shape[0]
    )
    return jnp.where((col_ids < old_len)[None], scores, NEG_FILL)


def fresh_scores(queries, fresh_keys, fresh_len, bias_dist):
    row_ids = jnp.arange(queries.shape[0], dtype=jnp.int32)[:, None]
    col_ids = jnp.arange(fresh_keys.shape[0], dtype=jnp.int32)[None, :]
    scores = jnp.einsum("qhe,khe->hqk", queries, fresh_keys, preferred_element_type=jnp.float32)
    scores = scores + shifted_bias(bias_dist, 0, queries.shape[0], fresh_keys.shape[0])
    admitted = (col_ids <= row_ids) & (col_ids < fresh_len)
    return jnp.where(admitted[None], scores, NEG_FILL)


def self_padded(
    queries, key_rows, value_rows, fresh_keys, fresh_values, old_len, fresh_len, bias_dist
):
    scores = jnp.concatenate(
        [
            cached_scores(queries, key_rows, 0, old_len, bias_dist),
            fresh_scores(queries, fresh_keys, fresh_len, bias_dist),
        ],
        axis=2,
    )
    weights = softmax_rows(scores)
    value_all = jnp.concatenate([value_rows, fresh_values], axis=0)
    return jnp.einsum(
        "hqk,khe->qhe", weights, value_all, preferred_element_type=jnp.float32
    ).astype(jnp.bfloat16)


def self_attend(queries, key_value, cache_dec, slot_old, slot_new, bias_dist, heads_dev):
    req_dev, cache_len = (cache_dec.shape[0], cache_dec.shape[1])
    cache_split = cache_dec.reshape(req_dev, cache_len, heads_dev, 2, -1)

    def one_request(request):
        queries_one, pair_one, cache_one, old_len, fresh_len = request
        return self_padded(
            queries_one,
            cache_one[:, :, 0],
            cache_one[:, :, 1],
            pair_one[:, 0],
            pair_one[:, 1],
            old_len,
            fresh_len,
            bias_dist,
        )

    return lax.map(one_request, (queries, key_value, cache_split, slot_old, slot_new))


def cross_attend(queries, key_value, slot_enc):
    scores = jnp.einsum(
        "rqhe,rkhe->rhqk", queries, key_value[:, :, 0], preferred_element_type=jnp.float32
    )
    col_ids = jnp.arange(key_value.shape[1], dtype=jnp.int32)
    scores = jnp.where(
        col_ids[None, None, None, :] < slot_enc[:, None, None, None], scores, NEG_FILL
    )
    weights = softmax_rows(scores)
    return jnp.einsum(
        "rhqk,rkhe->rqhe", weights, key_value[:, :, 1], preferred_element_type=jnp.float32
    ).astype(jnp.bfloat16)


def add_branch(residual, left, weight, gain):
    residual = residual + row_total(left, weight)
    normed = rms_rows(residual, gain)
    return (residual, normed)


TQ = 128


def stage_kernel(n_blk, final, extra, *refs):
    if extra:
        (part_ref, resid_ref, gain_ref, packed_ref, res_out, full_ref, wts_ref,
         recv_a, send_b, recv_b, x_send, x_recv, b_send, b_recv, ag_send, ag_recv, w_send, w_recv) = refs
    else:
        (part_ref, resid_ref, gain_ref, res_out, full_ref,
         recv_a, send_b, recv_b, x_send, x_recv, b_send, b_recv, ag_send, ag_recv) = refs
    me = lax.axis_index("blk")
    req = lax.axis_index("req")
    rows = resid_ref.shape[0]
    n_grp = n_blk // 2
    g = me // 2
    c = lax.rem(me, 2)
    partner = g * 2 + 1 - c
    half = n_grp * rows
    n_req = wts_ref.shape[0] if extra else 1
    barrier = pltpu.get_barrier_semaphore()
    for k in range(1, n_grp):
        peer = lax.rem(g + k, n_grp) * 2 + c
        pl.semaphore_signal(barrier, inc=1, device_id=(req, peer), device_id_type=MESH_IDS)
    pl.semaphore_signal(barrier, inc=1, device_id=(req, partner), device_id_type=MESH_IDS)
    for k in range(1, n_req):
        peer = lax.rem(req + k, n_req)
        pl.semaphore_signal(barrier, inc=1, device_id=(peer, me), device_id_type=MESH_IDS)
    pl.semaphore_wait(barrier, n_grp + n_req - 1)
    sends = []
    for k in range(n_grp):
        grp = lax.rem(g + 1 + k, n_grp)
        exchange = pltpu.make_async_remote_copy(
            src_ref=part_ref.at[pl.ds(pl.multiple_of((1 - c) * half + grp * rows, rows), rows)],
            dst_ref=recv_a.at[grp],
            send_sem=x_send.at[k],
            recv_sem=x_recv.at[grp],
            device_id=(req, partner),
            device_id_type=MESH_IDS,
        )
        exchange.start()
        sends.append(exchange)
    for k in range(1, n_req):
        peer = lax.rem(req + k, n_req)
        copy = pltpu.make_async_remote_copy(
            src_ref=packed_ref,
            dst_ref=wts_ref.at[req],
            send_sem=w_send.at[peer],
            recv_sem=w_recv.at[req],
            device_id=(peer, me),
            device_id_type=MESH_IDS,
        )
        copy.start()
        sends.append(copy)
    total = None
    for k in range(n_grp):
        grp = lax.rem(g + 1 + k, n_grp)
        incoming = pltpu.make_async_remote_copy(
            src_ref=part_ref.at[pl.ds(0, rows)],
            dst_ref=recv_a.at[grp],
            send_sem=x_send.at[k],
            recv_sem=x_recv.at[grp],
            device_id=(req, partner),
            device_id_type=MESH_IDS,
        )
        incoming.wait_recv()
        pair = part_ref[pl.ds(pl.multiple_of(c * half + grp * rows, rows), rows), :].astype(
            jnp.float32
        ) + recv_a[grp].astype(jnp.float32)
        if k == n_grp - 1:
            total = pair
        else:
            send_b[grp] = pair.astype(send_b.dtype)
            copy = pltpu.make_async_remote_copy(
                src_ref=send_b.at[grp],
                dst_ref=recv_b.at[g],
                send_sem=b_send.at[grp],
                recv_sem=b_recv.at[g],
                device_id=(req, grp * 2 + c),
                device_id_type=MESH_IDS,
            )
            copy.start()
            sends.append(copy)
    for k in range(1, n_grp):
        grp = lax.rem(g + n_grp - k, n_grp)
        incoming = pltpu.make_async_remote_copy(
            src_ref=send_b.at[0],
            dst_ref=recv_b.at[grp],
            send_sem=b_send.at[grp],
            recv_sem=b_recv.at[grp],
            device_id=(req, grp * 2 + c),
            device_id_type=MESH_IDS,
        )
        incoming.wait_recv()
        total = total + recv_b[grp].astype(jnp.float32)
    mine = pl.ds(pl.multiple_of(c * half + g * rows, rows), rows)
    resid = resid_ref[...] + total
    res_out[...] = resid
    if final:
        full_ref[mine, :] = resid.astype(full_ref.dtype)
    else:
        mean_square = jnp.mean(resid * resid, axis=-1, keepdims=True)
        full_ref[mine, :] = (resid * lax.rsqrt(mean_square + EPSILON) * gain_ref[...]).astype(
            full_ref.dtype
        )
    for k in range(1, n_grp):
        peer = lax.rem(g + k, n_grp) * 2 + c
        copy = pltpu.make_async_remote_copy(
            src_ref=full_ref.at[mine],
            dst_ref=full_ref.at[mine],
            send_sem=ag_send.at[k],
            recv_sem=ag_recv.at[g],
            device_id=(req, peer),
            device_id_type=MESH_IDS,
        )
        copy.start()
        sends.append(copy)
    copy = pltpu.make_async_remote_copy(
        src_ref=full_ref.at[mine],
        dst_ref=full_ref.at[mine],
        send_sem=ag_send.at[0],
        recv_sem=ag_recv.at[n_grp + g],
        device_id=(req, partner),
        device_id_type=MESH_IDS,
    )
    copy.start()
    sends.append(copy)
    for k in range(1, n_grp):
        grp = lax.rem(g + n_grp - k, n_grp)
        there = pl.ds(pl.multiple_of(c * half + grp * rows, rows), rows)
        incoming = pltpu.make_async_remote_copy(
            src_ref=full_ref.at[there],
            dst_ref=full_ref.at[there],
            send_sem=ag_send.at[0],
            recv_sem=ag_recv.at[grp],
            device_id=(req, grp * 2 + c),
            device_id_type=MESH_IDS,
        )
        incoming.wait_recv()
        forward = pltpu.make_async_remote_copy(
            src_ref=full_ref.at[there],
            dst_ref=full_ref.at[there],
            send_sem=ag_send.at[n_grp + k],
            recv_sem=ag_recv.at[n_grp + grp],
            device_id=(req, partner),
            device_id_type=MESH_IDS,
        )
        forward.start()
        sends.append(forward)
    for grp in range(n_grp):
        there = pl.ds(pl.multiple_of((1 - c) * half + grp * rows, rows), rows)
        incoming = pltpu.make_async_remote_copy(
            src_ref=full_ref.at[there],
            dst_ref=full_ref.at[there],
            send_sem=ag_send.at[0],
            recv_sem=ag_recv.at[n_grp + grp],
            device_id=(req, partner),
            device_id_type=MESH_IDS,
        )
        incoming.wait_recv()
    if extra:
        wts_ref[req] = packed_ref[...]
        for k in range(1, n_req):
            src = lax.rem(req + n_req - k, n_req)
            incoming = pltpu.make_async_remote_copy(
                src_ref=packed_ref,
                dst_ref=wts_ref.at[src],
                send_sem=w_send.at[src],
                recv_sem=w_recv.at[src],
                device_id=(src, me),
                device_id_type=MESH_IDS,
            )
            incoming.wait_recv()
    for copy in sends:
        copy.wait_send()


def blk_stage(part, resid, gain, final, packed=None):
    n_blk = lax.axis_size("blk")
    rows, width = resid.shape
    vmem = pl.BlockSpec(memory_space=pltpu.VMEM)
    extra = packed is not None
    outs = [
        jax.ShapeDtypeStruct((rows, width), jnp.float32),
        jax.ShapeDtypeStruct((rows * n_blk, width), jnp.bfloat16),
    ]
    n_grp = n_blk // 2
    scratch = [
        pltpu.VMEM((n_grp, rows, width), part.dtype),
        pltpu.VMEM((n_grp, rows, width), part.dtype),
        pltpu.VMEM((n_grp, rows, width), part.dtype),
        pltpu.SemaphoreType.DMA((n_grp,)),
        pltpu.SemaphoreType.DMA((n_grp,)),
        pltpu.SemaphoreType.DMA((n_grp,)),
        pltpu.SemaphoreType.DMA((n_grp,)),
        pltpu.SemaphoreType.DMA((n_blk,)),
        pltpu.SemaphoreType.DMA((n_blk,)),
    ]
    args = [part, resid, gain[None, :]]
    if extra:
        n_req = lax.axis_size("req")
        outs.append(jax.ShapeDtypeStruct((n_req,) + packed.shape, packed.dtype))
        scratch += [pltpu.SemaphoreType.DMA((n_req,)), pltpu.SemaphoreType.DMA((n_req,))]
        args.append(packed)
    return pl.pallas_call(
        functools.partial(stage_kernel, n_blk, final, extra),
        out_shape=tuple(outs),
        in_specs=[vmem] * len(args),
        out_specs=tuple([vmem] * len(outs)),
        scratch_shapes=scratch,
        compiler_params=pltpu.CompilerParams(
            collective_id=5 if extra else (4 if final else 3), has_side_effects=True
        ),
    )(*args)


def cross_kernel(len_ref, normed_ref, enc_ref, wq_ref, wkv_ref, wo_ref, out_ref):
    enc_len = len_ref[0]
    queries = jnp.dot(normed_ref[...], wq_ref[...], preferred_element_type=jnp.float32).astype(
        jnp.bfloat16
    )
    pair = jnp.dot(enc_ref[...], wkv_ref[...], preferred_element_type=jnp.float32).astype(
        jnp.bfloat16
    )
    keys = pair[:, :HD]
    values = pair[:, HD:]
    scores = lax.dot_general(
        queries, keys, (((1,), (1,)), ((), ())), preferred_element_type=jnp.float32
    )
    col = lax.broadcasted_iota(jnp.int32, scores.shape, 1)
    scores = jnp.where(col < enc_len, scores, NEG_FILL)
    top = jnp.max(scores, axis=1, keepdims=True)
    weights = jnp.exp(scores - top)
    weights = (weights / jnp.sum(weights, axis=1, keepdims=True)).astype(jnp.bfloat16)
    context = jnp.dot(weights, values, preferred_element_type=jnp.float32).astype(jnp.bfloat16)
    out_ref[...] = jnp.dot(context, wo_ref[...], preferred_element_type=jnp.float32).astype(
        out_ref.dtype
    )


def cross_branch(normed, enc, wq, wkv, wo, enc_len):
    vmem = pl.BlockSpec(memory_space=pltpu.VMEM)
    return pl.pallas_call(
        cross_kernel,
        out_shape=jax.ShapeDtypeStruct((normed.shape[0], wo.shape[1]), jnp.bfloat16),
        in_specs=[pl.BlockSpec(memory_space=pltpu.SMEM)] + [vmem] * 5,
        out_specs=vmem,
    )(enc_len.reshape(1).astype(jnp.int32), normed, enc, wq, wkv, wo)


def self_kernel(lens_ref, q_ref, c_ref, kn_ref, vn_ref, g_ref, f_ref, o_ref):
    old_len = lens_ref[0]
    fresh_len = lens_ref[1]
    n_q = q_ref.shape[0]
    n_ctx = c_ref.shape[0]
    wide_old = n_ctx + TQ
    wide_new = n_q + TQ
    k_old = c_ref[:, :HD]
    v_old = c_ref[:, HD:]
    k_new = kn_ref[...]
    v_new = vn_ref[...]
    dims = (((1,), (1,)), ((), ()))
    for t in range(n_q // TQ):
        q = q_ref[t * TQ : (t + 1) * TQ, :]
        start = n_q - TQ - t * TQ
        s_old = lax.dot_general(q, k_old, dims, preferred_element_type=jnp.float32)
        line = jnp.broadcast_to(g_ref[:, start : start + wide_old], (TQ, wide_old))
        bias = pltpu.roll(line, wide_old - (TQ - 1), 1, stride=1, stride_axis=0)[:, :n_ctx]
        col = lax.broadcasted_iota(jnp.int32, (TQ, n_ctx), 1)
        s_old = jnp.where(col < old_len, s_old + bias, NEG_FILL)
        s_new = lax.dot_general(q, k_new, dims, preferred_element_type=jnp.float32)
        line = jnp.broadcast_to(f_ref[:, start : start + wide_new], (TQ, wide_new))
        bias = pltpu.roll(line, wide_new - (TQ - 1), 1, stride=1, stride_axis=0)[:, :n_q]
        row = lax.broadcasted_iota(jnp.int32, (TQ, n_q), 0) + t * TQ
        col = lax.broadcasted_iota(jnp.int32, (TQ, n_q), 1)
        s_new = jnp.where((col <= row) & (col < fresh_len), s_new + bias, NEG_FILL)
        top = jnp.maximum(
            jnp.max(s_old, axis=1, keepdims=True), jnp.max(s_new, axis=1, keepdims=True)
        )
        p_old = jnp.exp(s_old - top)
        p_new = jnp.exp(s_new - top)
        total = jnp.sum(p_old, axis=1, keepdims=True) + jnp.sum(p_new, axis=1, keepdims=True)
        w_old = (p_old / total).astype(jnp.bfloat16)
        w_new = (p_new / total).astype(jnp.bfloat16)
        out = jnp.dot(w_old, v_old, preferred_element_type=jnp.float32) + jnp.dot(
            w_new, v_new, preferred_element_type=jnp.float32
        )
        o_ref[t * TQ : (t + 1) * TQ, :] = out.astype(jnp.bfloat16)


def bias_lines(line, old_len, n_q, n_ctx):
    span = line.shape[0]
    ext = jnp.concatenate([jnp.broadcast_to(line[:1], (n_ctx,)), line])
    rev = ext[::-1]
    g = lax.dynamic_slice_in_dim(rev, n_ctx - old_len, span)
    f = rev[n_ctx : n_ctx + 2 * n_q]
    return g[None, :], f[None, :]


def self_attention(q, cache_blk, k_new, v_new, line, old_len, fresh_len):
    n_q = q.shape[0]
    n_ctx = cache_blk.shape[0]
    g, f = bias_lines(line, old_len, n_q, n_ctx)
    lens = jnp.stack([old_len, fresh_len]).astype(jnp.int32)
    vmem = pl.BlockSpec(memory_space=pltpu.VMEM)
    return pl.pallas_call(
        self_kernel,
        out_shape=jax.ShapeDtypeStruct((n_q, HD), jnp.bfloat16),
        in_specs=[pl.BlockSpec(memory_space=pltpu.SMEM)] + [vmem] * 6,
        out_specs=vmem,
        compiler_params=pltpu.CompilerParams(vmem_limit_bytes=48 * 1024 * 1024),
    )(lens, q, cache_blk, k_new, v_new, g, f)


def pack_gather(pieces):
    flat = jnp.concatenate([w.reshape(-1) for w, _ in pieces])
    whole = lax.all_gather(flat, "req", axis=0, tiled=False)
    n_req = whole.shape[0]
    out, at = [], 0
    for w, axis in pieces:
        size = w.size
        part = whole[:, at : at + size].reshape((n_req,) + w.shape)
        at += size
        part = jnp.moveaxis(part, 0, axis)
        shape = list(w.shape)
        shape[axis] *= n_req
        out.append(part.reshape(shape))
    return out


MESH_IDS = pl.DeviceIdType.MESH


def greet_all(n_blk, me, req):
    barrier = pltpu.get_barrier_semaphore()
    for k in range(1, n_blk):
        peer = lax.rem(me + k, n_blk)
        pl.semaphore_signal(barrier, inc=1, device_id=(req, peer), device_id_type=MESH_IDS)
    pl.semaphore_wait(barrier, n_blk - 1)


def chunk_of(b, n_blk):
    return lax.rem(b, 2) * (n_blk // 2) + b // 2


def scatter_kernel(n_blk, part_ref, out_ref, recv, send_sem, recv_sem):
    me = lax.axis_index("blk")
    req = lax.axis_index("req")
    rows = out_ref.shape[0]
    greet_all(n_blk, me, req)
    copies = []
    for k in range(1, n_blk):
        peer = lax.rem(me + k, n_blk)
        copy = pltpu.make_async_remote_copy(
            src_ref=part_ref.at[pl.ds(pl.multiple_of(chunk_of(peer, n_blk) * rows, rows), rows)],
            dst_ref=recv.at[me],
            send_sem=send_sem.at[peer],
            recv_sem=recv_sem.at[me],
            device_id=(req, peer),
            device_id_type=MESH_IDS,
        )
        copy.start()
        copies.append(copy)
    own = pl.ds(pl.multiple_of(chunk_of(me, n_blk) * rows, rows), rows)
    total = part_ref[own, :].astype(jnp.float32)
    for k in range(1, n_blk):
        src = lax.rem(me + n_blk - k, n_blk)
        incoming = pltpu.make_async_remote_copy(
            src_ref=part_ref.at[pl.ds(0, rows)],
            dst_ref=recv.at[src],
            send_sem=send_sem.at[src],
            recv_sem=recv_sem.at[src],
            device_id=(req, src),
            device_id_type=MESH_IDS,
        )
        incoming.wait_recv()
        total = total + recv[src].astype(jnp.float32)
    for copy in copies:
        copy.wait_send()
    out_ref[...] = total


def gather_kernel(n_blk, piece_ref, out_ref, send_sem, recv_sem):
    b = lax.axis_index("blk")
    req = lax.axis_index("req")
    n_grp = n_blk // 2
    g = b // 2
    c = lax.rem(b, 2)
    partner = g * 2 + 1 - c
    rows = piece_ref.shape[0]
    half = n_grp * rows
    barrier = pltpu.get_barrier_semaphore()
    for k in range(1, n_grp):
        peer = lax.rem(g + k, n_grp) * 2 + c
        pl.semaphore_signal(barrier, inc=1, device_id=(req, peer), device_id_type=MESH_IDS)
    pl.semaphore_signal(barrier, inc=1, device_id=(req, partner), device_id_type=MESH_IDS)
    pl.semaphore_wait(barrier, n_grp)
    mine = pl.ds(pl.multiple_of(c * half + g * rows, rows), rows)
    sends = []
    for k in range(1, n_grp):
        peer = lax.rem(g + k, n_grp) * 2 + c
        copy = pltpu.make_async_remote_copy(
            src_ref=piece_ref,
            dst_ref=out_ref.at[mine],
            send_sem=send_sem.at[k],
            recv_sem=recv_sem.at[g],
            device_id=(req, peer),
            device_id_type=MESH_IDS,
        )
        copy.start()
        sends.append(copy)
    copy = pltpu.make_async_remote_copy(
        src_ref=piece_ref,
        dst_ref=out_ref.at[mine],
        send_sem=send_sem.at[0],
        recv_sem=recv_sem.at[n_grp + g],
        device_id=(req, partner),
        device_id_type=MESH_IDS,
    )
    copy.start()
    sends.append(copy)
    out_ref[mine, :] = piece_ref[...]
    for k in range(1, n_grp):
        grp = lax.rem(g + n_grp - k, n_grp)
        there = pl.ds(pl.multiple_of(c * half + grp * rows, rows), rows)
        incoming = pltpu.make_async_remote_copy(
            src_ref=piece_ref,
            dst_ref=out_ref.at[there],
            send_sem=send_sem.at[0],
            recv_sem=recv_sem.at[grp],
            device_id=(req, grp * 2 + c),
            device_id_type=MESH_IDS,
        )
        incoming.wait_recv()
        forward = pltpu.make_async_remote_copy(
            src_ref=out_ref.at[there],
            dst_ref=out_ref.at[there],
            send_sem=send_sem.at[n_grp + k],
            recv_sem=recv_sem.at[n_grp + grp],
            device_id=(req, partner),
            device_id_type=MESH_IDS,
        )
        forward.start()
        sends.append(forward)
    for grp in range(n_grp):
        there = pl.ds(pl.multiple_of((1 - c) * half + grp * rows, rows), rows)
        incoming = pltpu.make_async_remote_copy(
            src_ref=piece_ref,
            dst_ref=out_ref.at[there],
            send_sem=send_sem.at[0],
            recv_sem=recv_sem.at[n_grp + grp],
            device_id=(req, partner),
            device_id_type=MESH_IDS,
        )
        incoming.wait_recv()
    for copy in sends:
        copy.wait_send()


def blk_scatter(part):
    n_blk = lax.axis_size("blk")
    rows = part.shape[0] // n_blk
    vmem = pl.BlockSpec(memory_space=pltpu.VMEM)
    return pl.pallas_call(
        functools.partial(scatter_kernel, n_blk),
        out_shape=jax.ShapeDtypeStruct((rows, part.shape[1]), jnp.float32),
        in_specs=[vmem],
        out_specs=vmem,
        scratch_shapes=[
            pltpu.VMEM((n_blk, rows, part.shape[1]), part.dtype),
            pltpu.SemaphoreType.DMA((n_blk,)),
            pltpu.SemaphoreType.DMA((n_blk,)),
        ],
        compiler_params=pltpu.CompilerParams(collective_id=1, has_side_effects=True),
    )(part)


def blk_gather(piece):
    n_blk = lax.axis_size("blk")
    rows = piece.shape[0]
    vmem = pl.BlockSpec(memory_space=pltpu.VMEM)
    return pl.pallas_call(
        functools.partial(gather_kernel, n_blk),
        out_shape=jax.ShapeDtypeStruct((rows * n_blk, piece.shape[1]), piece.dtype),
        in_specs=[vmem],
        out_specs=vmem,
        scratch_shapes=[
            pltpu.SemaphoreType.DMA((n_blk,)),
            pltpu.SemaphoreType.DMA((n_blk,)),
        ],
        compiler_params=pltpu.CompilerParams(collective_id=2, has_side_effects=True),
    )(piece)


def prologue_kernel(n_req, n_blk, ordered_ref, packed_ref, cache_ref, wts_ref, w_send, w_recv, c_send, c_recv, local_sem):
    r = lax.axis_index("req")
    b = lax.axis_index("blk")
    n_slot, span, width = ordered_ref.shape
    piece = width // 2
    copies = []
    for k in range(1, n_req):
        peer = lax.rem(r + k, n_req)
        copy = pltpu.make_async_remote_copy(
            src_ref=packed_ref,
            dst_ref=wts_ref.at[r],
            send_sem=w_send.at[peer],
            recv_sem=w_recv.at[r],
            device_id=(peer, b),
            device_id_type=MESH_IDS,
        )
        copy.start()
        copies.append(copy)
    rows = pl.ds(pl.multiple_of(b * span, span), span)
    for k in range(n_slot):
        s = lax.rem(b + k, n_slot)
        for hh in range(2):
            head = 2 * r + hh
            is_self = jnp.logical_and(r == s, head == b)
            src = ordered_ref.at[s, :, pl.ds(hh * piece, piece)]
            copy = pltpu.make_async_remote_copy(
                src_ref=src,
                dst_ref=cache_ref.at[rows],
                send_sem=c_send.at[k * 2 + hh],
                recv_sem=c_recv.at[b],
                device_id=(s, head),
                device_id_type=MESH_IDS,
            )

            @pl.when(jnp.logical_not(is_self))
            def _():
                copy.start()

            @pl.when(is_self)
            def _():
                local = pltpu.make_async_copy(src, cache_ref.at[rows], local_sem.at[0])
                local.start()
                local.wait()

            copies.append((copy, is_self))
    wts_ref[r] = packed_ref[...]
    for k in range(1, n_req):
        src_req = lax.rem(r + n_req - k, n_req)
        incoming = pltpu.make_async_remote_copy(
            src_ref=packed_ref,
            dst_ref=wts_ref.at[src_req],
            send_sem=w_send.at[src_req],
            recv_sem=w_recv.at[src_req],
            device_id=(src_req, b),
            device_id_type=MESH_IDS,
        )
        incoming.wait_recv()
    owner = b // 2
    for j in range(n_blk):
        incoming = pltpu.make_async_remote_copy(
            src_ref=ordered_ref.at[0, :, pl.ds(0, piece)],
            dst_ref=cache_ref.at[pl.ds(j * span, span)],
            send_sem=c_send.at[0],
            recv_sem=c_recv.at[j],
            device_id=(owner, j),
            device_id_type=MESH_IDS,
        )

        @pl.when(jnp.logical_not(jnp.logical_and(owner == r, j == b)))
        def _():
            incoming.wait_recv()

    for item in copies:
        if isinstance(item, tuple):
            copy, is_self = item

            @pl.when(jnp.logical_not(is_self))
            def _():
                copy.wait_send()

        else:
            item.wait_send()


def prologue(ordered, packed):
    n_req = lax.axis_size("req")
    n_blk = lax.axis_size("blk")
    n_slot, span, width = ordered.shape
    any_spec = pl.BlockSpec(memory_space=pl.ANY)
    vmem = pl.BlockSpec(memory_space=pltpu.VMEM)
    return pl.pallas_call(
        functools.partial(prologue_kernel, n_req, n_blk),
        out_shape=(
            jax.ShapeDtypeStruct((span * n_blk, width // 2), ordered.dtype),
            jax.ShapeDtypeStruct((n_req,) + packed.shape, packed.dtype),
        ),
        in_specs=[any_spec, vmem],
        out_specs=(any_spec, vmem),
        scratch_shapes=[
            pltpu.SemaphoreType.DMA((n_req,)),
            pltpu.SemaphoreType.DMA((n_req,)),
            pltpu.SemaphoreType.DMA((2 * n_slot,)),
            pltpu.SemaphoreType.DMA((n_blk,)),
            pltpu.SemaphoreType.DMA((1,)),
        ],
        compiler_params=pltpu.CompilerParams(has_side_effects=True),
    )(ordered, packed)


def unpack(whole, pieces):
    n_req = whole.shape[0]
    whole = whole.reshape(n_req, -1)
    out, at = [], 0
    for w, axis in pieces:
        size = w.size
        part = whole[:, at : at + size].reshape((n_req,) + w.shape)
        at += size
        part = jnp.moveaxis(part, 0, axis)
        shape = list(w.shape)
        shape[axis] *= n_req
        out.append(part.reshape(shape))
    return out


def per_device(
    new_states,
    encoder_out,
    cache_in,
    slot_order,
    new_lengths,
    cache_lengths,
    enc_lengths,
    bucket_of,
    rel_bias,
    norm_gain,
    self_q,
    self_kv,
    self_out,
    cross_q,
    cross_kv,
    cross_out,
    ff_in,
    ff_out,
):
    blk_count = lax.axis_size("blk")
    heads_dev = H // blk_count
    width_dev = heads_dev * HD
    req_dev = cache_in.shape[0] // lax.axis_size("req")
    own_slots = lax.dynamic_slice_in_dim(slot_order, lax.axis_index("req") * req_dev, req_dev, 0)
    slot_new = pick_lengths(new_lengths, own_slots)
    slot_old = pick_lengths(cache_lengths, own_slots)
    slot_enc = pick_lengths(enc_lengths, own_slots)
    ordered = jnp.take(cache_in, slot_order, axis=0)
    onehot = (bucket_of[:, None] == jnp.arange(rel_bias.shape[0], dtype=jnp.int32)[None, :]).astype(
        jnp.float32
    )
    own_bias = lax.dynamic_slice_in_dim(rel_bias, lax.axis_index("blk") * heads_dev, heads_dev, 1)
    bias_dist = jnp.dot(onehot, own_bias, precision=lax.Precision.HIGHEST).T
    early = [(self_q, 0), (self_kv, 0), (self_out, 1)]
    late = [(cross_q, 0), (cross_kv, 0), (cross_out, 1), (ff_in, 0), (ff_out, 1)]
    flat = jnp.concatenate([w.reshape(-1) for w, _ in early])
    cache_blk, whole = prologue(ordered, flat.reshape(-1, 128))
    cache_dec = cache_blk[None]
    gathered = unpack(whole, early)
    late_gathered = pack_gather(late)
    wq_self, wkv_self, wo_self = gathered
    n_blk = lax.axis_size("blk")
    rows_dev = new_states.shape[0] // n_blk
    own_rows = lax.dynamic_slice_in_dim(
        new_states, chunk_of(lax.axis_index("blk"), n_blk) * rows_dev, rows_dev, 0
    ).astype(jnp.float32)
    normed = rms_rows(new_states.astype(jnp.float32), norm_gain[0])
    self_cat = jnp.concatenate([wq_self, wkv_self.reshape(wkv_self.shape[0], -1)], axis=1)
    projected = jnp.dot(normed, self_cat, preferred_element_type=jnp.float32).astype(
        jnp.bfloat16
    )
    context = self_attention(
        projected[:, :HD],
        cache_dec[0],
        projected[:, HD : 2 * HD],
        projected[:, 2 * HD :],
        bias_dist[0],
        slot_old[0],
        slot_new[0],
    )
    part = jnp.dot(context, wo_self, preferred_element_type=jnp.float32).astype(jnp.bfloat16)
    residual, normed = blk_stage(part, own_rows, norm_gain[1], False)
    wq_cross, wkv_cross, wo_cross, w_in, w_out = late_gathered
    part = cross_branch(
        normed,
        encoder_out,
        wq_cross,
        wkv_cross.reshape(wkv_cross.shape[0], -1),
        wo_cross,
        slot_enc[0],
    )
    residual, normed = blk_stage(part.astype(jnp.bfloat16), residual, norm_gain[2], False)
    ff_dev = w_in.shape[2]
    gate_up = jnp.dot(normed, w_in.reshape(w_in.shape[0], -1), preferred_element_type=jnp.float32)
    hidden = (jax.nn.gelu(gate_up[:, :ff_dev], approximate=True) * gate_up[:, ff_dev:]).astype(
        jnp.bfloat16
    )
    part = jnp.dot(hidden, w_out, preferred_element_type=jnp.float32).astype(jnp.bfloat16)
    _, layer_out = blk_stage(part, residual, norm_gain[2], True)
    return (layer_out, cache_dec)


def solution(mesh):
    in_specs = (
        P("req", None),
        P("req", None),
        P(None, "blk", "req"),
        P(),
        P(),
        P(),
        P(),
        P(),
        P(),
        P(),
        P("req", "blk"),
        P("req", None, "blk"),
        P("blk", "req"),
        P("req", "blk"),
        P("req", None, "blk"),
        P("blk", "req"),
        P("req", None, "blk"),
        P("blk", "req"),
    )
    out_specs = (P("req", None), P("req", None, "blk"))
    return jax.shard_map(
        per_device, mesh=mesh, in_specs=in_specs, out_specs=out_specs, check_vma=False
    )
```

```python
import functools

import jax
import jax.numpy as jnp
from jax import lax
from jax.sharding import PartitionSpec as P
from jax.experimental import pallas as pl
from jax.experimental.pallas import tpu as pltpu

H = 16
HD = 64


EPSILON = 1e-06
NEG_FILL = -1e30


def rms_rows(row_block, gain):
    mean_square = jnp.mean(row_block * row_block, axis=-1, keepdims=True)
    return (row_block * lax.rsqrt(mean_square + EPSILON) * gain).astype(jnp.bfloat16)


def softmax_rows(scores):
    row_top = jnp.max(scores, axis=-1, keepdims=True)
    weights = jnp.exp(scores - row_top)
    return (weights / jnp.sum(weights, axis=-1, keepdims=True)).astype(jnp.bfloat16)


def pick_lengths(table, own_slots):
    matches = own_slots[:, None] == jnp.arange(table.shape[0], dtype=jnp.int32)[None, :]
    return jnp.sum(jnp.where(matches, table[None, :], 0), axis=1)


def shifted_bias(bias_dist, base, row_count, col_count):
    heads_here, span_len = bias_dist.shape
    line_len = row_count + col_count - 1
    steps = jnp.arange(line_len + 1, dtype=jnp.int32)
    line = bias_dist[:, jnp.clip(base + row_count - 1 - steps, 0, span_len - 1)]
    tiled = jnp.broadcast_to(line[:, None, :], (heads_here, row_count, line_len + 1))
    flat = tiled.reshape(heads_here, row_count * (line_len + 1))[:, : row_count * line_len]
    skewed = flat.reshape(heads_here, row_count, line_len)
    return skewed[:, :, row_count - 1 : row_count - 1 + col_count]


def row_total(left, weight):
    term = jnp.dot(left, weight, preferred_element_type=jnp.float32)
    return lax.psum(term.astype(jnp.bfloat16), "blk").astype(jnp.float32)


def cached_scores(queries, key_rows, first_col, old_len, bias_dist):
    col_ids = first_col + jnp.arange(key_rows.shape[0], dtype=jnp.int32)[None, :]
    scores = jnp.einsum("qhe,khe->hqk", queries, key_rows, preferred_element_type=jnp.float32)
    scores = scores + shifted_bias(
        bias_dist, old_len - first_col, queries.shape[0], key_rows.shape[0]
    )
    return jnp.where((col_ids < old_len)[None], scores, NEG_FILL)


def fresh_scores(queries, fresh_keys, fresh_len, bias_dist):
    row_ids = jnp.arange(queries.shape[0], dtype=jnp.int32)[:, None]
    col_ids = jnp.arange(fresh_keys.shape[0], dtype=jnp.int32)[None, :]
    scores = jnp.einsum("qhe,khe->hqk", queries, fresh_keys, preferred_element_type=jnp.float32)
    scores = scores + shifted_bias(bias_dist, 0, queries.shape[0], fresh_keys.shape[0])
    admitted = (col_ids <= row_ids) & (col_ids < fresh_len)
    return jnp.where(admitted[None], scores, NEG_FILL)


def self_padded(
    queries, key_rows, value_rows, fresh_keys, fresh_values, old_len, fresh_len, bias_dist
):
    scores = jnp.concatenate(
        [
            cached_scores(queries, key_rows, 0, old_len, bias_dist),
            fresh_scores(queries, fresh_keys, fresh_len, bias_dist),
        ],
        axis=2,
    )
    weights = softmax_rows(scores)
    value_all = jnp.concatenate([value_rows, fresh_values], axis=0)
    return jnp.einsum(
        "hqk,khe->qhe", weights, value_all, preferred_element_type=jnp.float32
    ).astype(jnp.bfloat16)


def self_attend(queries, key_value, cache_dec, slot_old, slot_new, bias_dist, heads_dev):
    req_dev, cache_len = (cache_dec.shape[0], cache_dec.shape[1])
    cache_split = cache_dec.reshape(req_dev, cache_len, heads_dev, 2, -1)

    def one_request(request):
        queries_one, pair_one, cache_one, old_len, fresh_len = request
        return self_padded(
            queries_one,
            cache_one[:, :, 0],
            cache_one[:, :, 1],
            pair_one[:, 0],
            pair_one[:, 1],
            old_len,
            fresh_len,
            bias_dist,
        )

    return lax.map(one_request, (queries, key_value, cache_split, slot_old, slot_new))


def cross_attend(queries, key_value, slot_enc):
    scores = jnp.einsum(
        "rqhe,rkhe->rhqk", queries, key_value[:, :, 0], preferred_element_type=jnp.float32
    )
    col_ids = jnp.arange(key_value.shape[1], dtype=jnp.int32)
    scores = jnp.where(
        col_ids[None, None, None, :] < slot_enc[:, None, None, None], scores, NEG_FILL
    )
    weights = softmax_rows(scores)
    return jnp.einsum(
        "rhqk,rkhe->rqhe", weights, key_value[:, :, 1], preferred_element_type=jnp.float32
    ).astype(jnp.bfloat16)


def add_branch(residual, left, weight, gain):
    residual = residual + row_total(left, weight)
    normed = rms_rows(residual, gain)
    return (residual, normed)


TQ = 128


def stage_kernel(n_blk, final, extra, *refs):
    if extra:
        (part_ref, resid_ref, gain_ref, packed_ref, res_out, full_ref, wts_ref,
         recv_a, send_b, recv_b, x_send, x_recv, b_send, b_recv, ag_send, ag_recv, w_send, w_recv) = refs
    else:
        (part_ref, resid_ref, gain_ref, res_out, full_ref,
         recv_a, send_b, recv_b, x_send, x_recv, b_send, b_recv, ag_send, ag_recv) = refs
    me = lax.axis_index("blk")
    req = lax.axis_index("req")
    rows = resid_ref.shape[0]
    n_grp = n_blk // 2
    g = me // 2
    c = lax.rem(me, 2)
    partner = g * 2 + 1 - c
    half = n_grp * rows
    n_req = wts_ref.shape[0] if extra else 1
    barrier = pltpu.get_barrier_semaphore()
    for k in range(1, n_grp):
        peer = lax.rem(g + k, n_grp) * 2 + c
        pl.semaphore_signal(barrier, inc=1, device_id=(req, peer), device_id_type=MESH_IDS)
    pl.semaphore_signal(barrier, inc=1, device_id=(req, partner), device_id_type=MESH_IDS)
    for k in range(1, n_req):
        peer = lax.rem(req + k, n_req)
        pl.semaphore_signal(barrier, inc=1, device_id=(peer, me), device_id_type=MESH_IDS)
    pl.semaphore_wait(barrier, n_grp + n_req - 1)
    sends = []
    for k in range(n_grp):
        grp = lax.rem(g + 1 + k, n_grp)
        exchange = pltpu.make_async_remote_copy(
            src_ref=part_ref.at[pl.ds(pl.multiple_of((1 - c) * half + grp * rows, rows), rows)],
            dst_ref=recv_a.at[grp],
            send_sem=x_send.at[k],
            recv_sem=x_recv.at[grp],
            device_id=(req, partner),
            device_id_type=MESH_IDS,
        )
        exchange.start()
        sends.append(exchange)
    for k in range(1, n_req):
        peer = lax.rem(req + k, n_req)
        copy = pltpu.make_async_remote_copy(
            src_ref=packed_ref,
            dst_ref=wts_ref.at[req],
            send_sem=w_send.at[peer],
            recv_sem=w_recv.at[req],
            device_id=(peer, me),
            device_id_type=MESH_IDS,
        )
        copy.start()
        sends.append(copy)
    total = None
    for k in range(n_grp):
        grp = lax.rem(g + 1 + k, n_grp)
        incoming = pltpu.make_async_remote_copy(
            src_ref=part_ref.at[pl.ds(0, rows)],
            dst_ref=recv_a.at[grp],
            send_sem=x_send.at[k],
            recv_sem=x_recv.at[grp],
            device_id=(req, partner),
            device_id_type=MESH_IDS,
        )
        incoming.wait_recv()
        pair = part_ref[pl.ds(pl.multiple_of(c * half + grp * rows, rows), rows), :].astype(
            jnp.float32
        ) + recv_a[grp].astype(jnp.float32)
        if k == n_grp - 1:
            total = pair
        else:
            send_b[grp] = pair.astype(send_b.dtype)
            copy = pltpu.make_async_remote_copy(
                src_ref=send_b.at[grp],
                dst_ref=recv_b.at[g],
                send_sem=b_send.at[grp],
                recv_sem=b_recv.at[g],
                device_id=(req, grp * 2 + c),
                device_id_type=MESH_IDS,
            )
            copy.start()
            sends.append(copy)
    for k in range(1, n_grp):
        grp = lax.rem(g + n_grp - k, n_grp)
        incoming = pltpu.make_async_remote_copy(
            src_ref=send_b.at[0],
            dst_ref=recv_b.at[grp],
            send_sem=b_send.at[grp],
            recv_sem=b_recv.at[grp],
            device_id=(req, grp * 2 + c),
            device_id_type=MESH_IDS,
        )
        incoming.wait_recv()
        total = total + recv_b[grp].astype(jnp.float32)
    mine = pl.ds(pl.multiple_of(c * half + g * rows, rows), rows)
    resid = resid_ref[...] + total
    res_out[...] = resid
    if final:
        full_ref[mine, :] = resid.astype(full_ref.dtype)
    else:
        mean_square = jnp.mean(resid * resid, axis=-1, keepdims=True)
        full_ref[mine, :] = (resid * lax.rsqrt(mean_square + EPSILON) * gain_ref[...]).astype(
            full_ref.dtype
        )
    for k in range(1, n_grp):
        peer = lax.rem(g + k, n_grp) * 2 + c
        copy = pltpu.make_async_remote_copy(
            src_ref=full_ref.at[mine],
            dst_ref=full_ref.at[mine],
            send_sem=ag_send.at[k],
            recv_sem=ag_recv.at[g],
            device_id=(req, peer),
            device_id_type=MESH_IDS,
        )
        copy.start()
        sends.append(copy)
    copy = pltpu.make_async_remote_copy(
        src_ref=full_ref.at[mine],
        dst_ref=full_ref.at[mine],
        send_sem=ag_send.at[0],
        recv_sem=ag_recv.at[n_grp + g],
        device_id=(req, partner),
        device_id_type=MESH_IDS,
    )
    copy.start()
    sends.append(copy)
    for k in range(1, n_grp):
        grp = lax.rem(g + n_grp - k, n_grp)
        there = pl.ds(pl.multiple_of(c * half + grp * rows, rows), rows)
        incoming = pltpu.make_async_remote_copy(
            src_ref=full_ref.at[there],
            dst_ref=full_ref.at[there],
            send_sem=ag_send.at[0],
            recv_sem=ag_recv.at[grp],
            device_id=(req, grp * 2 + c),
            device_id_type=MESH_IDS,
        )
        incoming.wait_recv()
        forward = pltpu.make_async_remote_copy(
            src_ref=full_ref.at[there],
            dst_ref=full_ref.at[there],
            send_sem=ag_send.at[n_grp + k],
            recv_sem=ag_recv.at[n_grp + grp],
            device_id=(req, partner),
            device_id_type=MESH_IDS,
        )
        forward.start()
        sends.append(forward)
    for grp in range(n_grp):
        there = pl.ds(pl.multiple_of((1 - c) * half + grp * rows, rows), rows)
        incoming = pltpu.make_async_remote_copy(
            src_ref=full_ref.at[there],
            dst_ref=full_ref.at[there],
            send_sem=ag_send.at[0],
            recv_sem=ag_recv.at[n_grp + grp],
            device_id=(req, partner),
            device_id_type=MESH_IDS,
        )
        incoming.wait_recv()
    if extra:
        wts_ref[req] = packed_ref[...]
        for k in range(1, n_req):
            src = lax.rem(req + n_req - k, n_req)
            incoming = pltpu.make_async_remote_copy(
                src_ref=packed_ref,
                dst_ref=wts_ref.at[src],
                send_sem=w_send.at[src],
                recv_sem=w_recv.at[src],
                device_id=(src, me),
                device_id_type=MESH_IDS,
            )
            incoming.wait_recv()
    for copy in sends:
        copy.wait_send()


def blk_stage(part, resid, gain, final, packed=None):
    n_blk = lax.axis_size("blk")
    rows, width = resid.shape
    vmem = pl.BlockSpec(memory_space=pltpu.VMEM)
    extra = packed is not None
    outs = [
        jax.ShapeDtypeStruct((rows, width), jnp.float32),
        jax.ShapeDtypeStruct((rows * n_blk, width), jnp.bfloat16),
    ]
    n_grp = n_blk // 2
    scratch = [
        pltpu.VMEM((n_grp, rows, width), part.dtype),
        pltpu.VMEM((n_grp, rows, width), part.dtype),
        pltpu.VMEM((n_grp, rows, width), part.dtype),
        pltpu.SemaphoreType.DMA((n_grp,)),
        pltpu.SemaphoreType.DMA((n_grp,)),
        pltpu.SemaphoreType.DMA((n_grp,)),
        pltpu.SemaphoreType.DMA((n_grp,)),
        pltpu.SemaphoreType.DMA((n_blk,)),
        pltpu.SemaphoreType.DMA((n_blk,)),
    ]
    args = [part, resid, gain[None, :]]
    if extra:
        n_req = lax.axis_size("req")
        outs.append(jax.ShapeDtypeStruct((n_req,) + packed.shape, packed.dtype))
        scratch += [pltpu.SemaphoreType.DMA((n_req,)), pltpu.SemaphoreType.DMA((n_req,))]
        args.append(packed)
    return pl.pallas_call(
        functools.partial(stage_kernel, n_blk, final, extra),
        out_shape=tuple(outs),
        in_specs=[vmem] * len(args),
        out_specs=tuple([vmem] * len(outs)),
        scratch_shapes=scratch,
        compiler_params=pltpu.CompilerParams(
            collective_id=5 if extra else (4 if final else 3), has_side_effects=True
        ),
    )(*args)


def cross_kernel(n_req, spans, len_ref, normed_ref, enc_ref, w_ref, out_ref):
    enc_len = len_ref[0]
    (q_at, q_len), (kv_at, kv_len), (o_at, o_len) = spans
    nt = (((1,), (1,)), ((), ()))
    width = w_ref.shape[2]
    queries = None
    pair = None
    for r in range(n_req):
        cols = slice(r * width, (r + 1) * width)
        term = lax.dot_general(
            normed_ref[:, cols], w_ref[r, q_at : q_at + q_len, :], nt,
            preferred_element_type=jnp.float32,
        )
        queries = term if queries is None else queries + term
        term = lax.dot_general(
            enc_ref[:, cols], w_ref[r, kv_at : kv_at + kv_len, :], nt,
            preferred_element_type=jnp.float32,
        )
        pair = term if pair is None else pair + term
    queries = queries.astype(jnp.bfloat16)
    pair = pair.astype(jnp.bfloat16)
    keys = pair[:, :HD]
    values = pair[:, HD:]
    scores = lax.dot_general(queries, keys, nt, preferred_element_type=jnp.float32)
    col = lax.broadcasted_iota(jnp.int32, scores.shape, 1)
    scores = jnp.where(col < enc_len, scores, NEG_FILL)
    top = jnp.max(scores, axis=1, keepdims=True)
    weights = jnp.exp(scores - top)
    weights = (weights / jnp.sum(weights, axis=1, keepdims=True)).astype(jnp.bfloat16)
    context = jnp.dot(weights, values, preferred_element_type=jnp.float32).astype(jnp.bfloat16)
    for r in range(n_req):
        out_ref[:, r * width : (r + 1) * width] = jnp.dot(
            context, w_ref[r, o_at : o_at + o_len, :], preferred_element_type=jnp.float32
        ).astype(out_ref.dtype)


def ffn_kernel(n_req, spans, normed_ref, w_ref, out_ref):
    (i_at, i_len), (o_at, o_len) = spans
    nt = (((1,), (1,)), ((), ()))
    width = w_ref.shape[2]
    ff_dev = o_len
    gate_up = None
    for r in range(n_req):
        term = lax.dot_general(
            normed_ref[:, r * width : (r + 1) * width], w_ref[r, i_at : i_at + i_len, :], nt,
            preferred_element_type=jnp.float32,
        )
        gate_up = term if gate_up is None else gate_up + term
    hidden = (jax.nn.gelu(gate_up[:, :ff_dev], approximate=True) * gate_up[:, ff_dev:]).astype(
        jnp.bfloat16
    )
    for r in range(n_req):
        out_ref[:, r * width : (r + 1) * width] = jnp.dot(
            hidden, w_ref[r, o_at : o_at + o_len, :], preferred_element_type=jnp.float32
        ).astype(out_ref.dtype)


def block_spans(pieces):
    spans, at = [], 0
    for w, axis in pieces:
        rows = w.size // w.shape[0] if axis == 0 else w.shape[0]
        spans.append((at, rows))
        at += rows
    return spans


def cross_branch(normed, enc, blocks, spans, enc_len):
    vmem = pl.BlockSpec(memory_space=pltpu.VMEM)
    return pl.pallas_call(
        functools.partial(cross_kernel, blocks.shape[0], tuple(spans)),
        out_shape=jax.ShapeDtypeStruct(normed.shape, jnp.bfloat16),
        in_specs=[pl.BlockSpec(memory_space=pltpu.SMEM)] + [vmem] * 3,
        out_specs=vmem,
    )(enc_len.reshape(1).astype(jnp.int32), normed, enc, blocks)


def ffn_branch(normed, blocks, spans):
    vmem = pl.BlockSpec(memory_space=pltpu.VMEM)
    return pl.pallas_call(
        functools.partial(ffn_kernel, blocks.shape[0], tuple(spans)),
        out_shape=jax.ShapeDtypeStruct(normed.shape, jnp.bfloat16),
        in_specs=[vmem] * 2,
        out_specs=vmem,
    )(normed, blocks)


def self_kernel(lens_ref, q_ref, c_ref, kn_ref, vn_ref, g_ref, f_ref, o_ref):
    old_len = lens_ref[0]
    fresh_len = lens_ref[1]
    n_q = q_ref.shape[0]
    n_ctx = c_ref.shape[0]
    wide_old = n_ctx + TQ
    wide_new = n_q + TQ
    k_old = c_ref[:, :HD]
    v_old = c_ref[:, HD:]
    k_new = kn_ref[...]
    v_new = vn_ref[...]
    dims = (((1,), (1,)), ((), ()))
    for t in range(n_q // TQ):
        q = q_ref[t * TQ : (t + 1) * TQ, :]
        start = n_q - TQ - t * TQ
        s_old = lax.dot_general(q, k_old, dims, preferred_element_type=jnp.float32)
        line = jnp.broadcast_to(g_ref[:, start : start + wide_old], (TQ, wide_old))
        bias = pltpu.roll(line, wide_old - (TQ - 1), 1, stride=1, stride_axis=0)[:, :n_ctx]
        col = lax.broadcasted_iota(jnp.int32, (TQ, n_ctx), 1)
        s_old = jnp.where(col < old_len, s_old + bias, NEG_FILL)
        s_new = lax.dot_general(q, k_new, dims, preferred_element_type=jnp.float32)
        line = jnp.broadcast_to(f_ref[:, start : start + wide_new], (TQ, wide_new))
        bias = pltpu.roll(line, wide_new - (TQ - 1), 1, stride=1, stride_axis=0)[:, :n_q]
        row = lax.broadcasted_iota(jnp.int32, (TQ, n_q), 0) + t * TQ
        col = lax.broadcasted_iota(jnp.int32, (TQ, n_q), 1)
        s_new = jnp.where((col <= row) & (col < fresh_len), s_new + bias, NEG_FILL)
        top = jnp.maximum(
            jnp.max(s_old, axis=1, keepdims=True), jnp.max(s_new, axis=1, keepdims=True)
        )
        p_old = jnp.exp(s_old - top)
        p_new = jnp.exp(s_new - top)
        total = jnp.sum(p_old, axis=1, keepdims=True) + jnp.sum(p_new, axis=1, keepdims=True)
        w_old = (p_old / total).astype(jnp.bfloat16)
        w_new = (p_new / total).astype(jnp.bfloat16)
        out = jnp.dot(w_old, v_old, preferred_element_type=jnp.float32) + jnp.dot(
            w_new, v_new, preferred_element_type=jnp.float32
        )
        o_ref[t * TQ : (t + 1) * TQ, :] = out.astype(jnp.bfloat16)


def bias_lines(line, old_len, n_q, n_ctx):
    span = line.shape[0]
    ext = jnp.concatenate([jnp.broadcast_to(line[:1], (n_ctx,)), line])
    rev = ext[::-1]
    g = lax.dynamic_slice_in_dim(rev, n_ctx - old_len, span)
    f = rev[n_ctx : n_ctx + 2 * n_q]
    return g[None, :], f[None, :]


def self_attention(q, cache_blk, k_new, v_new, line, old_len, fresh_len):
    n_q = q.shape[0]
    n_ctx = cache_blk.shape[0]
    g, f = bias_lines(line, old_len, n_q, n_ctx)
    lens = jnp.stack([old_len, fresh_len]).astype(jnp.int32)
    vmem = pl.BlockSpec(memory_space=pltpu.VMEM)
    return pl.pallas_call(
        self_kernel,
        out_shape=jax.ShapeDtypeStruct((n_q, HD), jnp.bfloat16),
        in_specs=[pl.BlockSpec(memory_space=pltpu.SMEM)] + [vmem] * 6,
        out_specs=vmem,
        compiler_params=pltpu.CompilerParams(vmem_limit_bytes=48 * 1024 * 1024),
    )(lens, q, cache_blk, k_new, v_new, g, f)


def pack_gather(pieces):
    flat = jnp.concatenate([w.reshape(-1) for w, _ in pieces])
    whole = lax.all_gather(flat, "req", axis=0, tiled=False)
    n_req = whole.shape[0]
    out, at = [], 0
    for w, axis in pieces:
        size = w.size
        part = whole[:, at : at + size].reshape((n_req,) + w.shape)
        at += size
        part = jnp.moveaxis(part, 0, axis)
        shape = list(w.shape)
        shape[axis] *= n_req
        out.append(part.reshape(shape))
    return out


MESH_IDS = pl.DeviceIdType.MESH


def greet_all(n_blk, me, req):
    barrier = pltpu.get_barrier_semaphore()
    for k in range(1, n_blk):
        peer = lax.rem(me + k, n_blk)
        pl.semaphore_signal(barrier, inc=1, device_id=(req, peer), device_id_type=MESH_IDS)
    pl.semaphore_wait(barrier, n_blk - 1)


def chunk_of(b, n_blk):
    return lax.rem(b, 2) * (n_blk // 2) + b // 2


def scatter_kernel(n_blk, part_ref, out_ref, recv, send_sem, recv_sem):
    me = lax.axis_index("blk")
    req = lax.axis_index("req")
    rows = out_ref.shape[0]
    greet_all(n_blk, me, req)
    copies = []
    for k in range(1, n_blk):
        peer = lax.rem(me + k, n_blk)
        copy = pltpu.make_async_remote_copy(
            src_ref=part_ref.at[pl.ds(pl.multiple_of(chunk_of(peer, n_blk) * rows, rows), rows)],
            dst_ref=recv.at[me],
            send_sem=send_sem.at[peer],
            recv_sem=recv_sem.at[me],
            device_id=(req, peer),
            device_id_type=MESH_IDS,
        )
        copy.start()
        copies.append(copy)
    own = pl.ds(pl.multiple_of(chunk_of(me, n_blk) * rows, rows), rows)
    total = part_ref[own, :].astype(jnp.float32)
    for k in range(1, n_blk):
        src = lax.rem(me + n_blk - k, n_blk)
        incoming = pltpu.make_async_remote_copy(
            src_ref=part_ref.at[pl.ds(0, rows)],
            dst_ref=recv.at[src],
            send_sem=send_sem.at[src],
            recv_sem=recv_sem.at[src],
            device_id=(req, src),
            device_id_type=MESH_IDS,
        )
        incoming.wait_recv()
        total = total + recv[src].astype(jnp.float32)
    for copy in copies:
        copy.wait_send()
    out_ref[...] = total


def gather_kernel(n_blk, piece_ref, out_ref, send_sem, recv_sem):
    b = lax.axis_index("blk")
    req = lax.axis_index("req")
    n_grp = n_blk // 2
    g = b // 2
    c = lax.rem(b, 2)
    partner = g * 2 + 1 - c
    rows = piece_ref.shape[0]
    half = n_grp * rows
    barrier = pltpu.get_barrier_semaphore()
    for k in range(1, n_grp):
        peer = lax.rem(g + k, n_grp) * 2 + c
        pl.semaphore_signal(barrier, inc=1, device_id=(req, peer), device_id_type=MESH_IDS)
    pl.semaphore_signal(barrier, inc=1, device_id=(req, partner), device_id_type=MESH_IDS)
    pl.semaphore_wait(barrier, n_grp)
    mine = pl.ds(pl.multiple_of(c * half + g * rows, rows), rows)
    sends = []
    for k in range(1, n_grp):
        peer = lax.rem(g + k, n_grp) * 2 + c
        copy = pltpu.make_async_remote_copy(
            src_ref=piece_ref,
            dst_ref=out_ref.at[mine],
            send_sem=send_sem.at[k],
            recv_sem=recv_sem.at[g],
            device_id=(req, peer),
            device_id_type=MESH_IDS,
        )
        copy.start()
        sends.append(copy)
    copy = pltpu.make_async_remote_copy(
        src_ref=piece_ref,
        dst_ref=out_ref.at[mine],
        send_sem=send_sem.at[0],
        recv_sem=recv_sem.at[n_grp + g],
        device_id=(req, partner),
        device_id_type=MESH_IDS,
    )
    copy.start()
    sends.append(copy)
    out_ref[mine, :] = piece_ref[...]
    for k in range(1, n_grp):
        grp = lax.rem(g + n_grp - k, n_grp)
        there = pl.ds(pl.multiple_of(c * half + grp * rows, rows), rows)
        incoming = pltpu.make_async_remote_copy(
            src_ref=piece_ref,
            dst_ref=out_ref.at[there],
            send_sem=send_sem.at[0],
            recv_sem=recv_sem.at[grp],
            device_id=(req, grp * 2 + c),
            device_id_type=MESH_IDS,
        )
        incoming.wait_recv()
        forward = pltpu.make_async_remote_copy(
            src_ref=out_ref.at[there],
            dst_ref=out_ref.at[there],
            send_sem=send_sem.at[n_grp + k],
            recv_sem=recv_sem.at[n_grp + grp],
            device_id=(req, partner),
            device_id_type=MESH_IDS,
        )
        forward.start()
        sends.append(forward)
    for grp in range(n_grp):
        there = pl.ds(pl.multiple_of((1 - c) * half + grp * rows, rows), rows)
        incoming = pltpu.make_async_remote_copy(
            src_ref=piece_ref,
            dst_ref=out_ref.at[there],
            send_sem=send_sem.at[0],
            recv_sem=recv_sem.at[n_grp + grp],
            device_id=(req, partner),
            device_id_type=MESH_IDS,
        )
        incoming.wait_recv()
    for copy in sends:
        copy.wait_send()


def blk_scatter(part):
    n_blk = lax.axis_size("blk")
    rows = part.shape[0] // n_blk
    vmem = pl.BlockSpec(memory_space=pltpu.VMEM)
    return pl.pallas_call(
        functools.partial(scatter_kernel, n_blk),
        out_shape=jax.ShapeDtypeStruct((rows, part.shape[1]), jnp.float32),
        in_specs=[vmem],
        out_specs=vmem,
        scratch_shapes=[
            pltpu.VMEM((n_blk, rows, part.shape[1]), part.dtype),
            pltpu.SemaphoreType.DMA((n_blk,)),
            pltpu.SemaphoreType.DMA((n_blk,)),
        ],
        compiler_params=pltpu.CompilerParams(collective_id=1, has_side_effects=True),
    )(part)


def blk_gather(piece):
    n_blk = lax.axis_size("blk")
    rows = piece.shape[0]
    vmem = pl.BlockSpec(memory_space=pltpu.VMEM)
    return pl.pallas_call(
        functools.partial(gather_kernel, n_blk),
        out_shape=jax.ShapeDtypeStruct((rows * n_blk, piece.shape[1]), piece.dtype),
        in_specs=[vmem],
        out_specs=vmem,
        scratch_shapes=[
            pltpu.SemaphoreType.DMA((n_blk,)),
            pltpu.SemaphoreType.DMA((n_blk,)),
        ],
        compiler_params=pltpu.CompilerParams(collective_id=2, has_side_effects=True),
    )(piece)


def prologue_kernel(n_req, n_blk, ordered_ref, packed_ref, cache_ref, wts_ref, w_send, w_recv, c_send, c_recv, local_sem):
    r = lax.axis_index("req")
    b = lax.axis_index("blk")
    n_slot, span, width = ordered_ref.shape
    piece = width // 2
    copies = []
    for k in range(1, n_req):
        peer = lax.rem(r + k, n_req)
        copy = pltpu.make_async_remote_copy(
            src_ref=packed_ref,
            dst_ref=wts_ref.at[r],
            send_sem=w_send.at[peer],
            recv_sem=w_recv.at[r],
            device_id=(peer, b),
            device_id_type=MESH_IDS,
        )
        copy.start()
        copies.append(copy)
    rows = pl.ds(pl.multiple_of(b * span, span), span)
    for k in range(n_slot):
        s = lax.rem(b + k, n_slot)
        for hh in range(2):
            head = 2 * r + hh
            is_self = jnp.logical_and(r == s, head == b)
            src = ordered_ref.at[s, :, pl.ds(hh * piece, piece)]
            copy = pltpu.make_async_remote_copy(
                src_ref=src,
                dst_ref=cache_ref.at[rows],
                send_sem=c_send.at[k * 2 + hh],
                recv_sem=c_recv.at[b],
                device_id=(s, head),
                device_id_type=MESH_IDS,
            )

            @pl.when(jnp.logical_not(is_self))
            def _():
                copy.start()

            @pl.when(is_self)
            def _():
                local = pltpu.make_async_copy(src, cache_ref.at[rows], local_sem.at[0])
                local.start()
                local.wait()

            copies.append((copy, is_self))
    wts_ref[r] = packed_ref[...]
    for k in range(1, n_req):
        src_req = lax.rem(r + n_req - k, n_req)
        incoming = pltpu.make_async_remote_copy(
            src_ref=packed_ref,
            dst_ref=wts_ref.at[src_req],
            send_sem=w_send.at[src_req],
            recv_sem=w_recv.at[src_req],
            device_id=(src_req, b),
            device_id_type=MESH_IDS,
        )
        incoming.wait_recv()
    owner = b // 2
    for j in range(n_blk):
        incoming = pltpu.make_async_remote_copy(
            src_ref=ordered_ref.at[0, :, pl.ds(0, piece)],
            dst_ref=cache_ref.at[pl.ds(j * span, span)],
            send_sem=c_send.at[0],
            recv_sem=c_recv.at[j],
            device_id=(owner, j),
            device_id_type=MESH_IDS,
        )

        @pl.when(jnp.logical_not(jnp.logical_and(owner == r, j == b)))
        def _():
            incoming.wait_recv()

    for item in copies:
        if isinstance(item, tuple):
            copy, is_self = item

            @pl.when(jnp.logical_not(is_self))
            def _():
                copy.wait_send()

        else:
            item.wait_send()


def prologue(ordered, packed):
    n_req = lax.axis_size("req")
    n_blk = lax.axis_size("blk")
    n_slot, span, width = ordered.shape
    any_spec = pl.BlockSpec(memory_space=pl.ANY)
    vmem = pl.BlockSpec(memory_space=pltpu.VMEM)
    return pl.pallas_call(
        functools.partial(prologue_kernel, n_req, n_blk),
        out_shape=(
            jax.ShapeDtypeStruct((span * n_blk, width // 2), ordered.dtype),
            jax.ShapeDtypeStruct((n_req,) + packed.shape, packed.dtype),
        ),
        in_specs=[any_spec, vmem],
        out_specs=(any_spec, vmem),
        scratch_shapes=[
            pltpu.SemaphoreType.DMA((n_req,)),
            pltpu.SemaphoreType.DMA((n_req,)),
            pltpu.SemaphoreType.DMA((2 * n_slot,)),
            pltpu.SemaphoreType.DMA((n_blk,)),
            pltpu.SemaphoreType.DMA((1,)),
        ],
        compiler_params=pltpu.CompilerParams(has_side_effects=True),
    )(ordered, packed)


def unpack(whole, pieces):
    n_req = whole.shape[0]
    whole = whole.reshape(n_req, -1)
    out, at = [], 0
    for w, axis in pieces:
        size = w.size
        part = whole[:, at : at + size].reshape((n_req,) + w.shape)
        at += size
        part = jnp.moveaxis(part, 0, axis)
        shape = list(w.shape)
        shape[axis] *= n_req
        out.append(part.reshape(shape))
    return out


def lane_pack(pieces):
    blocks = []
    for w, axis in pieces:
        flat = w.reshape(w.shape[0], -1)
        blocks.append(flat.T if axis == 0 else flat)
    packed = jnp.concatenate(blocks, axis=0)
    return lax.all_gather(packed, "req", axis=0, tiled=False)


def per_device(
    new_states,
    encoder_out,
    cache_in,
    slot_order,
    new_lengths,
    cache_lengths,
    enc_lengths,
    bucket_of,
    rel_bias,
    norm_gain,
    self_q,
    self_kv,
    self_out,
    cross_q,
    cross_kv,
    cross_out,
    ff_in,
    ff_out,
):
    blk_count = lax.axis_size("blk")
    heads_dev = H // blk_count
    width_dev = heads_dev * HD
    req_dev = cache_in.shape[0] // lax.axis_size("req")
    own_slots = lax.dynamic_slice_in_dim(slot_order, lax.axis_index("req") * req_dev, req_dev, 0)
    slot_new = pick_lengths(new_lengths, own_slots)
    slot_old = pick_lengths(cache_lengths, own_slots)
    slot_enc = pick_lengths(enc_lengths, own_slots)
    ordered = jnp.take(cache_in, slot_order, axis=0)
    onehot = (bucket_of[:, None] == jnp.arange(rel_bias.shape[0], dtype=jnp.int32)[None, :]).astype(
        jnp.float32
    )
    own_bias = lax.dynamic_slice_in_dim(rel_bias, lax.axis_index("blk") * heads_dev, heads_dev, 1)
    bias_dist = jnp.dot(onehot, own_bias, precision=lax.Precision.HIGHEST).T
    early = [(self_q, 0), (self_kv, 0), (self_out, 1)]
    late = [(cross_q, 0), (cross_kv, 0), (cross_out, 1), (ff_in, 0), (ff_out, 1)]
    flat = jnp.concatenate([w.reshape(-1) for w, _ in early])
    cache_blk, whole = prologue(ordered, flat.reshape(-1, 128))
    cache_dec = cache_blk[None]
    gathered = unpack(whole, early)
    late_blocks = lane_pack(late)
    wq_self, wkv_self, wo_self = gathered
    n_blk = lax.axis_size("blk")
    rows_dev = new_states.shape[0] // n_blk
    own_rows = lax.dynamic_slice_in_dim(
        new_states, chunk_of(lax.axis_index("blk"), n_blk) * rows_dev, rows_dev, 0
    ).astype(jnp.float32)
    normed = rms_rows(new_states.astype(jnp.float32), norm_gain[0])
    self_cat = jnp.concatenate([wq_self, wkv_self.reshape(wkv_self.shape[0], -1)], axis=1)
    projected = jnp.dot(normed, self_cat, preferred_element_type=jnp.float32).astype(
        jnp.bfloat16
    )
    context = self_attention(
        projected[:, :HD],
        cache_dec[0],
        projected[:, HD : 2 * HD],
        projected[:, 2 * HD :],
        bias_dist[0],
        slot_old[0],
        slot_new[0],
    )
    part = jnp.dot(context, wo_self, preferred_element_type=jnp.float32).astype(jnp.bfloat16)
    residual, normed = blk_stage(part, own_rows, norm_gain[1], False)
    spans = block_spans(late)
    part = cross_branch(normed, encoder_out, late_blocks, spans[:3], slot_enc[0])
    residual, normed = blk_stage(part.astype(jnp.bfloat16), residual, norm_gain[2], False)
    part = ffn_branch(normed, late_blocks, spans[3:])
    _, layer_out = blk_stage(part, residual, norm_gain[2], True)
    return (layer_out, cache_dec)


def solution(mesh):
    in_specs = (
        P("req", None),
        P("req", None),
        P(None, "blk", "req"),
        P(),
        P(),
        P(),
        P(),
        P(),
        P(),
        P(),
        P("req", "blk"),
        P("req", None, "blk"),
        P("blk", "req"),
        P("req", "blk"),
        P("req", None, "blk"),
        P("blk", "req"),
        P("req", None, "blk"),
        P("blk", "req"),
    )
    out_specs = (P("req", None), P("req", None, "blk"))
    return jax.shard_map(
        per_device, mesh=mesh, in_specs=in_specs, out_specs=out_specs, check_vma=False
    )
```

```python
import functools

import jax
import jax.numpy as jnp
from jax import lax
from jax.sharding import PartitionSpec as P
from jax.experimental import pallas as pl
from jax.experimental.pallas import tpu as pltpu

H = 16
HD = 64


EPSILON = 1e-06
NEG_FILL = -1e30


def rms_rows(row_block, gain):
    mean_square = jnp.mean(row_block * row_block, axis=-1, keepdims=True)
    return (row_block * lax.rsqrt(mean_square + EPSILON) * gain).astype(jnp.bfloat16)


def softmax_rows(scores):
    row_top = jnp.max(scores, axis=-1, keepdims=True)
    weights = jnp.exp(scores - row_top)
    return (weights / jnp.sum(weights, axis=-1, keepdims=True)).astype(jnp.bfloat16)


def pick_lengths(table, own_slots):
    matches = own_slots[:, None] == jnp.arange(table.shape[0], dtype=jnp.int32)[None, :]
    return jnp.sum(jnp.where(matches, table[None, :], 0), axis=1)


def shifted_bias(bias_dist, base, row_count, col_count):
    heads_here, span_len = bias_dist.shape
    line_len = row_count + col_count - 1
    steps = jnp.arange(line_len + 1, dtype=jnp.int32)
    line = bias_dist[:, jnp.clip(base + row_count - 1 - steps, 0, span_len - 1)]
    tiled = jnp.broadcast_to(line[:, None, :], (heads_here, row_count, line_len + 1))
    flat = tiled.reshape(heads_here, row_count * (line_len + 1))[:, : row_count * line_len]
    skewed = flat.reshape(heads_here, row_count, line_len)
    return skewed[:, :, row_count - 1 : row_count - 1 + col_count]


def row_total(left, weight):
    term = jnp.dot(left, weight, preferred_element_type=jnp.float32)
    return lax.psum(term.astype(jnp.bfloat16), "blk").astype(jnp.float32)


def cached_scores(queries, key_rows, first_col, old_len, bias_dist):
    col_ids = first_col + jnp.arange(key_rows.shape[0], dtype=jnp.int32)[None, :]
    scores = jnp.einsum("qhe,khe->hqk", queries, key_rows, preferred_element_type=jnp.float32)
    scores = scores + shifted_bias(
        bias_dist, old_len - first_col, queries.shape[0], key_rows.shape[0]
    )
    return jnp.where((col_ids < old_len)[None], scores, NEG_FILL)


def fresh_scores(queries, fresh_keys, fresh_len, bias_dist):
    row_ids = jnp.arange(queries.shape[0], dtype=jnp.int32)[:, None]
    col_ids = jnp.arange(fresh_keys.shape[0], dtype=jnp.int32)[None, :]
    scores = jnp.einsum("qhe,khe->hqk", queries, fresh_keys, preferred_element_type=jnp.float32)
    scores = scores + shifted_bias(bias_dist, 0, queries.shape[0], fresh_keys.shape[0])
    admitted = (col_ids <= row_ids) & (col_ids < fresh_len)
    return jnp.where(admitted[None], scores, NEG_FILL)


def self_padded(
    queries, key_rows, value_rows, fresh_keys, fresh_values, old_len, fresh_len, bias_dist
):
    scores = jnp.concatenate(
        [
            cached_scores(queries, key_rows, 0, old_len, bias_dist),
            fresh_scores(queries, fresh_keys, fresh_len, bias_dist),
        ],
        axis=2,
    )
    weights = softmax_rows(scores)
    value_all = jnp.concatenate([value_rows, fresh_values], axis=0)
    return jnp.einsum(
        "hqk,khe->qhe", weights, value_all, preferred_element_type=jnp.float32
    ).astype(jnp.bfloat16)


def self_attend(queries, key_value, cache_dec, slot_old, slot_new, bias_dist, heads_dev):
    req_dev, cache_len = (cache_dec.shape[0], cache_dec.shape[1])
    cache_split = cache_dec.reshape(req_dev, cache_len, heads_dev, 2, -1)

    def one_request(request):
        queries_one, pair_one, cache_one, old_len, fresh_len = request
        return self_padded(
            queries_one,
            cache_one[:, :, 0],
            cache_one[:, :, 1],
            pair_one[:, 0],
            pair_one[:, 1],
            old_len,
            fresh_len,
            bias_dist,
        )

    return lax.map(one_request, (queries, key_value, cache_split, slot_old, slot_new))


def cross_attend(queries, key_value, slot_enc):
    scores = jnp.einsum(
        "rqhe,rkhe->rhqk", queries, key_value[:, :, 0], preferred_element_type=jnp.float32
    )
    col_ids = jnp.arange(key_value.shape[1], dtype=jnp.int32)
    scores = jnp.where(
        col_ids[None, None, None, :] < slot_enc[:, None, None, None], scores, NEG_FILL
    )
    weights = softmax_rows(scores)
    return jnp.einsum(
        "rhqk,rkhe->rqhe", weights, key_value[:, :, 1], preferred_element_type=jnp.float32
    ).astype(jnp.bfloat16)


def add_branch(residual, left, weight, gain):
    residual = residual + row_total(left, weight)
    normed = rms_rows(residual, gain)
    return (residual, normed)


TQ = 128


def stage_kernel(n_blk, final, extra, *refs):
    if extra:
        (part_ref, resid_ref, gain_ref, packed_ref, res_out, full_ref, wts_ref,
         recv_a, send_b, recv_b, x_send, x_recv, b_send, b_recv, ag_send, ag_recv, w_send, w_recv) = refs
    else:
        (part_ref, resid_ref, gain_ref, res_out, full_ref,
         recv_a, send_b, recv_b, x_send, x_recv, b_send, b_recv, ag_send, ag_recv) = refs
    me = lax.axis_index("blk")
    req = lax.axis_index("req")
    rows = resid_ref.shape[0]
    n_grp = n_blk // 2
    g = me // 2
    c = lax.rem(me, 2)
    partner = g * 2 + 1 - c
    half = n_grp * rows
    n_req = wts_ref.shape[0] if extra else 1
    barrier = pltpu.get_barrier_semaphore()
    for k in range(1, n_grp):
        peer = lax.rem(g + k, n_grp) * 2 + c
        pl.semaphore_signal(barrier, inc=1, device_id=(req, peer), device_id_type=MESH_IDS)
    pl.semaphore_signal(barrier, inc=1, device_id=(req, partner), device_id_type=MESH_IDS)
    for k in range(1, n_req):
        peer = lax.rem(req + k, n_req)
        pl.semaphore_signal(barrier, inc=1, device_id=(peer, me), device_id_type=MESH_IDS)
    pl.semaphore_wait(barrier, n_grp + n_req - 1)
    sends = []
    for k in range(n_grp):
        grp = lax.rem(g + 1 + k, n_grp)
        exchange = pltpu.make_async_remote_copy(
            src_ref=part_ref.at[pl.ds(pl.multiple_of((1 - c) * half + grp * rows, rows), rows)],
            dst_ref=recv_a.at[grp],
            send_sem=x_send.at[k],
            recv_sem=x_recv.at[grp],
            device_id=(req, partner),
            device_id_type=MESH_IDS,
        )
        exchange.start()
        sends.append(exchange)
    for k in range(1, n_req):
        peer = lax.rem(req + k, n_req)
        copy = pltpu.make_async_remote_copy(
            src_ref=packed_ref,
            dst_ref=wts_ref.at[req],
            send_sem=w_send.at[peer],
            recv_sem=w_recv.at[req],
            device_id=(peer, me),
            device_id_type=MESH_IDS,
        )
        copy.start()
        sends.append(copy)
    total = None
    for k in range(n_grp):
        grp = lax.rem(g + 1 + k, n_grp)
        incoming = pltpu.make_async_remote_copy(
            src_ref=part_ref.at[pl.ds(0, rows)],
            dst_ref=recv_a.at[grp],
            send_sem=x_send.at[k],
            recv_sem=x_recv.at[grp],
            device_id=(req, partner),
            device_id_type=MESH_IDS,
        )
        incoming.wait_recv()
        pair = part_ref[pl.ds(pl.multiple_of(c * half + grp * rows, rows), rows), :].astype(
            jnp.float32
        ) + recv_a[grp].astype(jnp.float32)
        if k == n_grp - 1:
            total = pair
        else:
            send_b[grp] = pair.astype(send_b.dtype)
            copy = pltpu.make_async_remote_copy(
                src_ref=send_b.at[grp],
                dst_ref=recv_b.at[g],
                send_sem=b_send.at[grp],
                recv_sem=b_recv.at[g],
                device_id=(req, grp * 2 + c),
                device_id_type=MESH_IDS,
            )
            copy.start()
            sends.append(copy)
    for k in range(1, n_grp):
        grp = lax.rem(g + n_grp - k, n_grp)
        incoming = pltpu.make_async_remote_copy(
            src_ref=send_b.at[0],
            dst_ref=recv_b.at[grp],
            send_sem=b_send.at[grp],
            recv_sem=b_recv.at[grp],
            device_id=(req, grp * 2 + c),
            device_id_type=MESH_IDS,
        )
        incoming.wait_recv()
        total = total + recv_b[grp].astype(jnp.float32)
    mine = pl.ds(pl.multiple_of(c * half + g * rows, rows), rows)
    resid = resid_ref[...] + total
    res_out[...] = resid
    if final:
        full_ref[mine, :] = resid.astype(full_ref.dtype)
    else:
        mean_square = jnp.mean(resid * resid, axis=-1, keepdims=True)
        full_ref[mine, :] = (resid * lax.rsqrt(mean_square + EPSILON) * gain_ref[...]).astype(
            full_ref.dtype
        )
    for k in range(1, n_grp):
        peer = lax.rem(g + k, n_grp) * 2 + c
        copy = pltpu.make_async_remote_copy(
            src_ref=full_ref.at[mine],
            dst_ref=full_ref.at[mine],
            send_sem=ag_send.at[k],
            recv_sem=ag_recv.at[g],
            device_id=(req, peer),
            device_id_type=MESH_IDS,
        )
        copy.start()
        sends.append(copy)
    copy = pltpu.make_async_remote_copy(
        src_ref=full_ref.at[mine],
        dst_ref=full_ref.at[mine],
        send_sem=ag_send.at[0],
        recv_sem=ag_recv.at[n_grp + g],
        device_id=(req, partner),
        device_id_type=MESH_IDS,
    )
    copy.start()
    sends.append(copy)
    for k in range(1, n_grp):
        grp = lax.rem(g + n_grp - k, n_grp)
        there = pl.ds(pl.multiple_of(c * half + grp * rows, rows), rows)
        incoming = pltpu.make_async_remote_copy(
            src_ref=full_ref.at[there],
            dst_ref=full_ref.at[there],
            send_sem=ag_send.at[0],
            recv_sem=ag_recv.at[grp],
            device_id=(req, grp * 2 + c),
            device_id_type=MESH_IDS,
        )
        incoming.wait_recv()
        forward = pltpu.make_async_remote_copy(
            src_ref=full_ref.at[there],
            dst_ref=full_ref.at[there],
            send_sem=ag_send.at[n_grp + k],
            recv_sem=ag_recv.at[n_grp + grp],
            device_id=(req, partner),
            device_id_type=MESH_IDS,
        )
        forward.start()
        sends.append(forward)
    for grp in range(n_grp):
        there = pl.ds(pl.multiple_of((1 - c) * half + grp * rows, rows), rows)
        incoming = pltpu.make_async_remote_copy(
            src_ref=full_ref.at[there],
            dst_ref=full_ref.at[there],
            send_sem=ag_send.at[0],
            recv_sem=ag_recv.at[n_grp + grp],
            device_id=(req, partner),
            device_id_type=MESH_IDS,
        )
        incoming.wait_recv()
    if extra:
        wts_ref[req] = packed_ref[...]
        for k in range(1, n_req):
            src = lax.rem(req + n_req - k, n_req)
            incoming = pltpu.make_async_remote_copy(
                src_ref=packed_ref,
                dst_ref=wts_ref.at[src],
                send_sem=w_send.at[src],
                recv_sem=w_recv.at[src],
                device_id=(src, me),
                device_id_type=MESH_IDS,
            )
            incoming.wait_recv()
    for copy in sends:
        copy.wait_send()


def blk_stage(part, resid, gain, final, packed=None):
    n_blk = lax.axis_size("blk")
    rows, width = resid.shape
    vmem = pl.BlockSpec(memory_space=pltpu.VMEM)
    extra = packed is not None
    outs = [
        jax.ShapeDtypeStruct((rows, width), jnp.float32),
        jax.ShapeDtypeStruct((rows * n_blk, width), jnp.bfloat16),
    ]
    n_grp = n_blk // 2
    scratch = [
        pltpu.VMEM((n_grp, rows, width), part.dtype),
        pltpu.VMEM((n_grp, rows, width), part.dtype),
        pltpu.VMEM((n_grp, rows, width), part.dtype),
        pltpu.SemaphoreType.DMA((n_grp,)),
        pltpu.SemaphoreType.DMA((n_grp,)),
        pltpu.SemaphoreType.DMA((n_grp,)),
        pltpu.SemaphoreType.DMA((n_grp,)),
        pltpu.SemaphoreType.DMA((n_blk,)),
        pltpu.SemaphoreType.DMA((n_blk,)),
    ]
    args = [part, resid, gain[None, :]]
    if extra:
        n_req = lax.axis_size("req")
        outs.append(jax.ShapeDtypeStruct((n_req,) + packed.shape, packed.dtype))
        scratch += [pltpu.SemaphoreType.DMA((n_req,)), pltpu.SemaphoreType.DMA((n_req,))]
        args.append(packed)
    return pl.pallas_call(
        functools.partial(stage_kernel, n_blk, final, extra),
        out_shape=tuple(outs),
        in_specs=[vmem] * len(args),
        out_specs=tuple([vmem] * len(outs)),
        scratch_shapes=scratch,
        compiler_params=pltpu.CompilerParams(
            collective_id=5 if extra else (4 if final else 3), has_side_effects=True
        ),
    )(*args)


def cross_kernel(n_req, spans, len_ref, normed_ref, enc_ref, w_ref, out_ref):
    enc_len = len_ref[0]
    (q_at, q_len), (kv_at, kv_len), (o_at, o_len) = spans
    nt = (((1,), (1,)), ((), ()))
    width = w_ref.shape[2]
    queries = None
    pair = None
    for r in range(n_req):
        cols = slice(r * width, (r + 1) * width)
        term = lax.dot_general(
            normed_ref[:, cols], w_ref[r, q_at : q_at + q_len, :], nt,
            preferred_element_type=jnp.float32,
        )
        queries = term if queries is None else queries + term
        term = lax.dot_general(
            enc_ref[:, cols], w_ref[r, kv_at : kv_at + kv_len, :], nt,
            preferred_element_type=jnp.float32,
        )
        pair = term if pair is None else pair + term
    queries = queries.astype(jnp.bfloat16)
    pair = pair.astype(jnp.bfloat16)
    keys = pair[:, :HD]
    values = pair[:, HD:]
    scores = lax.dot_general(queries, keys, nt, preferred_element_type=jnp.float32)
    col = lax.broadcasted_iota(jnp.int32, scores.shape, 1)
    scores = jnp.where(col < enc_len, scores, NEG_FILL)
    top = jnp.max(scores, axis=1, keepdims=True)
    weights = jnp.exp(scores - top)
    weights = (weights / jnp.sum(weights, axis=1, keepdims=True)).astype(jnp.bfloat16)
    context = jnp.dot(weights, values, preferred_element_type=jnp.float32).astype(jnp.bfloat16)
    for r in range(n_req):
        out_ref[:, r * width : (r + 1) * width] = jnp.dot(
            context, w_ref[r, o_at : o_at + o_len, :], preferred_element_type=jnp.float32
        ).astype(out_ref.dtype)


def ffn_kernel(n_req, spans, normed_ref, w_ref, out_ref):
    (i_at, i_len), (o_at, o_len) = spans
    nt = (((1,), (1,)), ((), ()))
    width = w_ref.shape[2]
    ff_dev = o_len
    gate_up = None
    for r in range(n_req):
        term = lax.dot_general(
            normed_ref[:, r * width : (r + 1) * width], w_ref[r, i_at : i_at + i_len, :], nt,
            preferred_element_type=jnp.float32,
        )
        gate_up = term if gate_up is None else gate_up + term
    hidden = (jax.nn.gelu(gate_up[:, :ff_dev], approximate=True) * gate_up[:, ff_dev:]).astype(
        jnp.bfloat16
    )
    for r in range(n_req):
        out_ref[:, r * width : (r + 1) * width] = jnp.dot(
            hidden, w_ref[r, o_at : o_at + o_len, :], preferred_element_type=jnp.float32
        ).astype(out_ref.dtype)


def block_spans(pieces):
    spans, at = [], 0
    for w, axis in pieces:
        rows = w.size // w.shape[0] if axis == 0 else w.shape[0]
        spans.append((at, rows))
        at += rows
    return spans


def cross_branch(normed, enc, blocks, spans, enc_len):
    vmem = pl.BlockSpec(memory_space=pltpu.VMEM)
    return pl.pallas_call(
        functools.partial(cross_kernel, blocks.shape[0], tuple(spans)),
        out_shape=jax.ShapeDtypeStruct(normed.shape, jnp.bfloat16),
        in_specs=[pl.BlockSpec(memory_space=pltpu.SMEM)] + [vmem] * 3,
        out_specs=vmem,
    )(enc_len.reshape(1).astype(jnp.int32), normed, enc, blocks)


def ffn_branch(normed, blocks, spans):
    vmem = pl.BlockSpec(memory_space=pltpu.VMEM)
    return pl.pallas_call(
        functools.partial(ffn_kernel, blocks.shape[0], tuple(spans)),
        out_shape=jax.ShapeDtypeStruct(normed.shape, jnp.bfloat16),
        in_specs=[vmem] * 2,
        out_specs=vmem,
    )(normed, blocks)


def self_kernel(lens_ref, q_ref, c_ref, kn_ref, vn_ref, g_ref, f_ref, o_ref):
    old_len = lens_ref[0]
    fresh_len = lens_ref[1]
    n_q = q_ref.shape[0]
    n_ctx = c_ref.shape[0]
    wide_old = n_ctx + TQ
    wide_new = n_q + TQ
    k_old = c_ref[:, :HD]
    v_old = c_ref[:, HD:]
    k_new = kn_ref[...]
    v_new = vn_ref[...]
    dims = (((1,), (1,)), ((), ()))
    for t in range(n_q // TQ):
        q = q_ref[t * TQ : (t + 1) * TQ, :]
        start = n_q - TQ - t * TQ
        s_old = lax.dot_general(q, k_old, dims, preferred_element_type=jnp.float32)
        line = jnp.broadcast_to(g_ref[:, start : start + wide_old], (TQ, wide_old))
        bias = pltpu.roll(line, wide_old - (TQ - 1), 1, stride=1, stride_axis=0)[:, :n_ctx]
        col = lax.broadcasted_iota(jnp.int32, (TQ, n_ctx), 1)
        s_old = jnp.where(col < old_len, s_old + bias, NEG_FILL)
        s_new = lax.dot_general(q, k_new, dims, preferred_element_type=jnp.float32)
        line = jnp.broadcast_to(f_ref[:, start : start + wide_new], (TQ, wide_new))
        bias = pltpu.roll(line, wide_new - (TQ - 1), 1, stride=1, stride_axis=0)[:, :n_q]
        row = lax.broadcasted_iota(jnp.int32, (TQ, n_q), 0) + t * TQ
        col = lax.broadcasted_iota(jnp.int32, (TQ, n_q), 1)
        s_new = jnp.where((col <= row) & (col < fresh_len), s_new + bias, NEG_FILL)
        top = jnp.maximum(
            jnp.max(s_old, axis=1, keepdims=True), jnp.max(s_new, axis=1, keepdims=True)
        )
        p_old = jnp.exp(s_old - top)
        p_new = jnp.exp(s_new - top)
        total = jnp.sum(p_old, axis=1, keepdims=True) + jnp.sum(p_new, axis=1, keepdims=True)
        w_old = (p_old / total).astype(jnp.bfloat16)
        w_new = (p_new / total).astype(jnp.bfloat16)
        out = jnp.dot(w_old, v_old, preferred_element_type=jnp.float32) + jnp.dot(
            w_new, v_new, preferred_element_type=jnp.float32
        )
        o_ref[t * TQ : (t + 1) * TQ, :] = out.astype(jnp.bfloat16)


def bias_lines(line, old_len, n_q, n_ctx):
    span = line.shape[0]
    ext = jnp.concatenate([jnp.broadcast_to(line[:1], (n_ctx,)), line])
    rev = ext[::-1]
    g = lax.dynamic_slice_in_dim(rev, n_ctx - old_len, span)
    f = rev[n_ctx : n_ctx + 2 * n_q]
    return g[None, :], f[None, :]


def self_attention(q, cache_blk, k_new, v_new, line, old_len, fresh_len):
    n_q = q.shape[0]
    n_ctx = cache_blk.shape[0]
    g, f = bias_lines(line, old_len, n_q, n_ctx)
    lens = jnp.stack([old_len, fresh_len]).astype(jnp.int32)
    vmem = pl.BlockSpec(memory_space=pltpu.VMEM)
    return pl.pallas_call(
        self_kernel,
        out_shape=jax.ShapeDtypeStruct((n_q, HD), jnp.bfloat16),
        in_specs=[pl.BlockSpec(memory_space=pltpu.SMEM)] + [vmem] * 6,
        out_specs=vmem,
        compiler_params=pltpu.CompilerParams(vmem_limit_bytes=48 * 1024 * 1024),
    )(lens, q, cache_blk, k_new, v_new, g, f)


def pack_gather(pieces):
    flat = jnp.concatenate([w.reshape(-1) for w, _ in pieces])
    whole = lax.all_gather(flat, "req", axis=0, tiled=False)
    n_req = whole.shape[0]
    out, at = [], 0
    for w, axis in pieces:
        size = w.size
        part = whole[:, at : at + size].reshape((n_req,) + w.shape)
        at += size
        part = jnp.moveaxis(part, 0, axis)
        shape = list(w.shape)
        shape[axis] *= n_req
        out.append(part.reshape(shape))
    return out


MESH_IDS = pl.DeviceIdType.MESH


def greet_all(n_blk, me, req):
    barrier = pltpu.get_barrier_semaphore()
    for k in range(1, n_blk):
        peer = lax.rem(me + k, n_blk)
        pl.semaphore_signal(barrier, inc=1, device_id=(req, peer), device_id_type=MESH_IDS)
    pl.semaphore_wait(barrier, n_blk - 1)


def chunk_of(b, n_blk):
    return lax.rem(b, 2) * (n_blk // 2) + b // 2


def scatter_kernel(n_blk, part_ref, out_ref, recv, send_sem, recv_sem):
    me = lax.axis_index("blk")
    req = lax.axis_index("req")
    rows = out_ref.shape[0]
    greet_all(n_blk, me, req)
    copies = []
    for k in range(1, n_blk):
        peer = lax.rem(me + k, n_blk)
        copy = pltpu.make_async_remote_copy(
            src_ref=part_ref.at[pl.ds(pl.multiple_of(chunk_of(peer, n_blk) * rows, rows), rows)],
            dst_ref=recv.at[me],
            send_sem=send_sem.at[peer],
            recv_sem=recv_sem.at[me],
            device_id=(req, peer),
            device_id_type=MESH_IDS,
        )
        copy.start()
        copies.append(copy)
    own = pl.ds(pl.multiple_of(chunk_of(me, n_blk) * rows, rows), rows)
    total = part_ref[own, :].astype(jnp.float32)
    for k in range(1, n_blk):
        src = lax.rem(me + n_blk - k, n_blk)
        incoming = pltpu.make_async_remote_copy(
            src_ref=part_ref.at[pl.ds(0, rows)],
            dst_ref=recv.at[src],
            send_sem=send_sem.at[src],
            recv_sem=recv_sem.at[src],
            device_id=(req, src),
            device_id_type=MESH_IDS,
        )
        incoming.wait_recv()
        total = total + recv[src].astype(jnp.float32)
    for copy in copies:
        copy.wait_send()
    out_ref[...] = total


def gather_kernel(n_blk, piece_ref, out_ref, send_sem, recv_sem):
    b = lax.axis_index("blk")
    req = lax.axis_index("req")
    n_grp = n_blk // 2
    g = b // 2
    c = lax.rem(b, 2)
    partner = g * 2 + 1 - c
    rows = piece_ref.shape[0]
    half = n_grp * rows
    barrier = pltpu.get_barrier_semaphore()
    for k in range(1, n_grp):
        peer = lax.rem(g + k, n_grp) * 2 + c
        pl.semaphore_signal(barrier, inc=1, device_id=(req, peer), device_id_type=MESH_IDS)
    pl.semaphore_signal(barrier, inc=1, device_id=(req, partner), device_id_type=MESH_IDS)
    pl.semaphore_wait(barrier, n_grp)
    mine = pl.ds(pl.multiple_of(c * half + g * rows, rows), rows)
    sends = []
    for k in range(1, n_grp):
        peer = lax.rem(g + k, n_grp) * 2 + c
        copy = pltpu.make_async_remote_copy(
            src_ref=piece_ref,
            dst_ref=out_ref.at[mine],
            send_sem=send_sem.at[k],
            recv_sem=recv_sem.at[g],
            device_id=(req, peer),
            device_id_type=MESH_IDS,
        )
        copy.start()
        sends.append(copy)
    copy = pltpu.make_async_remote_copy(
        src_ref=piece_ref,
        dst_ref=out_ref.at[mine],
        send_sem=send_sem.at[0],
        recv_sem=recv_sem.at[n_grp + g],
        device_id=(req, partner),
        device_id_type=MESH_IDS,
    )
    copy.start()
    sends.append(copy)
    out_ref[mine, :] = piece_ref[...]
    for k in range(1, n_grp):
        grp = lax.rem(g + n_grp - k, n_grp)
        there = pl.ds(pl.multiple_of(c * half + grp * rows, rows), rows)
        incoming = pltpu.make_async_remote_copy(
            src_ref=piece_ref,
            dst_ref=out_ref.at[there],
            send_sem=send_sem.at[0],
            recv_sem=recv_sem.at[grp],
            device_id=(req, grp * 2 + c),
            device_id_type=MESH_IDS,
        )
        incoming.wait_recv()
        forward = pltpu.make_async_remote_copy(
            src_ref=out_ref.at[there],
            dst_ref=out_ref.at[there],
            send_sem=send_sem.at[n_grp + k],
            recv_sem=recv_sem.at[n_grp + grp],
            device_id=(req, partner),
            device_id_type=MESH_IDS,
        )
        forward.start()
        sends.append(forward)
    for grp in range(n_grp):
        there = pl.ds(pl.multiple_of((1 - c) * half + grp * rows, rows), rows)
        incoming = pltpu.make_async_remote_copy(
            src_ref=piece_ref,
            dst_ref=out_ref.at[there],
            send_sem=send_sem.at[0],
            recv_sem=recv_sem.at[n_grp + grp],
            device_id=(req, partner),
            device_id_type=MESH_IDS,
        )
        incoming.wait_recv()
    for copy in sends:
        copy.wait_send()


def blk_scatter(part):
    n_blk = lax.axis_size("blk")
    rows = part.shape[0] // n_blk
    vmem = pl.BlockSpec(memory_space=pltpu.VMEM)
    return pl.pallas_call(
        functools.partial(scatter_kernel, n_blk),
        out_shape=jax.ShapeDtypeStruct((rows, part.shape[1]), jnp.float32),
        in_specs=[vmem],
        out_specs=vmem,
        scratch_shapes=[
            pltpu.VMEM((n_blk, rows, part.shape[1]), part.dtype),
            pltpu.SemaphoreType.DMA((n_blk,)),
            pltpu.SemaphoreType.DMA((n_blk,)),
        ],
        compiler_params=pltpu.CompilerParams(collective_id=1, has_side_effects=True),
    )(part)


def blk_gather(piece):
    n_blk = lax.axis_size("blk")
    rows = piece.shape[0]
    vmem = pl.BlockSpec(memory_space=pltpu.VMEM)
    return pl.pallas_call(
        functools.partial(gather_kernel, n_blk),
        out_shape=jax.ShapeDtypeStruct((rows * n_blk, piece.shape[1]), piece.dtype),
        in_specs=[vmem],
        out_specs=vmem,
        scratch_shapes=[
            pltpu.SemaphoreType.DMA((n_blk,)),
            pltpu.SemaphoreType.DMA((n_blk,)),
        ],
        compiler_params=pltpu.CompilerParams(collective_id=2, has_side_effects=True),
    )(piece)


def prologue_kernel(n_req, n_blk, ordered_ref, packed_ref, cache_ref, wts_ref, w_send, w_recv, c_send, c_recv, local_sem):
    r = lax.axis_index("req")
    b = lax.axis_index("blk")
    n_slot, span, width = ordered_ref.shape
    piece = width // 2
    copies = []
    for k in range(1, n_req):
        peer = lax.rem(r + k, n_req)
        copy = pltpu.make_async_remote_copy(
            src_ref=packed_ref,
            dst_ref=wts_ref.at[r],
            send_sem=w_send.at[peer],
            recv_sem=w_recv.at[r],
            device_id=(peer, b),
            device_id_type=MESH_IDS,
        )
        copy.start()
        copies.append(copy)
    rows = pl.ds(pl.multiple_of(b * span, span), span)
    for k in range(n_slot):
        s = lax.rem(b + k, n_slot)
        for hh in range(2):
            head = 2 * r + hh
            is_self = jnp.logical_and(r == s, head == b)
            src = ordered_ref.at[s, :, pl.ds(hh * piece, piece)]
            copy = pltpu.make_async_remote_copy(
                src_ref=src,
                dst_ref=cache_ref.at[rows],
                send_sem=c_send.at[k * 2 + hh],
                recv_sem=c_recv.at[b],
                device_id=(s, head),
                device_id_type=MESH_IDS,
            )

            @pl.when(jnp.logical_not(is_self))
            def _():
                copy.start()

            @pl.when(is_self)
            def _():
                local = pltpu.make_async_copy(src, cache_ref.at[rows], local_sem.at[0])
                local.start()
                local.wait()

            copies.append((copy, is_self))
    wts_ref[r] = packed_ref[...]
    for k in range(1, n_req):
        src_req = lax.rem(r + n_req - k, n_req)
        incoming = pltpu.make_async_remote_copy(
            src_ref=packed_ref,
            dst_ref=wts_ref.at[src_req],
            send_sem=w_send.at[src_req],
            recv_sem=w_recv.at[src_req],
            device_id=(src_req, b),
            device_id_type=MESH_IDS,
        )
        incoming.wait_recv()
    owner = b // 2
    for j in range(n_blk):
        incoming = pltpu.make_async_remote_copy(
            src_ref=ordered_ref.at[0, :, pl.ds(0, piece)],
            dst_ref=cache_ref.at[pl.ds(j * span, span)],
            send_sem=c_send.at[0],
            recv_sem=c_recv.at[j],
            device_id=(owner, j),
            device_id_type=MESH_IDS,
        )

        @pl.when(jnp.logical_not(jnp.logical_and(owner == r, j == b)))
        def _():
            incoming.wait_recv()

    for item in copies:
        if isinstance(item, tuple):
            copy, is_self = item

            @pl.when(jnp.logical_not(is_self))
            def _():
                copy.wait_send()

        else:
            item.wait_send()


def prologue(ordered, packed):
    n_req = lax.axis_size("req")
    n_blk = lax.axis_size("blk")
    n_slot, span, width = ordered.shape
    any_spec = pl.BlockSpec(memory_space=pl.ANY)
    vmem = pl.BlockSpec(memory_space=pltpu.VMEM)
    return pl.pallas_call(
        functools.partial(prologue_kernel, n_req, n_blk),
        out_shape=(
            jax.ShapeDtypeStruct((span * n_blk, width // 2), ordered.dtype),
            jax.ShapeDtypeStruct((n_req,) + packed.shape, packed.dtype),
        ),
        in_specs=[any_spec, vmem],
        out_specs=(any_spec, vmem),
        scratch_shapes=[
            pltpu.SemaphoreType.DMA((n_req,)),
            pltpu.SemaphoreType.DMA((n_req,)),
            pltpu.SemaphoreType.DMA((2 * n_slot,)),
            pltpu.SemaphoreType.DMA((n_blk,)),
            pltpu.SemaphoreType.DMA((1,)),
        ],
        compiler_params=pltpu.CompilerParams(has_side_effects=True),
    )(ordered, packed)


def unpack(whole, pieces):
    n_req = whole.shape[0]
    whole = whole.reshape(n_req, -1)
    out, at = [], 0
    for w, axis in pieces:
        size = w.size
        part = whole[:, at : at + size].reshape((n_req,) + w.shape)
        at += size
        part = jnp.moveaxis(part, 0, axis)
        shape = list(w.shape)
        shape[axis] *= n_req
        out.append(part.reshape(shape))
    return out


def lane_pack(pieces):
    blocks = []
    for w, axis in pieces:
        flat = w.reshape(w.shape[0], -1)
        blocks.append(flat.T if axis == 0 else flat)
    packed = jnp.concatenate(blocks, axis=0)
    return lax.all_gather(packed, "req", axis=0, tiled=False)


def per_device(
    new_states,
    encoder_out,
    cache_in,
    slot_order,
    new_lengths,
    cache_lengths,
    enc_lengths,
    bucket_of,
    rel_bias,
    norm_gain,
    self_q,
    self_kv,
    self_out,
    cross_q,
    cross_kv,
    cross_out,
    ff_in,
    ff_out,
):
    blk_count = lax.axis_size("blk")
    heads_dev = H // blk_count
    width_dev = heads_dev * HD
    req_dev = cache_in.shape[0] // lax.axis_size("req")
    own_slot = lax.dynamic_index_in_dim(slot_order, lax.axis_index("req"), 0, keepdims=False)
    tables = jnp.stack([new_lengths, cache_lengths, enc_lengths])
    picked = lax.dynamic_slice_in_dim(tables, own_slot, 1, 1)
    slot_new, slot_old, slot_enc = picked[0], picked[1], picked[2]
    ordered = jnp.take(cache_in, slot_order, axis=0)
    onehot = (bucket_of[:, None] == jnp.arange(rel_bias.shape[0], dtype=jnp.int32)[None, :]).astype(
        jnp.float32
    )
    own_bias = lax.dynamic_slice_in_dim(rel_bias, lax.axis_index("blk") * heads_dev, heads_dev, 1)
    bias_dist = jnp.dot(onehot, own_bias, precision=lax.Precision.HIGHEST).T
    early = [(self_q, 0), (self_kv, 0), (self_out, 1)]
    late = [(cross_q, 0), (cross_kv, 0), (cross_out, 1), (ff_in, 0), (ff_out, 1)]
    flat = jnp.concatenate([w.reshape(-1) for w, _ in early])
    cache_blk, whole = prologue(ordered, flat.reshape(-1, 128))
    cache_dec = cache_blk[None]
    gathered = unpack(whole, early)
    late_blocks = lane_pack(late)
    wq_self, wkv_self, wo_self = gathered
    n_blk = lax.axis_size("blk")
    rows_dev = new_states.shape[0] // n_blk
    own_rows = lax.dynamic_slice_in_dim(
        new_states, chunk_of(lax.axis_index("blk"), n_blk) * rows_dev, rows_dev, 0
    ).astype(jnp.float32)
    normed = rms_rows(new_states.astype(jnp.float32), norm_gain[0])
    self_cat = jnp.concatenate([wq_self, wkv_self.reshape(wkv_self.shape[0], -1)], axis=1)
    projected = jnp.dot(normed, self_cat, preferred_element_type=jnp.float32).astype(
        jnp.bfloat16
    )
    context = self_attention(
        projected[:, :HD],
        cache_dec[0],
        projected[:, HD : 2 * HD],
        projected[:, 2 * HD :],
        bias_dist[0],
        slot_old[0],
        slot_new[0],
    )
    part = jnp.dot(context, wo_self, preferred_element_type=jnp.float32).astype(jnp.bfloat16)
    residual, normed = blk_stage(part, own_rows, norm_gain[1], False)
    spans = block_spans(late)
    part = cross_branch(normed, encoder_out, late_blocks, spans[:3], slot_enc[0])
    residual, normed = blk_stage(part.astype(jnp.bfloat16), residual, norm_gain[2], False)
    part = ffn_branch(normed, late_blocks, spans[3:])
    _, layer_out = blk_stage(part, residual, norm_gain[2], True)
    return (layer_out, cache_dec)


def solution(mesh):
    in_specs = (
        P("req", None),
        P("req", None),
        P(None, "blk", "req"),
        P(),
        P(),
        P(),
        P(),
        P(),
        P(),
        P(),
        P("req", "blk"),
        P("req", None, "blk"),
        P("blk", "req"),
        P("req", "blk"),
        P("req", None, "blk"),
        P("blk", "req"),
        P("req", None, "blk"),
        P("blk", "req"),
    )
    out_specs = (P("req", None), P("req", None, "blk"))
    return jax.shard_map(
        per_device, mesh=mesh, in_specs=in_specs, out_specs=out_specs, check_vma=False
    )
```

```python
import functools

import jax
import jax.numpy as jnp
from jax import lax
from jax.sharding import PartitionSpec as P
from jax.experimental import pallas as pl
from jax.experimental.pallas import tpu as pltpu

H = 16
HD = 64


EPSILON = 1e-06
NEG_FILL = -1e30


def rms_rows(row_block, gain):
    mean_square = jnp.mean(row_block * row_block, axis=-1, keepdims=True)
    return (row_block * lax.rsqrt(mean_square + EPSILON) * gain).astype(jnp.bfloat16)


def softmax_rows(scores):
    row_top = jnp.max(scores, axis=-1, keepdims=True)
    weights = jnp.exp(scores - row_top)
    return (weights / jnp.sum(weights, axis=-1, keepdims=True)).astype(jnp.bfloat16)


def pick_lengths(table, own_slots):
    matches = own_slots[:, None] == jnp.arange(table.shape[0], dtype=jnp.int32)[None, :]
    return jnp.sum(jnp.where(matches, table[None, :], 0), axis=1)


def shifted_bias(bias_dist, base, row_count, col_count):
    heads_here, span_len = bias_dist.shape
    line_len = row_count + col_count - 1
    steps = jnp.arange(line_len + 1, dtype=jnp.int32)
    line = bias_dist[:, jnp.clip(base + row_count - 1 - steps, 0, span_len - 1)]
    tiled = jnp.broadcast_to(line[:, None, :], (heads_here, row_count, line_len + 1))
    flat = tiled.reshape(heads_here, row_count * (line_len + 1))[:, : row_count * line_len]
    skewed = flat.reshape(heads_here, row_count, line_len)
    return skewed[:, :, row_count - 1 : row_count - 1 + col_count]


def row_total(left, weight):
    term = jnp.dot(left, weight, preferred_element_type=jnp.float32)
    return lax.psum(term.astype(jnp.bfloat16), "blk").astype(jnp.float32)


def cached_scores(queries, key_rows, first_col, old_len, bias_dist):
    col_ids = first_col + jnp.arange(key_rows.shape[0], dtype=jnp.int32)[None, :]
    scores = jnp.einsum("qhe,khe->hqk", queries, key_rows, preferred_element_type=jnp.float32)
    scores = scores + shifted_bias(
        bias_dist, old_len - first_col, queries.shape[0], key_rows.shape[0]
    )
    return jnp.where((col_ids < old_len)[None], scores, NEG_FILL)


def fresh_scores(queries, fresh_keys, fresh_len, bias_dist):
    row_ids = jnp.arange(queries.shape[0], dtype=jnp.int32)[:, None]
    col_ids = jnp.arange(fresh_keys.shape[0], dtype=jnp.int32)[None, :]
    scores = jnp.einsum("qhe,khe->hqk", queries, fresh_keys, preferred_element_type=jnp.float32)
    scores = scores + shifted_bias(bias_dist, 0, queries.shape[0], fresh_keys.shape[0])
    admitted = (col_ids <= row_ids) & (col_ids < fresh_len)
    return jnp.where(admitted[None], scores, NEG_FILL)


def self_padded(
    queries, key_rows, value_rows, fresh_keys, fresh_values, old_len, fresh_len, bias_dist
):
    scores = jnp.concatenate(
        [
            cached_scores(queries, key_rows, 0, old_len, bias_dist),
            fresh_scores(queries, fresh_keys, fresh_len, bias_dist),
        ],
        axis=2,
    )
    weights = softmax_rows(scores)
    value_all = jnp.concatenate([value_rows, fresh_values], axis=0)
    return jnp.einsum(
        "hqk,khe->qhe", weights, value_all, preferred_element_type=jnp.float32
    ).astype(jnp.bfloat16)


def self_attend(queries, key_value, cache_dec, slot_old, slot_new, bias_dist, heads_dev):
    req_dev, cache_len = (cache_dec.shape[0], cache_dec.shape[1])
    cache_split = cache_dec.reshape(req_dev, cache_len, heads_dev, 2, -1)

    def one_request(request):
        queries_one, pair_one, cache_one, old_len, fresh_len = request
        return self_padded(
            queries_one,
            cache_one[:, :, 0],
            cache_one[:, :, 1],
            pair_one[:, 0],
            pair_one[:, 1],
            old_len,
            fresh_len,
            bias_dist,
        )

    return lax.map(one_request, (queries, key_value, cache_split, slot_old, slot_new))


def cross_attend(queries, key_value, slot_enc):
    scores = jnp.einsum(
        "rqhe,rkhe->rhqk", queries, key_value[:, :, 0], preferred_element_type=jnp.float32
    )
    col_ids = jnp.arange(key_value.shape[1], dtype=jnp.int32)
    scores = jnp.where(
        col_ids[None, None, None, :] < slot_enc[:, None, None, None], scores, NEG_FILL
    )
    weights = softmax_rows(scores)
    return jnp.einsum(
        "rhqk,rkhe->rqhe", weights, key_value[:, :, 1], preferred_element_type=jnp.float32
    ).astype(jnp.bfloat16)


def add_branch(residual, left, weight, gain):
    residual = residual + row_total(left, weight)
    normed = rms_rows(residual, gain)
    return (residual, normed)


TQ = 128


def stage_kernel(n_blk, final, extra, *refs):
    if extra:
        (part_ref, resid_ref, gain_ref, packed_ref, res_out, full_ref, wts_ref,
         recv_a, send_b, recv_b, x_send, x_recv, b_send, b_recv, ag_send, ag_recv, w_send, w_recv) = refs
    else:
        (part_ref, resid_ref, gain_ref, res_out, full_ref,
         recv_a, send_b, recv_b, x_send, x_recv, b_send, b_recv, ag_send, ag_recv) = refs
    me = lax.axis_index("blk")
    req = lax.axis_index("req")
    rows = resid_ref.shape[0]
    n_grp = n_blk // 2
    g = me // 2
    c = lax.rem(me, 2)
    partner = g * 2 + 1 - c
    half = n_grp * rows
    n_req = wts_ref.shape[0] if extra else 1
    barrier = pltpu.get_barrier_semaphore()
    for k in range(1, n_grp):
        peer = lax.rem(g + k, n_grp) * 2 + c
        pl.semaphore_signal(barrier, inc=1, device_id=(req, peer), device_id_type=MESH_IDS)
    pl.semaphore_signal(barrier, inc=1, device_id=(req, partner), device_id_type=MESH_IDS)
    for k in range(1, n_req):
        peer = lax.rem(req + k, n_req)
        pl.semaphore_signal(barrier, inc=1, device_id=(peer, me), device_id_type=MESH_IDS)
    pl.semaphore_wait(barrier, n_grp + n_req - 1)
    sends = []
    for k in range(n_grp):
        grp = lax.rem(g + 1 + k, n_grp)
        exchange = pltpu.make_async_remote_copy(
            src_ref=part_ref.at[pl.ds(pl.multiple_of((1 - c) * half + grp * rows, rows), rows)],
            dst_ref=recv_a.at[grp],
            send_sem=x_send.at[k],
            recv_sem=x_recv.at[grp],
            device_id=(req, partner),
            device_id_type=MESH_IDS,
        )
        exchange.start()
        sends.append(exchange)
    for k in range(1, n_req):
        peer = lax.rem(req + k, n_req)
        copy = pltpu.make_async_remote_copy(
            src_ref=packed_ref,
            dst_ref=wts_ref.at[req],
            send_sem=w_send.at[peer],
            recv_sem=w_recv.at[req],
            device_id=(peer, me),
            device_id_type=MESH_IDS,
        )
        copy.start()
        sends.append(copy)
    total = None
    for k in range(n_grp):
        grp = lax.rem(g + 1 + k, n_grp)
        incoming = pltpu.make_async_remote_copy(
            src_ref=part_ref.at[pl.ds(0, rows)],
            dst_ref=recv_a.at[grp],
            send_sem=x_send.at[k],
            recv_sem=x_recv.at[grp],
            device_id=(req, partner),
            device_id_type=MESH_IDS,
        )
        incoming.wait_recv()
        pair = part_ref[pl.ds(pl.multiple_of(c * half + grp * rows, rows), rows), :].astype(
            jnp.float32
        ) + recv_a[grp].astype(jnp.float32)
        if k == n_grp - 1:
            total = pair
        else:
            send_b[grp] = pair.astype(send_b.dtype)
            copy = pltpu.make_async_remote_copy(
                src_ref=send_b.at[grp],
                dst_ref=recv_b.at[g],
                send_sem=b_send.at[grp],
                recv_sem=b_recv.at[g],
                device_id=(req, grp * 2 + c),
                device_id_type=MESH_IDS,
            )
            copy.start()
            sends.append(copy)
    for k in range(1, n_grp):
        grp = lax.rem(g + n_grp - k, n_grp)
        incoming = pltpu.make_async_remote_copy(
            src_ref=send_b.at[0],
            dst_ref=recv_b.at[grp],
            send_sem=b_send.at[grp],
            recv_sem=b_recv.at[grp],
            device_id=(req, grp * 2 + c),
            device_id_type=MESH_IDS,
        )
        incoming.wait_recv()
        total = total + recv_b[grp].astype(jnp.float32)
    mine = pl.ds(pl.multiple_of(c * half + g * rows, rows), rows)
    resid = resid_ref[...] + total
    res_out[...] = resid
    if final:
        full_ref[mine, :] = resid.astype(full_ref.dtype)
    else:
        mean_square = jnp.mean(resid * resid, axis=-1, keepdims=True)
        full_ref[mine, :] = (resid * lax.rsqrt(mean_square + EPSILON) * gain_ref[...]).astype(
            full_ref.dtype
        )
    for k in range(1, n_grp):
        peer = lax.rem(g + k, n_grp) * 2 + c
        copy = pltpu.make_async_remote_copy(
            src_ref=full_ref.at[mine],
            dst_ref=full_ref.at[mine],
            send_sem=ag_send.at[k],
            recv_sem=ag_recv.at[g],
            device_id=(req, peer),
            device_id_type=MESH_IDS,
        )
        copy.start()
        sends.append(copy)
    copy = pltpu.make_async_remote_copy(
        src_ref=full_ref.at[mine],
        dst_ref=full_ref.at[mine],
        send_sem=ag_send.at[0],
        recv_sem=ag_recv.at[n_grp + g],
        device_id=(req, partner),
        device_id_type=MESH_IDS,
    )
    copy.start()
    sends.append(copy)
    for k in range(1, n_grp):
        grp = lax.rem(g + n_grp - k, n_grp)
        there = pl.ds(pl.multiple_of(c * half + grp * rows, rows), rows)
        incoming = pltpu.make_async_remote_copy(
            src_ref=full_ref.at[there],
            dst_ref=full_ref.at[there],
            send_sem=ag_send.at[0],
            recv_sem=ag_recv.at[grp],
            device_id=(req, grp * 2 + c),
            device_id_type=MESH_IDS,
        )
        incoming.wait_recv()
        forward = pltpu.make_async_remote_copy(
            src_ref=full_ref.at[there],
            dst_ref=full_ref.at[there],
            send_sem=ag_send.at[n_grp + k],
            recv_sem=ag_recv.at[n_grp + grp],
            device_id=(req, partner),
            device_id_type=MESH_IDS,
        )
        forward.start()
        sends.append(forward)
    for grp in range(n_grp):
        there = pl.ds(pl.multiple_of((1 - c) * half + grp * rows, rows), rows)
        incoming = pltpu.make_async_remote_copy(
            src_ref=full_ref.at[there],
            dst_ref=full_ref.at[there],
            send_sem=ag_send.at[0],
            recv_sem=ag_recv.at[n_grp + grp],
            device_id=(req, partner),
            device_id_type=MESH_IDS,
        )
        incoming.wait_recv()
    if extra:
        wts_ref[req] = packed_ref[...]
        for k in range(1, n_req):
            src = lax.rem(req + n_req - k, n_req)
            incoming = pltpu.make_async_remote_copy(
                src_ref=packed_ref,
                dst_ref=wts_ref.at[src],
                send_sem=w_send.at[src],
                recv_sem=w_recv.at[src],
                device_id=(src, me),
                device_id_type=MESH_IDS,
            )
            incoming.wait_recv()
    for copy in sends:
        copy.wait_send()


def blk_stage(part, resid, gain, final, packed=None):
    n_blk = lax.axis_size("blk")
    rows, width = resid.shape
    vmem = pl.BlockSpec(memory_space=pltpu.VMEM)
    extra = packed is not None
    outs = [
        jax.ShapeDtypeStruct((rows, width), jnp.float32),
        jax.ShapeDtypeStruct((rows * n_blk, width), jnp.bfloat16),
    ]
    n_grp = n_blk // 2
    scratch = [
        pltpu.VMEM((n_grp, rows, width), part.dtype),
        pltpu.VMEM((n_grp, rows, width), part.dtype),
        pltpu.VMEM((n_grp, rows, width), part.dtype),
        pltpu.SemaphoreType.DMA((n_grp,)),
        pltpu.SemaphoreType.DMA((n_grp,)),
        pltpu.SemaphoreType.DMA((n_grp,)),
        pltpu.SemaphoreType.DMA((n_grp,)),
        pltpu.SemaphoreType.DMA((n_blk,)),
        pltpu.SemaphoreType.DMA((n_blk,)),
    ]
    args = [part, resid, gain[None, :]]
    if extra:
        n_req = lax.axis_size("req")
        outs.append(jax.ShapeDtypeStruct((n_req,) + packed.shape, packed.dtype))
        scratch += [pltpu.SemaphoreType.DMA((n_req,)), pltpu.SemaphoreType.DMA((n_req,))]
        args.append(packed)
    return pl.pallas_call(
        functools.partial(stage_kernel, n_blk, final, extra),
        out_shape=tuple(outs),
        in_specs=[vmem] * len(args),
        out_specs=tuple([vmem] * len(outs)),
        scratch_shapes=scratch,
        compiler_params=pltpu.CompilerParams(
            collective_id=5 if extra else (4 if final else 3), has_side_effects=True
        ),
    )(*args)


def cross_kernel(n_req, spans, len_ref, normed_ref, enc_ref, w_ref, out_ref):
    enc_len = len_ref[0]
    (q_at, q_len), (kv_at, kv_len), (o_at, o_len) = spans
    nt = (((1,), (1,)), ((), ()))
    width = w_ref.shape[2]
    queries = None
    pair = None
    for r in range(n_req):
        cols = slice(r * width, (r + 1) * width)
        term = lax.dot_general(
            normed_ref[:, cols], w_ref[r, q_at : q_at + q_len, :], nt,
            preferred_element_type=jnp.float32,
        )
        queries = term if queries is None else queries + term
        term = lax.dot_general(
            enc_ref[:, cols], w_ref[r, kv_at : kv_at + kv_len, :], nt,
            preferred_element_type=jnp.float32,
        )
        pair = term if pair is None else pair + term
    queries = queries.astype(jnp.bfloat16)
    pair = pair.astype(jnp.bfloat16)
    keys = pair[:, :HD]
    values = pair[:, HD:]
    scores = lax.dot_general(queries, keys, nt, preferred_element_type=jnp.float32)
    col = lax.broadcasted_iota(jnp.int32, scores.shape, 1)
    scores = jnp.where(col < enc_len, scores, NEG_FILL)
    top = jnp.max(scores, axis=1, keepdims=True)
    weights = jnp.exp(scores - top)
    weights = (weights / jnp.sum(weights, axis=1, keepdims=True)).astype(jnp.bfloat16)
    context = jnp.dot(weights, values, preferred_element_type=jnp.float32).astype(jnp.bfloat16)
    for r in range(n_req):
        out_ref[:, r * width : (r + 1) * width] = jnp.dot(
            context, w_ref[r, o_at : o_at + o_len, :], preferred_element_type=jnp.float32
        ).astype(out_ref.dtype)


def ffn_kernel(n_req, spans, normed_ref, w_ref, out_ref):
    (i_at, i_len), (o_at, o_len) = spans
    nt = (((1,), (1,)), ((), ()))
    width = w_ref.shape[2]
    ff_dev = o_len
    gate_up = None
    for r in range(n_req):
        term = lax.dot_general(
            normed_ref[:, r * width : (r + 1) * width], w_ref[r, i_at : i_at + i_len, :], nt,
            preferred_element_type=jnp.float32,
        )
        gate_up = term if gate_up is None else gate_up + term
    hidden = (jax.nn.gelu(gate_up[:, :ff_dev], approximate=True) * gate_up[:, ff_dev:]).astype(
        jnp.bfloat16
    )
    for r in range(n_req):
        out_ref[:, r * width : (r + 1) * width] = jnp.dot(
            hidden, w_ref[r, o_at : o_at + o_len, :], preferred_element_type=jnp.float32
        ).astype(out_ref.dtype)


def block_spans(pieces):
    spans, at = [], 0
    for w, axis in pieces:
        rows = w.size // w.shape[0] if axis == 0 else w.shape[0]
        spans.append((at, rows))
        at += rows
    return spans


def cross_branch(normed, enc, blocks, spans, enc_len):
    vmem = pl.BlockSpec(memory_space=pltpu.VMEM)
    return pl.pallas_call(
        functools.partial(cross_kernel, blocks.shape[0], tuple(spans)),
        out_shape=jax.ShapeDtypeStruct(normed.shape, jnp.bfloat16),
        in_specs=[pl.BlockSpec(memory_space=pltpu.SMEM)] + [vmem] * 3,
        out_specs=vmem,
    )(enc_len.reshape(1).astype(jnp.int32), normed, enc, blocks)


def ffn_branch(normed, blocks, spans):
    vmem = pl.BlockSpec(memory_space=pltpu.VMEM)
    return pl.pallas_call(
        functools.partial(ffn_kernel, blocks.shape[0], tuple(spans)),
        out_shape=jax.ShapeDtypeStruct(normed.shape, jnp.bfloat16),
        in_specs=[vmem] * 2,
        out_specs=vmem,
    )(normed, blocks)


def self_kernel(lens_ref, q_ref, c_ref, kn_ref, vn_ref, g_ref, f_ref, o_ref):
    old_len = lens_ref[0]
    fresh_len = lens_ref[1]
    n_q = q_ref.shape[0]
    n_ctx = c_ref.shape[0]
    wide_old = n_ctx + TQ
    wide_new = n_q + TQ
    k_old = c_ref[:, :HD]
    v_old = c_ref[:, HD:]
    k_new = kn_ref[...]
    v_new = vn_ref[...]
    dims = (((1,), (1,)), ((), ()))
    for t in range(n_q // TQ):
        q = q_ref[t * TQ : (t + 1) * TQ, :]
        start = n_q - TQ - t * TQ
        s_old = lax.dot_general(q, k_old, dims, preferred_element_type=jnp.float32)
        line = jnp.broadcast_to(g_ref[:, start : start + wide_old], (TQ, wide_old))
        bias = pltpu.roll(line, wide_old - (TQ - 1), 1, stride=1, stride_axis=0)[:, :n_ctx]
        col = lax.broadcasted_iota(jnp.int32, (TQ, n_ctx), 1)
        s_old = jnp.where(col < old_len, s_old + bias, NEG_FILL)
        s_new = lax.dot_general(q, k_new, dims, preferred_element_type=jnp.float32)
        line = jnp.broadcast_to(f_ref[:, start : start + wide_new], (TQ, wide_new))
        bias = pltpu.roll(line, wide_new - (TQ - 1), 1, stride=1, stride_axis=0)[:, :n_q]
        row = lax.broadcasted_iota(jnp.int32, (TQ, n_q), 0) + t * TQ
        col = lax.broadcasted_iota(jnp.int32, (TQ, n_q), 1)
        s_new = jnp.where((col <= row) & (col < fresh_len), s_new + bias, NEG_FILL)
        top = jnp.maximum(
            jnp.max(s_old, axis=1, keepdims=True), jnp.max(s_new, axis=1, keepdims=True)
        )
        p_old = jnp.exp(s_old - top)
        p_new = jnp.exp(s_new - top)
        total = jnp.sum(p_old, axis=1, keepdims=True) + jnp.sum(p_new, axis=1, keepdims=True)
        w_old = (p_old / total).astype(jnp.bfloat16)
        w_new = (p_new / total).astype(jnp.bfloat16)
        out = jnp.dot(w_old, v_old, preferred_element_type=jnp.float32) + jnp.dot(
            w_new, v_new, preferred_element_type=jnp.float32
        )
        o_ref[t * TQ : (t + 1) * TQ, :] = out.astype(jnp.bfloat16)


def bias_lines(line, old_len, n_q, n_ctx):
    span = line.shape[0]
    ext = jnp.concatenate([jnp.broadcast_to(line[:1], (n_ctx,)), line])
    rev = ext[::-1]
    g = lax.dynamic_slice_in_dim(rev, n_ctx - old_len, span)
    f = rev[n_ctx : n_ctx + 2 * n_q]
    return g[None, :], f[None, :]


def self_attention(q, cache_blk, k_new, v_new, line, old_len, fresh_len):
    n_q = q.shape[0]
    n_ctx = cache_blk.shape[0]
    g, f = bias_lines(line, old_len, n_q, n_ctx)
    lens = jnp.stack([old_len, fresh_len]).astype(jnp.int32)
    vmem = pl.BlockSpec(memory_space=pltpu.VMEM)
    return pl.pallas_call(
        self_kernel,
        out_shape=jax.ShapeDtypeStruct((n_q, HD), jnp.bfloat16),
        in_specs=[pl.BlockSpec(memory_space=pltpu.SMEM)] + [vmem] * 6,
        out_specs=vmem,
        compiler_params=pltpu.CompilerParams(vmem_limit_bytes=48 * 1024 * 1024),
    )(lens, q, cache_blk, k_new, v_new, g, f)


def pack_gather(pieces):
    flat = jnp.concatenate([w.reshape(-1) for w, _ in pieces])
    whole = lax.all_gather(flat, "req", axis=0, tiled=False)
    n_req = whole.shape[0]
    out, at = [], 0
    for w, axis in pieces:
        size = w.size
        part = whole[:, at : at + size].reshape((n_req,) + w.shape)
        at += size
        part = jnp.moveaxis(part, 0, axis)
        shape = list(w.shape)
        shape[axis] *= n_req
        out.append(part.reshape(shape))
    return out


MESH_IDS = pl.DeviceIdType.MESH


def greet_all(n_blk, me, req):
    barrier = pltpu.get_barrier_semaphore()
    for k in range(1, n_blk):
        peer = lax.rem(me + k, n_blk)
        pl.semaphore_signal(barrier, inc=1, device_id=(req, peer), device_id_type=MESH_IDS)
    pl.semaphore_wait(barrier, n_blk - 1)


def chunk_of(b, n_blk):
    return lax.rem(b, 2) * (n_blk // 2) + b // 2


def scatter_kernel(n_blk, part_ref, out_ref, recv, send_sem, recv_sem):
    me = lax.axis_index("blk")
    req = lax.axis_index("req")
    rows = out_ref.shape[0]
    greet_all(n_blk, me, req)
    copies = []
    for k in range(1, n_blk):
        peer = lax.rem(me + k, n_blk)
        copy = pltpu.make_async_remote_copy(
            src_ref=part_ref.at[pl.ds(pl.multiple_of(chunk_of(peer, n_blk) * rows, rows), rows)],
            dst_ref=recv.at[me],
            send_sem=send_sem.at[peer],
            recv_sem=recv_sem.at[me],
            device_id=(req, peer),
            device_id_type=MESH_IDS,
        )
        copy.start()
        copies.append(copy)
    own = pl.ds(pl.multiple_of(chunk_of(me, n_blk) * rows, rows), rows)
    total = part_ref[own, :].astype(jnp.float32)
    for k in range(1, n_blk):
        src = lax.rem(me + n_blk - k, n_blk)
        incoming = pltpu.make_async_remote_copy(
            src_ref=part_ref.at[pl.ds(0, rows)],
            dst_ref=recv.at[src],
            send_sem=send_sem.at[src],
            recv_sem=recv_sem.at[src],
            device_id=(req, src),
            device_id_type=MESH_IDS,
        )
        incoming.wait_recv()
        total = total + recv[src].astype(jnp.float32)
    for copy in copies:
        copy.wait_send()
    out_ref[...] = total


def gather_kernel(n_blk, piece_ref, out_ref, send_sem, recv_sem):
    b = lax.axis_index("blk")
    req = lax.axis_index("req")
    n_grp = n_blk // 2
    g = b // 2
    c = lax.rem(b, 2)
    partner = g * 2 + 1 - c
    rows = piece_ref.shape[0]
    half = n_grp * rows
    barrier = pltpu.get_barrier_semaphore()
    for k in range(1, n_grp):
        peer = lax.rem(g + k, n_grp) * 2 + c
        pl.semaphore_signal(barrier, inc=1, device_id=(req, peer), device_id_type=MESH_IDS)
    pl.semaphore_signal(barrier, inc=1, device_id=(req, partner), device_id_type=MESH_IDS)
    pl.semaphore_wait(barrier, n_grp)
    mine = pl.ds(pl.multiple_of(c * half + g * rows, rows), rows)
    sends = []
    for k in range(1, n_grp):
        peer = lax.rem(g + k, n_grp) * 2 + c
        copy = pltpu.make_async_remote_copy(
            src_ref=piece_ref,
            dst_ref=out_ref.at[mine],
            send_sem=send_sem.at[k],
            recv_sem=recv_sem.at[g],
            device_id=(req, peer),
            device_id_type=MESH_IDS,
        )
        copy.start()
        sends.append(copy)
    copy = pltpu.make_async_remote_copy(
        src_ref=piece_ref,
        dst_ref=out_ref.at[mine],
        send_sem=send_sem.at[0],
        recv_sem=recv_sem.at[n_grp + g],
        device_id=(req, partner),
        device_id_type=MESH_IDS,
    )
    copy.start()
    sends.append(copy)
    out_ref[mine, :] = piece_ref[...]
    for k in range(1, n_grp):
        grp = lax.rem(g + n_grp - k, n_grp)
        there = pl.ds(pl.multiple_of(c * half + grp * rows, rows), rows)
        incoming = pltpu.make_async_remote_copy(
            src_ref=piece_ref,
            dst_ref=out_ref.at[there],
            send_sem=send_sem.at[0],
            recv_sem=recv_sem.at[grp],
            device_id=(req, grp * 2 + c),
            device_id_type=MESH_IDS,
        )
        incoming.wait_recv()
        forward = pltpu.make_async_remote_copy(
            src_ref=out_ref.at[there],
            dst_ref=out_ref.at[there],
            send_sem=send_sem.at[n_grp + k],
            recv_sem=recv_sem.at[n_grp + grp],
            device_id=(req, partner),
            device_id_type=MESH_IDS,
        )
        forward.start()
        sends.append(forward)
    for grp in range(n_grp):
        there = pl.ds(pl.multiple_of((1 - c) * half + grp * rows, rows), rows)
        incoming = pltpu.make_async_remote_copy(
            src_ref=piece_ref,
            dst_ref=out_ref.at[there],
            send_sem=send_sem.at[0],
            recv_sem=recv_sem.at[n_grp + grp],
            device_id=(req, partner),
            device_id_type=MESH_IDS,
        )
        incoming.wait_recv()
    for copy in sends:
        copy.wait_send()


def blk_scatter(part):
    n_blk = lax.axis_size("blk")
    rows = part.shape[0] // n_blk
    vmem = pl.BlockSpec(memory_space=pltpu.VMEM)
    return pl.pallas_call(
        functools.partial(scatter_kernel, n_blk),
        out_shape=jax.ShapeDtypeStruct((rows, part.shape[1]), jnp.float32),
        in_specs=[vmem],
        out_specs=vmem,
        scratch_shapes=[
            pltpu.VMEM((n_blk, rows, part.shape[1]), part.dtype),
            pltpu.SemaphoreType.DMA((n_blk,)),
            pltpu.SemaphoreType.DMA((n_blk,)),
        ],
        compiler_params=pltpu.CompilerParams(collective_id=1, has_side_effects=True),
    )(part)


def blk_gather(piece):
    n_blk = lax.axis_size("blk")
    rows = piece.shape[0]
    vmem = pl.BlockSpec(memory_space=pltpu.VMEM)
    return pl.pallas_call(
        functools.partial(gather_kernel, n_blk),
        out_shape=jax.ShapeDtypeStruct((rows * n_blk, piece.shape[1]), piece.dtype),
        in_specs=[vmem],
        out_specs=vmem,
        scratch_shapes=[
            pltpu.SemaphoreType.DMA((n_blk,)),
            pltpu.SemaphoreType.DMA((n_blk,)),
        ],
        compiler_params=pltpu.CompilerParams(collective_id=2, has_side_effects=True),
    )(piece)


def prologue_kernel(n_req, n_blk, ordered_ref, packed_ref, cache_ref, wts_ref, w_send, w_recv, c_send, c_recv, local_sem):
    r = lax.axis_index("req")
    b = lax.axis_index("blk")
    n_slot, span, width = ordered_ref.shape
    piece = width // 2
    copies = []
    for k in range(1, n_req):
        peer = lax.rem(r + k, n_req)
        copy = pltpu.make_async_remote_copy(
            src_ref=packed_ref,
            dst_ref=wts_ref.at[r],
            send_sem=w_send.at[peer],
            recv_sem=w_recv.at[r],
            device_id=(peer, b),
            device_id_type=MESH_IDS,
        )
        copy.start()
        copies.append(copy)
    rows = pl.ds(pl.multiple_of(b * span, span), span)
    for k in range(n_slot):
        s = lax.rem(b + k, n_slot)
        for hh in range(2):
            head = 2 * r + hh
            is_self = jnp.logical_and(r == s, head == b)
            src = ordered_ref.at[s, :, pl.ds(hh * piece, piece)]
            copy = pltpu.make_async_remote_copy(
                src_ref=src,
                dst_ref=cache_ref.at[rows],
                send_sem=c_send.at[k * 2 + hh],
                recv_sem=c_recv.at[b],
                device_id=(s, head),
                device_id_type=MESH_IDS,
            )

            @pl.when(jnp.logical_not(is_self))
            def _():
                copy.start()

            @pl.when(is_self)
            def _():
                local = pltpu.make_async_copy(src, cache_ref.at[rows], local_sem.at[0])
                local.start()
                local.wait()

            copies.append((copy, is_self))
    wts_ref[r] = packed_ref[...]
    for k in range(1, n_req):
        src_req = lax.rem(r + n_req - k, n_req)
        incoming = pltpu.make_async_remote_copy(
            src_ref=packed_ref,
            dst_ref=wts_ref.at[src_req],
            send_sem=w_send.at[src_req],
            recv_sem=w_recv.at[src_req],
            device_id=(src_req, b),
            device_id_type=MESH_IDS,
        )
        incoming.wait_recv()
    owner = b // 2
    for j in range(n_blk):
        incoming = pltpu.make_async_remote_copy(
            src_ref=ordered_ref.at[0, :, pl.ds(0, piece)],
            dst_ref=cache_ref.at[pl.ds(j * span, span)],
            send_sem=c_send.at[0],
            recv_sem=c_recv.at[j],
            device_id=(owner, j),
            device_id_type=MESH_IDS,
        )

        @pl.when(jnp.logical_not(jnp.logical_and(owner == r, j == b)))
        def _():
            incoming.wait_recv()

    for item in copies:
        if isinstance(item, tuple):
            copy, is_self = item

            @pl.when(jnp.logical_not(is_self))
            def _():
                copy.wait_send()

        else:
            item.wait_send()


def prologue(ordered, packed):
    n_req = lax.axis_size("req")
    n_blk = lax.axis_size("blk")
    n_slot, span, width = ordered.shape
    any_spec = pl.BlockSpec(memory_space=pl.ANY)
    vmem = pl.BlockSpec(memory_space=pltpu.VMEM)
    return pl.pallas_call(
        functools.partial(prologue_kernel, n_req, n_blk),
        out_shape=(
            jax.ShapeDtypeStruct((span * n_blk, width // 2), ordered.dtype),
            jax.ShapeDtypeStruct((n_req,) + packed.shape, packed.dtype),
        ),
        in_specs=[any_spec, vmem],
        out_specs=(any_spec, vmem),
        scratch_shapes=[
            pltpu.SemaphoreType.DMA((n_req,)),
            pltpu.SemaphoreType.DMA((n_req,)),
            pltpu.SemaphoreType.DMA((2 * n_slot,)),
            pltpu.SemaphoreType.DMA((n_blk,)),
            pltpu.SemaphoreType.DMA((1,)),
        ],
        compiler_params=pltpu.CompilerParams(has_side_effects=True),
    )(ordered, packed)


def unpack(whole, pieces):
    n_req = whole.shape[0]
    whole = whole.reshape(n_req, -1)
    out, at = [], 0
    for w, axis in pieces:
        size = w.size
        part = whole[:, at : at + size].reshape((n_req,) + w.shape)
        at += size
        part = jnp.moveaxis(part, 0, axis)
        shape = list(w.shape)
        shape[axis] *= n_req
        out.append(part.reshape(shape))
    return out


def lane_pack(pieces):
    blocks = []
    for w, axis in pieces:
        flat = w.reshape(w.shape[0], -1)
        blocks.append(flat.T if axis == 0 else flat)
    packed = jnp.concatenate(blocks, axis=0)
    return lax.all_gather(packed, "req", axis=0, tiled=False)


def per_device(
    new_states,
    encoder_out,
    cache_in,
    slot_order,
    new_lengths,
    cache_lengths,
    enc_lengths,
    bucket_of,
    rel_bias,
    norm_gain,
    self_q,
    self_kv,
    self_out,
    cross_q,
    cross_kv,
    cross_out,
    ff_in,
    ff_out,
):
    blk_count = lax.axis_size("blk")
    heads_dev = H // blk_count
    width_dev = heads_dev * HD
    req_dev = cache_in.shape[0] // lax.axis_size("req")
    own_slot = lax.dynamic_index_in_dim(slot_order, lax.axis_index("req"), 0, keepdims=False)
    tables = jnp.stack([new_lengths, cache_lengths, enc_lengths])
    picked = lax.dynamic_slice_in_dim(tables, own_slot, 1, 1)
    slot_new, slot_old, slot_enc = picked[0], picked[1], picked[2]
    ordered = jnp.take(cache_in, slot_order, axis=0)
    onehot = (bucket_of[:, None] == jnp.arange(rel_bias.shape[0], dtype=jnp.int32)[None, :]).astype(
        jnp.float32
    )
    own_bias = lax.dynamic_slice_in_dim(rel_bias, lax.axis_index("blk") * heads_dev, heads_dev, 1)
    bias_dist = jnp.dot(onehot, own_bias, precision=lax.Precision.HIGHEST).T
    early = [(self_q, 0), (self_kv, 0), (self_out, 1)]
    late = [(cross_q, 0), (cross_kv, 0), (cross_out, 1), (ff_in, 0), (ff_out, 1)]
    flat = jnp.concatenate([w.reshape(-1) for w, _ in early])
    cache_blk, whole = prologue(ordered, flat.reshape(-1, 128))
    cache_dec = cache_blk[None]
    ffn_parts, _ = lax.optimization_barrier(((ff_in, ff_out), cache_blk))
    ffn_blocks = lane_pack([(ffn_parts[0], 0), (ffn_parts[1], 1)])
    gathered = unpack(whole, early)
    cross_blocks = lane_pack(late[:3])
    wq_self, wkv_self, wo_self = gathered
    n_blk = lax.axis_size("blk")
    rows_dev = new_states.shape[0] // n_blk
    own_rows = lax.dynamic_slice_in_dim(
        new_states, chunk_of(lax.axis_index("blk"), n_blk) * rows_dev, rows_dev, 0
    ).astype(jnp.float32)
    normed = rms_rows(new_states.astype(jnp.float32), norm_gain[0])
    self_cat = jnp.concatenate([wq_self, wkv_self.reshape(wkv_self.shape[0], -1)], axis=1)
    projected = jnp.dot(normed, self_cat, preferred_element_type=jnp.float32).astype(
        jnp.bfloat16
    )
    context = self_attention(
        projected[:, :HD],
        cache_dec[0],
        projected[:, HD : 2 * HD],
        projected[:, 2 * HD :],
        bias_dist[0],
        slot_old[0],
        slot_new[0],
    )
    part = jnp.dot(context, wo_self, preferred_element_type=jnp.float32).astype(jnp.bfloat16)
    residual, normed = blk_stage(part, own_rows, norm_gain[1], False)
    spans = block_spans(late)
    part = cross_branch(normed, encoder_out, cross_blocks, spans[:3], slot_enc[0])
    residual, normed = blk_stage(part.astype(jnp.bfloat16), residual, norm_gain[2], False)
    part = ffn_branch(normed, ffn_blocks, block_spans([(ff_in, 0), (ff_out, 1)]))
    _, layer_out = blk_stage(part, residual, norm_gain[2], True)
    return (layer_out, cache_dec)


def solution(mesh):
    in_specs = (
        P("req", None),
        P("req", None),
        P(None, "blk", "req"),
        P(),
        P(),
        P(),
        P(),
        P(),
        P(),
        P(),
        P("req", "blk"),
        P("req", None, "blk"),
        P("blk", "req"),
        P("req", "blk"),
        P("req", None, "blk"),
        P("blk", "req"),
        P("req", None, "blk"),
        P("blk", "req"),
    )
    out_specs = (P("req", None), P("req", None, "blk"))
    return jax.shard_map(
        per_device, mesh=mesh, in_specs=in_specs, out_specs=out_specs, check_vma=False
    )
```

```python
import functools

import jax
import jax.numpy as jnp
from jax import lax
from jax.sharding import PartitionSpec as P
from jax.experimental import pallas as pl
from jax.experimental.pallas import tpu as pltpu

H = 16
HD = 64


EPSILON = 1e-06
NEG_FILL = -1e30


def rms_rows(row_block, gain):
    mean_square = jnp.mean(row_block * row_block, axis=-1, keepdims=True)
    return (row_block * lax.rsqrt(mean_square + EPSILON) * gain).astype(jnp.bfloat16)


def softmax_rows(scores):
    row_top = jnp.max(scores, axis=-1, keepdims=True)
    weights = jnp.exp(scores - row_top)
    return (weights / jnp.sum(weights, axis=-1, keepdims=True)).astype(jnp.bfloat16)


def pick_lengths(table, own_slots):
    matches = own_slots[:, None] == jnp.arange(table.shape[0], dtype=jnp.int32)[None, :]
    return jnp.sum(jnp.where(matches, table[None, :], 0), axis=1)


def shifted_bias(bias_dist, base, row_count, col_count):
    heads_here, span_len = bias_dist.shape
    line_len = row_count + col_count - 1
    steps = jnp.arange(line_len + 1, dtype=jnp.int32)
    line = bias_dist[:, jnp.clip(base + row_count - 1 - steps, 0, span_len - 1)]
    tiled = jnp.broadcast_to(line[:, None, :], (heads_here, row_count, line_len + 1))
    flat = tiled.reshape(heads_here, row_count * (line_len + 1))[:, : row_count * line_len]
    skewed = flat.reshape(heads_here, row_count, line_len)
    return skewed[:, :, row_count - 1 : row_count - 1 + col_count]


def row_total(left, weight):
    term = jnp.dot(left, weight, preferred_element_type=jnp.float32)
    return lax.psum(term.astype(jnp.bfloat16), "blk").astype(jnp.float32)


def cached_scores(queries, key_rows, first_col, old_len, bias_dist):
    col_ids = first_col + jnp.arange(key_rows.shape[0], dtype=jnp.int32)[None, :]
    scores = jnp.einsum("qhe,khe->hqk", queries, key_rows, preferred_element_type=jnp.float32)
    scores = scores + shifted_bias(
        bias_dist, old_len - first_col, queries.shape[0], key_rows.shape[0]
    )
    return jnp.where((col_ids < old_len)[None], scores, NEG_FILL)


def fresh_scores(queries, fresh_keys, fresh_len, bias_dist):
    row_ids = jnp.arange(queries.shape[0], dtype=jnp.int32)[:, None]
    col_ids = jnp.arange(fresh_keys.shape[0], dtype=jnp.int32)[None, :]
    scores = jnp.einsum("qhe,khe->hqk", queries, fresh_keys, preferred_element_type=jnp.float32)
    scores = scores + shifted_bias(bias_dist, 0, queries.shape[0], fresh_keys.shape[0])
    admitted = (col_ids <= row_ids) & (col_ids < fresh_len)
    return jnp.where(admitted[None], scores, NEG_FILL)


def self_padded(
    queries, key_rows, value_rows, fresh_keys, fresh_values, old_len, fresh_len, bias_dist
):
    scores = jnp.concatenate(
        [
            cached_scores(queries, key_rows, 0, old_len, bias_dist),
            fresh_scores(queries, fresh_keys, fresh_len, bias_dist),
        ],
        axis=2,
    )
    weights = softmax_rows(scores)
    value_all = jnp.concatenate([value_rows, fresh_values], axis=0)
    return jnp.einsum(
        "hqk,khe->qhe", weights, value_all, preferred_element_type=jnp.float32
    ).astype(jnp.bfloat16)


def self_attend(queries, key_value, cache_dec, slot_old, slot_new, bias_dist, heads_dev):
    req_dev, cache_len = (cache_dec.shape[0], cache_dec.shape[1])
    cache_split = cache_dec.reshape(req_dev, cache_len, heads_dev, 2, -1)

    def one_request(request):
        queries_one, pair_one, cache_one, old_len, fresh_len = request
        return self_padded(
            queries_one,
            cache_one[:, :, 0],
            cache_one[:, :, 1],
            pair_one[:, 0],
            pair_one[:, 1],
            old_len,
            fresh_len,
            bias_dist,
        )

    return lax.map(one_request, (queries, key_value, cache_split, slot_old, slot_new))


def cross_attend(queries, key_value, slot_enc):
    scores = jnp.einsum(
        "rqhe,rkhe->rhqk", queries, key_value[:, :, 0], preferred_element_type=jnp.float32
    )
    col_ids = jnp.arange(key_value.shape[1], dtype=jnp.int32)
    scores = jnp.where(
        col_ids[None, None, None, :] < slot_enc[:, None, None, None], scores, NEG_FILL
    )
    weights = softmax_rows(scores)
    return jnp.einsum(
        "rhqk,rkhe->rqhe", weights, key_value[:, :, 1], preferred_element_type=jnp.float32
    ).astype(jnp.bfloat16)


def add_branch(residual, left, weight, gain):
    residual = residual + row_total(left, weight)
    normed = rms_rows(residual, gain)
    return (residual, normed)


TQ = 128


def stage_kernel(n_blk, final, extra, *refs):
    if extra:
        (part_ref, resid_ref, gain_ref, packed_ref, res_out, full_ref, wts_ref,
         recv_a, send_b, recv_b, x_send, x_recv, b_send, b_recv, ag_send, ag_recv, w_send, w_recv) = refs
    else:
        (part_ref, resid_ref, gain_ref, res_out, full_ref,
         recv_a, send_b, recv_b, x_send, x_recv, b_send, b_recv, ag_send, ag_recv) = refs
    me = lax.axis_index("blk")
    req = lax.axis_index("req")
    rows = resid_ref.shape[0]
    n_grp = n_blk // 2
    g = me // 2
    c = lax.rem(me, 2)
    partner = g * 2 + 1 - c
    half = n_grp * rows
    n_req = wts_ref.shape[0] if extra else 1
    barrier = pltpu.get_barrier_semaphore()
    for k in range(1, n_grp):
        peer = lax.rem(g + k, n_grp) * 2 + c
        pl.semaphore_signal(barrier, inc=1, device_id=(req, peer), device_id_type=MESH_IDS)
    pl.semaphore_signal(barrier, inc=1, device_id=(req, partner), device_id_type=MESH_IDS)
    for k in range(1, n_req):
        peer = lax.rem(req + k, n_req)
        pl.semaphore_signal(barrier, inc=1, device_id=(peer, me), device_id_type=MESH_IDS)
    pl.semaphore_wait(barrier, n_grp + n_req - 1)
    sends = []
    for k in range(n_grp):
        grp = lax.rem(g + 1 + k, n_grp)
        exchange = pltpu.make_async_remote_copy(
            src_ref=part_ref.at[pl.ds(pl.multiple_of((1 - c) * half + grp * rows, rows), rows)],
            dst_ref=recv_a.at[grp],
            send_sem=x_send.at[k],
            recv_sem=x_recv.at[grp],
            device_id=(req, partner),
            device_id_type=MESH_IDS,
        )
        exchange.start()
        sends.append(exchange)
    for k in range(1, n_req):
        peer = lax.rem(req + k, n_req)
        copy = pltpu.make_async_remote_copy(
            src_ref=packed_ref,
            dst_ref=wts_ref.at[req],
            send_sem=w_send.at[peer],
            recv_sem=w_recv.at[req],
            device_id=(peer, me),
            device_id_type=MESH_IDS,
        )
        copy.start()
        sends.append(copy)
    total = None
    for k in range(n_grp):
        grp = lax.rem(g + 1 + k, n_grp)
        incoming = pltpu.make_async_remote_copy(
            src_ref=part_ref.at[pl.ds(0, rows)],
            dst_ref=recv_a.at[grp],
            send_sem=x_send.at[k],
            recv_sem=x_recv.at[grp],
            device_id=(req, partner),
            device_id_type=MESH_IDS,
        )
        incoming.wait_recv()
        pair = part_ref[pl.ds(pl.multiple_of(c * half + grp * rows, rows), rows), :].astype(
            jnp.float32
        ) + recv_a[grp].astype(jnp.float32)
        if k == n_grp - 1:
            total = pair
        else:
            send_b[grp] = pair.astype(send_b.dtype)
            copy = pltpu.make_async_remote_copy(
                src_ref=send_b.at[grp],
                dst_ref=recv_b.at[g],
                send_sem=b_send.at[grp],
                recv_sem=b_recv.at[g],
                device_id=(req, grp * 2 + c),
                device_id_type=MESH_IDS,
            )
            copy.start()
            sends.append(copy)
    for k in range(1, n_grp):
        grp = lax.rem(g + n_grp - k, n_grp)
        incoming = pltpu.make_async_remote_copy(
            src_ref=send_b.at[0],
            dst_ref=recv_b.at[grp],
            send_sem=b_send.at[grp],
            recv_sem=b_recv.at[grp],
            device_id=(req, grp * 2 + c),
            device_id_type=MESH_IDS,
        )
        incoming.wait_recv()
        total = total + recv_b[grp].astype(jnp.float32)
    mine = pl.ds(pl.multiple_of(c * half + g * rows, rows), rows)
    resid = resid_ref[...] + total
    res_out[...] = resid
    if final:
        full_ref[mine, :] = resid.astype(full_ref.dtype)
    else:
        mean_square = jnp.mean(resid * resid, axis=-1, keepdims=True)
        full_ref[mine, :] = (resid * lax.rsqrt(mean_square + EPSILON) * gain_ref[...]).astype(
            full_ref.dtype
        )
    for k in range(1, n_grp):
        peer = lax.rem(g + k, n_grp) * 2 + c
        copy = pltpu.make_async_remote_copy(
            src_ref=full_ref.at[mine],
            dst_ref=full_ref.at[mine],
            send_sem=ag_send.at[k],
            recv_sem=ag_recv.at[g],
            device_id=(req, peer),
            device_id_type=MESH_IDS,
        )
        copy.start()
        sends.append(copy)
    copy = pltpu.make_async_remote_copy(
        src_ref=full_ref.at[mine],
        dst_ref=full_ref.at[mine],
        send_sem=ag_send.at[0],
        recv_sem=ag_recv.at[n_grp + g],
        device_id=(req, partner),
        device_id_type=MESH_IDS,
    )
    copy.start()
    sends.append(copy)
    for k in range(1, n_grp):
        grp = lax.rem(g + n_grp - k, n_grp)
        there = pl.ds(pl.multiple_of(c * half + grp * rows, rows), rows)
        incoming = pltpu.make_async_remote_copy(
            src_ref=full_ref.at[there],
            dst_ref=full_ref.at[there],
            send_sem=ag_send.at[0],
            recv_sem=ag_recv.at[grp],
            device_id=(req, grp * 2 + c),
            device_id_type=MESH_IDS,
        )
        incoming.wait_recv()
        forward = pltpu.make_async_remote_copy(
            src_ref=full_ref.at[there],
            dst_ref=full_ref.at[there],
            send_sem=ag_send.at[n_grp + k],
            recv_sem=ag_recv.at[n_grp + grp],
            device_id=(req, partner),
            device_id_type=MESH_IDS,
        )
        forward.start()
        sends.append(forward)
    for grp in range(n_grp):
        there = pl.ds(pl.multiple_of((1 - c) * half + grp * rows, rows), rows)
        incoming = pltpu.make_async_remote_copy(
            src_ref=full_ref.at[there],
            dst_ref=full_ref.at[there],
            send_sem=ag_send.at[0],
            recv_sem=ag_recv.at[n_grp + grp],
            device_id=(req, partner),
            device_id_type=MESH_IDS,
        )
        incoming.wait_recv()
    if extra:
        wts_ref[req] = packed_ref[...]
        for k in range(1, n_req):
            src = lax.rem(req + n_req - k, n_req)
            incoming = pltpu.make_async_remote_copy(
                src_ref=packed_ref,
                dst_ref=wts_ref.at[src],
                send_sem=w_send.at[src],
                recv_sem=w_recv.at[src],
                device_id=(src, me),
                device_id_type=MESH_IDS,
            )
            incoming.wait_recv()
    for copy in sends:
        copy.wait_send()


def blk_stage(part, resid, gain, final, packed=None):
    n_blk = lax.axis_size("blk")
    rows, width = resid.shape
    vmem = pl.BlockSpec(memory_space=pltpu.VMEM)
    extra = packed is not None
    outs = [
        jax.ShapeDtypeStruct((rows, width), jnp.float32),
        jax.ShapeDtypeStruct((rows * n_blk, width), jnp.bfloat16),
    ]
    n_grp = n_blk // 2
    scratch = [
        pltpu.VMEM((n_grp, rows, width), part.dtype),
        pltpu.VMEM((n_grp, rows, width), part.dtype),
        pltpu.VMEM((n_grp, rows, width), part.dtype),
        pltpu.SemaphoreType.DMA((n_grp,)),
        pltpu.SemaphoreType.DMA((n_grp,)),
        pltpu.SemaphoreType.DMA((n_grp,)),
        pltpu.SemaphoreType.DMA((n_grp,)),
        pltpu.SemaphoreType.DMA((n_blk,)),
        pltpu.SemaphoreType.DMA((n_blk,)),
    ]
    args = [part, resid, gain[None, :]]
    if extra:
        n_req = lax.axis_size("req")
        outs.append(jax.ShapeDtypeStruct((n_req,) + packed.shape, packed.dtype))
        scratch += [pltpu.SemaphoreType.DMA((n_req,)), pltpu.SemaphoreType.DMA((n_req,))]
        args.append(packed)
    return pl.pallas_call(
        functools.partial(stage_kernel, n_blk, final, extra),
        out_shape=tuple(outs),
        in_specs=[vmem] * len(args),
        out_specs=tuple([vmem] * len(outs)),
        scratch_shapes=scratch,
        compiler_params=pltpu.CompilerParams(
            collective_id=5 if extra else (4 if final else 3), has_side_effects=True
        ),
    )(*args)


def cross_kernel(n_req, spans, len_ref, normed_ref, enc_ref, w_ref, out_ref):
    enc_len = len_ref[0]
    (q_at, q_len), (kv_at, kv_len), (o_at, o_len) = spans
    nt = (((1,), (1,)), ((), ()))
    width = w_ref.shape[2]
    queries = None
    pair = None
    for r in range(n_req):
        cols = slice(r * width, (r + 1) * width)
        term = lax.dot_general(
            normed_ref[:, cols], w_ref[r, q_at : q_at + q_len, :], nt,
            preferred_element_type=jnp.float32,
        )
        queries = term if queries is None else queries + term
        term = lax.dot_general(
            enc_ref[:, cols], w_ref[r, kv_at : kv_at + kv_len, :], nt,
            preferred_element_type=jnp.float32,
        )
        pair = term if pair is None else pair + term
    queries = queries.astype(jnp.bfloat16)
    pair = pair.astype(jnp.bfloat16)
    keys = pair[:, :HD]
    values = pair[:, HD:]
    scores = lax.dot_general(queries, keys, nt, preferred_element_type=jnp.float32)
    col = lax.broadcasted_iota(jnp.int32, scores.shape, 1)
    scores = jnp.where(col < enc_len, scores, NEG_FILL)
    top = jnp.max(scores, axis=1, keepdims=True)
    weights = jnp.exp(scores - top)
    weights = (weights / jnp.sum(weights, axis=1, keepdims=True)).astype(jnp.bfloat16)
    context = jnp.dot(weights, values, preferred_element_type=jnp.float32).astype(jnp.bfloat16)
    for r in range(n_req):
        out_ref[:, r * width : (r + 1) * width] = jnp.dot(
            context, w_ref[r, o_at : o_at + o_len, :], preferred_element_type=jnp.float32
        ).astype(out_ref.dtype)


def ffn_kernel(n_req, spans, normed_ref, w_ref, out_ref):
    (i_at, i_len), (o_at, o_len) = spans
    nt = (((1,), (1,)), ((), ()))
    width = w_ref.shape[2]
    ff_dev = o_len
    gate_up = None
    for r in range(n_req):
        term = lax.dot_general(
            normed_ref[:, r * width : (r + 1) * width], w_ref[r, i_at : i_at + i_len, :], nt,
            preferred_element_type=jnp.float32,
        )
        gate_up = term if gate_up is None else gate_up + term
    hidden = (jax.nn.gelu(gate_up[:, :ff_dev], approximate=True) * gate_up[:, ff_dev:]).astype(
        jnp.bfloat16
    )
    for r in range(n_req):
        out_ref[:, r * width : (r + 1) * width] = jnp.dot(
            hidden, w_ref[r, o_at : o_at + o_len, :], preferred_element_type=jnp.float32
        ).astype(out_ref.dtype)


def block_spans(pieces):
    spans, at = [], 0
    for w, axis in pieces:
        rows = w.size // w.shape[0] if axis == 0 else w.shape[0]
        spans.append((at, rows))
        at += rows
    return spans


def cross_branch(normed, enc, blocks, spans, enc_len):
    vmem = pl.BlockSpec(memory_space=pltpu.VMEM)
    return pl.pallas_call(
        functools.partial(cross_kernel, blocks.shape[0], tuple(spans)),
        out_shape=jax.ShapeDtypeStruct(normed.shape, jnp.bfloat16),
        in_specs=[pl.BlockSpec(memory_space=pltpu.SMEM)] + [vmem] * 3,
        out_specs=vmem,
    )(enc_len.reshape(1).astype(jnp.int32), normed, enc, blocks)


def ffn_branch(normed, blocks, spans):
    vmem = pl.BlockSpec(memory_space=pltpu.VMEM)
    return pl.pallas_call(
        functools.partial(ffn_kernel, blocks.shape[0], tuple(spans)),
        out_shape=jax.ShapeDtypeStruct(normed.shape, jnp.bfloat16),
        in_specs=[vmem] * 2,
        out_specs=vmem,
    )(normed, blocks)


def self_kernel(lens_ref, q_ref, c_ref, kn_ref, vn_ref, g_ref, f_ref, o_ref):
    old_len = lens_ref[0]
    fresh_len = lens_ref[1]
    n_q = q_ref.shape[0]
    n_ctx = c_ref.shape[0]
    wide_old = n_ctx + TQ
    wide_new = n_q + TQ
    k_old = c_ref[:, :HD]
    v_old = c_ref[:, HD:]
    k_new = kn_ref[...]
    v_new = vn_ref[...]
    dims = (((1,), (1,)), ((), ()))
    for t in range(n_q // TQ):
        q = q_ref[t * TQ : (t + 1) * TQ, :]
        start = n_q - TQ - t * TQ
        s_old = lax.dot_general(q, k_old, dims, preferred_element_type=jnp.float32)
        line = jnp.broadcast_to(g_ref[:, start : start + wide_old], (TQ, wide_old))
        bias = pltpu.roll(line, wide_old - (TQ - 1), 1, stride=1, stride_axis=0)[:, :n_ctx]
        col = lax.broadcasted_iota(jnp.int32, (TQ, n_ctx), 1)
        s_old = jnp.where(col < old_len, s_old + bias, NEG_FILL)
        s_new = lax.dot_general(q, k_new, dims, preferred_element_type=jnp.float32)
        line = jnp.broadcast_to(f_ref[:, start : start + wide_new], (TQ, wide_new))
        bias = pltpu.roll(line, wide_new - (TQ - 1), 1, stride=1, stride_axis=0)[:, :n_q]
        row = lax.broadcasted_iota(jnp.int32, (TQ, n_q), 0) + t * TQ
        col = lax.broadcasted_iota(jnp.int32, (TQ, n_q), 1)
        s_new = jnp.where((col <= row) & (col < fresh_len), s_new + bias, NEG_FILL)
        top = jnp.maximum(
            jnp.max(s_old, axis=1, keepdims=True), jnp.max(s_new, axis=1, keepdims=True)
        )
        p_old = jnp.exp(s_old - top)
        p_new = jnp.exp(s_new - top)
        total = jnp.sum(p_old, axis=1, keepdims=True) + jnp.sum(p_new, axis=1, keepdims=True)
        w_old = (p_old / total).astype(jnp.bfloat16)
        w_new = (p_new / total).astype(jnp.bfloat16)
        out = jnp.dot(w_old, v_old, preferred_element_type=jnp.float32) + jnp.dot(
            w_new, v_new, preferred_element_type=jnp.float32
        )
        o_ref[t * TQ : (t + 1) * TQ, :] = out.astype(jnp.bfloat16)


def bias_lines(line, old_len, n_q, n_ctx):
    span = line.shape[0]
    ext = jnp.concatenate([jnp.broadcast_to(line[:1], (n_ctx,)), line])
    rev = ext[::-1]
    g = lax.dynamic_slice_in_dim(rev, n_ctx - old_len, span)
    f = rev[n_ctx : n_ctx + 2 * n_q]
    return g[None, :], f[None, :]


def self_attention(q, cache_blk, k_new, v_new, line, old_len, fresh_len):
    n_q = q.shape[0]
    n_ctx = cache_blk.shape[0]
    g, f = bias_lines(line, old_len, n_q, n_ctx)
    lens = jnp.stack([old_len, fresh_len]).astype(jnp.int32)
    vmem = pl.BlockSpec(memory_space=pltpu.VMEM)
    return pl.pallas_call(
        self_kernel,
        out_shape=jax.ShapeDtypeStruct((n_q, HD), jnp.bfloat16),
        in_specs=[pl.BlockSpec(memory_space=pltpu.SMEM)] + [vmem] * 6,
        out_specs=vmem,
        compiler_params=pltpu.CompilerParams(vmem_limit_bytes=48 * 1024 * 1024),
    )(lens, q, cache_blk, k_new, v_new, g, f)


def self_full_kernel(n_req, spans, lens_ref, x_ref, gain_ref, w_ref, c_ref, g_ref, f_ref, o_ref, ctx_ref):
    old_len = lens_ref[0]
    fresh_len = lens_ref[1]
    (q_at, q_len), (kv_at, kv_len), (o_at, o_len) = spans
    nt = (((1,), (1,)), ((), ()))
    width = w_ref.shape[2]
    x = x_ref[...].astype(jnp.float32)
    mean_square = jnp.mean(x * x, axis=-1, keepdims=True)
    normed = (x * lax.rsqrt(mean_square + EPSILON) * gain_ref[...]).astype(jnp.bfloat16)
    queries = None
    pair = None
    for r in range(n_req):
        cols = slice(r * width, (r + 1) * width)
        term = lax.dot_general(
            normed[:, cols], w_ref[r, q_at : q_at + q_len, :], nt,
            preferred_element_type=jnp.float32,
        )
        queries = term if queries is None else queries + term
        term = lax.dot_general(
            normed[:, cols], w_ref[r, kv_at : kv_at + kv_len, :], nt,
            preferred_element_type=jnp.float32,
        )
        pair = term if pair is None else pair + term
    queries = queries.astype(jnp.bfloat16)
    pair = pair.astype(jnp.bfloat16)
    k_new = pair[:, :HD]
    v_new = pair[:, HD:]
    n_q = x_ref.shape[0]
    n_ctx = c_ref.shape[0]
    wide_old = n_ctx + TQ
    wide_new = n_q + TQ
    k_old = c_ref[:, :HD]
    v_old = c_ref[:, HD:]
    for t in range(n_q // TQ):
        q = queries[t * TQ : (t + 1) * TQ, :]
        start = n_q - TQ - t * TQ
        s_old = lax.dot_general(q, k_old, nt, preferred_element_type=jnp.float32)
        line = jnp.broadcast_to(g_ref[:, start : start + wide_old], (TQ, wide_old))
        bias = pltpu.roll(line, wide_old - (TQ - 1), 1, stride=1, stride_axis=0)[:, :n_ctx]
        col = lax.broadcasted_iota(jnp.int32, (TQ, n_ctx), 1)
        s_old = jnp.where(col < old_len, s_old + bias, NEG_FILL)
        s_new = lax.dot_general(q, k_new, nt, preferred_element_type=jnp.float32)
        line = jnp.broadcast_to(f_ref[:, start : start + wide_new], (TQ, wide_new))
        bias = pltpu.roll(line, wide_new - (TQ - 1), 1, stride=1, stride_axis=0)[:, :n_q]
        row = lax.broadcasted_iota(jnp.int32, (TQ, n_q), 0) + t * TQ
        col = lax.broadcasted_iota(jnp.int32, (TQ, n_q), 1)
        s_new = jnp.where((col <= row) & (col < fresh_len), s_new + bias, NEG_FILL)
        top = jnp.maximum(
            jnp.max(s_old, axis=1, keepdims=True), jnp.max(s_new, axis=1, keepdims=True)
        )
        p_old = jnp.exp(s_old - top)
        p_new = jnp.exp(s_new - top)
        total = jnp.sum(p_old, axis=1, keepdims=True) + jnp.sum(p_new, axis=1, keepdims=True)
        w_old = (p_old / total).astype(jnp.bfloat16)
        w_new = (p_new / total).astype(jnp.bfloat16)
        out = jnp.dot(w_old, v_old, preferred_element_type=jnp.float32) + jnp.dot(
            w_new, v_new, preferred_element_type=jnp.float32
        )
        ctx_ref[t * TQ : (t + 1) * TQ, :] = out.astype(jnp.bfloat16)
    context = ctx_ref[...]
    for r in range(n_req):
        o_ref[:, r * width : (r + 1) * width] = jnp.dot(
            context, w_ref[r, o_at : o_at + o_len, :], preferred_element_type=jnp.float32
        ).astype(o_ref.dtype)


def self_branch(states, gain, blocks, spans, cache_blk, line, old_len, fresh_len):
    n_q = states.shape[0]
    n_ctx = cache_blk.shape[0]
    g, f = bias_lines(line, old_len, n_q, n_ctx)
    lens = jnp.stack([old_len, fresh_len]).astype(jnp.int32)
    vmem = pl.BlockSpec(memory_space=pltpu.VMEM)
    return pl.pallas_call(
        functools.partial(self_full_kernel, blocks.shape[0], tuple(spans)),
        out_shape=jax.ShapeDtypeStruct(states.shape, jnp.bfloat16),
        in_specs=[pl.BlockSpec(memory_space=pltpu.SMEM)] + [vmem] * 6,
        out_specs=vmem,
        scratch_shapes=[pltpu.VMEM((n_q, HD), jnp.bfloat16)],
        compiler_params=pltpu.CompilerParams(vmem_limit_bytes=48 * 1024 * 1024),
    )(lens, states, gain[None, :], blocks, cache_blk, g, f)


def pack_gather(pieces):
    flat = jnp.concatenate([w.reshape(-1) for w, _ in pieces])
    whole = lax.all_gather(flat, "req", axis=0, tiled=False)
    n_req = whole.shape[0]
    out, at = [], 0
    for w, axis in pieces:
        size = w.size
        part = whole[:, at : at + size].reshape((n_req,) + w.shape)
        at += size
        part = jnp.moveaxis(part, 0, axis)
        shape = list(w.shape)
        shape[axis] *= n_req
        out.append(part.reshape(shape))
    return out


MESH_IDS = pl.DeviceIdType.MESH


def greet_all(n_blk, me, req):
    barrier = pltpu.get_barrier_semaphore()
    for k in range(1, n_blk):
        peer = lax.rem(me + k, n_blk)
        pl.semaphore_signal(barrier, inc=1, device_id=(req, peer), device_id_type=MESH_IDS)
    pl.semaphore_wait(barrier, n_blk - 1)


def chunk_of(b, n_blk):
    return lax.rem(b, 2) * (n_blk // 2) + b // 2


def scatter_kernel(n_blk, part_ref, out_ref, recv, send_sem, recv_sem):
    me = lax.axis_index("blk")
    req = lax.axis_index("req")
    rows = out_ref.shape[0]
    greet_all(n_blk, me, req)
    copies = []
    for k in range(1, n_blk):
        peer = lax.rem(me + k, n_blk)
        copy = pltpu.make_async_remote_copy(
            src_ref=part_ref.at[pl.ds(pl.multiple_of(chunk_of(peer, n_blk) * rows, rows), rows)],
            dst_ref=recv.at[me],
            send_sem=send_sem.at[peer],
            recv_sem=recv_sem.at[me],
            device_id=(req, peer),
            device_id_type=MESH_IDS,
        )
        copy.start()
        copies.append(copy)
    own = pl.ds(pl.multiple_of(chunk_of(me, n_blk) * rows, rows), rows)
    total = part_ref[own, :].astype(jnp.float32)
    for k in range(1, n_blk):
        src = lax.rem(me + n_blk - k, n_blk)
        incoming = pltpu.make_async_remote_copy(
            src_ref=part_ref.at[pl.ds(0, rows)],
            dst_ref=recv.at[src],
            send_sem=send_sem.at[src],
            recv_sem=recv_sem.at[src],
            device_id=(req, src),
            device_id_type=MESH_IDS,
        )
        incoming.wait_recv()
        total = total + recv[src].astype(jnp.float32)
    for copy in copies:
        copy.wait_send()
    out_ref[...] = total


def gather_kernel(n_blk, piece_ref, out_ref, send_sem, recv_sem):
    b = lax.axis_index("blk")
    req = lax.axis_index("req")
    n_grp = n_blk // 2
    g = b // 2
    c = lax.rem(b, 2)
    partner = g * 2 + 1 - c
    rows = piece_ref.shape[0]
    half = n_grp * rows
    barrier = pltpu.get_barrier_semaphore()
    for k in range(1, n_grp):
        peer = lax.rem(g + k, n_grp) * 2 + c
        pl.semaphore_signal(barrier, inc=1, device_id=(req, peer), device_id_type=MESH_IDS)
    pl.semaphore_signal(barrier, inc=1, device_id=(req, partner), device_id_type=MESH_IDS)
    pl.semaphore_wait(barrier, n_grp)
    mine = pl.ds(pl.multiple_of(c * half + g * rows, rows), rows)
    sends = []
    for k in range(1, n_grp):
        peer = lax.rem(g + k, n_grp) * 2 + c
        copy = pltpu.make_async_remote_copy(
            src_ref=piece_ref,
            dst_ref=out_ref.at[mine],
            send_sem=send_sem.at[k],
            recv_sem=recv_sem.at[g],
            device_id=(req, peer),
            device_id_type=MESH_IDS,
        )
        copy.start()
        sends.append(copy)
    copy = pltpu.make_async_remote_copy(
        src_ref=piece_ref,
        dst_ref=out_ref.at[mine],
        send_sem=send_sem.at[0],
        recv_sem=recv_sem.at[n_grp + g],
        device_id=(req, partner),
        device_id_type=MESH_IDS,
    )
    copy.start()
    sends.append(copy)
    out_ref[mine, :] = piece_ref[...]
    for k in range(1, n_grp):
        grp = lax.rem(g + n_grp - k, n_grp)
        there = pl.ds(pl.multiple_of(c * half + grp * rows, rows), rows)
        incoming = pltpu.make_async_remote_copy(
            src_ref=piece_ref,
            dst_ref=out_ref.at[there],
            send_sem=send_sem.at[0],
            recv_sem=recv_sem.at[grp],
            device_id=(req, grp * 2 + c),
            device_id_type=MESH_IDS,
        )
        incoming.wait_recv()
        forward = pltpu.make_async_remote_copy(
            src_ref=out_ref.at[there],
            dst_ref=out_ref.at[there],
            send_sem=send_sem.at[n_grp + k],
            recv_sem=recv_sem.at[n_grp + grp],
            device_id=(req, partner),
            device_id_type=MESH_IDS,
        )
        forward.start()
        sends.append(forward)
    for grp in range(n_grp):
        there = pl.ds(pl.multiple_of((1 - c) * half + grp * rows, rows), rows)
        incoming = pltpu.make_async_remote_copy(
            src_ref=piece_ref,
            dst_ref=out_ref.at[there],
            send_sem=send_sem.at[0],
            recv_sem=recv_sem.at[n_grp + grp],
            device_id=(req, partner),
            device_id_type=MESH_IDS,
        )
        incoming.wait_recv()
    for copy in sends:
        copy.wait_send()


def blk_scatter(part):
    n_blk = lax.axis_size("blk")
    rows = part.shape[0] // n_blk
    vmem = pl.BlockSpec(memory_space=pltpu.VMEM)
    return pl.pallas_call(
        functools.partial(scatter_kernel, n_blk),
        out_shape=jax.ShapeDtypeStruct((rows, part.shape[1]), jnp.float32),
        in_specs=[vmem],
        out_specs=vmem,
        scratch_shapes=[
            pltpu.VMEM((n_blk, rows, part.shape[1]), part.dtype),
            pltpu.SemaphoreType.DMA((n_blk,)),
            pltpu.SemaphoreType.DMA((n_blk,)),
        ],
        compiler_params=pltpu.CompilerParams(collective_id=1, has_side_effects=True),
    )(part)


def blk_gather(piece):
    n_blk = lax.axis_size("blk")
    rows = piece.shape[0]
    vmem = pl.BlockSpec(memory_space=pltpu.VMEM)
    return pl.pallas_call(
        functools.partial(gather_kernel, n_blk),
        out_shape=jax.ShapeDtypeStruct((rows * n_blk, piece.shape[1]), piece.dtype),
        in_specs=[vmem],
        out_specs=vmem,
        scratch_shapes=[
            pltpu.SemaphoreType.DMA((n_blk,)),
            pltpu.SemaphoreType.DMA((n_blk,)),
        ],
        compiler_params=pltpu.CompilerParams(collective_id=2, has_side_effects=True),
    )(piece)


def prologue_kernel(n_req, n_blk, ordered_ref, packed_ref, cache_ref, wts_ref, w_send, w_recv, c_send, c_recv, local_sem):
    r = lax.axis_index("req")
    b = lax.axis_index("blk")
    n_slot, span, width = ordered_ref.shape
    piece = width // 2
    copies = []
    for k in range(1, n_req):
        peer = lax.rem(r + k, n_req)
        copy = pltpu.make_async_remote_copy(
            src_ref=packed_ref,
            dst_ref=wts_ref.at[r],
            send_sem=w_send.at[peer],
            recv_sem=w_recv.at[r],
            device_id=(peer, b),
            device_id_type=MESH_IDS,
        )
        copy.start()
        copies.append(copy)
    rows = pl.ds(pl.multiple_of(b * span, span), span)
    for k in range(n_slot):
        s = lax.rem(b + k, n_slot)
        for hh in range(2):
            head = 2 * r + hh
            is_self = jnp.logical_and(r == s, head == b)
            src = ordered_ref.at[s, :, pl.ds(hh * piece, piece)]
            copy = pltpu.make_async_remote_copy(
                src_ref=src,
                dst_ref=cache_ref.at[rows],
                send_sem=c_send.at[k * 2 + hh],
                recv_sem=c_recv.at[b],
                device_id=(s, head),
                device_id_type=MESH_IDS,
            )

            @pl.when(jnp.logical_not(is_self))
            def _():
                copy.start()

            @pl.when(is_self)
            def _():
                local = pltpu.make_async_copy(src, cache_ref.at[rows], local_sem.at[0])
                local.start()
                local.wait()

            copies.append((copy, is_self))
    wts_ref[r] = packed_ref[...]
    for k in range(1, n_req):
        src_req = lax.rem(r + n_req - k, n_req)
        incoming = pltpu.make_async_remote_copy(
            src_ref=packed_ref,
            dst_ref=wts_ref.at[src_req],
            send_sem=w_send.at[src_req],
            recv_sem=w_recv.at[src_req],
            device_id=(src_req, b),
            device_id_type=MESH_IDS,
        )
        incoming.wait_recv()
    owner = b // 2
    for j in range(n_blk):
        incoming = pltpu.make_async_remote_copy(
            src_ref=ordered_ref.at[0, :, pl.ds(0, piece)],
            dst_ref=cache_ref.at[pl.ds(j * span, span)],
            send_sem=c_send.at[0],
            recv_sem=c_recv.at[j],
            device_id=(owner, j),
            device_id_type=MESH_IDS,
        )

        @pl.when(jnp.logical_not(jnp.logical_and(owner == r, j == b)))
        def _():
            incoming.wait_recv()

    for item in copies:
        if isinstance(item, tuple):
            copy, is_self = item

            @pl.when(jnp.logical_not(is_self))
            def _():
                copy.wait_send()

        else:
            item.wait_send()


def prologue(ordered, packed):
    n_req = lax.axis_size("req")
    n_blk = lax.axis_size("blk")
    n_slot, span, width = ordered.shape
    any_spec = pl.BlockSpec(memory_space=pl.ANY)
    vmem = pl.BlockSpec(memory_space=pltpu.VMEM)
    return pl.pallas_call(
        functools.partial(prologue_kernel, n_req, n_blk),
        out_shape=(
            jax.ShapeDtypeStruct((span * n_blk, width // 2), ordered.dtype),
            jax.ShapeDtypeStruct((n_req,) + packed.shape, packed.dtype),
        ),
        in_specs=[any_spec, vmem],
        out_specs=(any_spec, vmem),
        scratch_shapes=[
            pltpu.SemaphoreType.DMA((n_req,)),
            pltpu.SemaphoreType.DMA((n_req,)),
            pltpu.SemaphoreType.DMA((2 * n_slot,)),
            pltpu.SemaphoreType.DMA((n_blk,)),
            pltpu.SemaphoreType.DMA((1,)),
        ],
        compiler_params=pltpu.CompilerParams(has_side_effects=True),
    )(ordered, packed)


def unpack(whole, pieces):
    n_req = whole.shape[0]
    whole = whole.reshape(n_req, -1)
    out, at = [], 0
    for w, axis in pieces:
        size = w.size
        part = whole[:, at : at + size].reshape((n_req,) + w.shape)
        at += size
        part = jnp.moveaxis(part, 0, axis)
        shape = list(w.shape)
        shape[axis] *= n_req
        out.append(part.reshape(shape))
    return out


def lane_pack(pieces):
    blocks = []
    for w, axis in pieces:
        flat = w.reshape(w.shape[0], -1)
        blocks.append(flat.T if axis == 0 else flat)
    packed = jnp.concatenate(blocks, axis=0)
    return lax.all_gather(packed, "req", axis=0, tiled=False)


def per_device(
    new_states,
    encoder_out,
    cache_in,
    slot_order,
    new_lengths,
    cache_lengths,
    enc_lengths,
    bucket_of,
    rel_bias,
    norm_gain,
    self_q,
    self_kv,
    self_out,
    cross_q,
    cross_kv,
    cross_out,
    ff_in,
    ff_out,
):
    blk_count = lax.axis_size("blk")
    heads_dev = H // blk_count
    width_dev = heads_dev * HD
    req_dev = cache_in.shape[0] // lax.axis_size("req")
    own_slot = lax.dynamic_index_in_dim(slot_order, lax.axis_index("req"), 0, keepdims=False)
    tables = jnp.stack([new_lengths, cache_lengths, enc_lengths])
    picked = lax.dynamic_slice_in_dim(tables, own_slot, 1, 1)
    slot_new, slot_old, slot_enc = picked[0], picked[1], picked[2]
    ordered = jnp.take(cache_in, slot_order, axis=0)
    onehot = (bucket_of[:, None] == jnp.arange(rel_bias.shape[0], dtype=jnp.int32)[None, :]).astype(
        jnp.float32
    )
    own_bias = lax.dynamic_slice_in_dim(rel_bias, lax.axis_index("blk") * heads_dev, heads_dev, 1)
    bias_dist = jnp.dot(onehot, own_bias, precision=lax.Precision.HIGHEST).T
    early = [(self_q, 0), (self_kv, 0), (self_out, 1)]
    late = [(cross_q, 0), (cross_kv, 0), (cross_out, 1), (ff_in, 0), (ff_out, 1)]
    blocks = []
    for w, axis in early:
        two_d = w.reshape(w.shape[0], -1)
        blocks.append(two_d.T if axis == 0 else two_d)
    cache_blk, early_blocks = prologue(ordered, jnp.concatenate(blocks, axis=0))
    cache_dec = cache_blk[None]
    late_blocks = lane_pack(late)
    n_blk = lax.axis_size("blk")
    rows_dev = new_states.shape[0] // n_blk
    own_rows = lax.dynamic_slice_in_dim(
        new_states, chunk_of(lax.axis_index("blk"), n_blk) * rows_dev, rows_dev, 0
    ).astype(jnp.float32)
    part = self_branch(
        new_states,
        norm_gain[0],
        early_blocks,
        block_spans(early),
        cache_blk,
        bias_dist[0],
        slot_old[0],
        slot_new[0],
    )
    residual, normed = blk_stage(part, own_rows, norm_gain[1], False)
    spans = block_spans(late)
    part = cross_branch(normed, encoder_out, late_blocks, spans[:3], slot_enc[0])
    residual, normed = blk_stage(part.astype(jnp.bfloat16), residual, norm_gain[2], False)
    part = ffn_branch(normed, late_blocks, spans[3:])
    _, layer_out = blk_stage(part, residual, norm_gain[2], True)
    return (layer_out, cache_dec)


def solution(mesh):
    in_specs = (
        P("req", None),
        P("req", None),
        P(None, "blk", "req"),
        P(),
        P(),
        P(),
        P(),
        P(),
        P(),
        P(),
        P("req", "blk"),
        P("req", None, "blk"),
        P("blk", "req"),
        P("req", "blk"),
        P("req", None, "blk"),
        P("blk", "req"),
        P("req", None, "blk"),
        P("blk", "req"),
    )
    out_specs = (P("req", None), P("req", None, "blk"))
    return jax.shard_map(
        per_device, mesh=mesh, in_specs=in_specs, out_specs=out_specs, check_vma=False
    )
```

```python
import functools

import jax
import jax.numpy as jnp
from jax import lax
from jax.sharding import PartitionSpec as P
from jax.experimental import pallas as pl
from jax.experimental.pallas import tpu as pltpu

H = 16
HD = 64


EPSILON = 1e-06
NEG_FILL = -1e30


def rms_rows(row_block, gain):
    mean_square = jnp.mean(row_block * row_block, axis=-1, keepdims=True)
    return (row_block * lax.rsqrt(mean_square + EPSILON) * gain).astype(jnp.bfloat16)


def softmax_rows(scores):
    row_top = jnp.max(scores, axis=-1, keepdims=True)
    weights = jnp.exp(scores - row_top)
    return (weights / jnp.sum(weights, axis=-1, keepdims=True)).astype(jnp.bfloat16)


def pick_lengths(table, own_slots):
    matches = own_slots[:, None] == jnp.arange(table.shape[0], dtype=jnp.int32)[None, :]
    return jnp.sum(jnp.where(matches, table[None, :], 0), axis=1)


def shifted_bias(bias_dist, base, row_count, col_count):
    heads_here, span_len = bias_dist.shape
    line_len = row_count + col_count - 1
    steps = jnp.arange(line_len + 1, dtype=jnp.int32)
    line = bias_dist[:, jnp.clip(base + row_count - 1 - steps, 0, span_len - 1)]
    tiled = jnp.broadcast_to(line[:, None, :], (heads_here, row_count, line_len + 1))
    flat = tiled.reshape(heads_here, row_count * (line_len + 1))[:, : row_count * line_len]
    skewed = flat.reshape(heads_here, row_count, line_len)
    return skewed[:, :, row_count - 1 : row_count - 1 + col_count]


def row_total(left, weight):
    term = jnp.dot(left, weight, preferred_element_type=jnp.float32)
    return lax.psum(term.astype(jnp.bfloat16), "blk").astype(jnp.float32)


def cached_scores(queries, key_rows, first_col, old_len, bias_dist):
    col_ids = first_col + jnp.arange(key_rows.shape[0], dtype=jnp.int32)[None, :]
    scores = jnp.einsum("qhe,khe->hqk", queries, key_rows, preferred_element_type=jnp.float32)
    scores = scores + shifted_bias(
        bias_dist, old_len - first_col, queries.shape[0], key_rows.shape[0]
    )
    return jnp.where((col_ids < old_len)[None], scores, NEG_FILL)


def fresh_scores(queries, fresh_keys, fresh_len, bias_dist):
    row_ids = jnp.arange(queries.shape[0], dtype=jnp.int32)[:, None]
    col_ids = jnp.arange(fresh_keys.shape[0], dtype=jnp.int32)[None, :]
    scores = jnp.einsum("qhe,khe->hqk", queries, fresh_keys, preferred_element_type=jnp.float32)
    scores = scores + shifted_bias(bias_dist, 0, queries.shape[0], fresh_keys.shape[0])
    admitted = (col_ids <= row_ids) & (col_ids < fresh_len)
    return jnp.where(admitted[None], scores, NEG_FILL)


def self_padded(
    queries, key_rows, value_rows, fresh_keys, fresh_values, old_len, fresh_len, bias_dist
):
    scores = jnp.concatenate(
        [
            cached_scores(queries, key_rows, 0, old_len, bias_dist),
            fresh_scores(queries, fresh_keys, fresh_len, bias_dist),
        ],
        axis=2,
    )
    weights = softmax_rows(scores)
    value_all = jnp.concatenate([value_rows, fresh_values], axis=0)
    return jnp.einsum(
        "hqk,khe->qhe", weights, value_all, preferred_element_type=jnp.float32
    ).astype(jnp.bfloat16)


def self_attend(queries, key_value, cache_dec, slot_old, slot_new, bias_dist, heads_dev):
    req_dev, cache_len = (cache_dec.shape[0], cache_dec.shape[1])
    cache_split = cache_dec.reshape(req_dev, cache_len, heads_dev, 2, -1)

    def one_request(request):
        queries_one, pair_one, cache_one, old_len, fresh_len = request
        return self_padded(
            queries_one,
            cache_one[:, :, 0],
            cache_one[:, :, 1],
            pair_one[:, 0],
            pair_one[:, 1],
            old_len,
            fresh_len,
            bias_dist,
        )

    return lax.map(one_request, (queries, key_value, cache_split, slot_old, slot_new))


def cross_attend(queries, key_value, slot_enc):
    scores = jnp.einsum(
        "rqhe,rkhe->rhqk", queries, key_value[:, :, 0], preferred_element_type=jnp.float32
    )
    col_ids = jnp.arange(key_value.shape[1], dtype=jnp.int32)
    scores = jnp.where(
        col_ids[None, None, None, :] < slot_enc[:, None, None, None], scores, NEG_FILL
    )
    weights = softmax_rows(scores)
    return jnp.einsum(
        "rhqk,rkhe->rqhe", weights, key_value[:, :, 1], preferred_element_type=jnp.float32
    ).astype(jnp.bfloat16)


def add_branch(residual, left, weight, gain):
    residual = residual + row_total(left, weight)
    normed = rms_rows(residual, gain)
    return (residual, normed)


TQ = 128


def stage_kernel(n_blk, final, extra, *refs):
    if extra:
        (part_ref, resid_ref, gain_ref, packed_ref, res_out, full_ref, wts_ref,
         recv_a, send_b, recv_b, x_send, x_recv, b_send, b_recv, ag_send, ag_recv, w_send, w_recv) = refs
    else:
        (part_ref, resid_ref, gain_ref, res_out, full_ref,
         recv_a, send_b, recv_b, x_send, x_recv, b_send, b_recv, ag_send, ag_recv) = refs
    me = lax.axis_index("blk")
    req = lax.axis_index("req")
    rows = resid_ref.shape[0]
    n_grp = n_blk // 2
    g = me // 2
    c = lax.rem(me, 2)
    partner = g * 2 + 1 - c
    half = n_grp * rows
    n_req = wts_ref.shape[0] if extra else 1
    barrier = pltpu.get_barrier_semaphore()
    for k in range(1, n_grp):
        peer = lax.rem(g + k, n_grp) * 2 + c
        pl.semaphore_signal(barrier, inc=1, device_id=(req, peer), device_id_type=MESH_IDS)
    pl.semaphore_signal(barrier, inc=1, device_id=(req, partner), device_id_type=MESH_IDS)
    for k in range(1, n_req):
        peer = lax.rem(req + k, n_req)
        pl.semaphore_signal(barrier, inc=1, device_id=(peer, me), device_id_type=MESH_IDS)
    pl.semaphore_wait(barrier, n_grp + n_req - 1)
    sends = []
    for k in range(n_grp):
        grp = lax.rem(g + 1 + k, n_grp)
        exchange = pltpu.make_async_remote_copy(
            src_ref=part_ref.at[pl.ds(pl.multiple_of((1 - c) * half + grp * rows, rows), rows)],
            dst_ref=recv_a.at[grp],
            send_sem=x_send.at[k],
            recv_sem=x_recv.at[grp],
            device_id=(req, partner),
            device_id_type=MESH_IDS,
        )
        exchange.start()
        sends.append(exchange)
    for k in range(1, n_req):
        peer = lax.rem(req + k, n_req)
        copy = pltpu.make_async_remote_copy(
            src_ref=packed_ref,
            dst_ref=wts_ref.at[req],
            send_sem=w_send.at[peer],
            recv_sem=w_recv.at[req],
            device_id=(peer, me),
            device_id_type=MESH_IDS,
        )
        copy.start()
        sends.append(copy)
    total = None
    for k in range(n_grp):
        grp = lax.rem(g + 1 + k, n_grp)
        incoming = pltpu.make_async_remote_copy(
            src_ref=part_ref.at[pl.ds(0, rows)],
            dst_ref=recv_a.at[grp],
            send_sem=x_send.at[k],
            recv_sem=x_recv.at[grp],
            device_id=(req, partner),
            device_id_type=MESH_IDS,
        )
        incoming.wait_recv()
        pair = part_ref[pl.ds(pl.multiple_of(c * half + grp * rows, rows), rows), :].astype(
            jnp.float32
        ) + recv_a[grp].astype(jnp.float32)
        if k == n_grp - 1:
            total = pair
        else:
            send_b[grp] = pair.astype(send_b.dtype)
            copy = pltpu.make_async_remote_copy(
                src_ref=send_b.at[grp],
                dst_ref=recv_b.at[g],
                send_sem=b_send.at[grp],
                recv_sem=b_recv.at[g],
                device_id=(req, grp * 2 + c),
                device_id_type=MESH_IDS,
            )
            copy.start()
            sends.append(copy)
    for k in range(1, n_grp):
        grp = lax.rem(g + n_grp - k, n_grp)
        incoming = pltpu.make_async_remote_copy(
            src_ref=send_b.at[0],
            dst_ref=recv_b.at[grp],
            send_sem=b_send.at[grp],
            recv_sem=b_recv.at[grp],
            device_id=(req, grp * 2 + c),
            device_id_type=MESH_IDS,
        )
        incoming.wait_recv()
        total = total + recv_b[grp].astype(jnp.float32)
    mine = pl.ds(pl.multiple_of(c * half + g * rows, rows), rows)
    resid = resid_ref[...] + total
    res_out[...] = resid
    if final:
        full_ref[mine, :] = resid.astype(full_ref.dtype)
    else:
        mean_square = jnp.mean(resid * resid, axis=-1, keepdims=True)
        full_ref[mine, :] = (resid * lax.rsqrt(mean_square + EPSILON) * gain_ref[...]).astype(
            full_ref.dtype
        )
    for k in range(1, n_grp):
        peer = lax.rem(g + k, n_grp) * 2 + c
        copy = pltpu.make_async_remote_copy(
            src_ref=full_ref.at[mine],
            dst_ref=full_ref.at[mine],
            send_sem=ag_send.at[k],
            recv_sem=ag_recv.at[g],
            device_id=(req, peer),
            device_id_type=MESH_IDS,
        )
        copy.start()
        sends.append(copy)
    copy = pltpu.make_async_remote_copy(
        src_ref=full_ref.at[mine],
        dst_ref=full_ref.at[mine],
        send_sem=ag_send.at[0],
        recv_sem=ag_recv.at[n_grp + g],
        device_id=(req, partner),
        device_id_type=MESH_IDS,
    )
    copy.start()
    sends.append(copy)
    for k in range(1, n_grp):
        grp = lax.rem(g + n_grp - k, n_grp)
        there = pl.ds(pl.multiple_of(c * half + grp * rows, rows), rows)
        incoming = pltpu.make_async_remote_copy(
            src_ref=full_ref.at[there],
            dst_ref=full_ref.at[there],
            send_sem=ag_send.at[0],
            recv_sem=ag_recv.at[grp],
            device_id=(req, grp * 2 + c),
            device_id_type=MESH_IDS,
        )
        incoming.wait_recv()
        forward = pltpu.make_async_remote_copy(
            src_ref=full_ref.at[there],
            dst_ref=full_ref.at[there],
            send_sem=ag_send.at[n_grp + k],
            recv_sem=ag_recv.at[n_grp + grp],
            device_id=(req, partner),
            device_id_type=MESH_IDS,
        )
        forward.start()
        sends.append(forward)
    for grp in range(n_grp):
        there = pl.ds(pl.multiple_of((1 - c) * half + grp * rows, rows), rows)
        incoming = pltpu.make_async_remote_copy(
            src_ref=full_ref.at[there],
            dst_ref=full_ref.at[there],
            send_sem=ag_send.at[0],
            recv_sem=ag_recv.at[n_grp + grp],
            device_id=(req, partner),
            device_id_type=MESH_IDS,
        )
        incoming.wait_recv()
    if extra:
        wts_ref[req] = packed_ref[...]
        for k in range(1, n_req):
            src = lax.rem(req + n_req - k, n_req)
            incoming = pltpu.make_async_remote_copy(
                src_ref=packed_ref,
                dst_ref=wts_ref.at[src],
                send_sem=w_send.at[src],
                recv_sem=w_recv.at[src],
                device_id=(src, me),
                device_id_type=MESH_IDS,
            )
            incoming.wait_recv()
    for copy in sends:
        copy.wait_send()


def blk_stage(part, resid, gain, final, packed=None):
    n_blk = lax.axis_size("blk")
    rows, width = resid.shape
    vmem = pl.BlockSpec(memory_space=pltpu.VMEM)
    extra = packed is not None
    outs = [
        jax.ShapeDtypeStruct((rows, width), jnp.float32),
        jax.ShapeDtypeStruct((rows * n_blk, width), jnp.bfloat16),
    ]
    n_grp = n_blk // 2
    scratch = [
        pltpu.VMEM((n_grp, rows, width), part.dtype),
        pltpu.VMEM((n_grp, rows, width), part.dtype),
        pltpu.VMEM((n_grp, rows, width), part.dtype),
        pltpu.SemaphoreType.DMA((n_grp,)),
        pltpu.SemaphoreType.DMA((n_grp,)),
        pltpu.SemaphoreType.DMA((n_grp,)),
        pltpu.SemaphoreType.DMA((n_grp,)),
        pltpu.SemaphoreType.DMA((n_blk,)),
        pltpu.SemaphoreType.DMA((n_blk,)),
    ]
    args = [part, resid, gain[None, :]]
    if extra:
        n_req = lax.axis_size("req")
        outs.append(jax.ShapeDtypeStruct((n_req,) + packed.shape, packed.dtype))
        scratch += [pltpu.SemaphoreType.DMA((n_req,)), pltpu.SemaphoreType.DMA((n_req,))]
        args.append(packed)
    return pl.pallas_call(
        functools.partial(stage_kernel, n_blk, final, extra),
        out_shape=tuple(outs),
        in_specs=[vmem] * len(args),
        out_specs=tuple([vmem] * len(outs)),
        scratch_shapes=scratch,
        compiler_params=pltpu.CompilerParams(
            collective_id=5 if extra else (4 if final else 3), has_side_effects=True
        ),
    )(*args)


def cross_kernel(n_req, spans, len_ref, normed_ref, enc_ref, w_ref, out_ref):
    enc_len = len_ref[2]
    (q_at, q_len), (kv_at, kv_len), (o_at, o_len) = spans
    nt = (((1,), (1,)), ((), ()))
    width = w_ref.shape[2]
    queries = None
    pair = None
    for r in range(n_req):
        cols = slice(r * width, (r + 1) * width)
        term = lax.dot_general(
            normed_ref[:, cols], w_ref[r, q_at : q_at + q_len, :], nt,
            preferred_element_type=jnp.float32,
        )
        queries = term if queries is None else queries + term
        term = lax.dot_general(
            enc_ref[:, cols], w_ref[r, kv_at : kv_at + kv_len, :], nt,
            preferred_element_type=jnp.float32,
        )
        pair = term if pair is None else pair + term
    queries = queries.astype(jnp.bfloat16)
    pair = pair.astype(jnp.bfloat16)
    keys = pair[:, :HD]
    values = pair[:, HD:]
    scores = lax.dot_general(queries, keys, nt, preferred_element_type=jnp.float32)
    col = lax.broadcasted_iota(jnp.int32, scores.shape, 1)
    scores = jnp.where(col < enc_len, scores, NEG_FILL)
    top = jnp.max(scores, axis=1, keepdims=True)
    weights = jnp.exp(scores - top)
    weights = (weights / jnp.sum(weights, axis=1, keepdims=True)).astype(jnp.bfloat16)
    context = jnp.dot(weights, values, preferred_element_type=jnp.float32).astype(jnp.bfloat16)
    for r in range(n_req):
        out_ref[:, r * width : (r + 1) * width] = jnp.dot(
            context, w_ref[r, o_at : o_at + o_len, :], preferred_element_type=jnp.float32
        ).astype(out_ref.dtype)


def ffn_kernel(n_req, spans, normed_ref, w_ref, out_ref):
    (i_at, i_len), (o_at, o_len) = spans
    nt = (((1,), (1,)), ((), ()))
    width = w_ref.shape[2]
    ff_dev = o_len
    gate_up = None
    for r in range(n_req):
        term = lax.dot_general(
            normed_ref[:, r * width : (r + 1) * width], w_ref[r, i_at : i_at + i_len, :], nt,
            preferred_element_type=jnp.float32,
        )
        gate_up = term if gate_up is None else gate_up + term
    hidden = (jax.nn.gelu(gate_up[:, :ff_dev], approximate=True) * gate_up[:, ff_dev:]).astype(
        jnp.bfloat16
    )
    for r in range(n_req):
        out_ref[:, r * width : (r + 1) * width] = jnp.dot(
            hidden, w_ref[r, o_at : o_at + o_len, :], preferred_element_type=jnp.float32
        ).astype(out_ref.dtype)


def block_spans(pieces):
    spans, at = [], 0
    for w, axis in pieces:
        rows = w.size // w.shape[0] if axis == 0 else w.shape[0]
        spans.append((at, rows))
        at += rows
    return spans


def cross_branch(normed, enc, blocks, spans, enc_len):
    vmem = pl.BlockSpec(memory_space=pltpu.VMEM)
    return pl.pallas_call(
        functools.partial(cross_kernel, blocks.shape[0], tuple(spans)),
        out_shape=jax.ShapeDtypeStruct(normed.shape, jnp.bfloat16),
        in_specs=[pl.BlockSpec(memory_space=pltpu.SMEM)] + [vmem] * 3,
        out_specs=vmem,
    )(enc_len, normed, enc, blocks)


def ffn_branch(normed, blocks, spans):
    vmem = pl.BlockSpec(memory_space=pltpu.VMEM)
    return pl.pallas_call(
        functools.partial(ffn_kernel, blocks.shape[0], tuple(spans)),
        out_shape=jax.ShapeDtypeStruct(normed.shape, jnp.bfloat16),
        in_specs=[vmem] * 2,
        out_specs=vmem,
    )(normed, blocks)


def self_kernel(lens_ref, q_ref, c_ref, kn_ref, vn_ref, g_ref, f_ref, o_ref):
    old_len = lens_ref[0]
    fresh_len = lens_ref[1]
    n_q = q_ref.shape[0]
    n_ctx = c_ref.shape[0]
    wide_old = n_ctx + TQ
    wide_new = n_q + TQ
    k_old = c_ref[:, :HD]
    v_old = c_ref[:, HD:]
    k_new = kn_ref[...]
    v_new = vn_ref[...]
    dims = (((1,), (1,)), ((), ()))
    for t in range(n_q // TQ):
        q = q_ref[t * TQ : (t + 1) * TQ, :]
        start = n_q - TQ - t * TQ
        s_old = lax.dot_general(q, k_old, dims, preferred_element_type=jnp.float32)
        line = jnp.broadcast_to(g_ref[:, start : start + wide_old], (TQ, wide_old))
        bias = pltpu.roll(line, wide_old - (TQ - 1), 1, stride=1, stride_axis=0)[:, :n_ctx]
        col = lax.broadcasted_iota(jnp.int32, (TQ, n_ctx), 1)
        s_old = jnp.where(col < old_len, s_old + bias, NEG_FILL)
        s_new = lax.dot_general(q, k_new, dims, preferred_element_type=jnp.float32)
        line = jnp.broadcast_to(f_ref[:, start : start + wide_new], (TQ, wide_new))
        bias = pltpu.roll(line, wide_new - (TQ - 1), 1, stride=1, stride_axis=0)[:, :n_q]
        row = lax.broadcasted_iota(jnp.int32, (TQ, n_q), 0) + t * TQ
        col = lax.broadcasted_iota(jnp.int32, (TQ, n_q), 1)
        s_new = jnp.where((col <= row) & (col < fresh_len), s_new + bias, NEG_FILL)
        top = jnp.maximum(
            jnp.max(s_old, axis=1, keepdims=True), jnp.max(s_new, axis=1, keepdims=True)
        )
        p_old = jnp.exp(s_old - top)
        p_new = jnp.exp(s_new - top)
        total = jnp.sum(p_old, axis=1, keepdims=True) + jnp.sum(p_new, axis=1, keepdims=True)
        w_old = (p_old / total).astype(jnp.bfloat16)
        w_new = (p_new / total).astype(jnp.bfloat16)
        out = jnp.dot(w_old, v_old, preferred_element_type=jnp.float32) + jnp.dot(
            w_new, v_new, preferred_element_type=jnp.float32
        )
        o_ref[t * TQ : (t + 1) * TQ, :] = out.astype(jnp.bfloat16)


def bias_lines(line, old_len, n_q, n_ctx):
    span = line.shape[0]
    ext = jnp.concatenate([jnp.broadcast_to(line[:1], (n_ctx,)), line])
    rev = ext[::-1]
    g = lax.dynamic_slice_in_dim(rev, n_ctx - old_len, span)
    f = rev[n_ctx : n_ctx + 2 * n_q]
    return g[None, :], f[None, :]


def self_attention(q, cache_blk, k_new, v_new, line, old_len, fresh_len):
    n_q = q.shape[0]
    n_ctx = cache_blk.shape[0]
    g, f = bias_lines(line, old_len, n_q, n_ctx)
    lens = jnp.stack([old_len, fresh_len]).astype(jnp.int32)
    vmem = pl.BlockSpec(memory_space=pltpu.VMEM)
    return pl.pallas_call(
        self_kernel,
        out_shape=jax.ShapeDtypeStruct((n_q, HD), jnp.bfloat16),
        in_specs=[pl.BlockSpec(memory_space=pltpu.SMEM)] + [vmem] * 6,
        out_specs=vmem,
        compiler_params=pltpu.CompilerParams(vmem_limit_bytes=48 * 1024 * 1024),
    )(lens, q, cache_blk, k_new, v_new, g, f)


def self_full_kernel(n_req, spans, lens_ref, x_ref, gain_ref, w_ref, c_ref, g_ref, f_ref, o_ref, ctx_ref):
    fresh_len = lens_ref[0]
    old_len = lens_ref[1]
    (q_at, q_len), (kv_at, kv_len), (o_at, o_len) = spans
    nt = (((1,), (1,)), ((), ()))
    width = w_ref.shape[2]
    x = x_ref[...].astype(jnp.float32)
    mean_square = jnp.mean(x * x, axis=-1, keepdims=True)
    normed = (x * lax.rsqrt(mean_square + EPSILON) * gain_ref[...]).astype(jnp.bfloat16)
    queries = None
    pair = None
    for r in range(n_req):
        cols = slice(r * width, (r + 1) * width)
        term = lax.dot_general(
            normed[:, cols], w_ref[r, q_at : q_at + q_len, :], nt,
            preferred_element_type=jnp.float32,
        )
        queries = term if queries is None else queries + term
        term = lax.dot_general(
            normed[:, cols], w_ref[r, kv_at : kv_at + kv_len, :], nt,
            preferred_element_type=jnp.float32,
        )
        pair = term if pair is None else pair + term
    queries = queries.astype(jnp.bfloat16)
    pair = pair.astype(jnp.bfloat16)
    k_new = pair[:, :HD]
    v_new = pair[:, HD:]
    n_q = x_ref.shape[0]
    n_ctx = c_ref.shape[0]
    wide_old = n_ctx + TQ
    wide_new = n_q + TQ
    k_old = c_ref[:, :HD]
    v_old = c_ref[:, HD:]
    for t in range(n_q // TQ):
        q = queries[t * TQ : (t + 1) * TQ, :]
        start = n_q - TQ - t * TQ
        s_old = lax.dot_general(q, k_old, nt, preferred_element_type=jnp.float32)
        line = jnp.broadcast_to(g_ref[:, start : start + wide_old], (TQ, wide_old))
        bias = pltpu.roll(line, wide_old - (TQ - 1), 1, stride=1, stride_axis=0)[:, :n_ctx]
        col = lax.broadcasted_iota(jnp.int32, (TQ, n_ctx), 1)
        s_old = jnp.where(col < old_len, s_old + bias, NEG_FILL)
        s_new = lax.dot_general(q, k_new, nt, preferred_element_type=jnp.float32)
        line = jnp.broadcast_to(f_ref[:, start : start + wide_new], (TQ, wide_new))
        bias = pltpu.roll(line, wide_new - (TQ - 1), 1, stride=1, stride_axis=0)[:, :n_q]
        row = lax.broadcasted_iota(jnp.int32, (TQ, n_q), 0) + t * TQ
        col = lax.broadcasted_iota(jnp.int32, (TQ, n_q), 1)
        s_new = jnp.where((col <= row) & (col < fresh_len), s_new + bias, NEG_FILL)
        top = jnp.maximum(
            jnp.max(s_old, axis=1, keepdims=True), jnp.max(s_new, axis=1, keepdims=True)
        )
        p_old = jnp.exp(s_old - top)
        p_new = jnp.exp(s_new - top)
        total = jnp.sum(p_old, axis=1, keepdims=True) + jnp.sum(p_new, axis=1, keepdims=True)
        w_old = (p_old / total).astype(jnp.bfloat16)
        w_new = (p_new / total).astype(jnp.bfloat16)
        out = jnp.dot(w_old, v_old, preferred_element_type=jnp.float32) + jnp.dot(
            w_new, v_new, preferred_element_type=jnp.float32
        )
        ctx_ref[t * TQ : (t + 1) * TQ, :] = out.astype(jnp.bfloat16)
    context = ctx_ref[...]
    for r in range(n_req):
        o_ref[:, r * width : (r + 1) * width] = jnp.dot(
            context, w_ref[r, o_at : o_at + o_len, :], preferred_element_type=jnp.float32
        ).astype(o_ref.dtype)


def self_branch(states, gain, blocks, spans, cache_blk, line, lens):
    n_q = states.shape[0]
    n_ctx = cache_blk.shape[0]
    g, f = bias_lines(line, lens[1], n_q, n_ctx)
    vmem = pl.BlockSpec(memory_space=pltpu.VMEM)
    return pl.pallas_call(
        functools.partial(self_full_kernel, blocks.shape[0], tuple(spans)),
        out_shape=jax.ShapeDtypeStruct(states.shape, jnp.bfloat16),
        in_specs=[pl.BlockSpec(memory_space=pltpu.SMEM)] + [vmem] * 6,
        out_specs=vmem,
        scratch_shapes=[pltpu.VMEM((n_q, HD), jnp.bfloat16)],
        compiler_params=pltpu.CompilerParams(vmem_limit_bytes=48 * 1024 * 1024),
    )(lens, states, gain[None, :], blocks, cache_blk, g, f)


def pack_gather(pieces):
    flat = jnp.concatenate([w.reshape(-1) for w, _ in pieces])
    whole = lax.all_gather(flat, "req", axis=0, tiled=False)
    n_req = whole.shape[0]
    out, at = [], 0
    for w, axis in pieces:
        size = w.size
        part = whole[:, at : at + size].reshape((n_req,) + w.shape)
        at += size
        part = jnp.moveaxis(part, 0, axis)
        shape = list(w.shape)
        shape[axis] *= n_req
        out.append(part.reshape(shape))
    return out


MESH_IDS = pl.DeviceIdType.MESH


def greet_all(n_blk, me, req):
    barrier = pltpu.get_barrier_semaphore()
    for k in range(1, n_blk):
        peer = lax.rem(me + k, n_blk)
        pl.semaphore_signal(barrier, inc=1, device_id=(req, peer), device_id_type=MESH_IDS)
    pl.semaphore_wait(barrier, n_blk - 1)


def chunk_of(b, n_blk):
    return lax.rem(b, 2) * (n_blk // 2) + b // 2


def scatter_kernel(n_blk, part_ref, out_ref, recv, send_sem, recv_sem):
    me = lax.axis_index("blk")
    req = lax.axis_index("req")
    rows = out_ref.shape[0]
    greet_all(n_blk, me, req)
    copies = []
    for k in range(1, n_blk):
        peer = lax.rem(me + k, n_blk)
        copy = pltpu.make_async_remote_copy(
            src_ref=part_ref.at[pl.ds(pl.multiple_of(chunk_of(peer, n_blk) * rows, rows), rows)],
            dst_ref=recv.at[me],
            send_sem=send_sem.at[peer],
            recv_sem=recv_sem.at[me],
            device_id=(req, peer),
            device_id_type=MESH_IDS,
        )
        copy.start()
        copies.append(copy)
    own = pl.ds(pl.multiple_of(chunk_of(me, n_blk) * rows, rows), rows)
    total = part_ref[own, :].astype(jnp.float32)
    for k in range(1, n_blk):
        src = lax.rem(me + n_blk - k, n_blk)
        incoming = pltpu.make_async_remote_copy(
            src_ref=part_ref.at[pl.ds(0, rows)],
            dst_ref=recv.at[src],
            send_sem=send_sem.at[src],
            recv_sem=recv_sem.at[src],
            device_id=(req, src),
            device_id_type=MESH_IDS,
        )
        incoming.wait_recv()
        total = total + recv[src].astype(jnp.float32)
    for copy in copies:
        copy.wait_send()
    out_ref[...] = total


def gather_kernel(n_blk, piece_ref, out_ref, send_sem, recv_sem):
    b = lax.axis_index("blk")
    req = lax.axis_index("req")
    n_grp = n_blk // 2
    g = b // 2
    c = lax.rem(b, 2)
    partner = g * 2 + 1 - c
    rows = piece_ref.shape[0]
    half = n_grp * rows
    barrier = pltpu.get_barrier_semaphore()
    for k in range(1, n_grp):
        peer = lax.rem(g + k, n_grp) * 2 + c
        pl.semaphore_signal(barrier, inc=1, device_id=(req, peer), device_id_type=MESH_IDS)
    pl.semaphore_signal(barrier, inc=1, device_id=(req, partner), device_id_type=MESH_IDS)
    pl.semaphore_wait(barrier, n_grp)
    mine = pl.ds(pl.multiple_of(c * half + g * rows, rows), rows)
    sends = []
    for k in range(1, n_grp):
        peer = lax.rem(g + k, n_grp) * 2 + c
        copy = pltpu.make_async_remote_copy(
            src_ref=piece_ref,
            dst_ref=out_ref.at[mine],
            send_sem=send_sem.at[k],
            recv_sem=recv_sem.at[g],
            device_id=(req, peer),
            device_id_type=MESH_IDS,
        )
        copy.start()
        sends.append(copy)
    copy = pltpu.make_async_remote_copy(
        src_ref=piece_ref,
        dst_ref=out_ref.at[mine],
        send_sem=send_sem.at[0],
        recv_sem=recv_sem.at[n_grp + g],
        device_id=(req, partner),
        device_id_type=MESH_IDS,
    )
    copy.start()
    sends.append(copy)
    out_ref[mine, :] = piece_ref[...]
    for k in range(1, n_grp):
        grp = lax.rem(g + n_grp - k, n_grp)
        there = pl.ds(pl.multiple_of(c * half + grp * rows, rows), rows)
        incoming = pltpu.make_async_remote_copy(
            src_ref=piece_ref,
            dst_ref=out_ref.at[there],
            send_sem=send_sem.at[0],
            recv_sem=recv_sem.at[grp],
            device_id=(req, grp * 2 + c),
            device_id_type=MESH_IDS,
        )
        incoming.wait_recv()
        forward = pltpu.make_async_remote_copy(
            src_ref=out_ref.at[there],
            dst_ref=out_ref.at[there],
            send_sem=send_sem.at[n_grp + k],
            recv_sem=recv_sem.at[n_grp + grp],
            device_id=(req, partner),
            device_id_type=MESH_IDS,
        )
        forward.start()
        sends.append(forward)
    for grp in range(n_grp):
        there = pl.ds(pl.multiple_of((1 - c) * half + grp * rows, rows), rows)
        incoming = pltpu.make_async_remote_copy(
            src_ref=piece_ref,
            dst_ref=out_ref.at[there],
            send_sem=send_sem.at[0],
            recv_sem=recv_sem.at[n_grp + grp],
            device_id=(req, partner),
            device_id_type=MESH_IDS,
        )
        incoming.wait_recv()
    for copy in sends:
        copy.wait_send()


def blk_scatter(part):
    n_blk = lax.axis_size("blk")
    rows = part.shape[0] // n_blk
    vmem = pl.BlockSpec(memory_space=pltpu.VMEM)
    return pl.pallas_call(
        functools.partial(scatter_kernel, n_blk),
        out_shape=jax.ShapeDtypeStruct((rows, part.shape[1]), jnp.float32),
        in_specs=[vmem],
        out_specs=vmem,
        scratch_shapes=[
            pltpu.VMEM((n_blk, rows, part.shape[1]), part.dtype),
            pltpu.SemaphoreType.DMA((n_blk,)),
            pltpu.SemaphoreType.DMA((n_blk,)),
        ],
        compiler_params=pltpu.CompilerParams(collective_id=1, has_side_effects=True),
    )(part)


def blk_gather(piece):
    n_blk = lax.axis_size("blk")
    rows = piece.shape[0]
    vmem = pl.BlockSpec(memory_space=pltpu.VMEM)
    return pl.pallas_call(
        functools.partial(gather_kernel, n_blk),
        out_shape=jax.ShapeDtypeStruct((rows * n_blk, piece.shape[1]), piece.dtype),
        in_specs=[vmem],
        out_specs=vmem,
        scratch_shapes=[
            pltpu.SemaphoreType.DMA((n_blk,)),
            pltpu.SemaphoreType.DMA((n_blk,)),
        ],
        compiler_params=pltpu.CompilerParams(collective_id=2, has_side_effects=True),
    )(piece)


def prologue_kernel(n_req, n_blk, ordered_ref, packed_ref, cache_ref, wts_ref, w_send, w_recv, c_send, c_recv, local_sem):
    r = lax.axis_index("req")
    b = lax.axis_index("blk")
    n_slot, span, width = ordered_ref.shape
    piece = width // 2
    copies = []
    for k in range(1, n_req):
        peer = lax.rem(r + k, n_req)
        copy = pltpu.make_async_remote_copy(
            src_ref=packed_ref,
            dst_ref=wts_ref.at[r],
            send_sem=w_send.at[peer],
            recv_sem=w_recv.at[r],
            device_id=(peer, b),
            device_id_type=MESH_IDS,
        )
        copy.start()
        copies.append(copy)
    rows = pl.ds(pl.multiple_of(b * span, span), span)
    for k in range(n_slot):
        s = lax.rem(b + k, n_slot)
        for hh in range(2):
            head = 2 * r + hh
            is_self = jnp.logical_and(r == s, head == b)
            src = ordered_ref.at[s, :, pl.ds(hh * piece, piece)]
            copy = pltpu.make_async_remote_copy(
                src_ref=src,
                dst_ref=cache_ref.at[rows],
                send_sem=c_send.at[k * 2 + hh],
                recv_sem=c_recv.at[b],
                device_id=(s, head),
                device_id_type=MESH_IDS,
            )

            @pl.when(jnp.logical_not(is_self))
            def _():
                copy.start()

            @pl.when(is_self)
            def _():
                local = pltpu.make_async_copy(src, cache_ref.at[rows], local_sem.at[0])
                local.start()
                local.wait()

            copies.append((copy, is_self))
    wts_ref[r] = packed_ref[...]
    for k in range(1, n_req):
        src_req = lax.rem(r + n_req - k, n_req)
        incoming = pltpu.make_async_remote_copy(
            src_ref=packed_ref,
            dst_ref=wts_ref.at[src_req],
            send_sem=w_send.at[src_req],
            recv_sem=w_recv.at[src_req],
            device_id=(src_req, b),
            device_id_type=MESH_IDS,
        )
        incoming.wait_recv()
    owner = b // 2
    for j in range(n_blk):
        incoming = pltpu.make_async_remote_copy(
            src_ref=ordered_ref.at[0, :, pl.ds(0, piece)],
            dst_ref=cache_ref.at[pl.ds(j * span, span)],
            send_sem=c_send.at[0],
            recv_sem=c_recv.at[j],
            device_id=(owner, j),
            device_id_type=MESH_IDS,
        )

        @pl.when(jnp.logical_not(jnp.logical_and(owner == r, j == b)))
        def _():
            incoming.wait_recv()

    for item in copies:
        if isinstance(item, tuple):
            copy, is_self = item

            @pl.when(jnp.logical_not(is_self))
            def _():
                copy.wait_send()

        else:
            item.wait_send()


def prologue(ordered, packed):
    n_req = lax.axis_size("req")
    n_blk = lax.axis_size("blk")
    n_slot, span, width = ordered.shape
    any_spec = pl.BlockSpec(memory_space=pl.ANY)
    vmem = pl.BlockSpec(memory_space=pltpu.VMEM)
    return pl.pallas_call(
        functools.partial(prologue_kernel, n_req, n_blk),
        out_shape=(
            jax.ShapeDtypeStruct((span * n_blk, width // 2), ordered.dtype),
            jax.ShapeDtypeStruct((n_req,) + packed.shape, packed.dtype),
        ),
        in_specs=[any_spec, vmem],
        out_specs=(any_spec, vmem),
        scratch_shapes=[
            pltpu.SemaphoreType.DMA((n_req,)),
            pltpu.SemaphoreType.DMA((n_req,)),
            pltpu.SemaphoreType.DMA((2 * n_slot,)),
            pltpu.SemaphoreType.DMA((n_blk,)),
            pltpu.SemaphoreType.DMA((1,)),
        ],
        compiler_params=pltpu.CompilerParams(has_side_effects=True),
    )(ordered, packed)


def unpack(whole, pieces):
    n_req = whole.shape[0]
    whole = whole.reshape(n_req, -1)
    out, at = [], 0
    for w, axis in pieces:
        size = w.size
        part = whole[:, at : at + size].reshape((n_req,) + w.shape)
        at += size
        part = jnp.moveaxis(part, 0, axis)
        shape = list(w.shape)
        shape[axis] *= n_req
        out.append(part.reshape(shape))
    return out


def lane_pack(pieces):
    blocks = []
    for w, axis in pieces:
        flat = w.reshape(w.shape[0], -1)
        blocks.append(flat.T if axis == 0 else flat)
    packed = jnp.concatenate(blocks, axis=0)
    return lax.all_gather(packed, "req", axis=0, tiled=False)


def per_device(
    new_states,
    encoder_out,
    cache_in,
    slot_order,
    new_lengths,
    cache_lengths,
    enc_lengths,
    bucket_of,
    rel_bias,
    norm_gain,
    self_q,
    self_kv,
    self_out,
    cross_q,
    cross_kv,
    cross_out,
    ff_in,
    ff_out,
):
    blk_count = lax.axis_size("blk")
    heads_dev = H // blk_count
    width_dev = heads_dev * HD
    req_dev = cache_in.shape[0] // lax.axis_size("req")
    own_slot = lax.dynamic_index_in_dim(slot_order, lax.axis_index("req"), 0, keepdims=False)
    tables = jnp.stack([new_lengths, cache_lengths, enc_lengths])
    picked = lax.dynamic_slice_in_dim(tables, own_slot, 1, 1)
    lens = picked.reshape(-1).astype(jnp.int32)
    ordered = jnp.take(cache_in, slot_order, axis=0)
    onehot = (bucket_of[:, None] == jnp.arange(rel_bias.shape[0], dtype=jnp.int32)[None, :]).astype(
        jnp.float32
    )
    own_bias = lax.dynamic_slice_in_dim(rel_bias, lax.axis_index("blk") * heads_dev, heads_dev, 1)
    bias_dist = jnp.dot(onehot, own_bias, precision=lax.Precision.HIGHEST).T
    early = [(self_q, 0), (self_kv, 0), (self_out, 1)]
    late = [(cross_q, 0), (cross_kv, 0), (cross_out, 1), (ff_in, 0), (ff_out, 1)]
    blocks = []
    for w, axis in early:
        two_d = w.reshape(w.shape[0], -1)
        blocks.append(two_d.T if axis == 0 else two_d)
    cache_blk, early_blocks = prologue(ordered, jnp.concatenate(blocks, axis=0))
    cache_dec = cache_blk[None]
    late_blocks = lane_pack(late)
    n_blk = lax.axis_size("blk")
    rows_dev = new_states.shape[0] // n_blk
    own_rows = lax.dynamic_slice_in_dim(
        new_states, chunk_of(lax.axis_index("blk"), n_blk) * rows_dev, rows_dev, 0
    ).astype(jnp.float32)
    part = self_branch(
        new_states,
        norm_gain[0],
        early_blocks,
        block_spans(early),
        cache_blk,
        bias_dist[0],
        lens,
    )
    residual, normed = blk_stage(part, own_rows, norm_gain[1], False)
    spans = block_spans(late)
    part = cross_branch(normed, encoder_out, late_blocks, spans[:3], lens)
    residual, normed = blk_stage(part.astype(jnp.bfloat16), residual, norm_gain[2], False)
    part = ffn_branch(normed, late_blocks, spans[3:])
    _, layer_out = blk_stage(part, residual, norm_gain[2], True)
    return (layer_out, cache_dec)


def solution(mesh):
    in_specs = (
        P("req", None),
        P("req", None),
        P(None, "blk", "req"),
        P(),
        P(),
        P(),
        P(),
        P(),
        P(),
        P(),
        P("req", "blk"),
        P("req", None, "blk"),
        P("blk", "req"),
        P("req", "blk"),
        P("req", None, "blk"),
        P("blk", "req"),
        P("req", None, "blk"),
        P("blk", "req"),
    )
    out_specs = (P("req", None), P("req", None, "blk"))
    return jax.shard_map(
        per_device, mesh=mesh, in_specs=in_specs, out_specs=out_specs, check_vma=False
    )
```

```python
import functools

import jax
import jax.numpy as jnp
from jax import lax
from jax.sharding import PartitionSpec as P
from jax.experimental import pallas as pl
from jax.experimental.pallas import tpu as pltpu

H = 16
HD = 64


EPSILON = 1e-06
NEG_FILL = -1e30


def rms_rows(row_block, gain):
    mean_square = jnp.mean(row_block * row_block, axis=-1, keepdims=True)
    return (row_block * lax.rsqrt(mean_square + EPSILON) * gain).astype(jnp.bfloat16)


def softmax_rows(scores):
    row_top = jnp.max(scores, axis=-1, keepdims=True)
    weights = jnp.exp(scores - row_top)
    return (weights / jnp.sum(weights, axis=-1, keepdims=True)).astype(jnp.bfloat16)


def pick_lengths(table, own_slots):
    matches = own_slots[:, None] == jnp.arange(table.shape[0], dtype=jnp.int32)[None, :]
    return jnp.sum(jnp.where(matches, table[None, :], 0), axis=1)


def shifted_bias(bias_dist, base, row_count, col_count):
    heads_here, span_len = bias_dist.shape
    line_len = row_count + col_count - 1
    steps = jnp.arange(line_len + 1, dtype=jnp.int32)
    line = bias_dist[:, jnp.clip(base + row_count - 1 - steps, 0, span_len - 1)]
    tiled = jnp.broadcast_to(line[:, None, :], (heads_here, row_count, line_len + 1))
    flat = tiled.reshape(heads_here, row_count * (line_len + 1))[:, : row_count * line_len]
    skewed = flat.reshape(heads_here, row_count, line_len)
    return skewed[:, :, row_count - 1 : row_count - 1 + col_count]


def row_total(left, weight):
    term = jnp.dot(left, weight, preferred_element_type=jnp.float32)
    return lax.psum(term.astype(jnp.bfloat16), "blk").astype(jnp.float32)


def cached_scores(queries, key_rows, first_col, old_len, bias_dist):
    col_ids = first_col + jnp.arange(key_rows.shape[0], dtype=jnp.int32)[None, :]
    scores = jnp.einsum("qhe,khe->hqk", queries, key_rows, preferred_element_type=jnp.float32)
    scores = scores + shifted_bias(
        bias_dist, old_len - first_col, queries.shape[0], key_rows.shape[0]
    )
    return jnp.where((col_ids < old_len)[None], scores, NEG_FILL)


def fresh_scores(queries, fresh_keys, fresh_len, bias_dist):
    row_ids = jnp.arange(queries.shape[0], dtype=jnp.int32)[:, None]
    col_ids = jnp.arange(fresh_keys.shape[0], dtype=jnp.int32)[None, :]
    scores = jnp.einsum("qhe,khe->hqk", queries, fresh_keys, preferred_element_type=jnp.float32)
    scores = scores + shifted_bias(bias_dist, 0, queries.shape[0], fresh_keys.shape[0])
    admitted = (col_ids <= row_ids) & (col_ids < fresh_len)
    return jnp.where(admitted[None], scores, NEG_FILL)


def self_padded(
    queries, key_rows, value_rows, fresh_keys, fresh_values, old_len, fresh_len, bias_dist
):
    scores = jnp.concatenate(
        [
            cached_scores(queries, key_rows, 0, old_len, bias_dist),
            fresh_scores(queries, fresh_keys, fresh_len, bias_dist),
        ],
        axis=2,
    )
    weights = softmax_rows(scores)
    value_all = jnp.concatenate([value_rows, fresh_values], axis=0)
    return jnp.einsum(
        "hqk,khe->qhe", weights, value_all, preferred_element_type=jnp.float32
    ).astype(jnp.bfloat16)


def self_attend(queries, key_value, cache_dec, slot_old, slot_new, bias_dist, heads_dev):
    req_dev, cache_len = (cache_dec.shape[0], cache_dec.shape[1])
    cache_split = cache_dec.reshape(req_dev, cache_len, heads_dev, 2, -1)

    def one_request(request):
        queries_one, pair_one, cache_one, old_len, fresh_len = request
        return self_padded(
            queries_one,
            cache_one[:, :, 0],
            cache_one[:, :, 1],
            pair_one[:, 0],
            pair_one[:, 1],
            old_len,
            fresh_len,
            bias_dist,
        )

    return lax.map(one_request, (queries, key_value, cache_split, slot_old, slot_new))


def cross_attend(queries, key_value, slot_enc):
    scores = jnp.einsum(
        "rqhe,rkhe->rhqk", queries, key_value[:, :, 0], preferred_element_type=jnp.float32
    )
    col_ids = jnp.arange(key_value.shape[1], dtype=jnp.int32)
    scores = jnp.where(
        col_ids[None, None, None, :] < slot_enc[:, None, None, None], scores, NEG_FILL
    )
    weights = softmax_rows(scores)
    return jnp.einsum(
        "rhqk,rkhe->rqhe", weights, key_value[:, :, 1], preferred_element_type=jnp.float32
    ).astype(jnp.bfloat16)


def add_branch(residual, left, weight, gain):
    residual = residual + row_total(left, weight)
    normed = rms_rows(residual, gain)
    return (residual, normed)


TQ = 128


def stage_kernel(n_blk, final, extra, *refs):
    if extra:
        (part_ref, resid_ref, gain_ref, packed_ref, res_out, full_ref, wts_ref,
         recv_a, send_b, recv_b, x_send, x_recv, b_send, b_recv, ag_send, ag_recv, w_send, w_recv) = refs
    else:
        (part_ref, resid_ref, gain_ref, res_out, full_ref,
         recv_a, send_b, recv_b, x_send, x_recv, b_send, b_recv, ag_send, ag_recv) = refs
    me = lax.axis_index("blk")
    req = lax.axis_index("req")
    rows = resid_ref.shape[0]
    n_grp = n_blk // 2
    g = me // 2
    c = lax.rem(me, 2)
    partner = g * 2 + 1 - c
    half = n_grp * rows
    n_req = wts_ref.shape[0] if extra else 1
    barrier = pltpu.get_barrier_semaphore()
    for k in range(1, n_grp):
        peer = lax.rem(g + k, n_grp) * 2 + c
        pl.semaphore_signal(barrier, inc=1, device_id=(req, peer), device_id_type=MESH_IDS)
    pl.semaphore_signal(barrier, inc=1, device_id=(req, partner), device_id_type=MESH_IDS)
    for k in range(1, n_req):
        peer = lax.rem(req + k, n_req)
        pl.semaphore_signal(barrier, inc=1, device_id=(peer, me), device_id_type=MESH_IDS)
    pl.semaphore_wait(barrier, n_grp + n_req - 1)
    sends = []
    for k in range(n_grp):
        grp = lax.rem(g + 1 + k, n_grp)
        exchange = pltpu.make_async_remote_copy(
            src_ref=part_ref.at[pl.ds(pl.multiple_of((1 - c) * half + grp * rows, rows), rows)],
            dst_ref=recv_a.at[grp],
            send_sem=x_send.at[k],
            recv_sem=x_recv.at[grp],
            device_id=(req, partner),
            device_id_type=MESH_IDS,
        )
        exchange.start()
        sends.append(exchange)
    for k in range(1, n_req):
        peer = lax.rem(req + k, n_req)
        copy = pltpu.make_async_remote_copy(
            src_ref=packed_ref,
            dst_ref=wts_ref.at[req],
            send_sem=w_send.at[peer],
            recv_sem=w_recv.at[req],
            device_id=(peer, me),
            device_id_type=MESH_IDS,
        )
        copy.start()
        sends.append(copy)
    total = None
    for k in range(n_grp):
        grp = lax.rem(g + 1 + k, n_grp)
        incoming = pltpu.make_async_remote_copy(
            src_ref=part_ref.at[pl.ds(0, rows)],
            dst_ref=recv_a.at[grp],
            send_sem=x_send.at[k],
            recv_sem=x_recv.at[grp],
            device_id=(req, partner),
            device_id_type=MESH_IDS,
        )
        incoming.wait_recv()
        pair = part_ref[pl.ds(pl.multiple_of(c * half + grp * rows, rows), rows), :].astype(
            jnp.float32
        ) + recv_a[grp].astype(jnp.float32)
        if k == n_grp - 1:
            total = pair
        else:
            send_b[grp] = pair.astype(send_b.dtype)
            copy = pltpu.make_async_remote_copy(
                src_ref=send_b.at[grp],
                dst_ref=recv_b.at[g],
                send_sem=b_send.at[grp],
                recv_sem=b_recv.at[g],
                device_id=(req, grp * 2 + c),
                device_id_type=MESH_IDS,
            )
            copy.start()
            sends.append(copy)
    for k in range(1, n_grp):
        grp = lax.rem(g + n_grp - k, n_grp)
        incoming = pltpu.make_async_remote_copy(
            src_ref=send_b.at[0],
            dst_ref=recv_b.at[grp],
            send_sem=b_send.at[grp],
            recv_sem=b_recv.at[grp],
            device_id=(req, grp * 2 + c),
            device_id_type=MESH_IDS,
        )
        incoming.wait_recv()
        total = total + recv_b[grp].astype(jnp.float32)
    mine = pl.ds(pl.multiple_of(c * half + g * rows, rows), rows)
    resid = resid_ref[...] + total
    res_out[...] = resid
    if final:
        full_ref[mine, :] = resid.astype(full_ref.dtype)
    else:
        mean_square = jnp.mean(resid * resid, axis=-1, keepdims=True)
        full_ref[mine, :] = (resid * lax.rsqrt(mean_square + EPSILON) * gain_ref[...]).astype(
            full_ref.dtype
        )
    for k in range(1, n_grp):
        peer = lax.rem(g + k, n_grp) * 2 + c
        copy = pltpu.make_async_remote_copy(
            src_ref=full_ref.at[mine],
            dst_ref=full_ref.at[mine],
            send_sem=ag_send.at[k],
            recv_sem=ag_recv.at[g],
            device_id=(req, peer),
            device_id_type=MESH_IDS,
        )
        copy.start()
        sends.append(copy)
    copy = pltpu.make_async_remote_copy(
        src_ref=full_ref.at[mine],
        dst_ref=full_ref.at[mine],
        send_sem=ag_send.at[0],
        recv_sem=ag_recv.at[n_grp + g],
        device_id=(req, partner),
        device_id_type=MESH_IDS,
    )
    copy.start()
    sends.append(copy)
    for k in range(1, n_grp):
        grp = lax.rem(g + n_grp - k, n_grp)
        there = pl.ds(pl.multiple_of(c * half + grp * rows, rows), rows)
        incoming = pltpu.make_async_remote_copy(
            src_ref=full_ref.at[there],
            dst_ref=full_ref.at[there],
            send_sem=ag_send.at[0],
            recv_sem=ag_recv.at[grp],
            device_id=(req, grp * 2 + c),
            device_id_type=MESH_IDS,
        )
        incoming.wait_recv()
        forward = pltpu.make_async_remote_copy(
            src_ref=full_ref.at[there],
            dst_ref=full_ref.at[there],
            send_sem=ag_send.at[n_grp + k],
            recv_sem=ag_recv.at[n_grp + grp],
            device_id=(req, partner),
            device_id_type=MESH_IDS,
        )
        forward.start()
        sends.append(forward)
    for grp in range(n_grp):
        there = pl.ds(pl.multiple_of((1 - c) * half + grp * rows, rows), rows)
        incoming = pltpu.make_async_remote_copy(
            src_ref=full_ref.at[there],
            dst_ref=full_ref.at[there],
            send_sem=ag_send.at[0],
            recv_sem=ag_recv.at[n_grp + grp],
            device_id=(req, partner),
            device_id_type=MESH_IDS,
        )
        incoming.wait_recv()
    if extra:
        wts_ref[req] = packed_ref[...]
        for k in range(1, n_req):
            src = lax.rem(req + n_req - k, n_req)
            incoming = pltpu.make_async_remote_copy(
                src_ref=packed_ref,
                dst_ref=wts_ref.at[src],
                send_sem=w_send.at[src],
                recv_sem=w_recv.at[src],
                device_id=(src, me),
                device_id_type=MESH_IDS,
            )
            incoming.wait_recv()
    for copy in sends:
        copy.wait_send()


def blk_stage(part, resid, gain, final, packed=None):
    n_blk = lax.axis_size("blk")
    rows, width = resid.shape
    vmem = pl.BlockSpec(memory_space=pltpu.VMEM)
    extra = packed is not None
    outs = [
        jax.ShapeDtypeStruct((rows, width), jnp.float32),
        jax.ShapeDtypeStruct((rows * n_blk, width), jnp.bfloat16),
    ]
    n_grp = n_blk // 2
    scratch = [
        pltpu.VMEM((n_grp, rows, width), part.dtype),
        pltpu.VMEM((n_grp, rows, width), part.dtype),
        pltpu.VMEM((n_grp, rows, width), part.dtype),
        pltpu.SemaphoreType.DMA((n_grp,)),
        pltpu.SemaphoreType.DMA((n_grp,)),
        pltpu.SemaphoreType.DMA((n_grp,)),
        pltpu.SemaphoreType.DMA((n_grp,)),
        pltpu.SemaphoreType.DMA((n_blk,)),
        pltpu.SemaphoreType.DMA((n_blk,)),
    ]
    args = [part, resid, gain[None, :]]
    if extra:
        n_req = lax.axis_size("req")
        outs.append(jax.ShapeDtypeStruct((n_req,) + packed.shape, packed.dtype))
        scratch += [pltpu.SemaphoreType.DMA((n_req,)), pltpu.SemaphoreType.DMA((n_req,))]
        args.append(packed)
    return pl.pallas_call(
        functools.partial(stage_kernel, n_blk, final, extra),
        out_shape=tuple(outs),
        in_specs=[vmem] * len(args),
        out_specs=tuple([vmem] * len(outs)),
        scratch_shapes=scratch,
        compiler_params=pltpu.CompilerParams(
            collective_id=5 if extra else (4 if final else 3), has_side_effects=True
        ),
    )(*args)


def cross_kernel(n_req, spans, len_ref, normed_ref, enc_ref, w_ref, out_ref):
    enc_len = len_ref[2]
    (q_at, q_len), (kv_at, kv_len), (o_at, o_len) = spans
    nt = (((1,), (1,)), ((), ()))
    width = w_ref.shape[2]
    queries = None
    pair = None
    for r in range(n_req):
        cols = slice(r * width, (r + 1) * width)
        term = lax.dot_general(
            normed_ref[:, cols], w_ref[r, q_at : q_at + q_len, :], nt,
            preferred_element_type=jnp.float32,
        )
        queries = term if queries is None else queries + term
        term = lax.dot_general(
            enc_ref[:, cols], w_ref[r, kv_at : kv_at + kv_len, :], nt,
            preferred_element_type=jnp.float32,
        )
        pair = term if pair is None else pair + term
    queries = queries.astype(jnp.bfloat16)
    pair = pair.astype(jnp.bfloat16)
    keys = pair[:, :HD]
    values = pair[:, HD:]
    scores = lax.dot_general(queries, keys, nt, preferred_element_type=jnp.float32)
    col = lax.broadcasted_iota(jnp.int32, scores.shape, 1)
    scores = jnp.where(col < enc_len, scores, NEG_FILL)
    top = jnp.max(scores, axis=1, keepdims=True)
    weights = jnp.exp(scores - top)
    weights = (weights / jnp.sum(weights, axis=1, keepdims=True)).astype(jnp.bfloat16)
    context = jnp.dot(weights, values, preferred_element_type=jnp.float32).astype(jnp.bfloat16)
    for r in range(n_req):
        out_ref[:, r * width : (r + 1) * width] = jnp.dot(
            context, w_ref[r, o_at : o_at + o_len, :], preferred_element_type=jnp.float32
        ).astype(out_ref.dtype)


def ffn_kernel(n_req, spans, normed_ref, w_ref, out_ref):
    (i_at, i_len), (o_at, o_len) = spans
    nt = (((1,), (1,)), ((), ()))
    width = w_ref.shape[2]
    ff_dev = o_len
    gate_up = None
    for r in range(n_req):
        term = lax.dot_general(
            normed_ref[:, r * width : (r + 1) * width], w_ref[r, i_at : i_at + i_len, :], nt,
            preferred_element_type=jnp.float32,
        )
        gate_up = term if gate_up is None else gate_up + term
    hidden = (jax.nn.gelu(gate_up[:, :ff_dev], approximate=True) * gate_up[:, ff_dev:]).astype(
        jnp.bfloat16
    )
    for r in range(n_req):
        out_ref[:, r * width : (r + 1) * width] = jnp.dot(
            hidden, w_ref[r, o_at : o_at + o_len, :], preferred_element_type=jnp.float32
        ).astype(out_ref.dtype)


def block_spans(pieces):
    spans, at = [], 0
    for w, axis in pieces:
        rows = w.size // w.shape[0] if axis == 0 else w.shape[0]
        spans.append((at, rows))
        at += rows
    return spans


def cross_branch(normed, enc, blocks, spans, enc_len):
    vmem = pl.BlockSpec(memory_space=pltpu.VMEM)
    return pl.pallas_call(
        functools.partial(cross_kernel, blocks.shape[0], tuple(spans)),
        out_shape=jax.ShapeDtypeStruct(normed.shape, jnp.bfloat16),
        in_specs=[pl.BlockSpec(memory_space=pltpu.SMEM)] + [vmem] * 3,
        out_specs=vmem,
    )(enc_len, normed, enc, blocks)


def ffn_branch(normed, blocks, spans):
    vmem = pl.BlockSpec(memory_space=pltpu.VMEM)
    return pl.pallas_call(
        functools.partial(ffn_kernel, blocks.shape[0], tuple(spans)),
        out_shape=jax.ShapeDtypeStruct(normed.shape, jnp.bfloat16),
        in_specs=[vmem] * 2,
        out_specs=vmem,
    )(normed, blocks)


def self_kernel(lens_ref, q_ref, c_ref, kn_ref, vn_ref, g_ref, f_ref, o_ref):
    old_len = lens_ref[0]
    fresh_len = lens_ref[1]
    n_q = q_ref.shape[0]
    n_ctx = c_ref.shape[0]
    wide_old = n_ctx + TQ
    wide_new = n_q + TQ
    k_old = c_ref[:, :HD]
    v_old = c_ref[:, HD:]
    k_new = kn_ref[...]
    v_new = vn_ref[...]
    dims = (((1,), (1,)), ((), ()))
    for t in range(n_q // TQ):
        q = q_ref[t * TQ : (t + 1) * TQ, :]
        start = n_q - TQ - t * TQ
        s_old = lax.dot_general(q, k_old, dims, preferred_element_type=jnp.float32)
        line = jnp.broadcast_to(g_ref[:, start : start + wide_old], (TQ, wide_old))
        bias = pltpu.roll(line, wide_old - (TQ - 1), 1, stride=1, stride_axis=0)[:, :n_ctx]
        col = lax.broadcasted_iota(jnp.int32, (TQ, n_ctx), 1)
        s_old = jnp.where(col < old_len, s_old + bias, NEG_FILL)
        s_new = lax.dot_general(q, k_new, dims, preferred_element_type=jnp.float32)
        line = jnp.broadcast_to(f_ref[:, start : start + wide_new], (TQ, wide_new))
        bias = pltpu.roll(line, wide_new - (TQ - 1), 1, stride=1, stride_axis=0)[:, :n_q]
        row = lax.broadcasted_iota(jnp.int32, (TQ, n_q), 0) + t * TQ
        col = lax.broadcasted_iota(jnp.int32, (TQ, n_q), 1)
        s_new = jnp.where((col <= row) & (col < fresh_len), s_new + bias, NEG_FILL)
        top = jnp.maximum(
            jnp.max(s_old, axis=1, keepdims=True), jnp.max(s_new, axis=1, keepdims=True)
        )
        p_old = jnp.exp(s_old - top)
        p_new = jnp.exp(s_new - top)
        total = jnp.sum(p_old, axis=1, keepdims=True) + jnp.sum(p_new, axis=1, keepdims=True)
        w_old = (p_old / total).astype(jnp.bfloat16)
        w_new = (p_new / total).astype(jnp.bfloat16)
        out = jnp.dot(w_old, v_old, preferred_element_type=jnp.float32) + jnp.dot(
            w_new, v_new, preferred_element_type=jnp.float32
        )
        o_ref[t * TQ : (t + 1) * TQ, :] = out.astype(jnp.bfloat16)


def bias_lines(line, old_len, n_q, n_ctx):
    span = line.shape[0]
    ext = jnp.concatenate([jnp.broadcast_to(line[:1], (n_ctx,)), line])
    rev = ext[::-1]
    g = lax.dynamic_slice_in_dim(rev, n_ctx - old_len, span)
    f = rev[n_ctx : n_ctx + 2 * n_q]
    return g[None, :], f[None, :]


def self_attention(q, cache_blk, k_new, v_new, line, old_len, fresh_len):
    n_q = q.shape[0]
    n_ctx = cache_blk.shape[0]
    g, f = bias_lines(line, old_len, n_q, n_ctx)
    lens = jnp.stack([old_len, fresh_len]).astype(jnp.int32)
    vmem = pl.BlockSpec(memory_space=pltpu.VMEM)
    return pl.pallas_call(
        self_kernel,
        out_shape=jax.ShapeDtypeStruct((n_q, HD), jnp.bfloat16),
        in_specs=[pl.BlockSpec(memory_space=pltpu.SMEM)] + [vmem] * 6,
        out_specs=vmem,
        compiler_params=pltpu.CompilerParams(vmem_limit_bytes=48 * 1024 * 1024),
    )(lens, q, cache_blk, k_new, v_new, g, f)


def self_full_kernel(n_req, spans, lens_ref, x_ref, gain_ref, w_hbm, c_hbm, g_ref, f_ref, o_ref, ctx_ref, w_ref, c_ref, sems):
    w_copy = pltpu.make_async_copy(w_hbm, w_ref, sems.at[0])
    c_copy = pltpu.make_async_copy(c_hbm, c_ref, sems.at[1])
    w_copy.start()
    c_copy.start()
    fresh_len = lens_ref[0]
    old_len = lens_ref[1]
    (q_at, q_len), (kv_at, kv_len), (o_at, o_len) = spans
    nt = (((1,), (1,)), ((), ()))
    width = w_ref.shape[2]
    x = x_ref[...].astype(jnp.float32)
    mean_square = jnp.mean(x * x, axis=-1, keepdims=True)
    normed = (x * lax.rsqrt(mean_square + EPSILON) * gain_ref[...]).astype(jnp.bfloat16)
    w_copy.wait()
    queries = None
    pair = None
    for r in range(n_req):
        cols = slice(r * width, (r + 1) * width)
        term = lax.dot_general(
            normed[:, cols], w_ref[r, q_at : q_at + q_len, :], nt,
            preferred_element_type=jnp.float32,
        )
        queries = term if queries is None else queries + term
        term = lax.dot_general(
            normed[:, cols], w_ref[r, kv_at : kv_at + kv_len, :], nt,
            preferred_element_type=jnp.float32,
        )
        pair = term if pair is None else pair + term
    queries = queries.astype(jnp.bfloat16)
    pair = pair.astype(jnp.bfloat16)
    k_new = pair[:, :HD]
    v_new = pair[:, HD:]
    n_q = x_ref.shape[0]
    n_ctx = c_ref.shape[0]
    wide_old = n_ctx + TQ
    wide_new = n_q + TQ
    c_copy.wait()
    k_old = c_ref[:, :HD]
    v_old = c_ref[:, HD:]
    for t in range(n_q // TQ):
        q = queries[t * TQ : (t + 1) * TQ, :]
        start = n_q - TQ - t * TQ
        s_old = lax.dot_general(q, k_old, nt, preferred_element_type=jnp.float32)
        line = jnp.broadcast_to(g_ref[:, start : start + wide_old], (TQ, wide_old))
        bias = pltpu.roll(line, wide_old - (TQ - 1), 1, stride=1, stride_axis=0)[:, :n_ctx]
        col = lax.broadcasted_iota(jnp.int32, (TQ, n_ctx), 1)
        s_old = jnp.where(col < old_len, s_old + bias, NEG_FILL)
        s_new = lax.dot_general(q, k_new, nt, preferred_element_type=jnp.float32)
        line = jnp.broadcast_to(f_ref[:, start : start + wide_new], (TQ, wide_new))
        bias = pltpu.roll(line, wide_new - (TQ - 1), 1, stride=1, stride_axis=0)[:, :n_q]
        row = lax.broadcasted_iota(jnp.int32, (TQ, n_q), 0) + t * TQ
        col = lax.broadcasted_iota(jnp.int32, (TQ, n_q), 1)
        s_new = jnp.where((col <= row) & (col < fresh_len), s_new + bias, NEG_FILL)
        top = jnp.maximum(
            jnp.max(s_old, axis=1, keepdims=True), jnp.max(s_new, axis=1, keepdims=True)
        )
        p_old = jnp.exp(s_old - top)
        p_new = jnp.exp(s_new - top)
        total = jnp.sum(p_old, axis=1, keepdims=True) + jnp.sum(p_new, axis=1, keepdims=True)
        w_old = (p_old / total).astype(jnp.bfloat16)
        w_new = (p_new / total).astype(jnp.bfloat16)
        out = jnp.dot(w_old, v_old, preferred_element_type=jnp.float32) + jnp.dot(
            w_new, v_new, preferred_element_type=jnp.float32
        )
        ctx_ref[t * TQ : (t + 1) * TQ, :] = out.astype(jnp.bfloat16)
    context = ctx_ref[...]
    for r in range(n_req):
        o_ref[:, r * width : (r + 1) * width] = jnp.dot(
            context, w_ref[r, o_at : o_at + o_len, :], preferred_element_type=jnp.float32
        ).astype(o_ref.dtype)


def self_branch(states, gain, blocks, spans, cache_blk, line, lens):
    n_q = states.shape[0]
    n_ctx = cache_blk.shape[0]
    g, f = bias_lines(line, lens[1], n_q, n_ctx)
    vmem = pl.BlockSpec(memory_space=pltpu.VMEM)
    return pl.pallas_call(
        functools.partial(self_full_kernel, blocks.shape[0], tuple(spans)),
        out_shape=jax.ShapeDtypeStruct(states.shape, jnp.bfloat16),
        in_specs=[pl.BlockSpec(memory_space=pltpu.SMEM), vmem, vmem]
        + [pl.BlockSpec(memory_space=pl.ANY)] * 2
        + [vmem] * 2,
        out_specs=vmem,
        scratch_shapes=[
            pltpu.VMEM((n_q, HD), jnp.bfloat16),
            pltpu.VMEM(blocks.shape, blocks.dtype),
            pltpu.VMEM(cache_blk.shape, cache_blk.dtype),
            pltpu.SemaphoreType.DMA((2,)),
        ],
        compiler_params=pltpu.CompilerParams(vmem_limit_bytes=48 * 1024 * 1024),
    )(lens, states, gain[None, :], blocks, cache_blk, g, f)


def pack_gather(pieces):
    flat = jnp.concatenate([w.reshape(-1) for w, _ in pieces])
    whole = lax.all_gather(flat, "req", axis=0, tiled=False)
    n_req = whole.shape[0]
    out, at = [], 0
    for w, axis in pieces:
        size = w.size
        part = whole[:, at : at + size].reshape((n_req,) + w.shape)
        at += size
        part = jnp.moveaxis(part, 0, axis)
        shape = list(w.shape)
        shape[axis] *= n_req
        out.append(part.reshape(shape))
    return out


MESH_IDS = pl.DeviceIdType.MESH


def greet_all(n_blk, me, req):
    barrier = pltpu.get_barrier_semaphore()
    for k in range(1, n_blk):
        peer = lax.rem(me + k, n_blk)
        pl.semaphore_signal(barrier, inc=1, device_id=(req, peer), device_id_type=MESH_IDS)
    pl.semaphore_wait(barrier, n_blk - 1)


def chunk_of(b, n_blk):
    return lax.rem(b, 2) * (n_blk // 2) + b // 2


def scatter_kernel(n_blk, part_ref, out_ref, recv, send_sem, recv_sem):
    me = lax.axis_index("blk")
    req = lax.axis_index("req")
    rows = out_ref.shape[0]
    greet_all(n_blk, me, req)
    copies = []
    for k in range(1, n_blk):
        peer = lax.rem(me + k, n_blk)
        copy = pltpu.make_async_remote_copy(
            src_ref=part_ref.at[pl.ds(pl.multiple_of(chunk_of(peer, n_blk) * rows, rows), rows)],
            dst_ref=recv.at[me],
            send_sem=send_sem.at[peer],
            recv_sem=recv_sem.at[me],
            device_id=(req, peer),
            device_id_type=MESH_IDS,
        )
        copy.start()
        copies.append(copy)
    own = pl.ds(pl.multiple_of(chunk_of(me, n_blk) * rows, rows), rows)
    total = part_ref[own, :].astype(jnp.float32)
    for k in range(1, n_blk):
        src = lax.rem(me + n_blk - k, n_blk)
        incoming = pltpu.make_async_remote_copy(
            src_ref=part_ref.at[pl.ds(0, rows)],
            dst_ref=recv.at[src],
            send_sem=send_sem.at[src],
            recv_sem=recv_sem.at[src],
            device_id=(req, src),
            device_id_type=MESH_IDS,
        )
        incoming.wait_recv()
        total = total + recv[src].astype(jnp.float32)
    for copy in copies:
        copy.wait_send()
    out_ref[...] = total


def gather_kernel(n_blk, piece_ref, out_ref, send_sem, recv_sem):
    b = lax.axis_index("blk")
    req = lax.axis_index("req")
    n_grp = n_blk // 2
    g = b // 2
    c = lax.rem(b, 2)
    partner = g * 2 + 1 - c
    rows = piece_ref.shape[0]
    half = n_grp * rows
    barrier = pltpu.get_barrier_semaphore()
    for k in range(1, n_grp):
        peer = lax.rem(g + k, n_grp) * 2 + c
        pl.semaphore_signal(barrier, inc=1, device_id=(req, peer), device_id_type=MESH_IDS)
    pl.semaphore_signal(barrier, inc=1, device_id=(req, partner), device_id_type=MESH_IDS)
    pl.semaphore_wait(barrier, n_grp)
    mine = pl.ds(pl.multiple_of(c * half + g * rows, rows), rows)
    sends = []
    for k in range(1, n_grp):
        peer = lax.rem(g + k, n_grp) * 2 + c
        copy = pltpu.make_async_remote_copy(
            src_ref=piece_ref,
            dst_ref=out_ref.at[mine],
            send_sem=send_sem.at[k],
            recv_sem=recv_sem.at[g],
            device_id=(req, peer),
            device_id_type=MESH_IDS,
        )
        copy.start()
        sends.append(copy)
    copy = pltpu.make_async_remote_copy(
        src_ref=piece_ref,
        dst_ref=out_ref.at[mine],
        send_sem=send_sem.at[0],
        recv_sem=recv_sem.at[n_grp + g],
        device_id=(req, partner),
        device_id_type=MESH_IDS,
    )
    copy.start()
    sends.append(copy)
    out_ref[mine, :] = piece_ref[...]
    for k in range(1, n_grp):
        grp = lax.rem(g + n_grp - k, n_grp)
        there = pl.ds(pl.multiple_of(c * half + grp * rows, rows), rows)
        incoming = pltpu.make_async_remote_copy(
            src_ref=piece_ref,
            dst_ref=out_ref.at[there],
            send_sem=send_sem.at[0],
            recv_sem=recv_sem.at[grp],
            device_id=(req, grp * 2 + c),
            device_id_type=MESH_IDS,
        )
        incoming.wait_recv()
        forward = pltpu.make_async_remote_copy(
            src_ref=out_ref.at[there],
            dst_ref=out_ref.at[there],
            send_sem=send_sem.at[n_grp + k],
            recv_sem=recv_sem.at[n_grp + grp],
            device_id=(req, partner),
            device_id_type=MESH_IDS,
        )
        forward.start()
        sends.append(forward)
    for grp in range(n_grp):
        there = pl.ds(pl.multiple_of((1 - c) * half + grp * rows, rows), rows)
        incoming = pltpu.make_async_remote_copy(
            src_ref=piece_ref,
            dst_ref=out_ref.at[there],
            send_sem=send_sem.at[0],
            recv_sem=recv_sem.at[n_grp + grp],
            device_id=(req, partner),
            device_id_type=MESH_IDS,
        )
        incoming.wait_recv()
    for copy in sends:
        copy.wait_send()


def blk_scatter(part):
    n_blk = lax.axis_size("blk")
    rows = part.shape[0] // n_blk
    vmem = pl.BlockSpec(memory_space=pltpu.VMEM)
    return pl.pallas_call(
        functools.partial(scatter_kernel, n_blk),
        out_shape=jax.ShapeDtypeStruct((rows, part.shape[1]), jnp.float32),
        in_specs=[vmem],
        out_specs=vmem,
        scratch_shapes=[
            pltpu.VMEM((n_blk, rows, part.shape[1]), part.dtype),
            pltpu.SemaphoreType.DMA((n_blk,)),
            pltpu.SemaphoreType.DMA((n_blk,)),
        ],
        compiler_params=pltpu.CompilerParams(collective_id=1, has_side_effects=True),
    )(part)


def blk_gather(piece):
    n_blk = lax.axis_size("blk")
    rows = piece.shape[0]
    vmem = pl.BlockSpec(memory_space=pltpu.VMEM)
    return pl.pallas_call(
        functools.partial(gather_kernel, n_blk),
        out_shape=jax.ShapeDtypeStruct((rows * n_blk, piece.shape[1]), piece.dtype),
        in_specs=[vmem],
        out_specs=vmem,
        scratch_shapes=[
            pltpu.SemaphoreType.DMA((n_blk,)),
            pltpu.SemaphoreType.DMA((n_blk,)),
        ],
        compiler_params=pltpu.CompilerParams(collective_id=2, has_side_effects=True),
    )(piece)


def prologue_kernel(n_req, n_blk, ordered_ref, packed_ref, cache_ref, wts_ref, w_send, w_recv, c_send, c_recv, local_sem):
    r = lax.axis_index("req")
    b = lax.axis_index("blk")
    n_slot, span, width = ordered_ref.shape
    piece = width // 2
    copies = []
    for k in range(1, n_req):
        peer = lax.rem(r + k, n_req)
        copy = pltpu.make_async_remote_copy(
            src_ref=packed_ref,
            dst_ref=wts_ref.at[r],
            send_sem=w_send.at[peer],
            recv_sem=w_recv.at[r],
            device_id=(peer, b),
            device_id_type=MESH_IDS,
        )
        copy.start()
        copies.append(copy)
    rows = pl.ds(pl.multiple_of(b * span, span), span)
    for k in range(n_slot):
        s = lax.rem(b + k, n_slot)
        for hh in range(2):
            head = 2 * r + hh
            is_self = jnp.logical_and(r == s, head == b)
            src = ordered_ref.at[s, :, pl.ds(hh * piece, piece)]
            copy = pltpu.make_async_remote_copy(
                src_ref=src,
                dst_ref=cache_ref.at[rows],
                send_sem=c_send.at[k * 2 + hh],
                recv_sem=c_recv.at[b],
                device_id=(s, head),
                device_id_type=MESH_IDS,
            )

            @pl.when(jnp.logical_not(is_self))
            def _():
                copy.start()

            @pl.when(is_self)
            def _():
                local = pltpu.make_async_copy(src, cache_ref.at[rows], local_sem.at[0])
                local.start()
                local.wait()

            copies.append((copy, is_self))
    wts_ref[r] = packed_ref[...]
    for k in range(1, n_req):
        src_req = lax.rem(r + n_req - k, n_req)
        incoming = pltpu.make_async_remote_copy(
            src_ref=packed_ref,
            dst_ref=wts_ref.at[src_req],
            send_sem=w_send.at[src_req],
            recv_sem=w_recv.at[src_req],
            device_id=(src_req, b),
            device_id_type=MESH_IDS,
        )
        incoming.wait_recv()
    owner = b // 2
    for j in range(n_blk):
        incoming = pltpu.make_async_remote_copy(
            src_ref=ordered_ref.at[0, :, pl.ds(0, piece)],
            dst_ref=cache_ref.at[pl.ds(j * span, span)],
            send_sem=c_send.at[0],
            recv_sem=c_recv.at[j],
            device_id=(owner, j),
            device_id_type=MESH_IDS,
        )

        @pl.when(jnp.logical_not(jnp.logical_and(owner == r, j == b)))
        def _():
            incoming.wait_recv()

    for item in copies:
        if isinstance(item, tuple):
            copy, is_self = item

            @pl.when(jnp.logical_not(is_self))
            def _():
                copy.wait_send()

        else:
            item.wait_send()


def prologue(ordered, packed):
    n_req = lax.axis_size("req")
    n_blk = lax.axis_size("blk")
    n_slot, span, width = ordered.shape
    any_spec = pl.BlockSpec(memory_space=pl.ANY)
    vmem = pl.BlockSpec(memory_space=pltpu.VMEM)
    return pl.pallas_call(
        functools.partial(prologue_kernel, n_req, n_blk),
        out_shape=(
            jax.ShapeDtypeStruct((span * n_blk, width // 2), ordered.dtype),
            jax.ShapeDtypeStruct((n_req,) + packed.shape, packed.dtype),
        ),
        in_specs=[any_spec, vmem],
        out_specs=(any_spec, vmem),
        scratch_shapes=[
            pltpu.SemaphoreType.DMA((n_req,)),
            pltpu.SemaphoreType.DMA((n_req,)),
            pltpu.SemaphoreType.DMA((2 * n_slot,)),
            pltpu.SemaphoreType.DMA((n_blk,)),
            pltpu.SemaphoreType.DMA((1,)),
        ],
        compiler_params=pltpu.CompilerParams(has_side_effects=True),
    )(ordered, packed)


def unpack(whole, pieces):
    n_req = whole.shape[0]
    whole = whole.reshape(n_req, -1)
    out, at = [], 0
    for w, axis in pieces:
        size = w.size
        part = whole[:, at : at + size].reshape((n_req,) + w.shape)
        at += size
        part = jnp.moveaxis(part, 0, axis)
        shape = list(w.shape)
        shape[axis] *= n_req
        out.append(part.reshape(shape))
    return out


def lane_pack(pieces):
    blocks = []
    for w, axis in pieces:
        flat = w.reshape(w.shape[0], -1)
        blocks.append(flat.T if axis == 0 else flat)
    packed = jnp.concatenate(blocks, axis=0)
    return lax.all_gather(packed, "req", axis=0, tiled=False)


def per_device(
    new_states,
    encoder_out,
    cache_in,
    slot_order,
    new_lengths,
    cache_lengths,
    enc_lengths,
    bucket_of,
    rel_bias,
    norm_gain,
    self_q,
    self_kv,
    self_out,
    cross_q,
    cross_kv,
    cross_out,
    ff_in,
    ff_out,
):
    blk_count = lax.axis_size("blk")
    heads_dev = H // blk_count
    width_dev = heads_dev * HD
    req_dev = cache_in.shape[0] // lax.axis_size("req")
    own_slot = lax.dynamic_index_in_dim(slot_order, lax.axis_index("req"), 0, keepdims=False)
    tables = jnp.stack([new_lengths, cache_lengths, enc_lengths])
    picked = lax.dynamic_slice_in_dim(tables, own_slot, 1, 1)
    lens = picked.reshape(-1).astype(jnp.int32)
    ordered = jnp.take(cache_in, slot_order, axis=0)
    onehot = (bucket_of[:, None] == jnp.arange(rel_bias.shape[0], dtype=jnp.int32)[None, :]).astype(
        jnp.float32
    )
    own_bias = lax.dynamic_slice_in_dim(rel_bias, lax.axis_index("blk") * heads_dev, heads_dev, 1)
    bias_dist = jnp.dot(onehot, own_bias, precision=lax.Precision.HIGHEST).T
    early = [(self_q, 0), (self_kv, 0), (self_out, 1)]
    late = [(cross_q, 0), (cross_kv, 0), (cross_out, 1), (ff_in, 0), (ff_out, 1)]
    blocks = []
    for w, axis in early:
        two_d = w.reshape(w.shape[0], -1)
        blocks.append(two_d.T if axis == 0 else two_d)
    cache_blk, early_blocks = prologue(ordered, jnp.concatenate(blocks, axis=0))
    cache_dec = cache_blk[None]
    late_blocks = lane_pack(late)
    n_blk = lax.axis_size("blk")
    rows_dev = new_states.shape[0] // n_blk
    own_rows = lax.dynamic_slice_in_dim(
        new_states, chunk_of(lax.axis_index("blk"), n_blk) * rows_dev, rows_dev, 0
    ).astype(jnp.float32)
    part = self_branch(
        new_states,
        norm_gain[0],
        early_blocks,
        block_spans(early),
        cache_blk,
        bias_dist[0],
        lens,
    )
    residual, normed = blk_stage(part, own_rows, norm_gain[1], False)
    spans = block_spans(late)
    part = cross_branch(normed, encoder_out, late_blocks, spans[:3], lens)
    residual, normed = blk_stage(part.astype(jnp.bfloat16), residual, norm_gain[2], False)
    part = ffn_branch(normed, late_blocks, spans[3:])
    _, layer_out = blk_stage(part, residual, norm_gain[2], True)
    return (layer_out, cache_dec)


def solution(mesh):
    in_specs = (
        P("req", None),
        P("req", None),
        P(None, "blk", "req"),
        P(),
        P(),
        P(),
        P(),
        P(),
        P(),
        P(),
        P("req", "blk"),
        P("req", None, "blk"),
        P("blk", "req"),
        P("req", "blk"),
        P("req", None, "blk"),
        P("blk", "req"),
        P("req", None, "blk"),
        P("blk", "req"),
    )
    out_specs = (P("req", None), P("req", None, "blk"))
    return jax.shard_map(
        per_device, mesh=mesh, in_specs=in_specs, out_specs=out_specs, check_vma=False
    )
```

```python
import functools

import jax
import jax.numpy as jnp
from jax import lax
from jax.sharding import PartitionSpec as P
from jax.experimental import pallas as pl
from jax.experimental.pallas import tpu as pltpu

H = 16
HD = 64


EPSILON = 1e-06
NEG_FILL = -1e30


def rms_rows(row_block, gain):
    mean_square = jnp.mean(row_block * row_block, axis=-1, keepdims=True)
    return (row_block * lax.rsqrt(mean_square + EPSILON) * gain).astype(jnp.bfloat16)


def softmax_rows(scores):
    row_top = jnp.max(scores, axis=-1, keepdims=True)
    weights = jnp.exp(scores - row_top)
    return (weights / jnp.sum(weights, axis=-1, keepdims=True)).astype(jnp.bfloat16)


def pick_lengths(table, own_slots):
    matches = own_slots[:, None] == jnp.arange(table.shape[0], dtype=jnp.int32)[None, :]
    return jnp.sum(jnp.where(matches, table[None, :], 0), axis=1)


def shifted_bias(bias_dist, base, row_count, col_count):
    heads_here, span_len = bias_dist.shape
    line_len = row_count + col_count - 1
    steps = jnp.arange(line_len + 1, dtype=jnp.int32)
    line = bias_dist[:, jnp.clip(base + row_count - 1 - steps, 0, span_len - 1)]
    tiled = jnp.broadcast_to(line[:, None, :], (heads_here, row_count, line_len + 1))
    flat = tiled.reshape(heads_here, row_count * (line_len + 1))[:, : row_count * line_len]
    skewed = flat.reshape(heads_here, row_count, line_len)
    return skewed[:, :, row_count - 1 : row_count - 1 + col_count]


def row_total(left, weight):
    term = jnp.dot(left, weight, preferred_element_type=jnp.float32)
    return lax.psum(term.astype(jnp.bfloat16), "blk").astype(jnp.float32)


def cached_scores(queries, key_rows, first_col, old_len, bias_dist):
    col_ids = first_col + jnp.arange(key_rows.shape[0], dtype=jnp.int32)[None, :]
    scores = jnp.einsum("qhe,khe->hqk", queries, key_rows, preferred_element_type=jnp.float32)
    scores = scores + shifted_bias(
        bias_dist, old_len - first_col, queries.shape[0], key_rows.shape[0]
    )
    return jnp.where((col_ids < old_len)[None], scores, NEG_FILL)


def fresh_scores(queries, fresh_keys, fresh_len, bias_dist):
    row_ids = jnp.arange(queries.shape[0], dtype=jnp.int32)[:, None]
    col_ids = jnp.arange(fresh_keys.shape[0], dtype=jnp.int32)[None, :]
    scores = jnp.einsum("qhe,khe->hqk", queries, fresh_keys, preferred_element_type=jnp.float32)
    scores = scores + shifted_bias(bias_dist, 0, queries.shape[0], fresh_keys.shape[0])
    admitted = (col_ids <= row_ids) & (col_ids < fresh_len)
    return jnp.where(admitted[None], scores, NEG_FILL)


def self_padded(
    queries, key_rows, value_rows, fresh_keys, fresh_values, old_len, fresh_len, bias_dist
):
    scores = jnp.concatenate(
        [
            cached_scores(queries, key_rows, 0, old_len, bias_dist),
            fresh_scores(queries, fresh_keys, fresh_len, bias_dist),
        ],
        axis=2,
    )
    weights = softmax_rows(scores)
    value_all = jnp.concatenate([value_rows, fresh_values], axis=0)
    return jnp.einsum(
        "hqk,khe->qhe", weights, value_all, preferred_element_type=jnp.float32
    ).astype(jnp.bfloat16)


def self_attend(queries, key_value, cache_dec, slot_old, slot_new, bias_dist, heads_dev):
    req_dev, cache_len = (cache_dec.shape[0], cache_dec.shape[1])
    cache_split = cache_dec.reshape(req_dev, cache_len, heads_dev, 2, -1)

    def one_request(request):
        queries_one, pair_one, cache_one, old_len, fresh_len = request
        return self_padded(
            queries_one,
            cache_one[:, :, 0],
            cache_one[:, :, 1],
            pair_one[:, 0],
            pair_one[:, 1],
            old_len,
            fresh_len,
            bias_dist,
        )

    return lax.map(one_request, (queries, key_value, cache_split, slot_old, slot_new))


def cross_attend(queries, key_value, slot_enc):
    scores = jnp.einsum(
        "rqhe,rkhe->rhqk", queries, key_value[:, :, 0], preferred_element_type=jnp.float32
    )
    col_ids = jnp.arange(key_value.shape[1], dtype=jnp.int32)
    scores = jnp.where(
        col_ids[None, None, None, :] < slot_enc[:, None, None, None], scores, NEG_FILL
    )
    weights = softmax_rows(scores)
    return jnp.einsum(
        "rhqk,rkhe->rqhe", weights, key_value[:, :, 1], preferred_element_type=jnp.float32
    ).astype(jnp.bfloat16)


def add_branch(residual, left, weight, gain):
    residual = residual + row_total(left, weight)
    normed = rms_rows(residual, gain)
    return (residual, normed)


TQ = 128


def stage_kernel(n_blk, final, extra, *refs):
    if extra:
        (part_ref, resid_ref, gain_ref, packed_ref, res_out, full_ref, wts_ref,
         recv_a, send_b, recv_b, x_send, x_recv, b_send, b_recv, ag_send, ag_recv, w_send, w_recv) = refs
    else:
        (part_ref, resid_ref, gain_ref, res_out, full_ref,
         recv_a, send_b, recv_b, x_send, x_recv, b_send, b_recv, ag_send, ag_recv) = refs
    me = lax.axis_index("blk")
    req = lax.axis_index("req")
    rows = resid_ref.shape[0]
    n_grp = n_blk // 2
    g = me // 2
    c = lax.rem(me, 2)
    partner = g * 2 + 1 - c
    half = n_grp * rows
    n_req = wts_ref.shape[0] if extra else 1
    barrier = pltpu.get_barrier_semaphore()
    for k in range(1, n_grp):
        peer = lax.rem(g + k, n_grp) * 2 + c
        pl.semaphore_signal(barrier, inc=1, device_id=(req, peer), device_id_type=MESH_IDS)
    pl.semaphore_signal(barrier, inc=1, device_id=(req, partner), device_id_type=MESH_IDS)
    for k in range(1, n_req):
        peer = lax.rem(req + k, n_req)
        pl.semaphore_signal(barrier, inc=1, device_id=(peer, me), device_id_type=MESH_IDS)
    pl.semaphore_wait(barrier, n_grp + n_req - 1)
    sends = []
    for k in range(n_grp):
        grp = lax.rem(g + 1 + k, n_grp)
        exchange = pltpu.make_async_remote_copy(
            src_ref=part_ref.at[pl.ds(pl.multiple_of((1 - c) * half + grp * rows, rows), rows)],
            dst_ref=recv_a.at[grp],
            send_sem=x_send.at[k],
            recv_sem=x_recv.at[grp],
            device_id=(req, partner),
            device_id_type=MESH_IDS,
        )
        exchange.start()
        sends.append(exchange)
    for k in range(1, n_req):
        peer = lax.rem(req + k, n_req)
        copy = pltpu.make_async_remote_copy(
            src_ref=packed_ref,
            dst_ref=wts_ref.at[req],
            send_sem=w_send.at[peer],
            recv_sem=w_recv.at[req],
            device_id=(peer, me),
            device_id_type=MESH_IDS,
        )
        copy.start()
        sends.append(copy)
    total = None
    for k in range(n_grp):
        grp = lax.rem(g + 1 + k, n_grp)
        incoming = pltpu.make_async_remote_copy(
            src_ref=part_ref.at[pl.ds(0, rows)],
            dst_ref=recv_a.at[grp],
            send_sem=x_send.at[k],
            recv_sem=x_recv.at[grp],
            device_id=(req, partner),
            device_id_type=MESH_IDS,
        )
        incoming.wait_recv()
        pair = part_ref[pl.ds(pl.multiple_of(c * half + grp * rows, rows), rows), :].astype(
            jnp.float32
        ) + recv_a[grp].astype(jnp.float32)
        if k == n_grp - 1:
            total = pair
        else:
            send_b[grp] = pair.astype(send_b.dtype)
            copy = pltpu.make_async_remote_copy(
                src_ref=send_b.at[grp],
                dst_ref=recv_b.at[g],
                send_sem=b_send.at[grp],
                recv_sem=b_recv.at[g],
                device_id=(req, grp * 2 + c),
                device_id_type=MESH_IDS,
            )
            copy.start()
            sends.append(copy)
    for k in range(1, n_grp):
        grp = lax.rem(g + n_grp - k, n_grp)
        incoming = pltpu.make_async_remote_copy(
            src_ref=send_b.at[0],
            dst_ref=recv_b.at[grp],
            send_sem=b_send.at[grp],
            recv_sem=b_recv.at[grp],
            device_id=(req, grp * 2 + c),
            device_id_type=MESH_IDS,
        )
        incoming.wait_recv()
        total = total + recv_b[grp].astype(jnp.float32)
    mine = pl.ds(pl.multiple_of(c * half + g * rows, rows), rows)
    resid = resid_ref[...] + total
    res_out[...] = resid
    if final:
        full_ref[mine, :] = resid.astype(full_ref.dtype)
    else:
        mean_square = jnp.mean(resid * resid, axis=-1, keepdims=True)
        full_ref[mine, :] = (resid * lax.rsqrt(mean_square + EPSILON) * gain_ref[...]).astype(
            full_ref.dtype
        )
    for k in range(1, n_grp):
        peer = lax.rem(g + k, n_grp) * 2 + c
        copy = pltpu.make_async_remote_copy(
            src_ref=full_ref.at[mine],
            dst_ref=full_ref.at[mine],
            send_sem=ag_send.at[k],
            recv_sem=ag_recv.at[g],
            device_id=(req, peer),
            device_id_type=MESH_IDS,
        )
        copy.start()
        sends.append(copy)
    copy = pltpu.make_async_remote_copy(
        src_ref=full_ref.at[mine],
        dst_ref=full_ref.at[mine],
        send_sem=ag_send.at[0],
        recv_sem=ag_recv.at[n_grp + g],
        device_id=(req, partner),
        device_id_type=MESH_IDS,
    )
    copy.start()
    sends.append(copy)
    for k in range(1, n_grp):
        grp = lax.rem(g + n_grp - k, n_grp)
        there = pl.ds(pl.multiple_of(c * half + grp * rows, rows), rows)
        incoming = pltpu.make_async_remote_copy(
            src_ref=full_ref.at[there],
            dst_ref=full_ref.at[there],
            send_sem=ag_send.at[0],
            recv_sem=ag_recv.at[grp],
            device_id=(req, grp * 2 + c),
            device_id_type=MESH_IDS,
        )
        incoming.wait_recv()
        forward = pltpu.make_async_remote_copy(
            src_ref=full_ref.at[there],
            dst_ref=full_ref.at[there],
            send_sem=ag_send.at[n_grp + k],
            recv_sem=ag_recv.at[n_grp + grp],
            device_id=(req, partner),
            device_id_type=MESH_IDS,
        )
        forward.start()
        sends.append(forward)
    for grp in range(n_grp):
        there = pl.ds(pl.multiple_of((1 - c) * half + grp * rows, rows), rows)
        incoming = pltpu.make_async_remote_copy(
            src_ref=full_ref.at[there],
            dst_ref=full_ref.at[there],
            send_sem=ag_send.at[0],
            recv_sem=ag_recv.at[n_grp + grp],
            device_id=(req, partner),
            device_id_type=MESH_IDS,
        )
        incoming.wait_recv()
    if extra:
        wts_ref[req] = packed_ref[...]
        for k in range(1, n_req):
            src = lax.rem(req + n_req - k, n_req)
            incoming = pltpu.make_async_remote_copy(
                src_ref=packed_ref,
                dst_ref=wts_ref.at[src],
                send_sem=w_send.at[src],
                recv_sem=w_recv.at[src],
                device_id=(src, me),
                device_id_type=MESH_IDS,
            )
            incoming.wait_recv()
    for copy in sends:
        copy.wait_send()


def blk_stage(part, resid, gain, final, packed=None):
    n_blk = lax.axis_size("blk")
    rows, width = resid.shape
    vmem = pl.BlockSpec(memory_space=pltpu.VMEM)
    extra = packed is not None
    outs = [
        jax.ShapeDtypeStruct((rows, width), jnp.float32),
        jax.ShapeDtypeStruct((rows * n_blk, width), jnp.bfloat16),
    ]
    n_grp = n_blk // 2
    scratch = [
        pltpu.VMEM((n_grp, rows, width), part.dtype),
        pltpu.VMEM((n_grp, rows, width), part.dtype),
        pltpu.VMEM((n_grp, rows, width), part.dtype),
        pltpu.SemaphoreType.DMA((n_grp,)),
        pltpu.SemaphoreType.DMA((n_grp,)),
        pltpu.SemaphoreType.DMA((n_grp,)),
        pltpu.SemaphoreType.DMA((n_grp,)),
        pltpu.SemaphoreType.DMA((n_blk,)),
        pltpu.SemaphoreType.DMA((n_blk,)),
    ]
    args = [part, resid, gain[None, :]]
    if extra:
        n_req = lax.axis_size("req")
        outs.append(jax.ShapeDtypeStruct((n_req,) + packed.shape, packed.dtype))
        scratch += [pltpu.SemaphoreType.DMA((n_req,)), pltpu.SemaphoreType.DMA((n_req,))]
        args.append(packed)
    return pl.pallas_call(
        functools.partial(stage_kernel, n_blk, final, extra),
        out_shape=tuple(outs),
        in_specs=[vmem] * len(args),
        out_specs=tuple([vmem] * len(outs)),
        scratch_shapes=scratch,
        compiler_params=pltpu.CompilerParams(
            collective_id=5 if extra else (4 if final else 3),
            has_side_effects=True,
            vmem_limit_bytes=16 * 1024 * 1024,
        ),
    )(*args)


def cross_kernel(n_req, spans, len_ref, normed_ref, enc_ref, w_ref, out_ref):
    enc_len = len_ref[2]
    (q_at, q_len), (kv_at, kv_len), (o_at, o_len) = spans
    nt = (((1,), (1,)), ((), ()))
    width = w_ref.shape[2]
    queries = None
    pair = None
    for r in range(n_req):
        cols = slice(r * width, (r + 1) * width)
        term = lax.dot_general(
            normed_ref[:, cols], w_ref[r, q_at : q_at + q_len, :], nt,
            preferred_element_type=jnp.float32,
        )
        queries = term if queries is None else queries + term
        term = lax.dot_general(
            enc_ref[:, cols], w_ref[r, kv_at : kv_at + kv_len, :], nt,
            preferred_element_type=jnp.float32,
        )
        pair = term if pair is None else pair + term
    queries = queries.astype(jnp.bfloat16)
    pair = pair.astype(jnp.bfloat16)
    keys = pair[:, :HD]
    values = pair[:, HD:]
    scores = lax.dot_general(queries, keys, nt, preferred_element_type=jnp.float32)
    col = lax.broadcasted_iota(jnp.int32, scores.shape, 1)
    scores = jnp.where(col < enc_len, scores, NEG_FILL)
    top = jnp.max(scores, axis=1, keepdims=True)
    weights = jnp.exp(scores - top)
    weights = (weights / jnp.sum(weights, axis=1, keepdims=True)).astype(jnp.bfloat16)
    context = jnp.dot(weights, values, preferred_element_type=jnp.float32).astype(jnp.bfloat16)
    for r in range(n_req):
        out_ref[:, r * width : (r + 1) * width] = jnp.dot(
            context, w_ref[r, o_at : o_at + o_len, :], preferred_element_type=jnp.float32
        ).astype(out_ref.dtype)


def ffn_kernel(n_req, spans, normed_ref, w_ref, out_ref):
    (i_at, i_len), (o_at, o_len) = spans
    nt = (((1,), (1,)), ((), ()))
    width = w_ref.shape[2]
    ff_dev = o_len
    gate_up = None
    for r in range(n_req):
        term = lax.dot_general(
            normed_ref[:, r * width : (r + 1) * width], w_ref[r, i_at : i_at + i_len, :], nt,
            preferred_element_type=jnp.float32,
        )
        gate_up = term if gate_up is None else gate_up + term
    hidden = (jax.nn.gelu(gate_up[:, :ff_dev], approximate=True) * gate_up[:, ff_dev:]).astype(
        jnp.bfloat16
    )
    for r in range(n_req):
        out_ref[:, r * width : (r + 1) * width] = jnp.dot(
            hidden, w_ref[r, o_at : o_at + o_len, :], preferred_element_type=jnp.float32
        ).astype(out_ref.dtype)


def block_spans(pieces):
    spans, at = [], 0
    for w, axis in pieces:
        rows = w.size // w.shape[0] if axis == 0 else w.shape[0]
        spans.append((at, rows))
        at += rows
    return spans


def cross_branch(normed, enc, blocks, spans, enc_len):
    vmem = pl.BlockSpec(memory_space=pltpu.VMEM)
    return pl.pallas_call(
        functools.partial(cross_kernel, blocks.shape[0], tuple(spans)),
        out_shape=jax.ShapeDtypeStruct(normed.shape, jnp.bfloat16),
        in_specs=[pl.BlockSpec(memory_space=pltpu.SMEM)] + [vmem] * 3,
        out_specs=vmem,
        compiler_params=pltpu.CompilerParams(vmem_limit_bytes=16 * 1024 * 1024),
    )(enc_len, normed, enc, blocks)


def ffn_branch(normed, blocks, spans):
    vmem = pl.BlockSpec(memory_space=pltpu.VMEM)
    return pl.pallas_call(
        functools.partial(ffn_kernel, blocks.shape[0], tuple(spans)),
        out_shape=jax.ShapeDtypeStruct(normed.shape, jnp.bfloat16),
        in_specs=[vmem] * 2,
        out_specs=vmem,
        compiler_params=pltpu.CompilerParams(vmem_limit_bytes=16 * 1024 * 1024),
    )(normed, blocks)


def self_kernel(lens_ref, q_ref, c_ref, kn_ref, vn_ref, g_ref, f_ref, o_ref):
    old_len = lens_ref[0]
    fresh_len = lens_ref[1]
    n_q = q_ref.shape[0]
    n_ctx = c_ref.shape[0]
    wide_old = n_ctx + TQ
    wide_new = n_q + TQ
    k_old = c_ref[:, :HD]
    v_old = c_ref[:, HD:]
    k_new = kn_ref[...]
    v_new = vn_ref[...]
    dims = (((1,), (1,)), ((), ()))
    for t in range(n_q // TQ):
        q = q_ref[t * TQ : (t + 1) * TQ, :]
        start = n_q - TQ - t * TQ
        s_old = lax.dot_general(q, k_old, dims, preferred_element_type=jnp.float32)
        line = jnp.broadcast_to(g_ref[:, start : start + wide_old], (TQ, wide_old))
        bias = pltpu.roll(line, wide_old - (TQ - 1), 1, stride=1, stride_axis=0)[:, :n_ctx]
        col = lax.broadcasted_iota(jnp.int32, (TQ, n_ctx), 1)
        s_old = jnp.where(col < old_len, s_old + bias, NEG_FILL)
        s_new = lax.dot_general(q, k_new, dims, preferred_element_type=jnp.float32)
        line = jnp.broadcast_to(f_ref[:, start : start + wide_new], (TQ, wide_new))
        bias = pltpu.roll(line, wide_new - (TQ - 1), 1, stride=1, stride_axis=0)[:, :n_q]
        row = lax.broadcasted_iota(jnp.int32, (TQ, n_q), 0) + t * TQ
        col = lax.broadcasted_iota(jnp.int32, (TQ, n_q), 1)
        s_new = jnp.where((col <= row) & (col < fresh_len), s_new + bias, NEG_FILL)
        top = jnp.maximum(
            jnp.max(s_old, axis=1, keepdims=True), jnp.max(s_new, axis=1, keepdims=True)
        )
        p_old = jnp.exp(s_old - top)
        p_new = jnp.exp(s_new - top)
        total = jnp.sum(p_old, axis=1, keepdims=True) + jnp.sum(p_new, axis=1, keepdims=True)
        w_old = (p_old / total).astype(jnp.bfloat16)
        w_new = (p_new / total).astype(jnp.bfloat16)
        out = jnp.dot(w_old, v_old, preferred_element_type=jnp.float32) + jnp.dot(
            w_new, v_new, preferred_element_type=jnp.float32
        )
        o_ref[t * TQ : (t + 1) * TQ, :] = out.astype(jnp.bfloat16)


def bias_lines(line, old_len, n_q, n_ctx):
    span = line.shape[0]
    ext = jnp.concatenate([jnp.broadcast_to(line[:1], (n_ctx,)), line])
    rev = ext[::-1]
    g = lax.dynamic_slice_in_dim(rev, n_ctx - old_len, span)
    f = rev[n_ctx : n_ctx + 2 * n_q]
    return g[None, :], f[None, :]


def self_attention(q, cache_blk, k_new, v_new, line, old_len, fresh_len):
    n_q = q.shape[0]
    n_ctx = cache_blk.shape[0]
    g, f = bias_lines(line, old_len, n_q, n_ctx)
    lens = jnp.stack([old_len, fresh_len]).astype(jnp.int32)
    vmem = pl.BlockSpec(memory_space=pltpu.VMEM)
    return pl.pallas_call(
        self_kernel,
        out_shape=jax.ShapeDtypeStruct((n_q, HD), jnp.bfloat16),
        in_specs=[pl.BlockSpec(memory_space=pltpu.SMEM)] + [vmem] * 6,
        out_specs=vmem,
        compiler_params=pltpu.CompilerParams(vmem_limit_bytes=24 * 1024 * 1024),
    )(lens, q, cache_blk, k_new, v_new, g, f)


def self_full_kernel(n_req, spans, lens_ref, x_ref, gain_ref, w_ref, c_ref, g_ref, f_ref, o_ref, ctx_ref):
    fresh_len = lens_ref[0]
    old_len = lens_ref[1]
    (q_at, q_len), (kv_at, kv_len), (o_at, o_len) = spans
    nt = (((1,), (1,)), ((), ()))
    width = w_ref.shape[2]
    x = x_ref[...].astype(jnp.float32)
    mean_square = jnp.mean(x * x, axis=-1, keepdims=True)
    normed = (x * lax.rsqrt(mean_square + EPSILON) * gain_ref[...]).astype(jnp.bfloat16)
    queries = None
    pair = None
    for r in range(n_req):
        cols = slice(r * width, (r + 1) * width)
        term = lax.dot_general(
            normed[:, cols], w_ref[r, q_at : q_at + q_len, :], nt,
            preferred_element_type=jnp.float32,
        )
        queries = term if queries is None else queries + term
        term = lax.dot_general(
            normed[:, cols], w_ref[r, kv_at : kv_at + kv_len, :], nt,
            preferred_element_type=jnp.float32,
        )
        pair = term if pair is None else pair + term
    queries = queries.astype(jnp.bfloat16)
    pair = pair.astype(jnp.bfloat16)
    k_new = pair[:, :HD]
    v_new = pair[:, HD:]
    n_q = x_ref.shape[0]
    n_ctx = c_ref.shape[0]
    wide_old = n_ctx + TQ
    wide_new = n_q + TQ
    k_old = c_ref[:, :HD]
    v_old = c_ref[:, HD:]
    for t in range(n_q // TQ):
        q = queries[t * TQ : (t + 1) * TQ, :]
        start = n_q - TQ - t * TQ
        s_old = lax.dot_general(q, k_old, nt, preferred_element_type=jnp.float32)
        line = jnp.broadcast_to(g_ref[:, start : start + wide_old], (TQ, wide_old))
        bias = pltpu.roll(line, wide_old - (TQ - 1), 1, stride=1, stride_axis=0)[:, :n_ctx]
        col = lax.broadcasted_iota(jnp.int32, (TQ, n_ctx), 1)
        s_old = jnp.where(col < old_len, s_old + bias, NEG_FILL)
        s_new = lax.dot_general(q, k_new, nt, preferred_element_type=jnp.float32)
        line = jnp.broadcast_to(f_ref[:, start : start + wide_new], (TQ, wide_new))
        bias = pltpu.roll(line, wide_new - (TQ - 1), 1, stride=1, stride_axis=0)[:, :n_q]
        row = lax.broadcasted_iota(jnp.int32, (TQ, n_q), 0) + t * TQ
        col = lax.broadcasted_iota(jnp.int32, (TQ, n_q), 1)
        s_new = jnp.where((col <= row) & (col < fresh_len), s_new + bias, NEG_FILL)
        top = jnp.maximum(
            jnp.max(s_old, axis=1, keepdims=True), jnp.max(s_new, axis=1, keepdims=True)
        )
        p_old = jnp.exp(s_old - top)
        p_new = jnp.exp(s_new - top)
        total = jnp.sum(p_old, axis=1, keepdims=True) + jnp.sum(p_new, axis=1, keepdims=True)
        w_old = (p_old / total).astype(jnp.bfloat16)
        w_new = (p_new / total).astype(jnp.bfloat16)
        out = jnp.dot(w_old, v_old, preferred_element_type=jnp.float32) + jnp.dot(
            w_new, v_new, preferred_element_type=jnp.float32
        )
        ctx_ref[t * TQ : (t + 1) * TQ, :] = out.astype(jnp.bfloat16)
    context = ctx_ref[...]
    for r in range(n_req):
        o_ref[:, r * width : (r + 1) * width] = jnp.dot(
            context, w_ref[r, o_at : o_at + o_len, :], preferred_element_type=jnp.float32
        ).astype(o_ref.dtype)


def self_branch(states, gain, blocks, spans, cache_blk, line, lens):
    n_q = states.shape[0]
    n_ctx = cache_blk.shape[0]
    g, f = bias_lines(line, lens[1], n_q, n_ctx)
    vmem = pl.BlockSpec(memory_space=pltpu.VMEM)
    return pl.pallas_call(
        functools.partial(self_full_kernel, blocks.shape[0], tuple(spans)),
        out_shape=jax.ShapeDtypeStruct(states.shape, jnp.bfloat16),
        in_specs=[pl.BlockSpec(memory_space=pltpu.SMEM)] + [vmem] * 6,
        out_specs=vmem,
        scratch_shapes=[pltpu.VMEM((n_q, HD), jnp.bfloat16)],
        compiler_params=pltpu.CompilerParams(vmem_limit_bytes=24 * 1024 * 1024),
    )(lens, states, gain[None, :], blocks, cache_blk, g, f)


def pack_gather(pieces):
    flat = jnp.concatenate([w.reshape(-1) for w, _ in pieces])
    whole = lax.all_gather(flat, "req", axis=0, tiled=False)
    n_req = whole.shape[0]
    out, at = [], 0
    for w, axis in pieces:
        size = w.size
        part = whole[:, at : at + size].reshape((n_req,) + w.shape)
        at += size
        part = jnp.moveaxis(part, 0, axis)
        shape = list(w.shape)
        shape[axis] *= n_req
        out.append(part.reshape(shape))
    return out


MESH_IDS = pl.DeviceIdType.MESH


def greet_all(n_blk, me, req):
    barrier = pltpu.get_barrier_semaphore()
    for k in range(1, n_blk):
        peer = lax.rem(me + k, n_blk)
        pl.semaphore_signal(barrier, inc=1, device_id=(req, peer), device_id_type=MESH_IDS)
    pl.semaphore_wait(barrier, n_blk - 1)


def chunk_of(b, n_blk):
    return lax.rem(b, 2) * (n_blk // 2) + b // 2


def scatter_kernel(n_blk, part_ref, out_ref, recv, send_sem, recv_sem):
    me = lax.axis_index("blk")
    req = lax.axis_index("req")
    rows = out_ref.shape[0]
    greet_all(n_blk, me, req)
    copies = []
    for k in range(1, n_blk):
        peer = lax.rem(me + k, n_blk)
        copy = pltpu.make_async_remote_copy(
            src_ref=part_ref.at[pl.ds(pl.multiple_of(chunk_of(peer, n_blk) * rows, rows), rows)],
            dst_ref=recv.at[me],
            send_sem=send_sem.at[peer],
            recv_sem=recv_sem.at[me],
            device_id=(req, peer),
            device_id_type=MESH_IDS,
        )
        copy.start()
        copies.append(copy)
    own = pl.ds(pl.multiple_of(chunk_of(me, n_blk) * rows, rows), rows)
    total = part_ref[own, :].astype(jnp.float32)
    for k in range(1, n_blk):
        src = lax.rem(me + n_blk - k, n_blk)
        incoming = pltpu.make_async_remote_copy(
            src_ref=part_ref.at[pl.ds(0, rows)],
            dst_ref=recv.at[src],
            send_sem=send_sem.at[src],
            recv_sem=recv_sem.at[src],
            device_id=(req, src),
            device_id_type=MESH_IDS,
        )
        incoming.wait_recv()
        total = total + recv[src].astype(jnp.float32)
    for copy in copies:
        copy.wait_send()
    out_ref[...] = total


def gather_kernel(n_blk, piece_ref, out_ref, send_sem, recv_sem):
    b = lax.axis_index("blk")
    req = lax.axis_index("req")
    n_grp = n_blk // 2
    g = b // 2
    c = lax.rem(b, 2)
    partner = g * 2 + 1 - c
    rows = piece_ref.shape[0]
    half = n_grp * rows
    barrier = pltpu.get_barrier_semaphore()
    for k in range(1, n_grp):
        peer = lax.rem(g + k, n_grp) * 2 + c
        pl.semaphore_signal(barrier, inc=1, device_id=(req, peer), device_id_type=MESH_IDS)
    pl.semaphore_signal(barrier, inc=1, device_id=(req, partner), device_id_type=MESH_IDS)
    pl.semaphore_wait(barrier, n_grp)
    mine = pl.ds(pl.multiple_of(c * half + g * rows, rows), rows)
    sends = []
    for k in range(1, n_grp):
        peer = lax.rem(g + k, n_grp) * 2 + c
        copy = pltpu.make_async_remote_copy(
            src_ref=piece_ref,
            dst_ref=out_ref.at[mine],
            send_sem=send_sem.at[k],
            recv_sem=recv_sem.at[g],
            device_id=(req, peer),
            device_id_type=MESH_IDS,
        )
        copy.start()
        sends.append(copy)
    copy = pltpu.make_async_remote_copy(
        src_ref=piece_ref,
        dst_ref=out_ref.at[mine],
        send_sem=send_sem.at[0],
        recv_sem=recv_sem.at[n_grp + g],
        device_id=(req, partner),
        device_id_type=MESH_IDS,
    )
    copy.start()
    sends.append(copy)
    out_ref[mine, :] = piece_ref[...]
    for k in range(1, n_grp):
        grp = lax.rem(g + n_grp - k, n_grp)
        there = pl.ds(pl.multiple_of(c * half + grp * rows, rows), rows)
        incoming = pltpu.make_async_remote_copy(
            src_ref=piece_ref,
            dst_ref=out_ref.at[there],
            send_sem=send_sem.at[0],
            recv_sem=recv_sem.at[grp],
            device_id=(req, grp * 2 + c),
            device_id_type=MESH_IDS,
        )
        incoming.wait_recv()
        forward = pltpu.make_async_remote_copy(
            src_ref=out_ref.at[there],
            dst_ref=out_ref.at[there],
            send_sem=send_sem.at[n_grp + k],
            recv_sem=recv_sem.at[n_grp + grp],
            device_id=(req, partner),
            device_id_type=MESH_IDS,
        )
        forward.start()
        sends.append(forward)
    for grp in range(n_grp):
        there = pl.ds(pl.multiple_of((1 - c) * half + grp * rows, rows), rows)
        incoming = pltpu.make_async_remote_copy(
            src_ref=piece_ref,
            dst_ref=out_ref.at[there],
            send_sem=send_sem.at[0],
            recv_sem=recv_sem.at[n_grp + grp],
            device_id=(req, partner),
            device_id_type=MESH_IDS,
        )
        incoming.wait_recv()
    for copy in sends:
        copy.wait_send()


def blk_scatter(part):
    n_blk = lax.axis_size("blk")
    rows = part.shape[0] // n_blk
    vmem = pl.BlockSpec(memory_space=pltpu.VMEM)
    return pl.pallas_call(
        functools.partial(scatter_kernel, n_blk),
        out_shape=jax.ShapeDtypeStruct((rows, part.shape[1]), jnp.float32),
        in_specs=[vmem],
        out_specs=vmem,
        scratch_shapes=[
            pltpu.VMEM((n_blk, rows, part.shape[1]), part.dtype),
            pltpu.SemaphoreType.DMA((n_blk,)),
            pltpu.SemaphoreType.DMA((n_blk,)),
        ],
        compiler_params=pltpu.CompilerParams(collective_id=1, has_side_effects=True),
    )(part)


def blk_gather(piece):
    n_blk = lax.axis_size("blk")
    rows = piece.shape[0]
    vmem = pl.BlockSpec(memory_space=pltpu.VMEM)
    return pl.pallas_call(
        functools.partial(gather_kernel, n_blk),
        out_shape=jax.ShapeDtypeStruct((rows * n_blk, piece.shape[1]), piece.dtype),
        in_specs=[vmem],
        out_specs=vmem,
        scratch_shapes=[
            pltpu.SemaphoreType.DMA((n_blk,)),
            pltpu.SemaphoreType.DMA((n_blk,)),
        ],
        compiler_params=pltpu.CompilerParams(collective_id=2, has_side_effects=True),
    )(piece)


def prologue_kernel(n_req, n_blk, ordered_ref, packed_ref, cache_ref, wts_ref, w_send, w_recv, c_send, c_recv, local_sem):
    r = lax.axis_index("req")
    b = lax.axis_index("blk")
    n_slot, span, width = ordered_ref.shape
    piece = width // 2
    copies = []
    for k in range(1, n_req):
        peer = lax.rem(r + k, n_req)
        copy = pltpu.make_async_remote_copy(
            src_ref=packed_ref,
            dst_ref=wts_ref.at[r],
            send_sem=w_send.at[peer],
            recv_sem=w_recv.at[r],
            device_id=(peer, b),
            device_id_type=MESH_IDS,
        )
        copy.start()
        copies.append(copy)
    rows = pl.ds(pl.multiple_of(b * span, span), span)
    for k in range(n_slot):
        s = lax.rem(b + k, n_slot)
        for hh in range(2):
            head = 2 * r + hh
            is_self = jnp.logical_and(r == s, head == b)
            src = ordered_ref.at[s, :, pl.ds(hh * piece, piece)]
            copy = pltpu.make_async_remote_copy(
                src_ref=src,
                dst_ref=cache_ref.at[rows],
                send_sem=c_send.at[k * 2 + hh],
                recv_sem=c_recv.at[b],
                device_id=(s, head),
                device_id_type=MESH_IDS,
            )

            @pl.when(jnp.logical_not(is_self))
            def _():
                copy.start()

            @pl.when(is_self)
            def _():
                local = pltpu.make_async_copy(src, cache_ref.at[rows], local_sem.at[0])
                local.start()
                local.wait()

            copies.append((copy, is_self))
    wts_ref[r] = packed_ref[...]
    for k in range(1, n_req):
        src_req = lax.rem(r + n_req - k, n_req)
        incoming = pltpu.make_async_remote_copy(
            src_ref=packed_ref,
            dst_ref=wts_ref.at[src_req],
            send_sem=w_send.at[src_req],
            recv_sem=w_recv.at[src_req],
            device_id=(src_req, b),
            device_id_type=MESH_IDS,
        )
        incoming.wait_recv()
    owner = b // 2
    for j in range(n_blk):
        incoming = pltpu.make_async_remote_copy(
            src_ref=ordered_ref.at[0, :, pl.ds(0, piece)],
            dst_ref=cache_ref.at[pl.ds(j * span, span)],
            send_sem=c_send.at[0],
            recv_sem=c_recv.at[j],
            device_id=(owner, j),
            device_id_type=MESH_IDS,
        )

        @pl.when(jnp.logical_not(jnp.logical_and(owner == r, j == b)))
        def _():
            incoming.wait_recv()

    for item in copies:
        if isinstance(item, tuple):
            copy, is_self = item

            @pl.when(jnp.logical_not(is_self))
            def _():
                copy.wait_send()

        else:
            item.wait_send()


def prologue(ordered, packed):
    n_req = lax.axis_size("req")
    n_blk = lax.axis_size("blk")
    n_slot, span, width = ordered.shape
    any_spec = pl.BlockSpec(memory_space=pl.ANY)
    vmem = pl.BlockSpec(memory_space=pltpu.VMEM)
    return pl.pallas_call(
        functools.partial(prologue_kernel, n_req, n_blk),
        out_shape=(
            jax.ShapeDtypeStruct((span * n_blk, width // 2), ordered.dtype),
            jax.ShapeDtypeStruct((n_req,) + packed.shape, packed.dtype),
        ),
        in_specs=[any_spec, vmem],
        out_specs=(any_spec, vmem),
        scratch_shapes=[
            pltpu.SemaphoreType.DMA((n_req,)),
            pltpu.SemaphoreType.DMA((n_req,)),
            pltpu.SemaphoreType.DMA((2 * n_slot,)),
            pltpu.SemaphoreType.DMA((n_blk,)),
            pltpu.SemaphoreType.DMA((1,)),
        ],
        compiler_params=pltpu.CompilerParams(has_side_effects=True),
    )(ordered, packed)


def unpack(whole, pieces):
    n_req = whole.shape[0]
    whole = whole.reshape(n_req, -1)
    out, at = [], 0
    for w, axis in pieces:
        size = w.size
        part = whole[:, at : at + size].reshape((n_req,) + w.shape)
        at += size
        part = jnp.moveaxis(part, 0, axis)
        shape = list(w.shape)
        shape[axis] *= n_req
        out.append(part.reshape(shape))
    return out


def lane_pack(pieces):
    blocks = []
    for w, axis in pieces:
        flat = w.reshape(w.shape[0], -1)
        blocks.append(flat.T if axis == 0 else flat)
    packed = jnp.concatenate(blocks, axis=0)
    return lax.all_gather(packed, "req", axis=0, tiled=False)


def per_device(
    new_states,
    encoder_out,
    cache_in,
    slot_order,
    new_lengths,
    cache_lengths,
    enc_lengths,
    bucket_of,
    rel_bias,
    norm_gain,
    self_q,
    self_kv,
    self_out,
    cross_q,
    cross_kv,
    cross_out,
    ff_in,
    ff_out,
):
    blk_count = lax.axis_size("blk")
    heads_dev = H // blk_count
    width_dev = heads_dev * HD
    req_dev = cache_in.shape[0] // lax.axis_size("req")
    own_slot = lax.dynamic_index_in_dim(slot_order, lax.axis_index("req"), 0, keepdims=False)
    tables = jnp.stack([new_lengths, cache_lengths, enc_lengths])
    picked = lax.dynamic_slice_in_dim(tables, own_slot, 1, 1)
    lens = picked.reshape(-1).astype(jnp.int32)
    ordered = jnp.take(cache_in, slot_order, axis=0)
    onehot = (bucket_of[:, None] == jnp.arange(rel_bias.shape[0], dtype=jnp.int32)[None, :]).astype(
        jnp.float32
    )
    own_bias = lax.dynamic_slice_in_dim(rel_bias, lax.axis_index("blk") * heads_dev, heads_dev, 1)
    bias_dist = jnp.dot(onehot, own_bias, precision=lax.Precision.HIGHEST).T
    early = [(self_q, 0), (self_kv, 0), (self_out, 1)]
    late = [(cross_q, 0), (cross_kv, 0), (cross_out, 1), (ff_in, 0), (ff_out, 1)]
    blocks = []
    for w, axis in early:
        two_d = w.reshape(w.shape[0], -1)
        blocks.append(two_d.T if axis == 0 else two_d)
    cache_blk, early_blocks = prologue(ordered, jnp.concatenate(blocks, axis=0))
    cache_dec = cache_blk[None]
    late_blocks = lane_pack(late)
    n_blk = lax.axis_size("blk")
    rows_dev = new_states.shape[0] // n_blk
    own_rows = lax.dynamic_slice_in_dim(
        new_states, chunk_of(lax.axis_index("blk"), n_blk) * rows_dev, rows_dev, 0
    ).astype(jnp.float32)
    part = self_branch(
        new_states,
        norm_gain[0],
        early_blocks,
        block_spans(early),
        cache_blk,
        bias_dist[0],
        lens,
    )
    residual, normed = blk_stage(part, own_rows, norm_gain[1], False)
    spans = block_spans(late)
    part = cross_branch(normed, encoder_out, late_blocks, spans[:3], lens)
    residual, normed = blk_stage(part.astype(jnp.bfloat16), residual, norm_gain[2], False)
    part = ffn_branch(normed, late_blocks, spans[3:])
    _, layer_out = blk_stage(part, residual, norm_gain[2], True)
    return (layer_out, cache_dec)


def solution(mesh):
    in_specs = (
        P("req", None),
        P("req", None),
        P(None, "blk", "req"),
        P(),
        P(),
        P(),
        P(),
        P(),
        P(),
        P(),
        P("req", "blk"),
        P("req", None, "blk"),
        P("blk", "req"),
        P("req", "blk"),
        P("req", None, "blk"),
        P("blk", "req"),
        P("req", None, "blk"),
        P("blk", "req"),
    )
    out_specs = (P("req", None), P("req", None, "blk"))
    return jax.shard_map(
        per_device, mesh=mesh, in_specs=in_specs, out_specs=out_specs, check_vma=False
    )
```

```python
import functools

import jax
import jax.numpy as jnp
from jax import lax
from jax.sharding import PartitionSpec as P
from jax.experimental import pallas as pl
from jax.experimental.pallas import tpu as pltpu

H = 16
HD = 64


EPSILON = 1e-06
NEG_FILL = -1e30


def rms_rows(row_block, gain):
    mean_square = jnp.mean(row_block * row_block, axis=-1, keepdims=True)
    return (row_block * lax.rsqrt(mean_square + EPSILON) * gain).astype(jnp.bfloat16)


def softmax_rows(scores):
    row_top = jnp.max(scores, axis=-1, keepdims=True)
    weights = jnp.exp(scores - row_top)
    return (weights / jnp.sum(weights, axis=-1, keepdims=True)).astype(jnp.bfloat16)


def pick_lengths(table, own_slots):
    matches = own_slots[:, None] == jnp.arange(table.shape[0], dtype=jnp.int32)[None, :]
    return jnp.sum(jnp.where(matches, table[None, :], 0), axis=1)


def shifted_bias(bias_dist, base, row_count, col_count):
    heads_here, span_len = bias_dist.shape
    line_len = row_count + col_count - 1
    steps = jnp.arange(line_len + 1, dtype=jnp.int32)
    line = bias_dist[:, jnp.clip(base + row_count - 1 - steps, 0, span_len - 1)]
    tiled = jnp.broadcast_to(line[:, None, :], (heads_here, row_count, line_len + 1))
    flat = tiled.reshape(heads_here, row_count * (line_len + 1))[:, : row_count * line_len]
    skewed = flat.reshape(heads_here, row_count, line_len)
    return skewed[:, :, row_count - 1 : row_count - 1 + col_count]


def row_total(left, weight):
    term = jnp.dot(left, weight, preferred_element_type=jnp.float32)
    return lax.psum(term.astype(jnp.bfloat16), "blk").astype(jnp.float32)


def cached_scores(queries, key_rows, first_col, old_len, bias_dist):
    col_ids = first_col + jnp.arange(key_rows.shape[0], dtype=jnp.int32)[None, :]
    scores = jnp.einsum("qhe,khe->hqk", queries, key_rows, preferred_element_type=jnp.float32)
    scores = scores + shifted_bias(
        bias_dist, old_len - first_col, queries.shape[0], key_rows.shape[0]
    )
    return jnp.where((col_ids < old_len)[None], scores, NEG_FILL)


def fresh_scores(queries, fresh_keys, fresh_len, bias_dist):
    row_ids = jnp.arange(queries.shape[0], dtype=jnp.int32)[:, None]
    col_ids = jnp.arange(fresh_keys.shape[0], dtype=jnp.int32)[None, :]
    scores = jnp.einsum("qhe,khe->hqk", queries, fresh_keys, preferred_element_type=jnp.float32)
    scores = scores + shifted_bias(bias_dist, 0, queries.shape[0], fresh_keys.shape[0])
    admitted = (col_ids <= row_ids) & (col_ids < fresh_len)
    return jnp.where(admitted[None], scores, NEG_FILL)


def self_padded(
    queries, key_rows, value_rows, fresh_keys, fresh_values, old_len, fresh_len, bias_dist
):
    scores = jnp.concatenate(
        [
            cached_scores(queries, key_rows, 0, old_len, bias_dist),
            fresh_scores(queries, fresh_keys, fresh_len, bias_dist),
        ],
        axis=2,
    )
    weights = softmax_rows(scores)
    value_all = jnp.concatenate([value_rows, fresh_values], axis=0)
    return jnp.einsum(
        "hqk,khe->qhe", weights, value_all, preferred_element_type=jnp.float32
    ).astype(jnp.bfloat16)


def self_attend(queries, key_value, cache_dec, slot_old, slot_new, bias_dist, heads_dev):
    req_dev, cache_len = (cache_dec.shape[0], cache_dec.shape[1])
    cache_split = cache_dec.reshape(req_dev, cache_len, heads_dev, 2, -1)

    def one_request(request):
        queries_one, pair_one, cache_one, old_len, fresh_len = request
        return self_padded(
            queries_one,
            cache_one[:, :, 0],
            cache_one[:, :, 1],
            pair_one[:, 0],
            pair_one[:, 1],
            old_len,
            fresh_len,
            bias_dist,
        )

    return lax.map(one_request, (queries, key_value, cache_split, slot_old, slot_new))


def cross_attend(queries, key_value, slot_enc):
    scores = jnp.einsum(
        "rqhe,rkhe->rhqk", queries, key_value[:, :, 0], preferred_element_type=jnp.float32
    )
    col_ids = jnp.arange(key_value.shape[1], dtype=jnp.int32)
    scores = jnp.where(
        col_ids[None, None, None, :] < slot_enc[:, None, None, None], scores, NEG_FILL
    )
    weights = softmax_rows(scores)
    return jnp.einsum(
        "rhqk,rkhe->rqhe", weights, key_value[:, :, 1], preferred_element_type=jnp.float32
    ).astype(jnp.bfloat16)


def add_branch(residual, left, weight, gain):
    residual = residual + row_total(left, weight)
    normed = rms_rows(residual, gain)
    return (residual, normed)


TQ = 128


def stage_kernel(n_blk, final, extra, *refs):
    if extra:
        (part_ref, resid_ref, gain_ref, packed_ref, res_out, full_ref, wts_ref,
         recv_a, send_b, recv_b, x_send, x_recv, b_send, b_recv, ag_send, ag_recv, w_send, w_recv) = refs
    else:
        (part_ref, resid_ref, gain_ref, res_out, full_ref,
         recv_a, send_b, recv_b, x_send, x_recv, b_send, b_recv, ag_send, ag_recv) = refs
    me = lax.axis_index("blk")
    req = lax.axis_index("req")
    rows = resid_ref.shape[0]
    n_grp = n_blk // 2
    g = me // 2
    c = lax.rem(me, 2)
    partner = g * 2 + 1 - c
    half = n_grp * rows
    n_req = wts_ref.shape[0] if extra else 1
    barrier = pltpu.get_barrier_semaphore()
    for k in range(1, n_grp):
        peer = lax.rem(g + k, n_grp) * 2 + c
        pl.semaphore_signal(barrier, inc=1, device_id=(req, peer), device_id_type=MESH_IDS)
    pl.semaphore_signal(barrier, inc=1, device_id=(req, partner), device_id_type=MESH_IDS)
    for k in range(1, n_req):
        peer = lax.rem(req + k, n_req)
        pl.semaphore_signal(barrier, inc=1, device_id=(peer, me), device_id_type=MESH_IDS)
    pl.semaphore_wait(barrier, n_grp + n_req - 1)
    sends = []
    for k in range(n_grp):
        grp = lax.rem(g + 1 + k, n_grp)
        exchange = pltpu.make_async_remote_copy(
            src_ref=part_ref.at[pl.ds(pl.multiple_of((1 - c) * half + grp * rows, rows), rows)],
            dst_ref=recv_a.at[grp],
            send_sem=x_send.at[k],
            recv_sem=x_recv.at[grp],
            device_id=(req, partner),
            device_id_type=MESH_IDS,
        )
        exchange.start()
        sends.append(exchange)
    for k in range(1, n_req):
        peer = lax.rem(req + k, n_req)
        copy = pltpu.make_async_remote_copy(
            src_ref=packed_ref,
            dst_ref=wts_ref.at[req],
            send_sem=w_send.at[peer],
            recv_sem=w_recv.at[req],
            device_id=(peer, me),
            device_id_type=MESH_IDS,
        )
        copy.start()
        sends.append(copy)
    total = None
    for k in range(n_grp):
        grp = lax.rem(g + 1 + k, n_grp)
        incoming = pltpu.make_async_remote_copy(
            src_ref=part_ref.at[pl.ds(0, rows)],
            dst_ref=recv_a.at[grp],
            send_sem=x_send.at[k],
            recv_sem=x_recv.at[grp],
            device_id=(req, partner),
            device_id_type=MESH_IDS,
        )
        incoming.wait_recv()
        pair = part_ref[pl.ds(pl.multiple_of(c * half + grp * rows, rows), rows), :].astype(
            jnp.float32
        ) + recv_a[grp].astype(jnp.float32)
        if k == n_grp - 1:
            total = pair
        else:
            send_b[grp] = pair.astype(send_b.dtype)
            copy = pltpu.make_async_remote_copy(
                src_ref=send_b.at[grp],
                dst_ref=recv_b.at[g],
                send_sem=b_send.at[grp],
                recv_sem=b_recv.at[g],
                device_id=(req, grp * 2 + c),
                device_id_type=MESH_IDS,
            )
            copy.start()
            sends.append(copy)
    for k in range(1, n_grp):
        grp = lax.rem(g + n_grp - k, n_grp)
        incoming = pltpu.make_async_remote_copy(
            src_ref=send_b.at[0],
            dst_ref=recv_b.at[grp],
            send_sem=b_send.at[grp],
            recv_sem=b_recv.at[grp],
            device_id=(req, grp * 2 + c),
            device_id_type=MESH_IDS,
        )
        incoming.wait_recv()
        total = total + recv_b[grp].astype(jnp.float32)
    mine = pl.ds(pl.multiple_of(c * half + g * rows, rows), rows)
    resid = resid_ref[...] + total
    res_out[...] = resid
    if final:
        full_ref[mine, :] = resid.astype(full_ref.dtype)
    else:
        mean_square = jnp.mean(resid * resid, axis=-1, keepdims=True)
        full_ref[mine, :] = (resid * lax.rsqrt(mean_square + EPSILON) * gain_ref[...]).astype(
            full_ref.dtype
        )
    for k in range(1, n_grp):
        peer = lax.rem(g + k, n_grp) * 2 + c
        copy = pltpu.make_async_remote_copy(
            src_ref=full_ref.at[mine],
            dst_ref=full_ref.at[mine],
            send_sem=ag_send.at[k],
            recv_sem=ag_recv.at[g],
            device_id=(req, peer),
            device_id_type=MESH_IDS,
        )
        copy.start()
        sends.append(copy)
    copy = pltpu.make_async_remote_copy(
        src_ref=full_ref.at[mine],
        dst_ref=full_ref.at[mine],
        send_sem=ag_send.at[0],
        recv_sem=ag_recv.at[n_grp + g],
        device_id=(req, partner),
        device_id_type=MESH_IDS,
    )
    copy.start()
    sends.append(copy)
    for k in range(1, n_grp):
        grp = lax.rem(g + n_grp - k, n_grp)
        there = pl.ds(pl.multiple_of(c * half + grp * rows, rows), rows)
        incoming = pltpu.make_async_remote_copy(
            src_ref=full_ref.at[there],
            dst_ref=full_ref.at[there],
            send_sem=ag_send.at[0],
            recv_sem=ag_recv.at[grp],
            device_id=(req, grp * 2 + c),
            device_id_type=MESH_IDS,
        )
        incoming.wait_recv()
        forward = pltpu.make_async_remote_copy(
            src_ref=full_ref.at[there],
            dst_ref=full_ref.at[there],
            send_sem=ag_send.at[n_grp + k],
            recv_sem=ag_recv.at[n_grp + grp],
            device_id=(req, partner),
            device_id_type=MESH_IDS,
        )
        forward.start()
        sends.append(forward)
    for grp in range(n_grp):
        there = pl.ds(pl.multiple_of((1 - c) * half + grp * rows, rows), rows)
        incoming = pltpu.make_async_remote_copy(
            src_ref=full_ref.at[there],
            dst_ref=full_ref.at[there],
            send_sem=ag_send.at[0],
            recv_sem=ag_recv.at[n_grp + grp],
            device_id=(req, partner),
            device_id_type=MESH_IDS,
        )
        incoming.wait_recv()
    if extra:
        wts_ref[req] = packed_ref[...]
        for k in range(1, n_req):
            src = lax.rem(req + n_req - k, n_req)
            incoming = pltpu.make_async_remote_copy(
                src_ref=packed_ref,
                dst_ref=wts_ref.at[src],
                send_sem=w_send.at[src],
                recv_sem=w_recv.at[src],
                device_id=(src, me),
                device_id_type=MESH_IDS,
            )
            incoming.wait_recv()
    for copy in sends:
        copy.wait_send()


def blk_stage(part, resid, gain, final, packed=None):
    n_blk = lax.axis_size("blk")
    rows, width = resid.shape
    vmem = pl.BlockSpec(memory_space=pltpu.VMEM)
    extra = packed is not None
    outs = [
        jax.ShapeDtypeStruct((rows, width), jnp.float32),
        jax.ShapeDtypeStruct((rows * n_blk, width), jnp.bfloat16),
    ]
    n_grp = n_blk // 2
    scratch = [
        pltpu.VMEM((n_grp, rows, width), part.dtype),
        pltpu.VMEM((n_grp, rows, width), part.dtype),
        pltpu.VMEM((n_grp, rows, width), part.dtype),
        pltpu.SemaphoreType.DMA((n_grp,)),
        pltpu.SemaphoreType.DMA((n_grp,)),
        pltpu.SemaphoreType.DMA((n_grp,)),
        pltpu.SemaphoreType.DMA((n_grp,)),
        pltpu.SemaphoreType.DMA((n_blk,)),
        pltpu.SemaphoreType.DMA((n_blk,)),
    ]
    args = [part, resid, gain[None, :]]
    if extra:
        n_req = lax.axis_size("req")
        outs.append(jax.ShapeDtypeStruct((n_req,) + packed.shape, packed.dtype))
        scratch += [pltpu.SemaphoreType.DMA((n_req,)), pltpu.SemaphoreType.DMA((n_req,))]
        args.append(packed)
    return pl.pallas_call(
        functools.partial(stage_kernel, n_blk, final, extra),
        out_shape=tuple(outs),
        in_specs=[vmem] * len(args),
        out_specs=tuple([vmem] * len(outs)),
        scratch_shapes=scratch,
        compiler_params=pltpu.CompilerParams(
            collective_id=5 if extra else (4 if final else 3),
            has_side_effects=True,
            vmem_limit_bytes=16 * 1024 * 1024,
        ),
    )(*args)


def cross_kernel(n_req, spans, len_ref, normed_ref, enc_ref, w_ref, out_ref):
    enc_len = len_ref[2]
    (q_at, q_len), (kv_at, kv_len), (o_at, o_len) = spans
    nt = (((1,), (1,)), ((), ()))
    width = w_ref.shape[2]
    queries = None
    pair = None
    for r in range(n_req):
        cols = slice(r * width, (r + 1) * width)
        term = lax.dot_general(
            normed_ref[:, cols], w_ref[r, q_at : q_at + q_len, :], nt,
            preferred_element_type=jnp.float32,
        )
        queries = term if queries is None else queries + term
        term = lax.dot_general(
            enc_ref[:, cols], w_ref[r, kv_at : kv_at + kv_len, :], nt,
            preferred_element_type=jnp.float32,
        )
        pair = term if pair is None else pair + term
    queries = queries.astype(jnp.bfloat16)
    pair = pair.astype(jnp.bfloat16)
    keys = pair[:, :HD]
    values = pair[:, HD:]
    scores = lax.dot_general(queries, keys, nt, preferred_element_type=jnp.float32)
    col = lax.broadcasted_iota(jnp.int32, scores.shape, 1)
    scores = jnp.where(col < enc_len, scores, NEG_FILL)
    top = jnp.max(scores, axis=1, keepdims=True)
    weights = jnp.exp(scores - top)
    weights = (weights / jnp.sum(weights, axis=1, keepdims=True)).astype(jnp.bfloat16)
    context = jnp.dot(weights, values, preferred_element_type=jnp.float32).astype(jnp.bfloat16)
    for r in range(n_req):
        out_ref[:, r * width : (r + 1) * width] = jnp.dot(
            context, w_ref[r, o_at : o_at + o_len, :], preferred_element_type=jnp.float32
        ).astype(out_ref.dtype)


def ffn_kernel(n_req, spans, normed_ref, w_ref, out_ref):
    (i_at, i_len), (o_at, o_len) = spans
    nt = (((1,), (1,)), ((), ()))
    width = w_ref.shape[2]
    ff_dev = o_len
    gate_up = None
    for r in range(n_req):
        term = lax.dot_general(
            normed_ref[:, r * width : (r + 1) * width], w_ref[r, i_at : i_at + i_len, :], nt,
            preferred_element_type=jnp.float32,
        )
        gate_up = term if gate_up is None else gate_up + term
    hidden = (jax.nn.gelu(gate_up[:, :ff_dev], approximate=True) * gate_up[:, ff_dev:]).astype(
        jnp.bfloat16
    )
    for r in range(n_req):
        out_ref[:, r * width : (r + 1) * width] = jnp.dot(
            hidden, w_ref[r, o_at : o_at + o_len, :], preferred_element_type=jnp.float32
        ).astype(out_ref.dtype)


def block_spans(pieces):
    spans, at = [], 0
    for w, axis in pieces:
        rows = w.size // w.shape[0] if axis == 0 else w.shape[0]
        spans.append((at, rows))
        at += rows
    return spans


def cross_branch(normed, enc, blocks, spans, enc_len):
    vmem = pl.BlockSpec(memory_space=pltpu.VMEM)
    return pl.pallas_call(
        functools.partial(cross_kernel, blocks.shape[0], tuple(spans)),
        out_shape=jax.ShapeDtypeStruct(normed.shape, jnp.bfloat16),
        in_specs=[pl.BlockSpec(memory_space=pltpu.SMEM)] + [vmem] * 3,
        out_specs=vmem,
        compiler_params=pltpu.CompilerParams(vmem_limit_bytes=16 * 1024 * 1024),
    )(enc_len, normed, enc, blocks)


def ffn_branch(normed, blocks, spans):
    vmem = pl.BlockSpec(memory_space=pltpu.VMEM)
    return pl.pallas_call(
        functools.partial(ffn_kernel, blocks.shape[0], tuple(spans)),
        out_shape=jax.ShapeDtypeStruct(normed.shape, jnp.bfloat16),
        in_specs=[vmem] * 2,
        out_specs=vmem,
        compiler_params=pltpu.CompilerParams(vmem_limit_bytes=16 * 1024 * 1024),
    )(normed, blocks)


def self_kernel(lens_ref, q_ref, c_ref, kn_ref, vn_ref, g_ref, f_ref, o_ref):
    old_len = lens_ref[0]
    fresh_len = lens_ref[1]
    n_q = q_ref.shape[0]
    n_ctx = c_ref.shape[0]
    wide_old = n_ctx + TQ
    wide_new = n_q + TQ
    k_old = c_ref[:, :HD]
    v_old = c_ref[:, HD:]
    k_new = kn_ref[...]
    v_new = vn_ref[...]
    dims = (((1,), (1,)), ((), ()))
    for t in range(n_q // TQ):
        q = q_ref[t * TQ : (t + 1) * TQ, :]
        start = n_q - TQ - t * TQ
        s_old = lax.dot_general(q, k_old, dims, preferred_element_type=jnp.float32)
        line = jnp.broadcast_to(g_ref[:, start : start + wide_old], (TQ, wide_old))
        bias = pltpu.roll(line, wide_old - (TQ - 1), 1, stride=1, stride_axis=0)[:, :n_ctx]
        col = lax.broadcasted_iota(jnp.int32, (TQ, n_ctx), 1)
        s_old = jnp.where(col < old_len, s_old + bias, NEG_FILL)
        s_new = lax.dot_general(q, k_new, dims, preferred_element_type=jnp.float32)
        line = jnp.broadcast_to(f_ref[:, start : start + wide_new], (TQ, wide_new))
        bias = pltpu.roll(line, wide_new - (TQ - 1), 1, stride=1, stride_axis=0)[:, :n_q]
        row = lax.broadcasted_iota(jnp.int32, (TQ, n_q), 0) + t * TQ
        col = lax.broadcasted_iota(jnp.int32, (TQ, n_q), 1)
        s_new = jnp.where((col <= row) & (col < fresh_len), s_new + bias, NEG_FILL)
        top = jnp.maximum(
            jnp.max(s_old, axis=1, keepdims=True), jnp.max(s_new, axis=1, keepdims=True)
        )
        p_old = jnp.exp(s_old - top)
        p_new = jnp.exp(s_new - top)
        total = jnp.sum(p_old, axis=1, keepdims=True) + jnp.sum(p_new, axis=1, keepdims=True)
        w_old = (p_old / total).astype(jnp.bfloat16)
        w_new = (p_new / total).astype(jnp.bfloat16)
        out = jnp.dot(w_old, v_old, preferred_element_type=jnp.float32) + jnp.dot(
            w_new, v_new, preferred_element_type=jnp.float32
        )
        o_ref[t * TQ : (t + 1) * TQ, :] = out.astype(jnp.bfloat16)


def bias_lines(line, old_len, n_q, n_ctx):
    span = line.shape[0]
    ext = jnp.concatenate([jnp.broadcast_to(line[:1], (n_ctx,)), line])
    rev = ext[::-1]
    g = lax.dynamic_slice_in_dim(rev, n_ctx - old_len, span)
    f = rev[n_ctx : n_ctx + 2 * n_q]
    return g[None, :], f[None, :]


def self_attention(q, cache_blk, k_new, v_new, line, old_len, fresh_len):
    n_q = q.shape[0]
    n_ctx = cache_blk.shape[0]
    g, f = bias_lines(line, old_len, n_q, n_ctx)
    lens = jnp.stack([old_len, fresh_len]).astype(jnp.int32)
    vmem = pl.BlockSpec(memory_space=pltpu.VMEM)
    return pl.pallas_call(
        self_kernel,
        out_shape=jax.ShapeDtypeStruct((n_q, HD), jnp.bfloat16),
        in_specs=[pl.BlockSpec(memory_space=pltpu.SMEM)] + [vmem] * 6,
        out_specs=vmem,
        compiler_params=pltpu.CompilerParams(vmem_limit_bytes=24 * 1024 * 1024),
    )(lens, q, cache_blk, k_new, v_new, g, f)


def self_full_kernel(n_req, spans, lens_ref, x_ref, gain_ref, w_ref, c_ref, g_ref, f_ref, o_ref, ctx_ref):
    fresh_len = lens_ref[0]
    old_len = lens_ref[1]
    (q_at, q_len), (kv_at, kv_len), (o_at, o_len) = spans
    nt = (((1,), (1,)), ((), ()))
    width = w_ref.shape[2]
    x = x_ref[...].astype(jnp.float32)
    mean_square = jnp.mean(x * x, axis=-1, keepdims=True)
    normed = (x * lax.rsqrt(mean_square + EPSILON) * gain_ref[...]).astype(jnp.bfloat16)
    queries = None
    pair = None
    for r in range(n_req):
        cols = slice(r * width, (r + 1) * width)
        term = lax.dot_general(
            normed[:, cols], w_ref[r, q_at : q_at + q_len, :], nt,
            preferred_element_type=jnp.float32,
        )
        queries = term if queries is None else queries + term
        term = lax.dot_general(
            normed[:, cols], w_ref[r, kv_at : kv_at + kv_len, :], nt,
            preferred_element_type=jnp.float32,
        )
        pair = term if pair is None else pair + term
    queries = queries.astype(jnp.bfloat16)
    pair = pair.astype(jnp.bfloat16)
    k_new = pair[:, :HD]
    v_new = pair[:, HD:]
    n_q = x_ref.shape[0]
    n_ctx = c_ref.shape[0]
    wide_old = n_ctx + TQ
    wide_new = n_q + TQ
    k_old = c_ref[:, :HD]
    v_old = c_ref[:, HD:]
    for t in range(n_q // TQ):
        q = queries[t * TQ : (t + 1) * TQ, :]
        start = n_q - TQ - t * TQ
        s_old = lax.dot_general(q, k_old, nt, preferred_element_type=jnp.float32)
        line = jnp.broadcast_to(g_ref[:, start : start + wide_old], (TQ, wide_old))
        bias = pltpu.roll(line, wide_old - (TQ - 1), 1, stride=1, stride_axis=0)[:, :n_ctx]
        col = lax.broadcasted_iota(jnp.int32, (TQ, n_ctx), 1)
        s_old = jnp.where(col < old_len, s_old + bias, NEG_FILL)
        s_new = lax.dot_general(q, k_new, nt, preferred_element_type=jnp.float32)
        line = jnp.broadcast_to(f_ref[:, start : start + wide_new], (TQ, wide_new))
        bias = pltpu.roll(line, wide_new - (TQ - 1), 1, stride=1, stride_axis=0)[:, :n_q]
        row = lax.broadcasted_iota(jnp.int32, (TQ, n_q), 0) + t * TQ
        col = lax.broadcasted_iota(jnp.int32, (TQ, n_q), 1)
        s_new = jnp.where((col <= row) & (col < fresh_len), s_new + bias, NEG_FILL)
        top = jnp.maximum(
            jnp.max(s_old, axis=1, keepdims=True), jnp.max(s_new, axis=1, keepdims=True)
        )
        p_old = jnp.exp(s_old - top)
        p_new = jnp.exp(s_new - top)
        total = jnp.sum(p_old, axis=1, keepdims=True) + jnp.sum(p_new, axis=1, keepdims=True)
        w_old = (p_old / total).astype(jnp.bfloat16)
        w_new = (p_new / total).astype(jnp.bfloat16)
        out = jnp.dot(w_old, v_old, preferred_element_type=jnp.float32) + jnp.dot(
            w_new, v_new, preferred_element_type=jnp.float32
        )
        ctx_ref[t * TQ : (t + 1) * TQ, :] = out.astype(jnp.bfloat16)
    context = ctx_ref[...]
    for r in range(n_req):
        o_ref[:, r * width : (r + 1) * width] = jnp.dot(
            context, w_ref[r, o_at : o_at + o_len, :], preferred_element_type=jnp.float32
        ).astype(o_ref.dtype)


def self_branch(states, gain, blocks, spans, cache_blk, line, lens):
    n_q = states.shape[0]
    n_ctx = cache_blk.shape[0]
    g, f = bias_lines(line, lens[1], n_q, n_ctx)
    vmem = pl.BlockSpec(memory_space=pltpu.VMEM)
    return pl.pallas_call(
        functools.partial(self_full_kernel, blocks.shape[0], tuple(spans)),
        out_shape=jax.ShapeDtypeStruct(states.shape, jnp.bfloat16),
        in_specs=[pl.BlockSpec(memory_space=pltpu.SMEM)] + [vmem] * 6,
        out_specs=vmem,
        scratch_shapes=[pltpu.VMEM((n_q, HD), jnp.bfloat16)],
        compiler_params=pltpu.CompilerParams(vmem_limit_bytes=24 * 1024 * 1024),
    )(lens, states, gain[None, :], blocks, cache_blk, g, f)


def pack_gather(pieces):
    flat = jnp.concatenate([w.reshape(-1) for w, _ in pieces])
    whole = lax.all_gather(flat, "req", axis=0, tiled=False)
    n_req = whole.shape[0]
    out, at = [], 0
    for w, axis in pieces:
        size = w.size
        part = whole[:, at : at + size].reshape((n_req,) + w.shape)
        at += size
        part = jnp.moveaxis(part, 0, axis)
        shape = list(w.shape)
        shape[axis] *= n_req
        out.append(part.reshape(shape))
    return out


MESH_IDS = pl.DeviceIdType.MESH


def greet_all(n_blk, me, req):
    barrier = pltpu.get_barrier_semaphore()
    for k in range(1, n_blk):
        peer = lax.rem(me + k, n_blk)
        pl.semaphore_signal(barrier, inc=1, device_id=(req, peer), device_id_type=MESH_IDS)
    pl.semaphore_wait(barrier, n_blk - 1)


def chunk_of(b, n_blk):
    return lax.rem(b, 2) * (n_blk // 2) + b // 2


def scatter_kernel(n_blk, part_ref, out_ref, recv, send_sem, recv_sem):
    me = lax.axis_index("blk")
    req = lax.axis_index("req")
    rows = out_ref.shape[0]
    greet_all(n_blk, me, req)
    copies = []
    for k in range(1, n_blk):
        peer = lax.rem(me + k, n_blk)
        copy = pltpu.make_async_remote_copy(
            src_ref=part_ref.at[pl.ds(pl.multiple_of(chunk_of(peer, n_blk) * rows, rows), rows)],
            dst_ref=recv.at[me],
            send_sem=send_sem.at[peer],
            recv_sem=recv_sem.at[me],
            device_id=(req, peer),
            device_id_type=MESH_IDS,
        )
        copy.start()
        copies.append(copy)
    own = pl.ds(pl.multiple_of(chunk_of(me, n_blk) * rows, rows), rows)
    total = part_ref[own, :].astype(jnp.float32)
    for k in range(1, n_blk):
        src = lax.rem(me + n_blk - k, n_blk)
        incoming = pltpu.make_async_remote_copy(
            src_ref=part_ref.at[pl.ds(0, rows)],
            dst_ref=recv.at[src],
            send_sem=send_sem.at[src],
            recv_sem=recv_sem.at[src],
            device_id=(req, src),
            device_id_type=MESH_IDS,
        )
        incoming.wait_recv()
        total = total + recv[src].astype(jnp.float32)
    for copy in copies:
        copy.wait_send()
    out_ref[...] = total


def gather_kernel(n_blk, piece_ref, out_ref, send_sem, recv_sem):
    b = lax.axis_index("blk")
    req = lax.axis_index("req")
    n_grp = n_blk // 2
    g = b // 2
    c = lax.rem(b, 2)
    partner = g * 2 + 1 - c
    rows = piece_ref.shape[0]
    half = n_grp * rows
    barrier = pltpu.get_barrier_semaphore()
    for k in range(1, n_grp):
        peer = lax.rem(g + k, n_grp) * 2 + c
        pl.semaphore_signal(barrier, inc=1, device_id=(req, peer), device_id_type=MESH_IDS)
    pl.semaphore_signal(barrier, inc=1, device_id=(req, partner), device_id_type=MESH_IDS)
    pl.semaphore_wait(barrier, n_grp)
    mine = pl.ds(pl.multiple_of(c * half + g * rows, rows), rows)
    sends = []
    for k in range(1, n_grp):
        peer = lax.rem(g + k, n_grp) * 2 + c
        copy = pltpu.make_async_remote_copy(
            src_ref=piece_ref,
            dst_ref=out_ref.at[mine],
            send_sem=send_sem.at[k],
            recv_sem=recv_sem.at[g],
            device_id=(req, peer),
            device_id_type=MESH_IDS,
        )
        copy.start()
        sends.append(copy)
    copy = pltpu.make_async_remote_copy(
        src_ref=piece_ref,
        dst_ref=out_ref.at[mine],
        send_sem=send_sem.at[0],
        recv_sem=recv_sem.at[n_grp + g],
        device_id=(req, partner),
        device_id_type=MESH_IDS,
    )
    copy.start()
    sends.append(copy)
    out_ref[mine, :] = piece_ref[...]
    for k in range(1, n_grp):
        grp = lax.rem(g + n_grp - k, n_grp)
        there = pl.ds(pl.multiple_of(c * half + grp * rows, rows), rows)
        incoming = pltpu.make_async_remote_copy(
            src_ref=piece_ref,
            dst_ref=out_ref.at[there],
            send_sem=send_sem.at[0],
            recv_sem=recv_sem.at[grp],
            device_id=(req, grp * 2 + c),
            device_id_type=MESH_IDS,
        )
        incoming.wait_recv()
        forward = pltpu.make_async_remote_copy(
            src_ref=out_ref.at[there],
            dst_ref=out_ref.at[there],
            send_sem=send_sem.at[n_grp + k],
            recv_sem=recv_sem.at[n_grp + grp],
            device_id=(req, partner),
            device_id_type=MESH_IDS,
        )
        forward.start()
        sends.append(forward)
    for grp in range(n_grp):
        there = pl.ds(pl.multiple_of((1 - c) * half + grp * rows, rows), rows)
        incoming = pltpu.make_async_remote_copy(
            src_ref=piece_ref,
            dst_ref=out_ref.at[there],
            send_sem=send_sem.at[0],
            recv_sem=recv_sem.at[n_grp + grp],
            device_id=(req, partner),
            device_id_type=MESH_IDS,
        )
        incoming.wait_recv()
    for copy in sends:
        copy.wait_send()


def blk_scatter(part):
    n_blk = lax.axis_size("blk")
    rows = part.shape[0] // n_blk
    vmem = pl.BlockSpec(memory_space=pltpu.VMEM)
    return pl.pallas_call(
        functools.partial(scatter_kernel, n_blk),
        out_shape=jax.ShapeDtypeStruct((rows, part.shape[1]), jnp.float32),
        in_specs=[vmem],
        out_specs=vmem,
        scratch_shapes=[
            pltpu.VMEM((n_blk, rows, part.shape[1]), part.dtype),
            pltpu.SemaphoreType.DMA((n_blk,)),
            pltpu.SemaphoreType.DMA((n_blk,)),
        ],
        compiler_params=pltpu.CompilerParams(collective_id=1, has_side_effects=True),
    )(part)


def blk_gather(piece):
    n_blk = lax.axis_size("blk")
    rows = piece.shape[0]
    vmem = pl.BlockSpec(memory_space=pltpu.VMEM)
    return pl.pallas_call(
        functools.partial(gather_kernel, n_blk),
        out_shape=jax.ShapeDtypeStruct((rows * n_blk, piece.shape[1]), piece.dtype),
        in_specs=[vmem],
        out_specs=vmem,
        scratch_shapes=[
            pltpu.SemaphoreType.DMA((n_blk,)),
            pltpu.SemaphoreType.DMA((n_blk,)),
        ],
        compiler_params=pltpu.CompilerParams(collective_id=2, has_side_effects=True),
    )(piece)


def prologue_kernel(n_req, n_blk, ordered_ref, packed_ref, cache_ref, wts_ref, w_send, w_recv, c_send, c_recv, local_sem):
    r = lax.axis_index("req")
    b = lax.axis_index("blk")
    n_slot, span, width = ordered_ref.shape
    piece = width // 2
    copies = []
    for k in range(1, n_req):
        peer = lax.rem(r + k, n_req)
        copy = pltpu.make_async_remote_copy(
            src_ref=packed_ref,
            dst_ref=wts_ref.at[r],
            send_sem=w_send.at[peer],
            recv_sem=w_recv.at[r],
            device_id=(peer, b),
            device_id_type=MESH_IDS,
        )
        copy.start()
        copies.append(copy)
    rows = pl.ds(pl.multiple_of(b * span, span), span)
    for k in range(n_slot):
        s = lax.rem(b + k, n_slot)
        for hh in range(2):
            head = 2 * r + hh
            is_self = jnp.logical_and(r == s, head == b)
            src = ordered_ref.at[s, :, pl.ds(hh * piece, piece)]
            copy = pltpu.make_async_remote_copy(
                src_ref=src,
                dst_ref=cache_ref.at[rows],
                send_sem=c_send.at[k * 2 + hh],
                recv_sem=c_recv.at[b],
                device_id=(s, head),
                device_id_type=MESH_IDS,
            )

            @pl.when(jnp.logical_not(is_self))
            def _():
                copy.start()

            @pl.when(is_self)
            def _():
                local = pltpu.make_async_copy(src, cache_ref.at[rows], local_sem.at[0])
                local.start()
                local.wait()

            copies.append((copy, is_self))
    wts_ref[r] = packed_ref[...]
    for k in range(1, n_req):
        src_req = lax.rem(r + n_req - k, n_req)
        incoming = pltpu.make_async_remote_copy(
            src_ref=packed_ref,
            dst_ref=wts_ref.at[src_req],
            send_sem=w_send.at[src_req],
            recv_sem=w_recv.at[src_req],
            device_id=(src_req, b),
            device_id_type=MESH_IDS,
        )
        incoming.wait_recv()
    owner = b // 2
    for j in range(n_blk):
        incoming = pltpu.make_async_remote_copy(
            src_ref=ordered_ref.at[0, :, pl.ds(0, piece)],
            dst_ref=cache_ref.at[pl.ds(j * span, span)],
            send_sem=c_send.at[0],
            recv_sem=c_recv.at[j],
            device_id=(owner, j),
            device_id_type=MESH_IDS,
        )

        @pl.when(jnp.logical_not(jnp.logical_and(owner == r, j == b)))
        def _():
            incoming.wait_recv()

    for item in copies:
        if isinstance(item, tuple):
            copy, is_self = item

            @pl.when(jnp.logical_not(is_self))
            def _():
                copy.wait_send()

        else:
            item.wait_send()


def prologue(ordered, packed):
    n_req = lax.axis_size("req")
    n_blk = lax.axis_size("blk")
    n_slot, span, width = ordered.shape
    any_spec = pl.BlockSpec(memory_space=pl.ANY)
    vmem = pl.BlockSpec(memory_space=pltpu.VMEM)
    return pl.pallas_call(
        functools.partial(prologue_kernel, n_req, n_blk),
        out_shape=(
            jax.ShapeDtypeStruct((span * n_blk, width // 2), ordered.dtype),
            jax.ShapeDtypeStruct((n_req,) + packed.shape, packed.dtype),
        ),
        in_specs=[any_spec, vmem],
        out_specs=(any_spec, vmem),
        scratch_shapes=[
            pltpu.SemaphoreType.DMA((n_req,)),
            pltpu.SemaphoreType.DMA((n_req,)),
            pltpu.SemaphoreType.DMA((2 * n_slot,)),
            pltpu.SemaphoreType.DMA((n_blk,)),
            pltpu.SemaphoreType.DMA((1,)),
        ],
        compiler_params=pltpu.CompilerParams(
            has_side_effects=True, vmem_limit_bytes=32 * 1024 * 1024
        ),
    )(ordered, packed)


def unpack(whole, pieces):
    n_req = whole.shape[0]
    whole = whole.reshape(n_req, -1)
    out, at = [], 0
    for w, axis in pieces:
        size = w.size
        part = whole[:, at : at + size].reshape((n_req,) + w.shape)
        at += size
        part = jnp.moveaxis(part, 0, axis)
        shape = list(w.shape)
        shape[axis] *= n_req
        out.append(part.reshape(shape))
    return out


def lane_pack(pieces):
    blocks = []
    for w, axis in pieces:
        flat = w.reshape(w.shape[0], -1)
        blocks.append(flat.T if axis == 0 else flat)
    packed = jnp.concatenate(blocks, axis=0)
    return lax.all_gather(packed, "req", axis=0, tiled=False)


def per_device(
    new_states,
    encoder_out,
    cache_in,
    slot_order,
    new_lengths,
    cache_lengths,
    enc_lengths,
    bucket_of,
    rel_bias,
    norm_gain,
    self_q,
    self_kv,
    self_out,
    cross_q,
    cross_kv,
    cross_out,
    ff_in,
    ff_out,
):
    blk_count = lax.axis_size("blk")
    heads_dev = H // blk_count
    width_dev = heads_dev * HD
    req_dev = cache_in.shape[0] // lax.axis_size("req")
    own_slot = lax.dynamic_index_in_dim(slot_order, lax.axis_index("req"), 0, keepdims=False)
    tables = jnp.stack([new_lengths, cache_lengths, enc_lengths])
    picked = lax.dynamic_slice_in_dim(tables, own_slot, 1, 1)
    lens = picked.reshape(-1).astype(jnp.int32)
    ordered = jnp.take(cache_in, slot_order, axis=0)
    onehot = (bucket_of[:, None] == jnp.arange(rel_bias.shape[0], dtype=jnp.int32)[None, :]).astype(
        jnp.float32
    )
    own_bias = lax.dynamic_slice_in_dim(rel_bias, lax.axis_index("blk") * heads_dev, heads_dev, 1)
    bias_dist = jnp.dot(onehot, own_bias, precision=lax.Precision.HIGHEST).T
    early = [(self_q, 0), (self_kv, 0), (self_out, 1)]
    late = [(cross_q, 0), (cross_kv, 0), (cross_out, 1), (ff_in, 0), (ff_out, 1)]
    blocks = []
    for w, axis in early:
        two_d = w.reshape(w.shape[0], -1)
        blocks.append(two_d.T if axis == 0 else two_d)
    cache_blk, early_blocks = prologue(ordered, jnp.concatenate(blocks, axis=0))
    cache_dec = cache_blk[None]
    late_blocks = lane_pack(late)
    n_blk = lax.axis_size("blk")
    rows_dev = new_states.shape[0] // n_blk
    own_rows = lax.dynamic_slice_in_dim(
        new_states, chunk_of(lax.axis_index("blk"), n_blk) * rows_dev, rows_dev, 0
    ).astype(jnp.float32)
    part = self_branch(
        new_states,
        norm_gain[0],
        early_blocks,
        block_spans(early),
        cache_blk,
        bias_dist[0],
        lens,
    )
    residual, normed = blk_stage(part, own_rows, norm_gain[1], False)
    spans = block_spans(late)
    part = cross_branch(normed, encoder_out, late_blocks, spans[:3], lens)
    residual, normed = blk_stage(part.astype(jnp.bfloat16), residual, norm_gain[2], False)
    part = ffn_branch(normed, late_blocks, spans[3:])
    _, layer_out = blk_stage(part, residual, norm_gain[2], True)
    return (layer_out, cache_dec)


def solution(mesh):
    in_specs = (
        P("req", None),
        P("req", None),
        P(None, "blk", "req"),
        P(),
        P(),
        P(),
        P(),
        P(),
        P(),
        P(),
        P("req", "blk"),
        P("req", None, "blk"),
        P("blk", "req"),
        P("req", "blk"),
        P("req", None, "blk"),
        P("blk", "req"),
        P("req", None, "blk"),
        P("blk", "req"),
    )
    out_specs = (P("req", None), P("req", None, "blk"))
    return jax.shard_map(
        per_device, mesh=mesh, in_specs=in_specs, out_specs=out_specs, check_vma=False
    )
```
